128 devices in a mesh: grp: 16 (over z, y), tp: 8 (over x, core).
Axes of the slice: x: 4, y: 4, z: 4, core: 2. Of those that a mesh axis runs over, the one named last changes fastest.
Arguments:
- tokens: bfloat16 [1024, 4, 8192], P('grp', None, 'tp'), may hold values from -6 to 6
- adapter_id: int32 [1024], P('grp'), may hold values from 0 to 127, as said below
- pool_slot: int32 [128], replicated, may hold values from 0 to 127, as said below
- lengths: int32 [1024], P('grp'), may hold values from 1 to 64, as said below
- w_query: bfloat16 [8192, 8192], P(None, 'tp'), may hold values from -0.0625 to 0.0625
- w_key: bfloat16 [8192, 1024], P(None, 'tp'), may hold values from -0.0625 to 0.0625
- w_value: bfloat16 [8192, 1024], P(None, 'tp'), may hold values from -0.0625 to 0.0625
- pooled_down_weights: bfloat16 [128, 8192, 64], P('grp', 'tp'), may hold values from -0.0625 to 0.0625
- pool_up: bfloat16 [128, 64, 8192], P('grp', None, 'tp'), may hold values from -0.75 to 0.75
- cache_key: bfloat16 [1024, 64, 1024], P('grp', None, 'tp')
- cache_value: bfloat16 [1024, 64, 1024], P('grp', None, 'tp'), may hold values from -6 to 6
Outputs:
- attended: bfloat16 [1024, 4, 8192], P('grp', None, 'tp')
The draws below stay inside these ranges and needn't reach their ends.
Inputs may be any that keep to these rules, and one draw needn't show every extreme that they name: `adapter_id`: each aligned block of 64 rows (one group) uses adapters of exactly 8 owners (owner = pool_slot // 8), 8 rows each, and at most 2 distinct adapters of one owner, reached in every block; a single owner, the same for all blocks, serves 8 rows of every block. `pool_slot`: A permutation. `lengths`: each aligned block of 64 rows has a row of length 64.
All inputs are finite; a program needn't handle non-finite values.
Results may differ from the reference program's by a relative error of at most 0.012.
The reference program's roundings to bfloat16 on the way count: a program that leaves them out, or rounds other values in their place, can miss the bound.
Values may be sent and summed in bfloat16 or wider, within the bound.
A program may use at most 128 MiB of HBM per device.

```python
import math
import jax
import jax.numpy as jnp
from jax import lax

D = 8192
QH = 64
KVH = 8
HD = 128
R = 64
ROWS_GRP = 64
LEN = 64
ADP_GRP = 8
STEPS = 4
CAP = 8
ROWS_ALL = 1024
ADAPTERS = 128
N_GRP = 16


def routing(key):
    pool_order = jax.random.permutation(jax.random.fold_in(key, 11), ADAPTERS).astype(jnp.int32)
    inverse = jnp.zeros((ADAPTERS,), jnp.int32).at[pool_order].set(jnp.arange(ADAPTERS, dtype=jnp.int32))
    hot_owner = jax.random.randint(jax.random.fold_in(key, 12), (), 0, N_GRP).astype(jnp.int32)
    count_of_blocks = ROWS_GRP // CAP

    def one_group(group_key):
        keys = jax.random.split(group_key, 5)
        others = jax.random.permutation(keys[0], N_GRP - 1).astype(jnp.int32) + 1
        shifted = jnp.concatenate([jnp.zeros((1,), jnp.int32), others])
        owners = (hot_owner + shifted) % N_GRP
        first_slot = jax.random.randint(keys[1], (count_of_blocks,), 0, ADP_GRP).astype(jnp.int32)
        second_slot = (first_slot + jax.random.randint(keys[2], (count_of_blocks,), 1, ADP_GRP).astype(jnp.int32)) % ADP_GRP
        row_rank = jnp.arange(ROWS_GRP, dtype=jnp.int32) % CAP
        row_block = jnp.arange(ROWS_GRP, dtype=jnp.int32) // CAP
        coin_flip = jax.random.randint(keys[3], (ROWS_GRP,), 0, 2).astype(jnp.int32)
        chosen = jnp.where(row_rank == 0, 0, jnp.where(row_rank == 1, 1, coin_flip))
        slot_here = jnp.where(chosen == 0, first_slot[row_block], second_slot[row_block])
        pool_pos = owners[row_block] * ADP_GRP + slot_here
        shuffle = jax.random.permutation(keys[4], ROWS_GRP)
        return inverse[pool_pos[shuffle]]
    group_keys = jax.random.split(jax.random.fold_in(key, 13), N_GRP)
    identity = jax.vmap(one_group)(group_keys).reshape(-1).astype(jnp.int32)
    return (identity, pool_order)


def draw_adapter_id(key, part):
    return routing(key)[0]


def draw_pool_slot(key, part):
    return routing(key)[1]


def draw_lengths(key, part):
    base = jax.random.randint(jax.random.fold_in(key, 21), (N_GRP, ROWS_GRP), 1, LEN + 1).astype(jnp.int32)
    longest = jax.random.randint(jax.random.fold_in(key, 22), (N_GRP,), 0, ROWS_GRP).astype(jnp.int32)
    base = jnp.where(jnp.arange(ROWS_GRP, dtype=jnp.int32)[None, :] == longest[:, None], LEN, base)
    return base.reshape(-1).astype(jnp.int32)


def draw_cache_key(key, part):
    base = jax.random.normal(jax.random.fold_in(key, 31), (ROWS_ALL, LEN, KVH * HD), jnp.float32)
    return base.astype(jnp.bfloat16)


def shard_levels(key, shape, cuts, least, high):
    factor_of = 1.0
    for axis_at, blocks in cuts:
        heights = jax.random.uniform(jax.random.fold_in(jax.random.fold_in(key, 6), axis_at), (blocks,), jnp.float32, least / len(cuts), high / len(cuts))
        factor_of = factor_of * jnp.repeat(jnp.exp(heights), shape[axis_at] // blocks).reshape((-1,) + (1,) * (len(shape) - 1 - axis_at))
    return factor_of


def bell_draw(rng, shape, deviation, reach, cuts=(), kind=jnp.bfloat16):
    entries = jax.random.normal(rng, shape, jnp.float32) * deviation
    if len(cuts) > 0:
        entries = shard_levels(rng, shape, cuts, -0.22, 0.18) * entries
    return jnp.clip(entries, min=-reach, max=reach).astype(kind)


def setup_inputs(seed: int = 0) -> dict:
    splits = jax.random.split(jax.random.key(seed), 12)
    return {
        "tokens": bell_draw(splits[0], (ROWS_ALL, STEPS, D), 1.0, 6.0, ((0, 16), (2, 8))),
        "adapter_id": draw_adapter_id(jax.random.fold_in(splits[11], 71), 0),
        "pool_slot": draw_pool_slot(jax.random.fold_in(splits[11], 71), 0),
        "lengths": draw_lengths(jax.random.fold_in(splits[11], 71), 0),
        "w_query": bell_draw(splits[4], (D, QH * HD), D ** -0.5, 0.0625, ((1, 8),)),
        "w_key": bell_draw(splits[5], (D, KVH * HD), D ** -0.5, 0.0625, ((1, 8),)),
        "w_value": bell_draw(splits[6], (D, KVH * HD), D ** -0.5, 0.0625, ((1, 8),)),
        "pooled_down_weights": bell_draw(splits[7], (ADAPTERS, D, R), D ** -0.5, 0.0625, ((0, 16), (1, 8))),
        "pool_up": bell_draw(splits[8], (ADAPTERS, R, QH * HD), R ** -0.5, 0.75, ((0, 16), (2, 8))),
        "cache_key": draw_cache_key(jax.random.fold_in(splits[11], 71), 0),
        "cache_value": bell_draw(splits[10], (ROWS_ALL, LEN, KVH * HD), 1.0, 6.0, ((0, 16), (2, 8))),
    }


rope_base = 500000.0

def rotate(values, position):
    half_width = values.shape[-1] // 2
    inv_freq = jnp.exp(jnp.arange(half_width, dtype=jnp.float32) * (-2.0 * math.log(rope_base) / values.shape[-1]))
    angles = position.astype(jnp.float32)[:, :, None, None] * inv_freq
    cosine = jnp.cos(angles)
    sines = jnp.sin(angles)
    front_half = values[..., :half_width]
    back_half = values[..., half_width:]
    return jnp.concatenate([front_half * cosine - back_half * sines, back_half * cosine + front_half * sines], axis=-1)

def attend(queries, key_new, value_new, cache_key, cache_value, lengths):
    score_scale = 1.0 / math.sqrt(queries.shape[-1])
    cached = jnp.einsum('rskgd,rlkd->rskgl', queries.astype(jnp.float32), cache_key.astype(jnp.float32)) * score_scale
    fresh_scores = jnp.einsum('rskgd,rtkd->rskgt', queries.astype(jnp.float32), key_new.astype(jnp.float32)) * score_scale
    live_mask = jnp.arange(cache_key.shape[1], dtype=jnp.int32)[None, :] < lengths[:, None]
    cached = jnp.where(live_mask[:, None, None, None, :], cached, -1e+30)
    steps_here = key_new.shape[1]
    causal = jnp.arange(steps_here, dtype=jnp.int32)[:, None] >= jnp.arange(steps_here, dtype=jnp.int32)[None, :]
    fresh_scores = jnp.where(causal[None, :, None, None, :], fresh_scores, -1e+30)
    row_max = jnp.maximum(lax.optimization_barrier(jnp.max(cached, axis=-1)), lax.optimization_barrier(jnp.max(fresh_scores, axis=-1)))
    cache_exp = jnp.exp(cached - row_max[..., None])
    fresh_exp = jnp.exp(fresh_scores - row_max[..., None])
    weight_sum = lax.optimization_barrier(jnp.sum(cache_exp, axis=-1)) + lax.optimization_barrier(jnp.sum(fresh_exp, axis=-1))
    cache_weights = lax.optimization_barrier((cache_exp / weight_sum[..., None]).astype(jnp.bfloat16))
    fresh_weights = lax.optimization_barrier((fresh_exp / weight_sum[..., None]).astype(jnp.bfloat16))
    combined = jnp.einsum('rskgl,rlkd->rskgd', cache_weights.astype(jnp.float32), cache_value.astype(jnp.float32))
    combined = combined + jnp.einsum('rskgt,rtkd->rskgd', fresh_weights.astype(jnp.float32), value_new.astype(jnp.float32))
    return combined.astype(jnp.bfloat16)

def reference(tokens, adapter_id, pool_slot, lengths, w_query, w_key, w_value, pooled_down_weights, pool_up, cache_key, cache_value):
    group_size = QH // KVH

    def group_step(packed):
        tokens_per_group, group_ids, group_lengths, group_keys, group_values = packed
        pool_pos = pool_slot[group_ids]
        down_weight_panels = pooled_down_weights[pool_pos].astype(jnp.float32)
        up_weight_panels = pool_up[pool_pos].astype(jnp.float32)
        adapter_middle = lax.optimization_barrier(jnp.einsum('kjq,kqt->kjt', tokens_per_group.astype(jnp.float32), down_weight_panels).astype(jnp.bfloat16))
        adapter_output = lax.optimization_barrier(jnp.einsum('jzy,jya->jza', adapter_middle.astype(jnp.float32), up_weight_panels).astype(jnp.bfloat16))
        token_rows = tokens_per_group.reshape(ROWS_GRP * STEPS, D)
        base_query_rows = jnp.dot(token_rows, w_query, preferred_element_type=jnp.float32).reshape(ROWS_GRP, STEPS, QH * HD)
        base_query_rows = base_query_rows + adapter_output.astype(jnp.float32)
        key_base = jnp.dot(token_rows, w_key, preferred_element_type=jnp.float32)
        value_base = jnp.dot(token_rows, w_value, preferred_element_type=jnp.float32)
        position = group_lengths[:, None] + jnp.arange(STEPS, dtype=jnp.int32)[None, :]
        queries = rotate(base_query_rows.reshape(ROWS_GRP, STEPS, QH, HD), position)
        queries = lax.optimization_barrier(queries.astype(jnp.bfloat16)).reshape(ROWS_GRP, STEPS, KVH, group_size, HD)
        key_new = lax.optimization_barrier(rotate(key_base.reshape(ROWS_GRP, STEPS, KVH, HD), position).astype(jnp.bfloat16))
        value_new = lax.optimization_barrier(value_base.reshape(ROWS_GRP, STEPS, KVH, HD).astype(jnp.bfloat16))
        combined = attend(queries, key_new, value_new, group_keys, group_values, group_lengths)
        return combined.reshape(ROWS_GRP, STEPS, QH * HD)
    packed = (tokens.reshape(N_GRP, ROWS_GRP, STEPS, D), adapter_id.reshape(N_GRP, ROWS_GRP), lengths.reshape(N_GRP, ROWS_GRP), cache_key.reshape(N_GRP, ROWS_GRP, LEN, KVH, HD), cache_value.reshape(N_GRP, ROWS_GRP, LEN, KVH, HD))
    return lax.map(group_step, packed).reshape(ROWS_ALL, STEPS, QH * HD)
```

```python
import math

import jax
import jax.numpy as jnp
from jax import lax
from jax.sharding import PartitionSpec as P

HD = 128
CAP = 8


rope_base = 500000.0


def rotate(values, position):
    half_width = values.shape[-1] // 2
    inv_freq = jnp.exp(
        jnp.arange(half_width, dtype=jnp.float32) * (-2.0 * math.log(rope_base) / values.shape[-1])
    )
    angles = position.astype(jnp.float32)[:, :, None, None] * inv_freq
    cosine = jnp.cos(angles)
    sines = jnp.sin(angles)
    front_half = values[..., :half_width]
    back_half = values[..., half_width:]
    return jnp.concatenate(
        [front_half * cosine - back_half * sines, back_half * cosine + front_half * sines], axis=-1
    )


def attend(queries, key_new, value_new, cache_key, cache_value, lengths):
    score_scale = 1.0 / math.sqrt(queries.shape[-1])
    cached = (
        jnp.einsum("rskgd,rlkd->rskgl", queries, cache_key, preferred_element_type=jnp.float32)
        * score_scale
    )
    fresh_scores = (
        jnp.einsum("rskgd,rtkd->rskgt", queries, key_new, preferred_element_type=jnp.float32)
        * score_scale
    )
    live_mask = jnp.arange(cache_key.shape[1], dtype=jnp.int32)[None, :] < lengths[:, None]
    cached = jnp.where(live_mask[:, None, None, None, :], cached, -1e30)
    steps_here = key_new.shape[1]
    causal = (
        jnp.arange(steps_here, dtype=jnp.int32)[:, None]
        >= jnp.arange(steps_here, dtype=jnp.int32)[None, :]
    )
    fresh_scores = jnp.where(causal[None, :, None, None, :], fresh_scores, -1e30)
    row_max = jnp.maximum(jnp.max(cached, axis=-1), jnp.max(fresh_scores, axis=-1))
    cache_exp = jnp.exp(cached - row_max[..., None])
    fresh_exp = jnp.exp(fresh_scores - row_max[..., None])
    weight_sum = jnp.sum(cache_exp, axis=-1) + jnp.sum(fresh_exp, axis=-1)
    cache_weights = (cache_exp / weight_sum[..., None]).astype(jnp.bfloat16)
    fresh_weights = (fresh_exp / weight_sum[..., None]).astype(jnp.bfloat16)
    combined = jnp.einsum(
        "rskgl,rlkd->rskgd", cache_weights, cache_value, preferred_element_type=jnp.float32
    )
    combined = combined + jnp.einsum(
        "rskgt,rtkd->rskgd", fresh_weights, value_new, preferred_element_type=jnp.float32
    )
    return combined.astype(jnp.bfloat16)


def owner_adapter_term(received, slot_ids, down_local, up_local):
    sources, rows, part_width = received.shape
    local_adapters, unused_item, adapter_rank = down_local.shape
    query_width = up_local.shape[2]
    token_rows = received.reshape(sources * rows, part_width)
    every_down = jnp.einsum(
        "td,adr->tar", token_rows, down_local, preferred_element_type=jnp.float32
    )
    pick = slot_ids.reshape(sources * rows)[:, None] == jnp.arange(local_adapters, dtype=jnp.int32)[None, :]
    partial_value_sum = jnp.sum(jnp.where(pick[:, :, None], every_down, 0.0), axis=1)
    adapter_middle = lax.optimization_barrier(lax.psum(partial_value_sum, "tp")).astype(jnp.bfloat16)
    spread_rows = jnp.where(pick[:, :, None], adapter_middle[:, None, :], jnp.zeros((), jnp.bfloat16))
    spread_rows = spread_rows.reshape(sources * rows, local_adapters * adapter_rank)
    adapter_output = jnp.dot(
        spread_rows,
        up_local.reshape(local_adapters * adapter_rank, query_width),
        preferred_element_type=jnp.float32,
    ).astype(jnp.bfloat16)
    return adapter_output.reshape(sources, rows, query_width)


def body(
    tokens,
    adapter_id,
    pool_slot,
    lengths,
    w_query,
    w_key,
    w_value,
    pooled_down_weights,
    pool_up,
    cache_key,
    cache_value,
):
    group_count = lax.axis_size("grp")
    tp_count = lax.axis_size("tp")
    row_count, step_count, part_width = tokens.shape
    local_adapter_rows, unused_item, adapter_rank = pooled_down_weights.shape
    query_width = w_query.shape[1]
    kv_width = w_key.shape[1]
    kv_local = kv_width // HD
    q_local = query_width // HD
    group_size = q_local // kv_local
    count_of_tokens = row_count * step_count
    adapter_span = jnp.arange(pool_slot.shape[0], dtype=jnp.int32)
    pool_pos = jnp.sum(
        jnp.where(adapter_id[:, None] == adapter_span[None, :], pool_slot[None, :], 0), axis=1
    )
    owner_grp = pool_pos // local_adapter_rows
    local_slot = pool_pos % local_adapter_rows
    row_span = jnp.arange(row_count, dtype=jnp.int32)
    same_owner = (owner_grp[:, None] == owner_grp[None, :]) & (row_span[None, :] < row_span[:, None])
    owner_rank = jnp.sum(same_owner.astype(jnp.int32), axis=1)
    send_slot = owner_grp * CAP + owner_rank
    slot_span = jnp.arange(group_count * CAP, dtype=jnp.int32)
    place = (slot_span[:, None] == send_slot[None, :]).astype(jnp.bfloat16)
    token_flat = tokens.reshape(row_count, step_count * part_width)
    send_tokens = jnp.dot(place, token_flat, preferred_element_type=jnp.float32).astype(jnp.bfloat16)
    send_ids = jnp.dot(
        place, local_slot.astype(jnp.bfloat16)[:, None], preferred_element_type=jnp.float32
    ).astype(jnp.bfloat16)
    send_ids = jnp.broadcast_to(send_ids, (group_count * CAP, 128))
    packed = jnp.concatenate(
        [
            send_tokens.reshape(group_count, CAP * step_count * part_width),
            send_ids.reshape(group_count, CAP * 128),
        ],
        axis=1,
    )
    got = lax.all_to_all(packed, "grp", split_axis=0, concat_axis=0, tiled=True)
    got_tokens = got[:, : CAP * step_count * part_width].reshape(
        group_count, CAP * step_count, part_width
    )
    got_ids = got[:, CAP * step_count * part_width :].reshape(group_count, CAP, 128)[:, :, 0]
    got_ids = jnp.repeat(got_ids.astype(jnp.int32), step_count, axis=1)
    owner_out = owner_adapter_term(got_tokens, got_ids, pooled_down_weights, pool_up)
    back = lax.all_to_all(
        owner_out.reshape(group_count, CAP * step_count * query_width),
        "grp",
        split_axis=0,
        concat_axis=0,
        tiled=True,
    )
    back = back.reshape(group_count * CAP, step_count * query_width)
    adapter_output = jnp.dot(
        jnp.transpose(place), back, preferred_element_type=jnp.float32
    ).reshape(count_of_tokens, query_width)

    pieces = lax.all_gather(tokens.reshape(count_of_tokens, part_width), "tp", axis=0, tiled=False)

    def add_term(matrix):
        return jnp.einsum(
            "ptd,pdo->to",
            pieces,
            matrix.reshape(tp_count, part_width, matrix.shape[1]),
            preferred_element_type=jnp.float32,
        )

    base_query_rows = add_term(w_query)
    key_base = add_term(w_key)
    value_base = add_term(w_value)
    base_query_rows = base_query_rows + adapter_output
    position = lengths[:, None] + jnp.arange(step_count, dtype=jnp.int32)[None, :]
    queries = rotate(base_query_rows.reshape(row_count, step_count, q_local, HD), position)
    queries = queries.astype(jnp.bfloat16).reshape(row_count, step_count, kv_local, group_size, HD)
    key_new = rotate(key_base.reshape(row_count, step_count, kv_local, HD), position).astype(
        jnp.bfloat16
    )
    value_new = value_base.reshape(row_count, step_count, kv_local, HD).astype(jnp.bfloat16)
    cache_keys = cache_key.reshape(row_count, cache_key.shape[1], kv_local, HD)
    cache_values = cache_value.reshape(row_count, cache_value.shape[1], kv_local, HD)
    combined = attend(queries, key_new, value_new, cache_keys, cache_values, lengths)
    return combined.reshape(row_count, step_count, query_width)


def solution(mesh):
    in_specs = (
        P("grp", None, "tp"),
        P("grp"),
        P(),
        P("grp"),
        P(None, "tp"),
        P(None, "tp"),
        P(None, "tp"),
        P("grp", "tp", None),
        P("grp", None, "tp"),
        P("grp", None, "tp"),
        P("grp", None, "tp"),
    )
    out_specs = P("grp", None, "tp")
    return jax.shard_map(body, mesh=mesh, in_specs=in_specs, out_specs=out_specs, check_vma=False)
```

```python
import math

import jax
import jax.numpy as jnp
from jax import lax
from jax.experimental import pallas as pl
from jax.experimental.pallas import tpu as pltpu
from jax.sharding import PartitionSpec as P

MESH = pl.DeviceIdType.MESH

HD = 128
CAP = 8


rope_base = 500000.0


def rotate(values, position):
    half_width = values.shape[-1] // 2
    inv_freq = jnp.exp(
        jnp.arange(half_width, dtype=jnp.float32) * (-2.0 * math.log(rope_base) / values.shape[-1])
    )
    angles = position.astype(jnp.float32)[:, :, None, None] * inv_freq
    cosine = jnp.cos(angles)
    sines = jnp.sin(angles)
    front_half = values[..., :half_width]
    back_half = values[..., half_width:]
    return jnp.concatenate(
        [front_half * cosine - back_half * sines, back_half * cosine + front_half * sines], axis=-1
    )


def attend(queries, key_new, value_new, cache_key, cache_value, lengths):
    score_scale = 1.0 / math.sqrt(queries.shape[-1])
    cached = (
        jnp.einsum("rskgd,rlkd->rskgl", queries, cache_key, preferred_element_type=jnp.float32)
        * score_scale
    )
    fresh_scores = (
        jnp.einsum("rskgd,rtkd->rskgt", queries, key_new, preferred_element_type=jnp.float32)
        * score_scale
    )
    live_mask = jnp.arange(cache_key.shape[1], dtype=jnp.int32)[None, :] < lengths[:, None]
    cached = jnp.where(live_mask[:, None, None, None, :], cached, -1e30)
    steps_here = key_new.shape[1]
    causal = (
        jnp.arange(steps_here, dtype=jnp.int32)[:, None]
        >= jnp.arange(steps_here, dtype=jnp.int32)[None, :]
    )
    fresh_scores = jnp.where(causal[None, :, None, None, :], fresh_scores, -1e30)
    row_max = jnp.maximum(jnp.max(cached, axis=-1), jnp.max(fresh_scores, axis=-1))
    cache_exp = jnp.exp(cached - row_max[..., None])
    fresh_exp = jnp.exp(fresh_scores - row_max[..., None])
    weight_sum = jnp.sum(cache_exp, axis=-1) + jnp.sum(fresh_exp, axis=-1)
    cache_weights = (cache_exp / weight_sum[..., None]).astype(jnp.bfloat16)
    fresh_weights = (fresh_exp / weight_sum[..., None]).astype(jnp.bfloat16)
    combined = jnp.einsum(
        "rskgl,rlkd->rskgd", cache_weights, cache_value, preferred_element_type=jnp.float32
    )
    combined = combined + jnp.einsum(
        "rskgt,rtkd->rskgd", fresh_weights, value_new, preferred_element_type=jnp.float32
    )
    return combined.astype(jnp.bfloat16)


def exchange_kernel(axis, count, send_ref, got_ref, send_sem, recv_sem, local_sem):
    me = lax.axis_index(axis)
    barrier = pltpu.get_barrier_semaphore()
    for offset in range(1, count):
        peer = lax.rem(me + offset, count)
        pl.semaphore_signal(barrier, inc=1, device_id={axis: peer}, device_id_type=MESH)
    pl.semaphore_wait(barrier, count - 1)
    local = pltpu.make_async_copy(send_ref.at[me], got_ref.at[me], local_sem)
    local.start()
    outgoing = []
    for offset in range(1, count):
        peer = lax.rem(me + offset, count)
        copy = pltpu.make_async_remote_copy(
            src_ref=send_ref.at[peer],
            dst_ref=got_ref.at[me],
            send_sem=send_sem.at[offset],
            recv_sem=recv_sem.at[offset],
            device_id={axis: peer},
            device_id_type=MESH,
        )
        copy.start()
        outgoing.append(copy)
    for offset in range(1, count):
        outgoing[offset - 1].wait_send()
        source = lax.rem(me + count - offset, count)
        incoming = pltpu.make_async_remote_copy(
            src_ref=send_ref.at[source],
            dst_ref=got_ref.at[source],
            send_sem=send_sem.at[offset],
            recv_sem=recv_sem.at[offset],
            device_id={axis: source},
            device_id_type=MESH,
        )
        incoming.wait_recv()
    local.wait()


def exchange(values, axis, count, collective):
    return pl.pallas_call(
        lambda *refs: exchange_kernel(axis, count, *refs),
        out_shape=jax.ShapeDtypeStruct(values.shape, values.dtype),
        in_specs=[pl.BlockSpec(memory_space=pltpu.VMEM)],
        out_specs=pl.BlockSpec(memory_space=pltpu.VMEM),
        scratch_shapes=[
            pltpu.SemaphoreType.DMA((count,)),
            pltpu.SemaphoreType.DMA((count,)),
            pltpu.SemaphoreType.DMA(()),
        ],
        compiler_params=pltpu.CompilerParams(collective_id=collective, has_side_effects=True),
    )(values)


def sum_kernel(axis, count, part_ref, total_ref, held, send_sem, recv_sem):
    me = lax.axis_index(axis)
    barrier = pltpu.get_barrier_semaphore()
    for offset in range(1, count):
        peer = lax.rem(me + offset, count)
        pl.semaphore_signal(barrier, inc=1, device_id={axis: peer}, device_id_type=MESH)
    pl.semaphore_wait(barrier, count - 1)
    outgoing = []
    for offset in range(1, count):
        peer = lax.rem(me + offset, count)
        copy = pltpu.make_async_remote_copy(
            src_ref=part_ref,
            dst_ref=held.at[me],
            send_sem=send_sem.at[offset],
            recv_sem=recv_sem.at[offset],
            device_id={axis: peer},
            device_id_type=MESH,
        )
        copy.start()
        outgoing.append(copy)
    held[me] = part_ref[...]
    for offset in range(1, count):
        outgoing[offset - 1].wait_send()
        source = lax.rem(me + count - offset, count)
        incoming = pltpu.make_async_remote_copy(
            src_ref=part_ref,
            dst_ref=held.at[source],
            send_sem=send_sem.at[offset],
            recv_sem=recv_sem.at[offset],
            device_id={axis: source},
            device_id_type=MESH,
        )
        incoming.wait_recv()
    total = held[0]
    for index in range(1, count):
        total = total + held[index]
    total_ref[...] = total.astype(total_ref.dtype)


def axis_sum(values, axis, count, collective, out_dtype):
    return pl.pallas_call(
        lambda *refs: sum_kernel(axis, count, *refs),
        out_shape=jax.ShapeDtypeStruct(values.shape, out_dtype),
        in_specs=[pl.BlockSpec(memory_space=pltpu.VMEM)],
        out_specs=pl.BlockSpec(memory_space=pltpu.VMEM),
        scratch_shapes=[
            pltpu.VMEM((count,) + values.shape, values.dtype),
            pltpu.SemaphoreType.DMA((count,)),
            pltpu.SemaphoreType.DMA((count,)),
        ],
        compiler_params=pltpu.CompilerParams(collective_id=collective, has_side_effects=True),
    )(values)


def owner_adapter_term(received, slot_ids, down_local, up_local):
    sources, rows, part_width = received.shape
    local_adapters, unused_item, adapter_rank = down_local.shape
    query_width = up_local.shape[2]
    token_rows = received.reshape(sources * rows, part_width)
    every_down = jnp.einsum(
        "td,adr->tar", token_rows, down_local, preferred_element_type=jnp.float32
    )
    pick = slot_ids.reshape(sources * rows)[:, None] == jnp.arange(local_adapters, dtype=jnp.int32)[None, :]
    partial_value_sum = jnp.sum(jnp.where(pick[:, :, None], every_down, 0.0), axis=1)
    tp_count = lax.axis_size("tp")
    summed = axis_sum(partial_value_sum.reshape(-1, 128), "tp", tp_count, 2, jnp.bfloat16)
    adapter_middle = summed.reshape(sources * rows, adapter_rank)
    spread_rows = jnp.where(pick[:, :, None], adapter_middle[:, None, :], jnp.zeros((), jnp.bfloat16))
    spread_rows = spread_rows.reshape(sources * rows, local_adapters * adapter_rank)
    adapter_output = jnp.dot(
        spread_rows,
        up_local.reshape(local_adapters * adapter_rank, query_width),
        preferred_element_type=jnp.float32,
    ).astype(jnp.bfloat16)
    return adapter_output.reshape(sources, rows, query_width)


def body(
    tokens,
    adapter_id,
    pool_slot,
    lengths,
    w_query,
    w_key,
    w_value,
    pooled_down_weights,
    pool_up,
    cache_key,
    cache_value,
):
    group_count = lax.axis_size("grp")
    tp_count = lax.axis_size("tp")
    row_count, step_count, part_width = tokens.shape
    local_adapter_rows, unused_item, adapter_rank = pooled_down_weights.shape
    query_width = w_query.shape[1]
    kv_width = w_key.shape[1]
    kv_local = kv_width // HD
    q_local = query_width // HD
    group_size = q_local // kv_local
    count_of_tokens = row_count * step_count
    adapter_span = jnp.arange(pool_slot.shape[0], dtype=jnp.int32)
    pool_pos = jnp.sum(
        jnp.where(adapter_id[:, None] == adapter_span[None, :], pool_slot[None, :], 0), axis=1
    )
    owner_grp = pool_pos // local_adapter_rows
    local_slot = pool_pos % local_adapter_rows
    row_span = jnp.arange(row_count, dtype=jnp.int32)
    same_owner = (owner_grp[:, None] == owner_grp[None, :]) & (row_span[None, :] < row_span[:, None])
    owner_rank = jnp.sum(same_owner.astype(jnp.int32), axis=1)
    send_slot = owner_grp * CAP + owner_rank
    slot_span = jnp.arange(group_count * CAP, dtype=jnp.int32)
    place = (slot_span[:, None] == send_slot[None, :]).astype(jnp.bfloat16)
    token_flat = tokens.reshape(row_count, step_count * part_width)
    send_tokens = jnp.dot(place, token_flat, preferred_element_type=jnp.float32).astype(jnp.bfloat16)
    send_ids = jnp.dot(
        place, local_slot.astype(jnp.bfloat16)[:, None], preferred_element_type=jnp.float32
    ).astype(jnp.bfloat16)
    send_ids = jnp.broadcast_to(
        send_ids.reshape(group_count * CAP, 1, 1), (group_count * CAP, step_count, 128)
    )
    packed = jnp.concatenate(
        [send_tokens.reshape(group_count * CAP, step_count, part_width), send_ids], axis=2
    ).reshape(group_count, CAP * step_count, part_width + 128)
    got = exchange(packed, "grp", group_count, 0)
    got_tokens = got[:, :, :part_width]
    got_ids = got[:, :, part_width].astype(jnp.int32)
    owner_out = owner_adapter_term(got_tokens, got_ids, pooled_down_weights, pool_up)
    back = exchange(owner_out, "grp", group_count, 1)
    back = back.reshape(group_count * CAP, step_count * query_width)
    adapter_output = jnp.dot(
        jnp.transpose(place), back, preferred_element_type=jnp.float32
    ).reshape(count_of_tokens, query_width)

    pieces = lax.all_gather(tokens.reshape(count_of_tokens, part_width), "tp", axis=0, tiled=False)

    def add_term(matrix):
        return jnp.einsum(
            "ptd,pdo->to",
            pieces,
            matrix.reshape(tp_count, part_width, matrix.shape[1]),
            preferred_element_type=jnp.float32,
        )

    base_query_rows = add_term(w_query)
    key_base = add_term(w_key)
    value_base = add_term(w_value)
    base_query_rows = base_query_rows + adapter_output
    position = lengths[:, None] + jnp.arange(step_count, dtype=jnp.int32)[None, :]
    queries = rotate(base_query_rows.reshape(row_count, step_count, q_local, HD), position)
    queries = queries.astype(jnp.bfloat16).reshape(row_count, step_count, kv_local, group_size, HD)
    key_new = rotate(key_base.reshape(row_count, step_count, kv_local, HD), position).astype(
        jnp.bfloat16
    )
    value_new = value_base.reshape(row_count, step_count, kv_local, HD).astype(jnp.bfloat16)
    cache_keys = cache_key.reshape(row_count, cache_key.shape[1], kv_local, HD)
    cache_values = cache_value.reshape(row_count, cache_value.shape[1], kv_local, HD)
    combined = attend(queries, key_new, value_new, cache_keys, cache_values, lengths)
    return combined.reshape(row_count, step_count, query_width)


def solution(mesh):
    in_specs = (
        P("grp", None, "tp"),
        P("grp"),
        P(),
        P("grp"),
        P(None, "tp"),
        P(None, "tp"),
        P(None, "tp"),
        P("grp", "tp", None),
        P("grp", None, "tp"),
        P("grp", None, "tp"),
        P("grp", None, "tp"),
    )
    out_specs = P("grp", None, "tp")
    return jax.shard_map(body, mesh=mesh, in_specs=in_specs, out_specs=out_specs, check_vma=False)
```

```python
import math

import jax
import jax.numpy as jnp
from jax import lax
from jax.experimental import pallas as pl
from jax.experimental.pallas import tpu as pltpu
from jax.sharding import PartitionSpec as P

MESH = pl.DeviceIdType.MESH

HD = 128
CAP = 8


rope_base = 500000.0


def rotate(values, position):
    half_width = values.shape[-1] // 2
    inv_freq = jnp.exp(
        jnp.arange(half_width, dtype=jnp.float32) * (-2.0 * math.log(rope_base) / values.shape[-1])
    )
    angles = position.astype(jnp.float32)[:, :, None, None] * inv_freq
    cosine = jnp.cos(angles)
    sines = jnp.sin(angles)
    front_half = values[..., :half_width]
    back_half = values[..., half_width:]
    return jnp.concatenate(
        [front_half * cosine - back_half * sines, back_half * cosine + front_half * sines], axis=-1
    )


def attend(queries, key_new, value_new, cache_key, cache_value, lengths):
    score_scale = 1.0 / math.sqrt(queries.shape[-1])
    cached = (
        jnp.einsum("rskgd,rlkd->rskgl", queries, cache_key, preferred_element_type=jnp.float32)
        * score_scale
    )
    fresh_scores = (
        jnp.einsum("rskgd,rtkd->rskgt", queries, key_new, preferred_element_type=jnp.float32)
        * score_scale
    )
    live_mask = jnp.arange(cache_key.shape[1], dtype=jnp.int32)[None, :] < lengths[:, None]
    cached = jnp.where(live_mask[:, None, None, None, :], cached, -1e30)
    steps_here = key_new.shape[1]
    causal = (
        jnp.arange(steps_here, dtype=jnp.int32)[:, None]
        >= jnp.arange(steps_here, dtype=jnp.int32)[None, :]
    )
    fresh_scores = jnp.where(causal[None, :, None, None, :], fresh_scores, -1e30)
    row_max = jnp.maximum(jnp.max(cached, axis=-1), jnp.max(fresh_scores, axis=-1))
    cache_exp = jnp.exp(cached - row_max[..., None])
    fresh_exp = jnp.exp(fresh_scores - row_max[..., None])
    weight_sum = jnp.sum(cache_exp, axis=-1) + jnp.sum(fresh_exp, axis=-1)
    cache_weights = (cache_exp / weight_sum[..., None]).astype(jnp.bfloat16)
    fresh_weights = (fresh_exp / weight_sum[..., None]).astype(jnp.bfloat16)
    combined = jnp.einsum(
        "rskgl,rlkd->rskgd", cache_weights, cache_value, preferred_element_type=jnp.float32
    )
    combined = combined + jnp.einsum(
        "rskgt,rtkd->rskgd", fresh_weights, value_new, preferred_element_type=jnp.float32
    )
    return combined.astype(jnp.bfloat16)


def exchange_kernel(axis, count, send_ref, got_ref, send_sem, recv_sem, local_sem):
    me = lax.axis_index(axis)
    barrier = pltpu.get_barrier_semaphore()
    for offset in range(1, count):
        peer = lax.rem(me + offset, count)
        pl.semaphore_signal(barrier, inc=1, device_id={axis: peer}, device_id_type=MESH)
    pl.semaphore_wait(barrier, count - 1)
    local = pltpu.make_async_copy(send_ref.at[me], got_ref.at[me], local_sem)
    local.start()
    outgoing = []
    for offset in range(1, count):
        peer = lax.rem(me + offset, count)
        copy = pltpu.make_async_remote_copy(
            src_ref=send_ref.at[peer],
            dst_ref=got_ref.at[me],
            send_sem=send_sem.at[offset],
            recv_sem=recv_sem.at[offset],
            device_id={axis: peer},
            device_id_type=MESH,
        )
        copy.start()
        outgoing.append(copy)
    for offset in range(1, count):
        outgoing[offset - 1].wait_send()
        source = lax.rem(me + count - offset, count)
        incoming = pltpu.make_async_remote_copy(
            src_ref=send_ref.at[source],
            dst_ref=got_ref.at[source],
            send_sem=send_sem.at[offset],
            recv_sem=recv_sem.at[offset],
            device_id={axis: source},
            device_id_type=MESH,
        )
        incoming.wait_recv()
    local.wait()


def exchange(values, axis, count, collective):
    return pl.pallas_call(
        lambda *refs: exchange_kernel(axis, count, *refs),
        out_shape=jax.ShapeDtypeStruct(values.shape, values.dtype),
        in_specs=[pl.BlockSpec(memory_space=pltpu.VMEM)],
        out_specs=pl.BlockSpec(memory_space=pltpu.VMEM),
        scratch_shapes=[
            pltpu.SemaphoreType.DMA((count,)),
            pltpu.SemaphoreType.DMA((count,)),
            pltpu.SemaphoreType.DMA(()),
        ],
        compiler_params=pltpu.CompilerParams(collective_id=collective, has_side_effects=True),
    )(values)


def sum_kernel(axis, count, part_ref, total_ref, held, first_send, first_recv, second_send, second_recv):
    me = lax.axis_index(axis)
    barrier = pltpu.get_barrier_semaphore()
    for offset in range(1, count):
        peer = lax.rem(me + offset, count)
        pl.semaphore_signal(barrier, inc=1, device_id={axis: peer}, device_id_type=MESH)
    pl.semaphore_wait(barrier, count - 1)
    outgoing = []
    for offset in range(1, count):
        peer = lax.rem(me + offset, count)
        copy = pltpu.make_async_remote_copy(
            src_ref=part_ref.at[peer],
            dst_ref=held.at[me],
            send_sem=first_send.at[offset],
            recv_sem=first_recv.at[offset],
            device_id={axis: peer},
            device_id_type=MESH,
        )
        copy.start()
        outgoing.append(copy)
    held[me] = part_ref[me]
    for offset in range(1, count):
        outgoing[offset - 1].wait_send()
        source = lax.rem(me + count - offset, count)
        incoming = pltpu.make_async_remote_copy(
            src_ref=part_ref.at[source],
            dst_ref=held.at[source],
            send_sem=first_send.at[offset],
            recv_sem=first_recv.at[offset],
            device_id={axis: source},
            device_id_type=MESH,
        )
        incoming.wait_recv()
    total = held[0]
    for index in range(1, count):
        total = total + held[index]
    total_ref[me] = total.astype(total_ref.dtype)
    outgoing = []
    for offset in range(1, count):
        peer = lax.rem(me + offset, count)
        copy = pltpu.make_async_remote_copy(
            src_ref=total_ref.at[me],
            dst_ref=total_ref.at[me],
            send_sem=second_send.at[offset],
            recv_sem=second_recv.at[offset],
            device_id={axis: peer},
            device_id_type=MESH,
        )
        copy.start()
        outgoing.append(copy)
    for offset in range(1, count):
        outgoing[offset - 1].wait_send()
        source = lax.rem(me + count - offset, count)
        incoming = pltpu.make_async_remote_copy(
            src_ref=total_ref.at[source],
            dst_ref=total_ref.at[source],
            send_sem=second_send.at[offset],
            recv_sem=second_recv.at[offset],
            device_id={axis: source},
            device_id_type=MESH,
        )
        incoming.wait_recv()


def axis_sum(values, axis, count, collective, out_dtype):
    chunks = values.reshape(count, -1, 128)
    summed = pl.pallas_call(
        lambda *refs: sum_kernel(axis, count, *refs),
        out_shape=jax.ShapeDtypeStruct(chunks.shape, out_dtype),
        in_specs=[pl.BlockSpec(memory_space=pltpu.VMEM)],
        out_specs=pl.BlockSpec(memory_space=pltpu.VMEM),
        scratch_shapes=[
            pltpu.VMEM(chunks.shape, values.dtype),
            pltpu.SemaphoreType.DMA((count,)),
            pltpu.SemaphoreType.DMA((count,)),
            pltpu.SemaphoreType.DMA((count,)),
            pltpu.SemaphoreType.DMA((count,)),
        ],
        compiler_params=pltpu.CompilerParams(collective_id=collective, has_side_effects=True),
    )(chunks)
    return summed.reshape(values.shape)


def owner_adapter_term(received, slot_ids, down_local, up_local):
    sources, rows, part_width = received.shape
    local_adapters, unused_item, adapter_rank = down_local.shape
    query_width = up_local.shape[2]
    token_rows = received.reshape(sources * rows, part_width)
    every_down = jnp.einsum(
        "td,adr->tar", token_rows, down_local, preferred_element_type=jnp.float32
    )
    pick = slot_ids.reshape(sources * rows)[:, None] == jnp.arange(local_adapters, dtype=jnp.int32)[None, :]
    partial_value_sum = jnp.sum(jnp.where(pick[:, :, None], every_down, 0.0), axis=1)
    tp_count = lax.axis_size("tp")
    summed = axis_sum(partial_value_sum.reshape(-1, 128), "tp", tp_count, 2, jnp.bfloat16)
    adapter_middle = summed.reshape(sources * rows, adapter_rank)
    spread_rows = jnp.where(pick[:, :, None], adapter_middle[:, None, :], jnp.zeros((), jnp.bfloat16))
    spread_rows = spread_rows.reshape(sources * rows, local_adapters * adapter_rank)
    adapter_output = jnp.dot(
        spread_rows,
        up_local.reshape(local_adapters * adapter_rank, query_width),
        preferred_element_type=jnp.float32,
    ).astype(jnp.bfloat16)
    return adapter_output.reshape(sources, rows, query_width)


def body(
    tokens,
    adapter_id,
    pool_slot,
    lengths,
    w_query,
    w_key,
    w_value,
    pooled_down_weights,
    pool_up,
    cache_key,
    cache_value,
):
    group_count = lax.axis_size("grp")
    tp_count = lax.axis_size("tp")
    row_count, step_count, part_width = tokens.shape
    local_adapter_rows, unused_item, adapter_rank = pooled_down_weights.shape
    query_width = w_query.shape[1]
    kv_width = w_key.shape[1]
    kv_local = kv_width // HD
    q_local = query_width // HD
    group_size = q_local // kv_local
    count_of_tokens = row_count * step_count
    adapter_span = jnp.arange(pool_slot.shape[0], dtype=jnp.int32)
    pool_pos = jnp.sum(
        jnp.where(adapter_id[:, None] == adapter_span[None, :], pool_slot[None, :], 0), axis=1
    )
    owner_grp = pool_pos // local_adapter_rows
    local_slot = pool_pos % local_adapter_rows
    row_span = jnp.arange(row_count, dtype=jnp.int32)
    same_owner = (owner_grp[:, None] == owner_grp[None, :]) & (row_span[None, :] < row_span[:, None])
    owner_rank = jnp.sum(same_owner.astype(jnp.int32), axis=1)
    send_slot = owner_grp * CAP + owner_rank
    slot_span = jnp.arange(group_count * CAP, dtype=jnp.int32)
    place = (slot_span[:, None] == send_slot[None, :]).astype(jnp.bfloat16)
    token_flat = tokens.reshape(row_count, step_count * part_width)
    send_tokens = jnp.dot(place, token_flat, preferred_element_type=jnp.float32).astype(jnp.bfloat16)
    send_ids = jnp.dot(
        place, local_slot.astype(jnp.bfloat16)[:, None], preferred_element_type=jnp.float32
    ).astype(jnp.bfloat16)
    send_ids = jnp.broadcast_to(
        send_ids.reshape(group_count * CAP, 1, 1), (group_count * CAP, step_count, 128)
    )
    packed = jnp.concatenate(
        [send_tokens.reshape(group_count * CAP, step_count, part_width), send_ids], axis=2
    ).reshape(group_count, CAP * step_count, part_width + 128)
    got = exchange(packed, "grp", group_count, 0)
    got_tokens = got[:, :, :part_width]
    got_ids = got[:, :, part_width].astype(jnp.int32)
    owner_out = owner_adapter_term(got_tokens, got_ids, pooled_down_weights, pool_up)
    back = exchange(owner_out, "grp", group_count, 1)
    back = back.reshape(group_count * CAP, step_count * query_width)
    adapter_output = jnp.dot(
        jnp.transpose(place), back, preferred_element_type=jnp.float32
    ).reshape(count_of_tokens, query_width)

    pieces = lax.all_gather(tokens.reshape(count_of_tokens, part_width), "tp", axis=0, tiled=False)

    def add_term(matrix):
        return jnp.einsum(
            "ptd,pdo->to",
            pieces,
            matrix.reshape(tp_count, part_width, matrix.shape[1]),
            preferred_element_type=jnp.float32,
        )

    base_query_rows = add_term(w_query)
    key_base = add_term(w_key)
    value_base = add_term(w_value)
    base_query_rows = base_query_rows + adapter_output
    position = lengths[:, None] + jnp.arange(step_count, dtype=jnp.int32)[None, :]
    queries = rotate(base_query_rows.reshape(row_count, step_count, q_local, HD), position)
    queries = queries.astype(jnp.bfloat16).reshape(row_count, step_count, kv_local, group_size, HD)
    key_new = rotate(key_base.reshape(row_count, step_count, kv_local, HD), position).astype(
        jnp.bfloat16
    )
    value_new = value_base.reshape(row_count, step_count, kv_local, HD).astype(jnp.bfloat16)
    cache_keys = cache_key.reshape(row_count, cache_key.shape[1], kv_local, HD)
    cache_values = cache_value.reshape(row_count, cache_value.shape[1], kv_local, HD)
    combined = attend(queries, key_new, value_new, cache_keys, cache_values, lengths)
    return combined.reshape(row_count, step_count, query_width)


def solution(mesh):
    in_specs = (
        P("grp", None, "tp"),
        P("grp"),
        P(),
        P("grp"),
        P(None, "tp"),
        P(None, "tp"),
        P(None, "tp"),
        P("grp", "tp", None),
        P("grp", None, "tp"),
        P("grp", None, "tp"),
        P("grp", None, "tp"),
    )
    out_specs = P("grp", None, "tp")
    return jax.shard_map(body, mesh=mesh, in_specs=in_specs, out_specs=out_specs, check_vma=False)
```

```python
import math

import jax
import jax.numpy as jnp
from jax import lax
from jax.experimental import pallas as pl
from jax.experimental.pallas import tpu as pltpu
from jax.sharding import PartitionSpec as P

MESH = pl.DeviceIdType.MESH

HD = 128
CAP = 8


rope_base = 500000.0


def rotate(values, position):
    half_width = values.shape[-1] // 2
    inv_freq = jnp.exp(
        jnp.arange(half_width, dtype=jnp.float32) * (-2.0 * math.log(rope_base) / values.shape[-1])
    )
    angles = position.astype(jnp.float32)[:, :, None, None] * inv_freq
    cosine = jnp.cos(angles)
    sines = jnp.sin(angles)
    front_half = values[..., :half_width]
    back_half = values[..., half_width:]
    return jnp.concatenate(
        [front_half * cosine - back_half * sines, back_half * cosine + front_half * sines], axis=-1
    )


def attend(queries, key_new, value_new, cache_key, cache_value, lengths):
    score_scale = 1.0 / math.sqrt(queries.shape[-1])
    cached = (
        jnp.einsum("rskgd,rlkd->rskgl", queries, cache_key, preferred_element_type=jnp.float32)
        * score_scale
    )
    fresh_scores = (
        jnp.einsum("rskgd,rtkd->rskgt", queries, key_new, preferred_element_type=jnp.float32)
        * score_scale
    )
    live_mask = jnp.arange(cache_key.shape[1], dtype=jnp.int32)[None, :] < lengths[:, None]
    cached = jnp.where(live_mask[:, None, None, None, :], cached, -1e30)
    steps_here = key_new.shape[1]
    causal = (
        jnp.arange(steps_here, dtype=jnp.int32)[:, None]
        >= jnp.arange(steps_here, dtype=jnp.int32)[None, :]
    )
    fresh_scores = jnp.where(causal[None, :, None, None, :], fresh_scores, -1e30)
    row_max = jnp.maximum(jnp.max(cached, axis=-1), jnp.max(fresh_scores, axis=-1))
    cache_exp = jnp.exp(cached - row_max[..., None])
    fresh_exp = jnp.exp(fresh_scores - row_max[..., None])
    weight_sum = jnp.sum(cache_exp, axis=-1) + jnp.sum(fresh_exp, axis=-1)
    cache_weights = (cache_exp / weight_sum[..., None]).astype(jnp.bfloat16)
    fresh_weights = (fresh_exp / weight_sum[..., None]).astype(jnp.bfloat16)
    combined = jnp.einsum(
        "rskgl,rlkd->rskgd", cache_weights, cache_value, preferred_element_type=jnp.float32
    )
    combined = combined + jnp.einsum(
        "rskgt,rtkd->rskgd", fresh_weights, value_new, preferred_element_type=jnp.float32
    )
    return combined.astype(jnp.bfloat16)


def exchange_kernel(axis, count, send_ref, got_ref, send_sem, recv_sem, local_sem):
    me = lax.axis_index(axis)
    barrier = pltpu.get_barrier_semaphore()
    for offset in range(1, count):
        peer = lax.rem(me + offset, count)
        pl.semaphore_signal(barrier, inc=1, device_id={axis: peer}, device_id_type=MESH)
    pl.semaphore_wait(barrier, count - 1)
    local = pltpu.make_async_copy(send_ref.at[me], got_ref.at[me], local_sem)
    local.start()
    outgoing = []
    for offset in range(1, count):
        peer = lax.rem(me + offset, count)
        copy = pltpu.make_async_remote_copy(
            src_ref=send_ref.at[peer],
            dst_ref=got_ref.at[me],
            send_sem=send_sem.at[offset],
            recv_sem=recv_sem.at[offset],
            device_id={axis: peer},
            device_id_type=MESH,
        )
        copy.start()
        outgoing.append(copy)
    for offset in range(1, count):
        outgoing[offset - 1].wait_send()
        source = lax.rem(me + count - offset, count)
        incoming = pltpu.make_async_remote_copy(
            src_ref=send_ref.at[source],
            dst_ref=got_ref.at[source],
            send_sem=send_sem.at[offset],
            recv_sem=recv_sem.at[offset],
            device_id={axis: source},
            device_id_type=MESH,
        )
        incoming.wait_recv()
    local.wait()


def exchange(values, axis, count, collective):
    return pl.pallas_call(
        lambda *refs: exchange_kernel(axis, count, *refs),
        out_shape=jax.ShapeDtypeStruct(values.shape, values.dtype),
        in_specs=[pl.BlockSpec(memory_space=pltpu.VMEM)],
        out_specs=pl.BlockSpec(memory_space=pltpu.VMEM),
        scratch_shapes=[
            pltpu.SemaphoreType.DMA((count,)),
            pltpu.SemaphoreType.DMA((count,)),
            pltpu.SemaphoreType.DMA(()),
        ],
        compiler_params=pltpu.CompilerParams(collective_id=collective, has_side_effects=True),
    )(values)


def exchange_project_kernel(
    axis, count, send_ref, pieces_ref, wq_hbm, wk_ref, wv_ref,
    got_ref, q_ref, k_ref, v_ref,
    wq_buf, send_sem, recv_sem, local_sem, wq_sem,
):
    me = lax.axis_index(axis)
    barrier = pltpu.get_barrier_semaphore()
    for offset in range(1, count):
        peer = lax.rem(me + offset, count)
        pl.semaphore_signal(barrier, inc=1, device_id={axis: peer}, device_id_type=MESH)
    pl.semaphore_wait(barrier, count - 1)
    local = pltpu.make_async_copy(send_ref.at[me], got_ref.at[me], local_sem)
    local.start()
    outgoing = []
    for offset in range(1, count):
        peer = lax.rem(me + offset, count)
        copy = pltpu.make_async_remote_copy(
            src_ref=send_ref.at[peer],
            dst_ref=got_ref.at[me],
            send_sem=send_sem.at[offset],
            recv_sem=recv_sem.at[offset],
            device_id={axis: peer},
            device_id_type=MESH,
        )
        copy.start()
        outgoing.append(copy)

    piece_count, unused_item, piece_width = pieces_ref.shape

    def chunk_copy(index, slot):
        return pltpu.make_async_copy(
            wq_hbm.at[pl.ds(pl.multiple_of(index * piece_width, piece_width), piece_width)],
            wq_buf.at[slot],
            wq_sem.at[slot],
        )

    chunk_copy(0, 0).start()
    q_ref[...] = jnp.zeros_like(q_ref)
    k_ref[...] = jnp.zeros_like(k_ref)
    v_ref[...] = jnp.zeros_like(v_ref)

    def project(index, carry):
        slot = lax.rem(index, 2)
        chunk_copy(index, slot).wait()

        @pl.when(index + 1 < piece_count)
        def _():
            chunk_copy(index + 1, 1 - slot).start()

        rows = pl.ds(pl.multiple_of(index * piece_width, piece_width), piece_width)
        piece = pieces_ref[index]
        q_ref[...] += jnp.dot(piece, wq_buf[slot], preferred_element_type=jnp.float32)
        k_ref[...] += jnp.dot(piece, wk_ref[rows, :], preferred_element_type=jnp.float32)
        v_ref[...] += jnp.dot(piece, wv_ref[rows, :], preferred_element_type=jnp.float32)
        return carry

    lax.fori_loop(0, piece_count, project, 0)

    for offset in range(1, count):
        outgoing[offset - 1].wait_send()
        source = lax.rem(me + count - offset, count)
        incoming = pltpu.make_async_remote_copy(
            src_ref=send_ref.at[source],
            dst_ref=got_ref.at[source],
            send_sem=send_sem.at[offset],
            recv_sem=recv_sem.at[offset],
            device_id={axis: source},
            device_id_type=MESH,
        )
        incoming.wait_recv()
    local.wait()


def exchange_project(values, pieces, w_query, w_key, w_value, axis, count, collective):
    piece_count, token_count, piece_width = pieces.shape
    vmem = pl.BlockSpec(memory_space=pltpu.VMEM)
    return pl.pallas_call(
        lambda *refs: exchange_project_kernel(axis, count, *refs),
        out_shape=(
            jax.ShapeDtypeStruct(values.shape, values.dtype),
            jax.ShapeDtypeStruct((token_count, w_query.shape[1]), jnp.float32),
            jax.ShapeDtypeStruct((token_count, w_key.shape[1]), jnp.float32),
            jax.ShapeDtypeStruct((token_count, w_value.shape[1]), jnp.float32),
        ),
        in_specs=[vmem, vmem, pl.BlockSpec(memory_space=pl.ANY), vmem, vmem],
        out_specs=(vmem, vmem, vmem, vmem),
        scratch_shapes=[
            pltpu.VMEM((2, piece_width, w_query.shape[1]), w_query.dtype),
            pltpu.SemaphoreType.DMA((count,)),
            pltpu.SemaphoreType.DMA((count,)),
            pltpu.SemaphoreType.DMA(()),
            pltpu.SemaphoreType.DMA((2,)),
        ],
        compiler_params=pltpu.CompilerParams(
            collective_id=collective, has_side_effects=True, vmem_limit_bytes=60 * 1024 * 1024
        ),
    )(values, pieces, w_query, w_key, w_value)


def sum_kernel(axis, count, part_ref, total_ref, held, first_send, first_recv, second_send, second_recv):
    me = lax.axis_index(axis)
    barrier = pltpu.get_barrier_semaphore()
    for offset in range(1, count):
        peer = lax.rem(me + offset, count)
        pl.semaphore_signal(barrier, inc=1, device_id={axis: peer}, device_id_type=MESH)
    pl.semaphore_wait(barrier, count - 1)
    outgoing = []
    for offset in range(1, count):
        peer = lax.rem(me + offset, count)
        copy = pltpu.make_async_remote_copy(
            src_ref=part_ref.at[peer],
            dst_ref=held.at[me],
            send_sem=first_send.at[offset],
            recv_sem=first_recv.at[offset],
            device_id={axis: peer},
            device_id_type=MESH,
        )
        copy.start()
        outgoing.append(copy)
    held[me] = part_ref[me]
    for offset in range(1, count):
        outgoing[offset - 1].wait_send()
        source = lax.rem(me + count - offset, count)
        incoming = pltpu.make_async_remote_copy(
            src_ref=part_ref.at[source],
            dst_ref=held.at[source],
            send_sem=first_send.at[offset],
            recv_sem=first_recv.at[offset],
            device_id={axis: source},
            device_id_type=MESH,
        )
        incoming.wait_recv()
    total = held[0]
    for index in range(1, count):
        total = total + held[index]
    total_ref[me] = total.astype(total_ref.dtype)
    outgoing = []
    for offset in range(1, count):
        peer = lax.rem(me + offset, count)
        copy = pltpu.make_async_remote_copy(
            src_ref=total_ref.at[me],
            dst_ref=total_ref.at[me],
            send_sem=second_send.at[offset],
            recv_sem=second_recv.at[offset],
            device_id={axis: peer},
            device_id_type=MESH,
        )
        copy.start()
        outgoing.append(copy)
    for offset in range(1, count):
        outgoing[offset - 1].wait_send()
        source = lax.rem(me + count - offset, count)
        incoming = pltpu.make_async_remote_copy(
            src_ref=total_ref.at[source],
            dst_ref=total_ref.at[source],
            send_sem=second_send.at[offset],
            recv_sem=second_recv.at[offset],
            device_id={axis: source},
            device_id_type=MESH,
        )
        incoming.wait_recv()


def axis_sum(values, axis, count, collective, out_dtype):
    chunks = values.reshape(count, -1, 128)
    summed = pl.pallas_call(
        lambda *refs: sum_kernel(axis, count, *refs),
        out_shape=jax.ShapeDtypeStruct(chunks.shape, out_dtype),
        in_specs=[pl.BlockSpec(memory_space=pltpu.VMEM)],
        out_specs=pl.BlockSpec(memory_space=pltpu.VMEM),
        scratch_shapes=[
            pltpu.VMEM(chunks.shape, values.dtype),
            pltpu.SemaphoreType.DMA((count,)),
            pltpu.SemaphoreType.DMA((count,)),
            pltpu.SemaphoreType.DMA((count,)),
            pltpu.SemaphoreType.DMA((count,)),
        ],
        compiler_params=pltpu.CompilerParams(collective_id=collective, has_side_effects=True),
    )(chunks)
    return summed.reshape(values.shape)


def owner_adapter_term(received, slot_ids, down_local, up_local):
    sources, rows, part_width = received.shape
    local_adapters, unused_item, adapter_rank = down_local.shape
    query_width = up_local.shape[2]
    token_rows = received.reshape(sources * rows, part_width)
    every_down = jnp.einsum(
        "td,adr->tar", token_rows, down_local, preferred_element_type=jnp.float32
    )
    pick = slot_ids.reshape(sources * rows)[:, None] == jnp.arange(local_adapters, dtype=jnp.int32)[None, :]
    partial_value_sum = jnp.sum(jnp.where(pick[:, :, None], every_down, 0.0), axis=1)
    tp_count = lax.axis_size("tp")
    summed = axis_sum(partial_value_sum.reshape(-1, 128), "tp", tp_count, 2, jnp.bfloat16)
    adapter_middle = summed.reshape(sources * rows, adapter_rank)
    spread_rows = jnp.where(pick[:, :, None], adapter_middle[:, None, :], jnp.zeros((), jnp.bfloat16))
    spread_rows = spread_rows.reshape(sources * rows, local_adapters * adapter_rank)
    adapter_output = jnp.dot(
        spread_rows,
        up_local.reshape(local_adapters * adapter_rank, query_width),
        preferred_element_type=jnp.float32,
    ).astype(jnp.bfloat16)
    return adapter_output.reshape(sources, rows, query_width)


def body(
    tokens,
    adapter_id,
    pool_slot,
    lengths,
    w_query,
    w_key,
    w_value,
    pooled_down_weights,
    pool_up,
    cache_key,
    cache_value,
):
    group_count = lax.axis_size("grp")
    tp_count = lax.axis_size("tp")
    row_count, step_count, part_width = tokens.shape
    local_adapter_rows, unused_item, adapter_rank = pooled_down_weights.shape
    query_width = w_query.shape[1]
    kv_width = w_key.shape[1]
    kv_local = kv_width // HD
    q_local = query_width // HD
    group_size = q_local // kv_local
    count_of_tokens = row_count * step_count
    adapter_span = jnp.arange(pool_slot.shape[0], dtype=jnp.int32)
    pool_pos = jnp.sum(
        jnp.where(adapter_id[:, None] == adapter_span[None, :], pool_slot[None, :], 0), axis=1
    )
    owner_grp = pool_pos // local_adapter_rows
    local_slot = pool_pos % local_adapter_rows
    row_span = jnp.arange(row_count, dtype=jnp.int32)
    same_owner = (owner_grp[:, None] == owner_grp[None, :]) & (row_span[None, :] < row_span[:, None])
    owner_rank = jnp.sum(same_owner.astype(jnp.int32), axis=1)
    send_slot = owner_grp * CAP + owner_rank
    slot_span = jnp.arange(group_count * CAP, dtype=jnp.int32)
    place = (slot_span[:, None] == send_slot[None, :]).astype(jnp.bfloat16)
    token_flat = tokens.reshape(row_count, step_count * part_width)
    send_tokens = jnp.dot(place, token_flat, preferred_element_type=jnp.float32).astype(jnp.bfloat16)
    send_ids = jnp.dot(
        place, local_slot.astype(jnp.bfloat16)[:, None], preferred_element_type=jnp.float32
    ).astype(jnp.bfloat16)
    send_ids = jnp.broadcast_to(
        send_ids.reshape(group_count * CAP, 1, 1), (group_count * CAP, step_count, 128)
    )
    packed = jnp.concatenate(
        [send_tokens.reshape(group_count * CAP, step_count, part_width), send_ids], axis=2
    ).reshape(group_count, CAP * step_count, part_width + 128)
    got = exchange(packed, "grp", group_count, 0)
    got_tokens = got[:, :, :part_width]
    got_ids = got[:, :, part_width].astype(jnp.int32)
    owner_out = owner_adapter_term(got_tokens, got_ids, pooled_down_weights, pool_up)
    pieces = lax.all_gather(tokens.reshape(count_of_tokens, part_width), "tp", axis=0, tiled=False)
    back, base_query_rows, key_base, value_base = exchange_project(
        owner_out, pieces, w_query, w_key, w_value, "grp", group_count, 1
    )
    back = back.reshape(group_count * CAP, step_count * query_width)
    adapter_output = jnp.dot(
        jnp.transpose(place), back, preferred_element_type=jnp.float32
    ).reshape(count_of_tokens, query_width)
    base_query_rows = base_query_rows + adapter_output
    position = lengths[:, None] + jnp.arange(step_count, dtype=jnp.int32)[None, :]
    queries = rotate(base_query_rows.reshape(row_count, step_count, q_local, HD), position)
    queries = queries.astype(jnp.bfloat16).reshape(row_count, step_count, kv_local, group_size, HD)
    key_new = rotate(key_base.reshape(row_count, step_count, kv_local, HD), position).astype(
        jnp.bfloat16
    )
    value_new = value_base.reshape(row_count, step_count, kv_local, HD).astype(jnp.bfloat16)
    cache_keys = cache_key.reshape(row_count, cache_key.shape[1], kv_local, HD)
    cache_values = cache_value.reshape(row_count, cache_value.shape[1], kv_local, HD)
    combined = attend(queries, key_new, value_new, cache_keys, cache_values, lengths)
    return combined.reshape(row_count, step_count, query_width)


def solution(mesh):
    in_specs = (
        P("grp", None, "tp"),
        P("grp"),
        P(),
        P("grp"),
        P(None, "tp"),
        P(None, "tp"),
        P(None, "tp"),
        P("grp", "tp", None),
        P("grp", None, "tp"),
        P("grp", None, "tp"),
        P("grp", None, "tp"),
    )
    out_specs = P("grp", None, "tp")
    return jax.shard_map(body, mesh=mesh, in_specs=in_specs, out_specs=out_specs, check_vma=False)
```

```python
import math

import jax
import jax.numpy as jnp
from jax import lax
from jax.experimental import pallas as pl
from jax.experimental.pallas import tpu as pltpu
from jax.sharding import PartitionSpec as P

MESH = pl.DeviceIdType.MESH

HD = 128
CAP = 8


rope_base = 500000.0


def rotate(values, position):
    half_width = values.shape[-1] // 2
    inv_freq = jnp.exp(
        jnp.arange(half_width, dtype=jnp.float32) * (-2.0 * math.log(rope_base) / values.shape[-1])
    )
    angles = position.astype(jnp.float32)[:, :, None, None] * inv_freq
    cosine = jnp.cos(angles)
    sines = jnp.sin(angles)
    front_half = values[..., :half_width]
    back_half = values[..., half_width:]
    return jnp.concatenate(
        [front_half * cosine - back_half * sines, back_half * cosine + front_half * sines], axis=-1
    )


def attend(queries, key_new, value_new, cache_key, cache_value, lengths):
    score_scale = 1.0 / math.sqrt(queries.shape[-1])
    cached = (
        jnp.einsum("rskgd,rlkd->rskgl", queries, cache_key, preferred_element_type=jnp.float32)
        * score_scale
    )
    fresh_scores = (
        jnp.einsum("rskgd,rtkd->rskgt", queries, key_new, preferred_element_type=jnp.float32)
        * score_scale
    )
    live_mask = jnp.arange(cache_key.shape[1], dtype=jnp.int32)[None, :] < lengths[:, None]
    cached = jnp.where(live_mask[:, None, None, None, :], cached, -1e30)
    steps_here = key_new.shape[1]
    causal = (
        jnp.arange(steps_here, dtype=jnp.int32)[:, None]
        >= jnp.arange(steps_here, dtype=jnp.int32)[None, :]
    )
    fresh_scores = jnp.where(causal[None, :, None, None, :], fresh_scores, -1e30)
    row_max = jnp.maximum(jnp.max(cached, axis=-1), jnp.max(fresh_scores, axis=-1))
    cache_exp = jnp.exp(cached - row_max[..., None])
    fresh_exp = jnp.exp(fresh_scores - row_max[..., None])
    weight_sum = jnp.sum(cache_exp, axis=-1) + jnp.sum(fresh_exp, axis=-1)
    cache_weights = (cache_exp / weight_sum[..., None]).astype(jnp.bfloat16)
    fresh_weights = (fresh_exp / weight_sum[..., None]).astype(jnp.bfloat16)
    combined = jnp.einsum(
        "rskgl,rlkd->rskgd", cache_weights, cache_value, preferred_element_type=jnp.float32
    )
    combined = combined + jnp.einsum(
        "rskgt,rtkd->rskgd", fresh_weights, value_new, preferred_element_type=jnp.float32
    )
    return combined.astype(jnp.bfloat16)


TORUS_ORDER = (
    (0, 1), (1, 0), (0, 3), (3, 0), (1, 1), (3, 3), (1, 3), (3, 1),
    (0, 2), (2, 0), (2, 1), (1, 2), (2, 3), (3, 2), (2, 2),
)


def peer_offsets(count):
    if count == 16:
        def shifted(me, dz, dy):
            return lax.rem(me // 4 + dz, 4) * 4 + lax.rem(lax.rem(me, 4) + dy, 4)

        return [
            (lambda me, a=dz, b=dy: shifted(me, a, b), lambda me, a=dz, b=dy: shifted(me, 4 - a, 4 - b))
            for dz, dy in TORUS_ORDER
        ]
    return [
        (lambda me, d=offset: lax.rem(me + d, count), lambda me, d=offset: lax.rem(me + count - d, count))
        for offset in range(1, count)
    ]


def exchange_kernel(axis, count, send_ref, got_ref, send_sem, recv_sem, local_sem):
    me = lax.axis_index(axis)
    barrier = pltpu.get_barrier_semaphore()
    offsets = peer_offsets(count)
    for offset in range(1, count):
        peer = offsets[offset - 1][0](me)
        pl.semaphore_signal(barrier, inc=1, device_id={axis: peer}, device_id_type=MESH)
    pl.semaphore_wait(barrier, count - 1)
    local = pltpu.make_async_copy(send_ref.at[me], got_ref.at[me], local_sem)
    local.start()
    outgoing = []
    for offset in range(1, count):
        peer = offsets[offset - 1][0](me)
        copy = pltpu.make_async_remote_copy(
            src_ref=send_ref.at[peer],
            dst_ref=got_ref.at[me],
            send_sem=send_sem.at[offset],
            recv_sem=recv_sem.at[offset],
            device_id={axis: peer},
            device_id_type=MESH,
        )
        copy.start()
        outgoing.append(copy)
    for offset in range(1, count):
        outgoing[offset - 1].wait_send()
        source = offsets[offset - 1][1](me)
        incoming = pltpu.make_async_remote_copy(
            src_ref=send_ref.at[source],
            dst_ref=got_ref.at[source],
            send_sem=send_sem.at[offset],
            recv_sem=recv_sem.at[offset],
            device_id={axis: source},
            device_id_type=MESH,
        )
        incoming.wait_recv()
    local.wait()


def exchange(values, axis, count, collective):
    return pl.pallas_call(
        lambda *refs: exchange_kernel(axis, count, *refs),
        out_shape=jax.ShapeDtypeStruct(values.shape, values.dtype),
        in_specs=[pl.BlockSpec(memory_space=pltpu.VMEM)],
        out_specs=pl.BlockSpec(memory_space=pltpu.VMEM),
        scratch_shapes=[
            pltpu.SemaphoreType.DMA((count,)),
            pltpu.SemaphoreType.DMA((count,)),
            pltpu.SemaphoreType.DMA(()),
        ],
        compiler_params=pltpu.CompilerParams(collective_id=collective, has_side_effects=True),
    )(values)


def exchange_project_kernel(
    axis, count, send_ref, pieces_ref, wq_hbm, wk_ref, wv_ref,
    got_ref, q_ref, k_ref, v_ref,
    wq_buf, send_sem, recv_sem, local_sem, wq_sem,
):
    me = lax.axis_index(axis)
    barrier = pltpu.get_barrier_semaphore()
    offsets = peer_offsets(count)
    for offset in range(1, count):
        peer = offsets[offset - 1][0](me)
        pl.semaphore_signal(barrier, inc=1, device_id={axis: peer}, device_id_type=MESH)
    pl.semaphore_wait(barrier, count - 1)
    local = pltpu.make_async_copy(send_ref.at[me], got_ref.at[me], local_sem)
    local.start()
    outgoing = []
    for offset in range(1, count):
        peer = offsets[offset - 1][0](me)
        copy = pltpu.make_async_remote_copy(
            src_ref=send_ref.at[peer],
            dst_ref=got_ref.at[me],
            send_sem=send_sem.at[offset],
            recv_sem=recv_sem.at[offset],
            device_id={axis: peer},
            device_id_type=MESH,
        )
        copy.start()
        outgoing.append(copy)

    piece_count, unused_item, piece_width = pieces_ref.shape

    def chunk_copy(index, slot):
        return pltpu.make_async_copy(
            wq_hbm.at[pl.ds(pl.multiple_of(index * piece_width, piece_width), piece_width)],
            wq_buf.at[slot],
            wq_sem.at[slot],
        )

    chunk_copy(0, 0).start()
    q_ref[...] = jnp.zeros_like(q_ref)
    k_ref[...] = jnp.zeros_like(k_ref)
    v_ref[...] = jnp.zeros_like(v_ref)

    def project(index, carry):
        slot = lax.rem(index, 2)
        chunk_copy(index, slot).wait()

        @pl.when(index + 1 < piece_count)
        def _():
            chunk_copy(index + 1, 1 - slot).start()

        rows = pl.ds(pl.multiple_of(index * piece_width, piece_width), piece_width)
        piece = pieces_ref[index]
        q_ref[...] += jnp.dot(piece, wq_buf[slot], preferred_element_type=jnp.float32)
        k_ref[...] += jnp.dot(piece, wk_ref[rows, :], preferred_element_type=jnp.float32)
        v_ref[...] += jnp.dot(piece, wv_ref[rows, :], preferred_element_type=jnp.float32)
        return carry

    lax.fori_loop(0, piece_count, project, 0)

    for offset in range(1, count):
        outgoing[offset - 1].wait_send()
        source = offsets[offset - 1][1](me)
        incoming = pltpu.make_async_remote_copy(
            src_ref=send_ref.at[source],
            dst_ref=got_ref.at[source],
            send_sem=send_sem.at[offset],
            recv_sem=recv_sem.at[offset],
            device_id={axis: source},
            device_id_type=MESH,
        )
        incoming.wait_recv()
    local.wait()


def exchange_project(values, pieces, w_query, w_key, w_value, axis, count, collective):
    piece_count, token_count, piece_width = pieces.shape
    vmem = pl.BlockSpec(memory_space=pltpu.VMEM)
    return pl.pallas_call(
        lambda *refs: exchange_project_kernel(axis, count, *refs),
        out_shape=(
            jax.ShapeDtypeStruct(values.shape, values.dtype),
            jax.ShapeDtypeStruct((token_count, w_query.shape[1]), jnp.float32),
            jax.ShapeDtypeStruct((token_count, w_key.shape[1]), jnp.float32),
            jax.ShapeDtypeStruct((token_count, w_value.shape[1]), jnp.float32),
        ),
        in_specs=[vmem, vmem, pl.BlockSpec(memory_space=pl.ANY), vmem, vmem],
        out_specs=(vmem, vmem, vmem, vmem),
        scratch_shapes=[
            pltpu.VMEM((2, piece_width, w_query.shape[1]), w_query.dtype),
            pltpu.SemaphoreType.DMA((count,)),
            pltpu.SemaphoreType.DMA((count,)),
            pltpu.SemaphoreType.DMA(()),
            pltpu.SemaphoreType.DMA((2,)),
        ],
        compiler_params=pltpu.CompilerParams(
            collective_id=collective, has_side_effects=True, vmem_limit_bytes=60 * 1024 * 1024
        ),
    )(values, pieces, w_query, w_key, w_value)


def sum_kernel(axis, count, part_ref, total_ref, held, first_send, first_recv, second_send, second_recv):
    me = lax.axis_index(axis)
    barrier = pltpu.get_barrier_semaphore()
    for offset in range(1, count):
        peer = lax.rem(me + offset, count)
        pl.semaphore_signal(barrier, inc=1, device_id={axis: peer}, device_id_type=MESH)
    pl.semaphore_wait(barrier, count - 1)
    outgoing = []
    for offset in range(1, count):
        peer = lax.rem(me + offset, count)
        copy = pltpu.make_async_remote_copy(
            src_ref=part_ref.at[peer],
            dst_ref=held.at[me],
            send_sem=first_send.at[offset],
            recv_sem=first_recv.at[offset],
            device_id={axis: peer},
            device_id_type=MESH,
        )
        copy.start()
        outgoing.append(copy)
    held[me] = part_ref[me]
    for offset in range(1, count):
        outgoing[offset - 1].wait_send()
        source = lax.rem(me + count - offset, count)
        incoming = pltpu.make_async_remote_copy(
            src_ref=part_ref.at[source],
            dst_ref=held.at[source],
            send_sem=first_send.at[offset],
            recv_sem=first_recv.at[offset],
            device_id={axis: source},
            device_id_type=MESH,
        )
        incoming.wait_recv()
    total = held[0]
    for index in range(1, count):
        total = total + held[index]
    total_ref[me] = total.astype(total_ref.dtype)
    outgoing = []
    for offset in range(1, count):
        peer = lax.rem(me + offset, count)
        copy = pltpu.make_async_remote_copy(
            src_ref=total_ref.at[me],
            dst_ref=total_ref.at[me],
            send_sem=second_send.at[offset],
            recv_sem=second_recv.at[offset],
            device_id={axis: peer},
            device_id_type=MESH,
        )
        copy.start()
        outgoing.append(copy)
    for offset in range(1, count):
        outgoing[offset - 1].wait_send()
        source = lax.rem(me + count - offset, count)
        incoming = pltpu.make_async_remote_copy(
            src_ref=total_ref.at[source],
            dst_ref=total_ref.at[source],
            send_sem=second_send.at[offset],
            recv_sem=second_recv.at[offset],
            device_id={axis: source},
            device_id_type=MESH,
        )
        incoming.wait_recv()


def axis_sum(values, axis, count, collective, out_dtype):
    chunks = values.reshape(count, -1, 128)
    summed = pl.pallas_call(
        lambda *refs: sum_kernel(axis, count, *refs),
        out_shape=jax.ShapeDtypeStruct(chunks.shape, out_dtype),
        in_specs=[pl.BlockSpec(memory_space=pltpu.VMEM)],
        out_specs=pl.BlockSpec(memory_space=pltpu.VMEM),
        scratch_shapes=[
            pltpu.VMEM(chunks.shape, values.dtype),
            pltpu.SemaphoreType.DMA((count,)),
            pltpu.SemaphoreType.DMA((count,)),
            pltpu.SemaphoreType.DMA((count,)),
            pltpu.SemaphoreType.DMA((count,)),
        ],
        compiler_params=pltpu.CompilerParams(collective_id=collective, has_side_effects=True),
    )(chunks)
    return summed.reshape(values.shape)


def owner_adapter_term(received, slot_ids, down_local, up_local):
    sources, rows, part_width = received.shape
    local_adapters, unused_item, adapter_rank = down_local.shape
    query_width = up_local.shape[2]
    token_rows = received.reshape(sources * rows, part_width)
    every_down = jnp.einsum(
        "td,adr->tar", token_rows, down_local, preferred_element_type=jnp.float32
    )
    pick = slot_ids.reshape(sources * rows)[:, None] == jnp.arange(local_adapters, dtype=jnp.int32)[None, :]
    partial_value_sum = jnp.sum(jnp.where(pick[:, :, None], every_down, 0.0), axis=1)
    tp_count = lax.axis_size("tp")
    summed = axis_sum(partial_value_sum.reshape(-1, 128), "tp", tp_count, 2, jnp.bfloat16)
    adapter_middle = summed.reshape(sources * rows, adapter_rank)
    spread_rows = jnp.where(pick[:, :, None], adapter_middle[:, None, :], jnp.zeros((), jnp.bfloat16))
    spread_rows = spread_rows.reshape(sources * rows, local_adapters * adapter_rank)
    adapter_output = jnp.dot(
        spread_rows,
        up_local.reshape(local_adapters * adapter_rank, query_width),
        preferred_element_type=jnp.float32,
    ).astype(jnp.bfloat16)
    return adapter_output.reshape(sources, rows, query_width)


def body(
    tokens,
    adapter_id,
    pool_slot,
    lengths,
    w_query,
    w_key,
    w_value,
    pooled_down_weights,
    pool_up,
    cache_key,
    cache_value,
):
    group_count = lax.axis_size("grp")
    tp_count = lax.axis_size("tp")
    row_count, step_count, part_width = tokens.shape
    local_adapter_rows, unused_item, adapter_rank = pooled_down_weights.shape
    query_width = w_query.shape[1]
    kv_width = w_key.shape[1]
    kv_local = kv_width // HD
    q_local = query_width // HD
    group_size = q_local // kv_local
    count_of_tokens = row_count * step_count
    adapter_span = jnp.arange(pool_slot.shape[0], dtype=jnp.int32)
    pool_pos = jnp.sum(
        jnp.where(adapter_id[:, None] == adapter_span[None, :], pool_slot[None, :], 0), axis=1
    )
    owner_grp = pool_pos // local_adapter_rows
    local_slot = pool_pos % local_adapter_rows
    row_span = jnp.arange(row_count, dtype=jnp.int32)
    same_owner = (owner_grp[:, None] == owner_grp[None, :]) & (row_span[None, :] < row_span[:, None])
    owner_rank = jnp.sum(same_owner.astype(jnp.int32), axis=1)
    send_slot = owner_grp * CAP + owner_rank
    slot_span = jnp.arange(group_count * CAP, dtype=jnp.int32)
    place = (slot_span[:, None] == send_slot[None, :]).astype(jnp.bfloat16)
    token_flat = tokens.reshape(row_count, step_count * part_width)
    send_tokens = jnp.dot(place, token_flat, preferred_element_type=jnp.float32).astype(jnp.bfloat16)
    send_ids = jnp.dot(
        place, local_slot.astype(jnp.bfloat16)[:, None], preferred_element_type=jnp.float32
    ).astype(jnp.bfloat16)
    send_ids = jnp.broadcast_to(
        send_ids.reshape(group_count * CAP, 1, 1), (group_count * CAP, step_count, 128)
    )
    packed = jnp.concatenate(
        [send_tokens.reshape(group_count * CAP, step_count, part_width), send_ids], axis=2
    ).reshape(group_count, CAP * step_count, part_width + 128)
    got = exchange(packed, "grp", group_count, 0)
    got_tokens = got[:, :, :part_width]
    got_ids = got[:, :, part_width].astype(jnp.int32)
    owner_out = owner_adapter_term(got_tokens, got_ids, pooled_down_weights, pool_up)
    pieces = lax.all_gather(tokens.reshape(count_of_tokens, part_width), "tp", axis=0, tiled=False)
    back, base_query_rows, key_base, value_base = exchange_project(
        owner_out, pieces, w_query, w_key, w_value, "grp", group_count, 1
    )
    back = back.reshape(group_count * CAP, step_count * query_width)
    adapter_output = jnp.dot(
        jnp.transpose(place), back, preferred_element_type=jnp.float32
    ).reshape(count_of_tokens, query_width)
    base_query_rows = base_query_rows + adapter_output
    position = lengths[:, None] + jnp.arange(step_count, dtype=jnp.int32)[None, :]
    queries = rotate(base_query_rows.reshape(row_count, step_count, q_local, HD), position)
    queries = queries.astype(jnp.bfloat16).reshape(row_count, step_count, kv_local, group_size, HD)
    key_new = rotate(key_base.reshape(row_count, step_count, kv_local, HD), position).astype(
        jnp.bfloat16
    )
    value_new = value_base.reshape(row_count, step_count, kv_local, HD).astype(jnp.bfloat16)
    cache_keys = cache_key.reshape(row_count, cache_key.shape[1], kv_local, HD)
    cache_values = cache_value.reshape(row_count, cache_value.shape[1], kv_local, HD)
    combined = attend(queries, key_new, value_new, cache_keys, cache_values, lengths)
    return combined.reshape(row_count, step_count, query_width)


def solution(mesh):
    in_specs = (
        P("grp", None, "tp"),
        P("grp"),
        P(),
        P("grp"),
        P(None, "tp"),
        P(None, "tp"),
        P(None, "tp"),
        P("grp", "tp", None),
        P("grp", None, "tp"),
        P("grp", None, "tp"),
        P("grp", None, "tp"),
    )
    out_specs = P("grp", None, "tp")
    return jax.shard_map(body, mesh=mesh, in_specs=in_specs, out_specs=out_specs, check_vma=False)
```

```python
import math

import jax
import jax.numpy as jnp
from jax import lax
from jax.experimental import pallas as pl
from jax.experimental.pallas import tpu as pltpu
from jax.sharding import PartitionSpec as P

MESH = pl.DeviceIdType.MESH

HD = 128
CAP = 8


rope_base = 500000.0


def rotate(values, position):
    half_width = values.shape[-1] // 2
    inv_freq = jnp.exp(
        jnp.arange(half_width, dtype=jnp.float32) * (-2.0 * math.log(rope_base) / values.shape[-1])
    )
    angles = position.astype(jnp.float32)[:, :, None, None] * inv_freq
    cosine = jnp.cos(angles)
    sines = jnp.sin(angles)
    front_half = values[..., :half_width]
    back_half = values[..., half_width:]
    return jnp.concatenate(
        [front_half * cosine - back_half * sines, back_half * cosine + front_half * sines], axis=-1
    )


def attend(queries, key_new, value_new, cache_key, cache_value, lengths):
    score_scale = 1.0 / math.sqrt(queries.shape[-1])
    cached = (
        jnp.einsum("rskgd,rlkd->rskgl", queries, cache_key, preferred_element_type=jnp.float32)
        * score_scale
    )
    fresh_scores = (
        jnp.einsum("rskgd,rtkd->rskgt", queries, key_new, preferred_element_type=jnp.float32)
        * score_scale
    )
    live_mask = jnp.arange(cache_key.shape[1], dtype=jnp.int32)[None, :] < lengths[:, None]
    cached = jnp.where(live_mask[:, None, None, None, :], cached, -1e30)
    steps_here = key_new.shape[1]
    causal = (
        jnp.arange(steps_here, dtype=jnp.int32)[:, None]
        >= jnp.arange(steps_here, dtype=jnp.int32)[None, :]
    )
    fresh_scores = jnp.where(causal[None, :, None, None, :], fresh_scores, -1e30)
    row_max = jnp.maximum(jnp.max(cached, axis=-1), jnp.max(fresh_scores, axis=-1))
    cache_exp = jnp.exp(cached - row_max[..., None])
    fresh_exp = jnp.exp(fresh_scores - row_max[..., None])
    weight_sum = jnp.sum(cache_exp, axis=-1) + jnp.sum(fresh_exp, axis=-1)
    cache_weights = (cache_exp / weight_sum[..., None]).astype(jnp.bfloat16)
    fresh_weights = (fresh_exp / weight_sum[..., None]).astype(jnp.bfloat16)
    combined = jnp.einsum(
        "rskgl,rlkd->rskgd", cache_weights, cache_value, preferred_element_type=jnp.float32
    )
    combined = combined + jnp.einsum(
        "rskgt,rtkd->rskgd", fresh_weights, value_new, preferred_element_type=jnp.float32
    )
    return combined.astype(jnp.bfloat16)


TORUS_ORDER = (
    (0, 1), (1, 0), (0, 3), (3, 0), (1, 1), (3, 3), (1, 3), (3, 1),
    (0, 2), (2, 0), (2, 1), (1, 2), (2, 3), (3, 2), (2, 2),
)


def peer_offsets(count):
    if count == 16:
        def shifted(me, dz, dy):
            return lax.rem(me // 4 + dz, 4) * 4 + lax.rem(lax.rem(me, 4) + dy, 4)

        return [
            (lambda me, a=dz, b=dy: shifted(me, a, b), lambda me, a=dz, b=dy: shifted(me, 4 - a, 4 - b))
            for dz, dy in TORUS_ORDER
        ]
    return [
        (lambda me, d=offset: lax.rem(me + d, count), lambda me, d=offset: lax.rem(me + count - d, count))
        for offset in range(1, count)
    ]


def exchange_kernel(axis, count, arrays, *refs):
    send_refs = refs[:arrays]
    got_refs = refs[arrays : 2 * arrays]
    send_sem, recv_sem, local_sem = refs[2 * arrays :]
    me = lax.axis_index(axis)
    barrier = pltpu.get_barrier_semaphore()
    offsets = peer_offsets(count)
    for offset in range(1, count):
        peer = offsets[offset - 1][0](me)
        pl.semaphore_signal(barrier, inc=1, device_id={axis: peer}, device_id_type=MESH)
    pl.semaphore_wait(barrier, count - 1)
    locals_ = []
    for which in range(arrays):
        local = pltpu.make_async_copy(
            send_refs[which].at[me], got_refs[which].at[me], local_sem.at[which]
        )
        local.start()
        locals_.append(local)
    outgoing = []
    for offset in range(1, count):
        peer = offsets[offset - 1][0](me)
        for which in range(arrays):
            copy = pltpu.make_async_remote_copy(
                src_ref=send_refs[which].at[peer],
                dst_ref=got_refs[which].at[me],
                send_sem=send_sem.at[which, offset],
                recv_sem=recv_sem.at[which, offset],
                device_id={axis: peer},
                device_id_type=MESH,
            )
            copy.start()
            outgoing.append(copy)
    for offset in range(1, count):
        source = offsets[offset - 1][1](me)
        for which in range(arrays):
            outgoing[(offset - 1) * arrays + which].wait_send()
            incoming = pltpu.make_async_remote_copy(
                src_ref=send_refs[which].at[source],
                dst_ref=got_refs[which].at[source],
                send_sem=send_sem.at[which, offset],
                recv_sem=recv_sem.at[which, offset],
                device_id={axis: source},
                device_id_type=MESH,
            )
            incoming.wait_recv()
    for local in locals_:
        local.wait()


def exchange(values, axis, count, collective):
    arrays = len(values)
    vmem = pl.BlockSpec(memory_space=pltpu.VMEM)
    return pl.pallas_call(
        lambda *refs: exchange_kernel(axis, count, arrays, *refs),
        out_shape=tuple(jax.ShapeDtypeStruct(v.shape, v.dtype) for v in values),
        in_specs=[vmem] * arrays,
        out_specs=tuple([vmem] * arrays),
        scratch_shapes=[
            pltpu.SemaphoreType.DMA((arrays, count)),
            pltpu.SemaphoreType.DMA((arrays, count)),
            pltpu.SemaphoreType.DMA((arrays,)),
        ],
        compiler_params=pltpu.CompilerParams(collective_id=collective, has_side_effects=True),
    )(*values)


def exchange_project_kernel(
    axis, count, send_ref, pieces_ref, wq_hbm, wk_ref, wv_ref,
    got_ref, q_ref, k_ref, v_ref,
    wq_buf, send_sem, recv_sem, local_sem, wq_sem,
):
    me = lax.axis_index(axis)
    barrier = pltpu.get_barrier_semaphore()
    offsets = peer_offsets(count)
    for offset in range(1, count):
        peer = offsets[offset - 1][0](me)
        pl.semaphore_signal(barrier, inc=1, device_id={axis: peer}, device_id_type=MESH)
    pl.semaphore_wait(barrier, count - 1)
    local = pltpu.make_async_copy(send_ref.at[me], got_ref.at[me], local_sem)
    local.start()
    outgoing = []
    for offset in range(1, count):
        peer = offsets[offset - 1][0](me)
        copy = pltpu.make_async_remote_copy(
            src_ref=send_ref.at[peer],
            dst_ref=got_ref.at[me],
            send_sem=send_sem.at[offset],
            recv_sem=recv_sem.at[offset],
            device_id={axis: peer},
            device_id_type=MESH,
        )
        copy.start()
        outgoing.append(copy)

    piece_count, unused_item, piece_width = pieces_ref.shape

    def chunk_copy(index, slot):
        return pltpu.make_async_copy(
            wq_hbm.at[pl.ds(pl.multiple_of(index * piece_width, piece_width), piece_width)],
            wq_buf.at[slot],
            wq_sem.at[slot],
        )

    chunk_copy(0, 0).start()
    q_ref[...] = jnp.zeros_like(q_ref)
    k_ref[...] = jnp.zeros_like(k_ref)
    v_ref[...] = jnp.zeros_like(v_ref)

    def project(index, carry):
        slot = lax.rem(index, 2)
        chunk_copy(index, slot).wait()

        @pl.when(index + 1 < piece_count)
        def _():
            chunk_copy(index + 1, 1 - slot).start()

        rows = pl.ds(pl.multiple_of(index * piece_width, piece_width), piece_width)
        piece = pieces_ref[index]
        q_ref[...] += jnp.dot(piece, wq_buf[slot], preferred_element_type=jnp.float32)
        k_ref[...] += jnp.dot(piece, wk_ref[rows, :], preferred_element_type=jnp.float32)
        v_ref[...] += jnp.dot(piece, wv_ref[rows, :], preferred_element_type=jnp.float32)
        return carry

    lax.fori_loop(0, piece_count, project, 0)

    for offset in range(1, count):
        outgoing[offset - 1].wait_send()
        source = offsets[offset - 1][1](me)
        incoming = pltpu.make_async_remote_copy(
            src_ref=send_ref.at[source],
            dst_ref=got_ref.at[source],
            send_sem=send_sem.at[offset],
            recv_sem=recv_sem.at[offset],
            device_id={axis: source},
            device_id_type=MESH,
        )
        incoming.wait_recv()
    local.wait()


def exchange_project(values, pieces, w_query, w_key, w_value, axis, count, collective):
    piece_count, token_count, piece_width = pieces.shape
    vmem = pl.BlockSpec(memory_space=pltpu.VMEM)
    return pl.pallas_call(
        lambda *refs: exchange_project_kernel(axis, count, *refs),
        out_shape=(
            jax.ShapeDtypeStruct(values.shape, values.dtype),
            jax.ShapeDtypeStruct((token_count, w_query.shape[1]), jnp.float32),
            jax.ShapeDtypeStruct((token_count, w_key.shape[1]), jnp.float32),
            jax.ShapeDtypeStruct((token_count, w_value.shape[1]), jnp.float32),
        ),
        in_specs=[vmem, vmem, pl.BlockSpec(memory_space=pl.ANY), vmem, vmem],
        out_specs=(vmem, vmem, vmem, vmem),
        scratch_shapes=[
            pltpu.VMEM((2, piece_width, w_query.shape[1]), w_query.dtype),
            pltpu.SemaphoreType.DMA((count,)),
            pltpu.SemaphoreType.DMA((count,)),
            pltpu.SemaphoreType.DMA(()),
            pltpu.SemaphoreType.DMA((2,)),
        ],
        compiler_params=pltpu.CompilerParams(
            collective_id=collective, has_side_effects=True, vmem_limit_bytes=60 * 1024 * 1024
        ),
    )(values, pieces, w_query, w_key, w_value)


def sum_kernel(axis, count, part_ref, total_ref, held, first_send, first_recv, second_send, second_recv):
    me = lax.axis_index(axis)
    barrier = pltpu.get_barrier_semaphore()
    for offset in range(1, count):
        peer = lax.rem(me + offset, count)
        pl.semaphore_signal(barrier, inc=1, device_id={axis: peer}, device_id_type=MESH)
    pl.semaphore_wait(barrier, count - 1)
    outgoing = []
    for offset in range(1, count):
        peer = lax.rem(me + offset, count)
        copy = pltpu.make_async_remote_copy(
            src_ref=part_ref.at[peer],
            dst_ref=held.at[me],
            send_sem=first_send.at[offset],
            recv_sem=first_recv.at[offset],
            device_id={axis: peer},
            device_id_type=MESH,
        )
        copy.start()
        outgoing.append(copy)
    held[me] = part_ref[me]
    for offset in range(1, count):
        outgoing[offset - 1].wait_send()
        source = lax.rem(me + count - offset, count)
        incoming = pltpu.make_async_remote_copy(
            src_ref=part_ref.at[source],
            dst_ref=held.at[source],
            send_sem=first_send.at[offset],
            recv_sem=first_recv.at[offset],
            device_id={axis: source},
            device_id_type=MESH,
        )
        incoming.wait_recv()
    total = held[0]
    for index in range(1, count):
        total = total + held[index]
    total_ref[me] = total.astype(total_ref.dtype)
    outgoing = []
    for offset in range(1, count):
        peer = lax.rem(me + offset, count)
        copy = pltpu.make_async_remote_copy(
            src_ref=total_ref.at[me],
            dst_ref=total_ref.at[me],
            send_sem=second_send.at[offset],
            recv_sem=second_recv.at[offset],
            device_id={axis: peer},
            device_id_type=MESH,
        )
        copy.start()
        outgoing.append(copy)
    for offset in range(1, count):
        outgoing[offset - 1].wait_send()
        source = lax.rem(me + count - offset, count)
        incoming = pltpu.make_async_remote_copy(
            src_ref=total_ref.at[source],
            dst_ref=total_ref.at[source],
            send_sem=second_send.at[offset],
            recv_sem=second_recv.at[offset],
            device_id={axis: source},
            device_id_type=MESH,
        )
        incoming.wait_recv()


def axis_sum(values, axis, count, collective, out_dtype):
    chunks = values.reshape(count, -1, 128)
    summed = pl.pallas_call(
        lambda *refs: sum_kernel(axis, count, *refs),
        out_shape=jax.ShapeDtypeStruct(chunks.shape, out_dtype),
        in_specs=[pl.BlockSpec(memory_space=pltpu.VMEM)],
        out_specs=pl.BlockSpec(memory_space=pltpu.VMEM),
        scratch_shapes=[
            pltpu.VMEM(chunks.shape, values.dtype),
            pltpu.SemaphoreType.DMA((count,)),
            pltpu.SemaphoreType.DMA((count,)),
            pltpu.SemaphoreType.DMA((count,)),
            pltpu.SemaphoreType.DMA((count,)),
        ],
        compiler_params=pltpu.CompilerParams(collective_id=collective, has_side_effects=True),
    )(chunks)
    return summed.reshape(values.shape)


def owner_adapter_term(received, slot_ids, down_local, up_local):
    sources, rows, part_width = received.shape
    local_adapters, unused_item, adapter_rank = down_local.shape
    query_width = up_local.shape[2]
    token_rows = received.reshape(sources * rows, part_width)
    every_down = jnp.einsum(
        "td,adr->tar", token_rows, down_local, preferred_element_type=jnp.float32
    )
    pick = slot_ids.reshape(sources * rows)[:, None] == jnp.arange(local_adapters, dtype=jnp.int32)[None, :]
    partial_value_sum = jnp.sum(jnp.where(pick[:, :, None], every_down, 0.0), axis=1)
    tp_count = lax.axis_size("tp")
    summed = axis_sum(partial_value_sum.reshape(-1, 128), "tp", tp_count, 2, jnp.bfloat16)
    adapter_middle = summed.reshape(sources * rows, adapter_rank)
    spread_rows = jnp.where(pick[:, :, None], adapter_middle[:, None, :], jnp.zeros((), jnp.bfloat16))
    spread_rows = spread_rows.reshape(sources * rows, local_adapters * adapter_rank)
    adapter_output = jnp.dot(
        spread_rows,
        up_local.reshape(local_adapters * adapter_rank, query_width),
        preferred_element_type=jnp.float32,
    ).astype(jnp.bfloat16)
    return adapter_output.reshape(sources, rows, query_width)


def body(
    tokens,
    adapter_id,
    pool_slot,
    lengths,
    w_query,
    w_key,
    w_value,
    pooled_down_weights,
    pool_up,
    cache_key,
    cache_value,
):
    group_count = lax.axis_size("grp")
    tp_count = lax.axis_size("tp")
    row_count, step_count, part_width = tokens.shape
    local_adapter_rows, unused_item, adapter_rank = pooled_down_weights.shape
    query_width = w_query.shape[1]
    kv_width = w_key.shape[1]
    kv_local = kv_width // HD
    q_local = query_width // HD
    group_size = q_local // kv_local
    count_of_tokens = row_count * step_count
    adapter_span = jnp.arange(pool_slot.shape[0], dtype=jnp.int32)
    pool_pos = jnp.sum(
        jnp.where(adapter_id[:, None] == adapter_span[None, :], pool_slot[None, :], 0), axis=1
    )
    owner_grp = pool_pos // local_adapter_rows
    local_slot = pool_pos % local_adapter_rows
    row_span = jnp.arange(row_count, dtype=jnp.int32)
    same_owner = (owner_grp[:, None] == owner_grp[None, :]) & (row_span[None, :] < row_span[:, None])
    owner_rank = jnp.sum(same_owner.astype(jnp.int32), axis=1)
    send_slot = owner_grp * CAP + owner_rank
    slot_span = jnp.arange(group_count * CAP, dtype=jnp.int32)
    place = (slot_span[:, None] == send_slot[None, :]).astype(jnp.bfloat16)
    token_slot = (send_slot[:, None] * step_count + jnp.arange(step_count, dtype=jnp.int32)[None, :]).reshape(-1)
    token_span = jnp.arange(group_count * CAP * step_count, dtype=jnp.int32)
    place_tokens = (token_span[:, None] == token_slot[None, :]).astype(jnp.bfloat16)
    token_rows = tokens.reshape(count_of_tokens, part_width)
    send_tokens = jnp.dot(place_tokens, token_rows, preferred_element_type=jnp.float32).astype(jnp.bfloat16)
    send_tokens = send_tokens.reshape(group_count, CAP * step_count, part_width)
    send_ids = jnp.dot(
        place, local_slot.astype(jnp.bfloat16)[:, None], preferred_element_type=jnp.float32
    ).astype(jnp.bfloat16)
    send_ids = jnp.broadcast_to(send_ids.reshape(group_count, CAP, 1), (group_count, CAP, 128))
    send_ids = jnp.concatenate([send_ids, jnp.zeros_like(send_ids)], axis=1)
    got_tokens, got_ids = exchange((send_tokens, send_ids), "grp", group_count, 0)
    got_ids = jnp.repeat(got_ids[:, :CAP, 0].astype(jnp.int32), step_count, axis=1)
    owner_out = owner_adapter_term(got_tokens, got_ids, pooled_down_weights, pool_up)
    pieces = lax.all_gather(token_rows, "tp", axis=0, tiled=False)
    back, base_query_rows, key_base, value_base = exchange_project(
        owner_out, pieces, w_query, w_key, w_value, "grp", group_count, 1
    )
    adapter_output = jnp.dot(
        jnp.transpose(place_tokens),
        back.reshape(group_count * CAP * step_count, query_width),
        preferred_element_type=jnp.float32,
    )
    base_query_rows = base_query_rows + adapter_output
    position = lengths[:, None] + jnp.arange(step_count, dtype=jnp.int32)[None, :]
    queries = rotate(base_query_rows.reshape(row_count, step_count, q_local, HD), position)
    queries = queries.astype(jnp.bfloat16).reshape(row_count, step_count, kv_local, group_size, HD)
    key_new = rotate(key_base.reshape(row_count, step_count, kv_local, HD), position).astype(
        jnp.bfloat16
    )
    value_new = value_base.reshape(row_count, step_count, kv_local, HD).astype(jnp.bfloat16)
    cache_keys = cache_key.reshape(row_count, cache_key.shape[1], kv_local, HD)
    cache_values = cache_value.reshape(row_count, cache_value.shape[1], kv_local, HD)
    combined = attend(queries, key_new, value_new, cache_keys, cache_values, lengths)
    return combined.reshape(row_count, step_count, query_width)


def solution(mesh):
    in_specs = (
        P("grp", None, "tp"),
        P("grp"),
        P(),
        P("grp"),
        P(None, "tp"),
        P(None, "tp"),
        P(None, "tp"),
        P("grp", "tp", None),
        P("grp", None, "tp"),
        P("grp", None, "tp"),
        P("grp", None, "tp"),
    )
    out_specs = P("grp", None, "tp")
    return jax.shard_map(body, mesh=mesh, in_specs=in_specs, out_specs=out_specs, check_vma=False)
```

```python
import math

import jax
import jax.numpy as jnp
from jax import lax
from jax.experimental import pallas as pl
from jax.experimental.pallas import tpu as pltpu
from jax.sharding import PartitionSpec as P

MESH = pl.DeviceIdType.MESH

HD = 128
CAP = 8


rope_base = 500000.0


def rotate(values, position):
    half_width = values.shape[-1] // 2
    inv_freq = jnp.exp(
        jnp.arange(half_width, dtype=jnp.float32) * (-2.0 * math.log(rope_base) / values.shape[-1])
    )
    angles = position.astype(jnp.float32)[:, :, None, None] * inv_freq
    cosine = jnp.cos(angles)
    sines = jnp.sin(angles)
    front_half = values[..., :half_width]
    back_half = values[..., half_width:]
    return jnp.concatenate(
        [front_half * cosine - back_half * sines, back_half * cosine + front_half * sines], axis=-1
    )


def attend(queries, key_new, value_new, cache_key, cache_value, lengths):
    score_scale = 1.0 / math.sqrt(queries.shape[-1])
    cached = (
        jnp.einsum("rskgd,rlkd->rskgl", queries, cache_key, preferred_element_type=jnp.float32)
        * score_scale
    )
    fresh_scores = (
        jnp.einsum("rskgd,rtkd->rskgt", queries, key_new, preferred_element_type=jnp.float32)
        * score_scale
    )
    live_mask = jnp.arange(cache_key.shape[1], dtype=jnp.int32)[None, :] < lengths[:, None]
    cached = jnp.where(live_mask[:, None, None, None, :], cached, -1e30)
    steps_here = key_new.shape[1]
    causal = (
        jnp.arange(steps_here, dtype=jnp.int32)[:, None]
        >= jnp.arange(steps_here, dtype=jnp.int32)[None, :]
    )
    fresh_scores = jnp.where(causal[None, :, None, None, :], fresh_scores, -1e30)
    row_max = jnp.maximum(jnp.max(cached, axis=-1), jnp.max(fresh_scores, axis=-1))
    cache_exp = jnp.exp(cached - row_max[..., None])
    fresh_exp = jnp.exp(fresh_scores - row_max[..., None])
    weight_sum = jnp.sum(cache_exp, axis=-1) + jnp.sum(fresh_exp, axis=-1)
    cache_weights = (cache_exp / weight_sum[..., None]).astype(jnp.bfloat16)
    fresh_weights = (fresh_exp / weight_sum[..., None]).astype(jnp.bfloat16)
    combined = jnp.einsum(
        "rskgl,rlkd->rskgd", cache_weights, cache_value, preferred_element_type=jnp.float32
    )
    combined = combined + jnp.einsum(
        "rskgt,rtkd->rskgd", fresh_weights, value_new, preferred_element_type=jnp.float32
    )
    return combined.astype(jnp.bfloat16)


TORUS_ORDER = (
    (0, 1), (1, 0), (0, 3), (3, 0), (1, 1), (3, 3), (1, 3), (3, 1),
    (0, 2), (2, 0), (2, 1), (1, 2), (2, 3), (3, 2), (2, 2),
)


def peer_offsets(count):
    if count == 16:
        def shifted(me, dz, dy):
            return lax.rem(me // 4 + dz, 4) * 4 + lax.rem(lax.rem(me, 4) + dy, 4)

        return [
            (lambda me, a=dz, b=dy: shifted(me, a, b), lambda me, a=dz, b=dy: shifted(me, 4 - a, 4 - b))
            for dz, dy in TORUS_ORDER
        ]
    return [
        (lambda me, d=offset: lax.rem(me + d, count), lambda me, d=offset: lax.rem(me + count - d, count))
        for offset in range(1, count)
    ]


def exchange_kernel(axis, count, arrays, *refs):
    send_refs = refs[:arrays]
    got_refs = refs[arrays : 2 * arrays]
    send_sem, recv_sem, local_sem = refs[2 * arrays :]
    me = lax.axis_index(axis)
    barrier = pltpu.get_barrier_semaphore()
    offsets = peer_offsets(count)
    for offset in range(1, count):
        peer = offsets[offset - 1][0](me)
        pl.semaphore_signal(barrier, inc=1, device_id={axis: peer}, device_id_type=MESH)
    pl.semaphore_wait(barrier, count - 1)
    locals_ = []
    for which in range(arrays):
        local = pltpu.make_async_copy(
            send_refs[which].at[me], got_refs[which].at[me], local_sem.at[which]
        )
        local.start()
        locals_.append(local)
    outgoing = []
    for offset in range(1, count):
        peer = offsets[offset - 1][0](me)
        for which in range(arrays):
            copy = pltpu.make_async_remote_copy(
                src_ref=send_refs[which].at[peer],
                dst_ref=got_refs[which].at[me],
                send_sem=send_sem.at[which, offset],
                recv_sem=recv_sem.at[which, offset],
                device_id={axis: peer},
                device_id_type=MESH,
            )
            copy.start()
            outgoing.append(copy)
    for offset in range(1, count):
        source = offsets[offset - 1][1](me)
        for which in range(arrays):
            outgoing[(offset - 1) * arrays + which].wait_send()
            incoming = pltpu.make_async_remote_copy(
                src_ref=send_refs[which].at[source],
                dst_ref=got_refs[which].at[source],
                send_sem=send_sem.at[which, offset],
                recv_sem=recv_sem.at[which, offset],
                device_id={axis: source},
                device_id_type=MESH,
            )
            incoming.wait_recv()
    for local in locals_:
        local.wait()


def exchange(values, axis, count, collective):
    arrays = len(values)
    vmem = pl.BlockSpec(memory_space=pltpu.VMEM)
    return pl.pallas_call(
        lambda *refs: exchange_kernel(axis, count, arrays, *refs),
        out_shape=tuple(jax.ShapeDtypeStruct(v.shape, v.dtype) for v in values),
        in_specs=[vmem] * arrays,
        out_specs=tuple([vmem] * arrays),
        scratch_shapes=[
            pltpu.SemaphoreType.DMA((arrays, count)),
            pltpu.SemaphoreType.DMA((arrays, count)),
            pltpu.SemaphoreType.DMA((arrays,)),
        ],
        compiler_params=pltpu.CompilerParams(collective_id=collective, has_side_effects=True),
    )(*values)


def exchange_gather_kernel(
    axis, count, gather_axis, chips, arrays, *refs
):
    send_refs = refs[:arrays]
    piece_ref = refs[arrays]
    got_refs = refs[arrays + 1 : 2 * arrays + 1]
    pieces_ref = refs[2 * arrays + 1]
    send_sem, recv_sem, local_sem, chip_send, chip_recv, core_send, core_recv, piece_sem = refs[
        2 * arrays + 2 :
    ]
    me = lax.axis_index(axis)
    mine = lax.axis_index(gather_axis)
    chip = mine // 2
    core = lax.rem(mine, 2)
    partner = chip * 2 + (1 - core)

    def chip_peer(step):
        return lax.rem(chip + step, chips) * 2 + core

    barrier = pltpu.get_barrier_semaphore()
    offsets = peer_offsets(count)
    for offset in range(1, count):
        peer = offsets[offset - 1][0](me)
        pl.semaphore_signal(barrier, inc=1, device_id={axis: peer}, device_id_type=MESH)
    for step in range(1, chips):
        pl.semaphore_signal(
            barrier, inc=1, device_id={gather_axis: chip_peer(step)}, device_id_type=MESH
        )
    pl.semaphore_signal(barrier, inc=1, device_id={gather_axis: partner}, device_id_type=MESH)
    pl.semaphore_wait(barrier, count - 1 + chips)

    own_piece = pltpu.make_async_copy(piece_ref, pieces_ref.at[mine], piece_sem)
    own_piece.start()
    chip_copies = []
    for step in range(1, chips):
        copy = pltpu.make_async_remote_copy(
            src_ref=piece_ref,
            dst_ref=pieces_ref.at[mine],
            send_sem=chip_send.at[step],
            recv_sem=chip_recv.at[step],
            device_id={gather_axis: chip_peer(step)},
            device_id_type=MESH,
        )
        copy.start()
        chip_copies.append(copy)
    core_copies = []
    copy = pltpu.make_async_remote_copy(
        src_ref=piece_ref,
        dst_ref=pieces_ref.at[mine],
        send_sem=core_send.at[0],
        recv_sem=core_recv.at[0],
        device_id={gather_axis: partner},
        device_id_type=MESH,
    )
    copy.start()
    core_copies.append(copy)

    locals_ = []
    for which in range(arrays):
        local = pltpu.make_async_copy(
            send_refs[which].at[me], got_refs[which].at[me], local_sem.at[which]
        )
        local.start()
        locals_.append(local)
    outgoing = []
    for offset in range(1, count):
        peer = offsets[offset - 1][0](me)
        for which in range(arrays):
            copy = pltpu.make_async_remote_copy(
                src_ref=send_refs[which].at[peer],
                dst_ref=got_refs[which].at[me],
                send_sem=send_sem.at[which, offset],
                recv_sem=recv_sem.at[which, offset],
                device_id={axis: peer},
                device_id_type=MESH,
            )
            copy.start()
            outgoing.append(copy)

    for step in range(1, chips):
        chip_copies[step - 1].wait_send()
        source = chip_peer(chips - step)
        incoming = pltpu.make_async_remote_copy(
            src_ref=piece_ref,
            dst_ref=pieces_ref.at[source],
            send_sem=chip_send.at[step],
            recv_sem=chip_recv.at[step],
            device_id={gather_axis: source},
            device_id_type=MESH,
        )
        incoming.wait_recv()
        copy = pltpu.make_async_remote_copy(
            src_ref=pieces_ref.at[source],
            dst_ref=pieces_ref.at[source],
            send_sem=core_send.at[step],
            recv_sem=core_recv.at[step],
            device_id={gather_axis: partner},
            device_id_type=MESH,
        )
        copy.start()
        core_copies.append(copy)
    for step in range(chips):
        core_copies[step].wait_send()
        source = lax.rem(chip + chips - step, chips) * 2 + (1 - core)
        incoming = pltpu.make_async_remote_copy(
            src_ref=piece_ref,
            dst_ref=pieces_ref.at[source],
            send_sem=core_send.at[step],
            recv_sem=core_recv.at[step],
            device_id={gather_axis: partner},
            device_id_type=MESH,
        )
        incoming.wait_recv()

    for offset in range(1, count):
        source = offsets[offset - 1][1](me)
        for which in range(arrays):
            outgoing[(offset - 1) * arrays + which].wait_send()
            incoming = pltpu.make_async_remote_copy(
                src_ref=send_refs[which].at[source],
                dst_ref=got_refs[which].at[source],
                send_sem=send_sem.at[which, offset],
                recv_sem=recv_sem.at[which, offset],
                device_id={axis: source},
                device_id_type=MESH,
            )
            incoming.wait_recv()
    for local in locals_:
        local.wait()
    own_piece.wait()


def exchange_gather(values, piece, axis, count, gather_axis, gather_count, collective):
    arrays = len(values)
    chips = gather_count // 2
    vmem = pl.BlockSpec(memory_space=pltpu.VMEM)
    outs = pl.pallas_call(
        lambda *refs: exchange_gather_kernel(axis, count, gather_axis, chips, arrays, *refs),
        out_shape=tuple(jax.ShapeDtypeStruct(v.shape, v.dtype) for v in values)
        + (jax.ShapeDtypeStruct((gather_count,) + piece.shape, piece.dtype),),
        in_specs=[vmem] * (arrays + 1),
        out_specs=tuple([vmem] * (arrays + 1)),
        scratch_shapes=[
            pltpu.SemaphoreType.DMA((arrays, count)),
            pltpu.SemaphoreType.DMA((arrays, count)),
            pltpu.SemaphoreType.DMA((arrays,)),
            pltpu.SemaphoreType.DMA((chips,)),
            pltpu.SemaphoreType.DMA((chips,)),
            pltpu.SemaphoreType.DMA((chips,)),
            pltpu.SemaphoreType.DMA((chips,)),
            pltpu.SemaphoreType.DMA(()),
        ],
        compiler_params=pltpu.CompilerParams(collective_id=collective, has_side_effects=True),
    )(*values, piece)
    return outs[:arrays], outs[arrays]


def exchange_project_kernel(
    axis, count, send_ref, pieces_ref, wq_hbm, wk_ref, wv_ref,
    got_ref, q_ref, k_ref, v_ref,
    wq_buf, send_sem, recv_sem, local_sem, wq_sem,
):
    me = lax.axis_index(axis)
    barrier = pltpu.get_barrier_semaphore()
    offsets = peer_offsets(count)
    for offset in range(1, count):
        peer = offsets[offset - 1][0](me)
        pl.semaphore_signal(barrier, inc=1, device_id={axis: peer}, device_id_type=MESH)
    pl.semaphore_wait(barrier, count - 1)
    local = pltpu.make_async_copy(send_ref.at[me], got_ref.at[me], local_sem)
    local.start()
    outgoing = []
    for offset in range(1, count):
        peer = offsets[offset - 1][0](me)
        copy = pltpu.make_async_remote_copy(
            src_ref=send_ref.at[peer],
            dst_ref=got_ref.at[me],
            send_sem=send_sem.at[offset],
            recv_sem=recv_sem.at[offset],
            device_id={axis: peer},
            device_id_type=MESH,
        )
        copy.start()
        outgoing.append(copy)

    piece_count, unused_item, piece_width = pieces_ref.shape

    def chunk_copy(index, slot):
        return pltpu.make_async_copy(
            wq_hbm.at[pl.ds(pl.multiple_of(index * piece_width, piece_width), piece_width)],
            wq_buf.at[slot],
            wq_sem.at[slot],
        )

    chunk_copy(0, 0).start()
    q_ref[...] = jnp.zeros_like(q_ref)
    k_ref[...] = jnp.zeros_like(k_ref)
    v_ref[...] = jnp.zeros_like(v_ref)

    def project(index, carry):
        slot = lax.rem(index, 2)
        chunk_copy(index, slot).wait()

        @pl.when(index + 1 < piece_count)
        def _():
            chunk_copy(index + 1, 1 - slot).start()

        rows = pl.ds(pl.multiple_of(index * piece_width, piece_width), piece_width)
        piece = pieces_ref[index]
        q_ref[...] += jnp.dot(piece, wq_buf[slot], preferred_element_type=jnp.float32)
        k_ref[...] += jnp.dot(piece, wk_ref[rows, :], preferred_element_type=jnp.float32)
        v_ref[...] += jnp.dot(piece, wv_ref[rows, :], preferred_element_type=jnp.float32)
        return carry

    lax.fori_loop(0, piece_count, project, 0)

    for offset in range(1, count):
        outgoing[offset - 1].wait_send()
        source = offsets[offset - 1][1](me)
        incoming = pltpu.make_async_remote_copy(
            src_ref=send_ref.at[source],
            dst_ref=got_ref.at[source],
            send_sem=send_sem.at[offset],
            recv_sem=recv_sem.at[offset],
            device_id={axis: source},
            device_id_type=MESH,
        )
        incoming.wait_recv()
    local.wait()


def exchange_project(values, pieces, w_query, w_key, w_value, axis, count, collective):
    piece_count, token_count, piece_width = pieces.shape
    vmem = pl.BlockSpec(memory_space=pltpu.VMEM)
    return pl.pallas_call(
        lambda *refs: exchange_project_kernel(axis, count, *refs),
        out_shape=(
            jax.ShapeDtypeStruct(values.shape, values.dtype),
            jax.ShapeDtypeStruct((token_count, w_query.shape[1]), jnp.float32),
            jax.ShapeDtypeStruct((token_count, w_key.shape[1]), jnp.float32),
            jax.ShapeDtypeStruct((token_count, w_value.shape[1]), jnp.float32),
        ),
        in_specs=[vmem, vmem, pl.BlockSpec(memory_space=pl.ANY), vmem, vmem],
        out_specs=(vmem, vmem, vmem, vmem),
        scratch_shapes=[
            pltpu.VMEM((2, piece_width, w_query.shape[1]), w_query.dtype),
            pltpu.SemaphoreType.DMA((count,)),
            pltpu.SemaphoreType.DMA((count,)),
            pltpu.SemaphoreType.DMA(()),
            pltpu.SemaphoreType.DMA((2,)),
        ],
        compiler_params=pltpu.CompilerParams(
            collective_id=collective, has_side_effects=True, vmem_limit_bytes=60 * 1024 * 1024
        ),
    )(values, pieces, w_query, w_key, w_value)


def sum_kernel(axis, count, part_ref, total_ref, held, first_send, first_recv, second_send, second_recv):
    me = lax.axis_index(axis)
    barrier = pltpu.get_barrier_semaphore()
    for offset in range(1, count):
        peer = lax.rem(me + offset, count)
        pl.semaphore_signal(barrier, inc=1, device_id={axis: peer}, device_id_type=MESH)
    pl.semaphore_wait(barrier, count - 1)
    outgoing = []
    for offset in range(1, count):
        peer = lax.rem(me + offset, count)
        copy = pltpu.make_async_remote_copy(
            src_ref=part_ref.at[peer],
            dst_ref=held.at[me],
            send_sem=first_send.at[offset],
            recv_sem=first_recv.at[offset],
            device_id={axis: peer},
            device_id_type=MESH,
        )
        copy.start()
        outgoing.append(copy)
    held[me] = part_ref[me]
    for offset in range(1, count):
        outgoing[offset - 1].wait_send()
        source = lax.rem(me + count - offset, count)
        incoming = pltpu.make_async_remote_copy(
            src_ref=part_ref.at[source],
            dst_ref=held.at[source],
            send_sem=first_send.at[offset],
            recv_sem=first_recv.at[offset],
            device_id={axis: source},
            device_id_type=MESH,
        )
        incoming.wait_recv()
    total = held[0]
    for index in range(1, count):
        total = total + held[index]
    total_ref[me] = total.astype(total_ref.dtype)
    outgoing = []
    for offset in range(1, count):
        peer = lax.rem(me + offset, count)
        copy = pltpu.make_async_remote_copy(
            src_ref=total_ref.at[me],
            dst_ref=total_ref.at[me],
            send_sem=second_send.at[offset],
            recv_sem=second_recv.at[offset],
            device_id={axis: peer},
            device_id_type=MESH,
        )
        copy.start()
        outgoing.append(copy)
    for offset in range(1, count):
        outgoing[offset - 1].wait_send()
        source = lax.rem(me + count - offset, count)
        incoming = pltpu.make_async_remote_copy(
            src_ref=total_ref.at[source],
            dst_ref=total_ref.at[source],
            send_sem=second_send.at[offset],
            recv_sem=second_recv.at[offset],
            device_id={axis: source},
            device_id_type=MESH,
        )
        incoming.wait_recv()


def axis_sum(values, axis, count, collective, out_dtype):
    chunks = values.reshape(count, -1, 128)
    summed = pl.pallas_call(
        lambda *refs: sum_kernel(axis, count, *refs),
        out_shape=jax.ShapeDtypeStruct(chunks.shape, out_dtype),
        in_specs=[pl.BlockSpec(memory_space=pltpu.VMEM)],
        out_specs=pl.BlockSpec(memory_space=pltpu.VMEM),
        scratch_shapes=[
            pltpu.VMEM(chunks.shape, values.dtype),
            pltpu.SemaphoreType.DMA((count,)),
            pltpu.SemaphoreType.DMA((count,)),
            pltpu.SemaphoreType.DMA((count,)),
            pltpu.SemaphoreType.DMA((count,)),
        ],
        compiler_params=pltpu.CompilerParams(collective_id=collective, has_side_effects=True),
    )(chunks)
    return summed.reshape(values.shape)


def owner_adapter_term(received, slot_ids, down_local, up_local):
    sources, rows, part_width = received.shape
    local_adapters, unused_item, adapter_rank = down_local.shape
    query_width = up_local.shape[2]
    token_rows = received.reshape(sources * rows, part_width)
    every_down = jnp.einsum(
        "td,adr->tar", token_rows, down_local, preferred_element_type=jnp.float32
    )
    pick = slot_ids.reshape(sources * rows)[:, None] == jnp.arange(local_adapters, dtype=jnp.int32)[None, :]
    partial_value_sum = jnp.sum(jnp.where(pick[:, :, None], every_down, 0.0), axis=1)
    tp_count = lax.axis_size("tp")
    summed = axis_sum(partial_value_sum.reshape(-1, 128), "tp", tp_count, 2, jnp.bfloat16)
    adapter_middle = summed.reshape(sources * rows, adapter_rank)
    spread_rows = jnp.where(pick[:, :, None], adapter_middle[:, None, :], jnp.zeros((), jnp.bfloat16))
    spread_rows = spread_rows.reshape(sources * rows, local_adapters * adapter_rank)
    adapter_output = jnp.dot(
        spread_rows,
        up_local.reshape(local_adapters * adapter_rank, query_width),
        preferred_element_type=jnp.float32,
    ).astype(jnp.bfloat16)
    return adapter_output.reshape(sources, rows, query_width)


def body(
    tokens,
    adapter_id,
    pool_slot,
    lengths,
    w_query,
    w_key,
    w_value,
    pooled_down_weights,
    pool_up,
    cache_key,
    cache_value,
):
    group_count = lax.axis_size("grp")
    tp_count = lax.axis_size("tp")
    row_count, step_count, part_width = tokens.shape
    local_adapter_rows, unused_item, adapter_rank = pooled_down_weights.shape
    query_width = w_query.shape[1]
    kv_width = w_key.shape[1]
    kv_local = kv_width // HD
    q_local = query_width // HD
    group_size = q_local // kv_local
    count_of_tokens = row_count * step_count
    adapter_span = jnp.arange(pool_slot.shape[0], dtype=jnp.int32)
    pool_pos = jnp.sum(
        jnp.where(adapter_id[:, None] == adapter_span[None, :], pool_slot[None, :], 0), axis=1
    )
    owner_grp = pool_pos // local_adapter_rows
    local_slot = pool_pos % local_adapter_rows
    row_span = jnp.arange(row_count, dtype=jnp.int32)
    same_owner = (owner_grp[:, None] == owner_grp[None, :]) & (row_span[None, :] < row_span[:, None])
    owner_rank = jnp.sum(same_owner.astype(jnp.int32), axis=1)
    send_slot = owner_grp * CAP + owner_rank
    slot_span = jnp.arange(group_count * CAP, dtype=jnp.int32)
    place = (slot_span[:, None] == send_slot[None, :]).astype(jnp.bfloat16)
    token_slot = (send_slot[:, None] * step_count + jnp.arange(step_count, dtype=jnp.int32)[None, :]).reshape(-1)
    token_span = jnp.arange(group_count * CAP * step_count, dtype=jnp.int32)
    place_tokens = (token_span[:, None] == token_slot[None, :]).astype(jnp.bfloat16)
    token_rows = tokens.reshape(count_of_tokens, part_width)
    send_tokens = jnp.dot(place_tokens, token_rows, preferred_element_type=jnp.float32).astype(jnp.bfloat16)
    send_tokens = send_tokens.reshape(group_count, CAP * step_count, part_width)
    send_ids = jnp.dot(
        place, local_slot.astype(jnp.bfloat16)[:, None], preferred_element_type=jnp.float32
    ).astype(jnp.bfloat16)
    send_ids = jnp.broadcast_to(send_ids.reshape(group_count, CAP, 1), (group_count, CAP, 128))
    send_ids = jnp.concatenate([send_ids, jnp.zeros_like(send_ids)], axis=1)
    (got_tokens, got_ids), pieces = exchange_gather(
        (send_tokens, send_ids), token_rows, "grp", group_count, "tp", tp_count, 0
    )
    got_ids = jnp.repeat(got_ids[:, :CAP, 0].astype(jnp.int32), step_count, axis=1)
    owner_out = owner_adapter_term(got_tokens, got_ids, pooled_down_weights, pool_up)
    back, base_query_rows, key_base, value_base = exchange_project(
        owner_out, pieces, w_query, w_key, w_value, "grp", group_count, 1
    )
    adapter_output = jnp.dot(
        jnp.transpose(place_tokens),
        back.reshape(group_count * CAP * step_count, query_width),
        preferred_element_type=jnp.float32,
    )
    base_query_rows = base_query_rows + adapter_output
    position = lengths[:, None] + jnp.arange(step_count, dtype=jnp.int32)[None, :]
    queries = rotate(base_query_rows.reshape(row_count, step_count, q_local, HD), position)
    queries = queries.astype(jnp.bfloat16).reshape(row_count, step_count, kv_local, group_size, HD)
    key_new = rotate(key_base.reshape(row_count, step_count, kv_local, HD), position).astype(
        jnp.bfloat16
    )
    value_new = value_base.reshape(row_count, step_count, kv_local, HD).astype(jnp.bfloat16)
    cache_keys = cache_key.reshape(row_count, cache_key.shape[1], kv_local, HD)
    cache_values = cache_value.reshape(row_count, cache_value.shape[1], kv_local, HD)
    combined = attend(queries, key_new, value_new, cache_keys, cache_values, lengths)
    return combined.reshape(row_count, step_count, query_width)


def solution(mesh):
    in_specs = (
        P("grp", None, "tp"),
        P("grp"),
        P(),
        P("grp"),
        P(None, "tp"),
        P(None, "tp"),
        P(None, "tp"),
        P("grp", "tp", None),
        P("grp", None, "tp"),
        P("grp", None, "tp"),
        P("grp", None, "tp"),
    )
    out_specs = P("grp", None, "tp")
    return jax.shard_map(body, mesh=mesh, in_specs=in_specs, out_specs=out_specs, check_vma=False)
```

```python
import math

import jax
import jax.numpy as jnp
from jax import lax
from jax.experimental import pallas as pl
from jax.experimental.pallas import tpu as pltpu
from jax.sharding import PartitionSpec as P

MESH = pl.DeviceIdType.MESH

HD = 128
CAP = 8


rope_base = 500000.0


def rotate(values, position):
    half_width = values.shape[-1] // 2
    inv_freq = jnp.exp(
        jnp.arange(half_width, dtype=jnp.float32) * (-2.0 * math.log(rope_base) / values.shape[-1])
    )
    angles = position.astype(jnp.float32)[:, :, None, None] * inv_freq
    cosine = jnp.cos(angles)
    sines = jnp.sin(angles)
    front_half = values[..., :half_width]
    back_half = values[..., half_width:]
    return jnp.concatenate(
        [front_half * cosine - back_half * sines, back_half * cosine + front_half * sines], axis=-1
    )


def attend(queries, key_new, value_new, cache_key, cache_value, lengths):
    score_scale = 1.0 / math.sqrt(queries.shape[-1])
    cached = (
        jnp.einsum("rskgd,rlkd->rskgl", queries, cache_key, preferred_element_type=jnp.float32)
        * score_scale
    )
    fresh_scores = (
        jnp.einsum("rskgd,rtkd->rskgt", queries, key_new, preferred_element_type=jnp.float32)
        * score_scale
    )
    live_mask = jnp.arange(cache_key.shape[1], dtype=jnp.int32)[None, :] < lengths[:, None]
    cached = jnp.where(live_mask[:, None, None, None, :], cached, -1e30)
    steps_here = key_new.shape[1]
    causal = (
        jnp.arange(steps_here, dtype=jnp.int32)[:, None]
        >= jnp.arange(steps_here, dtype=jnp.int32)[None, :]
    )
    fresh_scores = jnp.where(causal[None, :, None, None, :], fresh_scores, -1e30)
    row_max = jnp.maximum(jnp.max(cached, axis=-1), jnp.max(fresh_scores, axis=-1))
    cache_exp = jnp.exp(cached - row_max[..., None])
    fresh_exp = jnp.exp(fresh_scores - row_max[..., None])
    weight_sum = jnp.sum(cache_exp, axis=-1) + jnp.sum(fresh_exp, axis=-1)
    cache_weights = (cache_exp / weight_sum[..., None]).astype(jnp.bfloat16)
    fresh_weights = (fresh_exp / weight_sum[..., None]).astype(jnp.bfloat16)
    combined = jnp.einsum(
        "rskgl,rlkd->rskgd", cache_weights, cache_value, preferred_element_type=jnp.float32
    )
    combined = combined + jnp.einsum(
        "rskgt,rtkd->rskgd", fresh_weights, value_new, preferred_element_type=jnp.float32
    )
    return combined.astype(jnp.bfloat16)


TORUS_ORDER = (
    (0, 1), (1, 0), (0, 3), (3, 0), (1, 1), (3, 3), (1, 3), (3, 1),
    (0, 2), (2, 0), (2, 1), (1, 2), (2, 3), (3, 2), (2, 2),
)


def peer_offsets(count):
    if count == 16:
        def shifted(me, dz, dy):
            return lax.rem(me // 4 + dz, 4) * 4 + lax.rem(lax.rem(me, 4) + dy, 4)

        return [
            (lambda me, a=dz, b=dy: shifted(me, a, b), lambda me, a=dz, b=dy: shifted(me, 4 - a, 4 - b))
            for dz, dy in TORUS_ORDER
        ]
    return [
        (lambda me, d=offset: lax.rem(me + d, count), lambda me, d=offset: lax.rem(me + count - d, count))
        for offset in range(1, count)
    ]


def exchange_kernel(axis, count, arrays, *refs):
    send_refs = refs[:arrays]
    got_refs = refs[arrays : 2 * arrays]
    send_sem, recv_sem, local_sem = refs[2 * arrays :]
    me = lax.axis_index(axis)
    barrier = pltpu.get_barrier_semaphore()
    offsets = peer_offsets(count)
    for offset in range(1, count):
        peer = offsets[offset - 1][0](me)
        pl.semaphore_signal(barrier, inc=1, device_id={axis: peer}, device_id_type=MESH)
    pl.semaphore_wait(barrier, count - 1)
    locals_ = []
    for which in range(arrays):
        local = pltpu.make_async_copy(
            send_refs[which].at[me], got_refs[which].at[me], local_sem.at[which]
        )
        local.start()
        locals_.append(local)
    outgoing = []
    for offset in range(1, count):
        peer = offsets[offset - 1][0](me)
        for which in range(arrays):
            copy = pltpu.make_async_remote_copy(
                src_ref=send_refs[which].at[peer],
                dst_ref=got_refs[which].at[me],
                send_sem=send_sem.at[which, offset],
                recv_sem=recv_sem.at[which, offset],
                device_id={axis: peer},
                device_id_type=MESH,
            )
            copy.start()
            outgoing.append(copy)
    for offset in range(1, count):
        source = offsets[offset - 1][1](me)
        for which in range(arrays):
            outgoing[(offset - 1) * arrays + which].wait_send()
            incoming = pltpu.make_async_remote_copy(
                src_ref=send_refs[which].at[source],
                dst_ref=got_refs[which].at[source],
                send_sem=send_sem.at[which, offset],
                recv_sem=recv_sem.at[which, offset],
                device_id={axis: source},
                device_id_type=MESH,
            )
            incoming.wait_recv()
    for local in locals_:
        local.wait()


def exchange(values, axis, count, collective):
    arrays = len(values)
    vmem = pl.BlockSpec(memory_space=pltpu.VMEM)
    return pl.pallas_call(
        lambda *refs: exchange_kernel(axis, count, arrays, *refs),
        out_shape=tuple(jax.ShapeDtypeStruct(v.shape, v.dtype) for v in values),
        in_specs=[vmem] * arrays,
        out_specs=tuple([vmem] * arrays),
        scratch_shapes=[
            pltpu.SemaphoreType.DMA((arrays, count)),
            pltpu.SemaphoreType.DMA((arrays, count)),
            pltpu.SemaphoreType.DMA((arrays,)),
        ],
        compiler_params=pltpu.CompilerParams(collective_id=collective, has_side_effects=True),
    )(*values)


def exchange_project_kernel(
    axis, count, gather_axis, send_ref, chip_pieces, wq_hbm, wk_ref, wv_ref,
    got_ref, q_ref, k_ref, v_ref,
    partner_pieces, wq_buf, send_sem, recv_sem, local_sem, wq_sem, partner_send, partner_recv,
):
    me = lax.axis_index(axis)
    mine = lax.axis_index(gather_axis)
    core = lax.rem(mine, 2)
    partner = (mine // 2) * 2 + (1 - core)
    barrier = pltpu.get_barrier_semaphore()
    offsets = peer_offsets(count)
    for offset in range(1, count):
        peer = offsets[offset - 1][0](me)
        pl.semaphore_signal(barrier, inc=1, device_id={axis: peer}, device_id_type=MESH)
    pl.semaphore_signal(barrier, inc=1, device_id={gather_axis: partner}, device_id_type=MESH)
    pl.semaphore_wait(barrier, count)
    to_partner = pltpu.make_async_remote_copy(
        src_ref=chip_pieces,
        dst_ref=partner_pieces,
        send_sem=partner_send,
        recv_sem=partner_recv,
        device_id={gather_axis: partner},
        device_id_type=MESH,
    )
    to_partner.start()
    local = pltpu.make_async_copy(send_ref.at[me], got_ref.at[me], local_sem)
    local.start()
    outgoing = []
    for offset in range(1, count):
        peer = offsets[offset - 1][0](me)
        copy = pltpu.make_async_remote_copy(
            src_ref=send_ref.at[peer],
            dst_ref=got_ref.at[me],
            send_sem=send_sem.at[offset],
            recv_sem=recv_sem.at[offset],
            device_id={axis: peer},
            device_id_type=MESH,
        )
        copy.start()
        outgoing.append(copy)

    chips, unused_item, piece_width = chip_pieces.shape
    steps = 2 * chips

    def chunk_copy(step, slot):
        index = lax.rem(step, chips) * 2 + core + (step // chips) * (1 - 2 * core)
        return pltpu.make_async_copy(
            wq_hbm.at[pl.ds(pl.multiple_of(index * piece_width, piece_width), piece_width)],
            wq_buf.at[slot],
            wq_sem.at[slot],
        )

    chunk_copy(0, 0).start()
    q_ref[...] = jnp.zeros_like(q_ref)
    k_ref[...] = jnp.zeros_like(k_ref)
    v_ref[...] = jnp.zeros_like(v_ref)

    def project(step, piece):
        slot = lax.rem(step, 2)
        chunk_copy(step, slot).wait()

        @pl.when(step + 1 < steps)
        def _():
            chunk_copy(step + 1, 1 - slot).start()

        index = lax.rem(step, chips) * 2 + core + (step // chips) * (1 - 2 * core)
        rows = pl.ds(pl.multiple_of(index * piece_width, piece_width), piece_width)
        q_ref[...] += jnp.dot(piece, wq_buf[slot], preferred_element_type=jnp.float32)
        k_ref[...] += jnp.dot(piece, wk_ref[rows, :], preferred_element_type=jnp.float32)
        v_ref[...] += jnp.dot(piece, wv_ref[rows, :], preferred_element_type=jnp.float32)

    def own_step(step, carry):
        project(step, chip_pieces[step])
        return carry

    def partner_step(step, carry):
        project(step, partner_pieces[step - chips])
        return carry

    lax.fori_loop(0, chips, own_step, 0)
    to_partner.wait_send()
    to_partner.wait_recv()
    lax.fori_loop(chips, steps, partner_step, 0)

    for offset in range(1, count):
        outgoing[offset - 1].wait_send()
        source = offsets[offset - 1][1](me)
        incoming = pltpu.make_async_remote_copy(
            src_ref=send_ref.at[source],
            dst_ref=got_ref.at[source],
            send_sem=send_sem.at[offset],
            recv_sem=recv_sem.at[offset],
            device_id={axis: source},
            device_id_type=MESH,
        )
        incoming.wait_recv()
    local.wait()


def exchange_project(values, chip_pieces, w_query, w_key, w_value, axis, count, gather_axis, collective):
    chips, token_count, piece_width = chip_pieces.shape
    vmem = pl.BlockSpec(memory_space=pltpu.VMEM)
    return pl.pallas_call(
        lambda *refs: exchange_project_kernel(axis, count, gather_axis, *refs),
        out_shape=(
            jax.ShapeDtypeStruct(values.shape, values.dtype),
            jax.ShapeDtypeStruct((token_count, w_query.shape[1]), jnp.float32),
            jax.ShapeDtypeStruct((token_count, w_key.shape[1]), jnp.float32),
            jax.ShapeDtypeStruct((token_count, w_value.shape[1]), jnp.float32),
        ),
        in_specs=[vmem, vmem, pl.BlockSpec(memory_space=pl.ANY), vmem, vmem],
        out_specs=(vmem, vmem, vmem, vmem),
        scratch_shapes=[
            pltpu.VMEM(chip_pieces.shape, chip_pieces.dtype),
            pltpu.VMEM((2, piece_width, w_query.shape[1]), w_query.dtype),
            pltpu.SemaphoreType.DMA((count,)),
            pltpu.SemaphoreType.DMA((count,)),
            pltpu.SemaphoreType.DMA(()),
            pltpu.SemaphoreType.DMA((2,)),
            pltpu.SemaphoreType.DMA(()),
            pltpu.SemaphoreType.DMA(()),
        ],
        compiler_params=pltpu.CompilerParams(
            collective_id=collective, has_side_effects=True, vmem_limit_bytes=60 * 1024 * 1024
        ),
    )(values, chip_pieces, w_query, w_key, w_value)


def sum_kernel(axis, count, part_ref, piece_ref, total_ref, chip_pieces, held, first_send, first_recv,
               second_send, second_recv, chip_send, chip_recv, piece_sem):
    me = lax.axis_index(axis)
    chips = count // 2
    chip = me // 2
    core = lax.rem(me, 2)

    def chip_peer(step):
        return lax.rem(chip + step, chips) * 2 + core

    barrier = pltpu.get_barrier_semaphore()
    for offset in range(1, count):
        peer = lax.rem(me + offset, count)
        pl.semaphore_signal(barrier, inc=1, device_id={axis: peer}, device_id_type=MESH)
    pl.semaphore_wait(barrier, count - 1)
    outgoing = []
    for offset in range(1, count):
        peer = lax.rem(me + offset, count)
        copy = pltpu.make_async_remote_copy(
            src_ref=part_ref.at[peer],
            dst_ref=held.at[me],
            send_sem=first_send.at[offset],
            recv_sem=first_recv.at[offset],
            device_id={axis: peer},
            device_id_type=MESH,
        )
        copy.start()
        outgoing.append(copy)
    own_piece = pltpu.make_async_copy(piece_ref, chip_pieces.at[chip], piece_sem)
    own_piece.start()
    chip_copies = []
    for step in range(1, chips):
        copy = pltpu.make_async_remote_copy(
            src_ref=piece_ref,
            dst_ref=chip_pieces.at[chip],
            send_sem=chip_send.at[step],
            recv_sem=chip_recv.at[step],
            device_id={axis: chip_peer(step)},
            device_id_type=MESH,
        )
        copy.start()
        chip_copies.append(copy)
    held[me] = part_ref[me]
    for offset in range(1, count):
        outgoing[offset - 1].wait_send()
        source = lax.rem(me + count - offset, count)
        incoming = pltpu.make_async_remote_copy(
            src_ref=part_ref.at[source],
            dst_ref=held.at[source],
            send_sem=first_send.at[offset],
            recv_sem=first_recv.at[offset],
            device_id={axis: source},
            device_id_type=MESH,
        )
        incoming.wait_recv()
    total = held[0]
    for index in range(1, count):
        total = total + held[index]
    total_ref[me] = total.astype(total_ref.dtype)
    outgoing = []
    for offset in range(1, count):
        peer = lax.rem(me + offset, count)
        copy = pltpu.make_async_remote_copy(
            src_ref=total_ref.at[me],
            dst_ref=total_ref.at[me],
            send_sem=second_send.at[offset],
            recv_sem=second_recv.at[offset],
            device_id={axis: peer},
            device_id_type=MESH,
        )
        copy.start()
        outgoing.append(copy)
    for offset in range(1, count):
        outgoing[offset - 1].wait_send()
        source = lax.rem(me + count - offset, count)
        incoming = pltpu.make_async_remote_copy(
            src_ref=total_ref.at[source],
            dst_ref=total_ref.at[source],
            send_sem=second_send.at[offset],
            recv_sem=second_recv.at[offset],
            device_id={axis: source},
            device_id_type=MESH,
        )
        incoming.wait_recv()
    for step in range(1, chips):
        chip_copies[step - 1].wait_send()
        source_chip = lax.rem(chip + chips - step, chips)
        incoming = pltpu.make_async_remote_copy(
            src_ref=piece_ref,
            dst_ref=chip_pieces.at[source_chip],
            send_sem=chip_send.at[step],
            recv_sem=chip_recv.at[step],
            device_id={axis: source_chip * 2 + core},
            device_id_type=MESH,
        )
        incoming.wait_recv()
    own_piece.wait()


def axis_sum(values, piece, axis, count, collective, out_dtype):
    chunks = values.reshape(count, -1, 128)
    chips = count // 2
    vmem = pl.BlockSpec(memory_space=pltpu.VMEM)
    summed, chip_pieces = pl.pallas_call(
        lambda *refs: sum_kernel(axis, count, *refs),
        out_shape=(
            jax.ShapeDtypeStruct(chunks.shape, out_dtype),
            jax.ShapeDtypeStruct((chips,) + piece.shape, piece.dtype),
        ),
        in_specs=[vmem, vmem],
        out_specs=(vmem, vmem),
        scratch_shapes=[
            pltpu.VMEM(chunks.shape, values.dtype),
            pltpu.SemaphoreType.DMA((count,)),
            pltpu.SemaphoreType.DMA((count,)),
            pltpu.SemaphoreType.DMA((count,)),
            pltpu.SemaphoreType.DMA((count,)),
            pltpu.SemaphoreType.DMA((chips,)),
            pltpu.SemaphoreType.DMA((chips,)),
            pltpu.SemaphoreType.DMA(()),
        ],
        compiler_params=pltpu.CompilerParams(collective_id=collective, has_side_effects=True),
    )(chunks, piece)
    return summed.reshape(values.shape), chip_pieces


def owner_adapter_term(received, slot_ids, piece, down_local, up_local):
    sources, rows, part_width = received.shape
    local_adapters, unused_item, adapter_rank = down_local.shape
    query_width = up_local.shape[2]
    token_rows = received.reshape(sources * rows, part_width)
    every_down = jnp.einsum(
        "td,adr->tar", token_rows, down_local, preferred_element_type=jnp.float32
    )
    pick = slot_ids.reshape(sources * rows)[:, None] == jnp.arange(local_adapters, dtype=jnp.int32)[None, :]
    partial_value_sum = jnp.sum(jnp.where(pick[:, :, None], every_down, 0.0), axis=1)
    tp_count = lax.axis_size("tp")
    summed, chip_pieces = axis_sum(
        partial_value_sum.reshape(-1, 128), piece, "tp", tp_count, 2, jnp.bfloat16
    )
    adapter_middle = summed.reshape(sources * rows, adapter_rank)
    spread_rows = jnp.where(pick[:, :, None], adapter_middle[:, None, :], jnp.zeros((), jnp.bfloat16))
    spread_rows = spread_rows.reshape(sources * rows, local_adapters * adapter_rank)
    adapter_output = jnp.dot(
        spread_rows,
        up_local.reshape(local_adapters * adapter_rank, query_width),
        preferred_element_type=jnp.float32,
    ).astype(jnp.bfloat16)
    return adapter_output.reshape(sources, rows, query_width), chip_pieces


def body(
    tokens,
    adapter_id,
    pool_slot,
    lengths,
    w_query,
    w_key,
    w_value,
    pooled_down_weights,
    pool_up,
    cache_key,
    cache_value,
):
    group_count = lax.axis_size("grp")
    tp_count = lax.axis_size("tp")
    row_count, step_count, part_width = tokens.shape
    local_adapter_rows, unused_item, adapter_rank = pooled_down_weights.shape
    query_width = w_query.shape[1]
    kv_width = w_key.shape[1]
    kv_local = kv_width // HD
    q_local = query_width // HD
    group_size = q_local // kv_local
    count_of_tokens = row_count * step_count
    adapter_span = jnp.arange(pool_slot.shape[0], dtype=jnp.int32)
    pool_pos = jnp.sum(
        jnp.where(adapter_id[:, None] == adapter_span[None, :], pool_slot[None, :], 0), axis=1
    )
    owner_grp = pool_pos // local_adapter_rows
    local_slot = pool_pos % local_adapter_rows
    row_span = jnp.arange(row_count, dtype=jnp.int32)
    same_owner = (owner_grp[:, None] == owner_grp[None, :]) & (row_span[None, :] < row_span[:, None])
    owner_rank = jnp.sum(same_owner.astype(jnp.int32), axis=1)
    send_slot = owner_grp * CAP + owner_rank
    slot_span = jnp.arange(group_count * CAP, dtype=jnp.int32)
    place = (slot_span[:, None] == send_slot[None, :]).astype(jnp.bfloat16)
    token_slot = (send_slot[:, None] * step_count + jnp.arange(step_count, dtype=jnp.int32)[None, :]).reshape(-1)
    token_span = jnp.arange(group_count * CAP * step_count, dtype=jnp.int32)
    place_tokens = (token_span[:, None] == token_slot[None, :]).astype(jnp.bfloat16)
    token_rows = tokens.reshape(count_of_tokens, part_width)
    send_tokens = jnp.dot(place_tokens, token_rows, preferred_element_type=jnp.float32).astype(jnp.bfloat16)
    send_tokens = send_tokens.reshape(group_count, CAP * step_count, part_width)
    send_ids = jnp.dot(
        place, local_slot.astype(jnp.bfloat16)[:, None], preferred_element_type=jnp.float32
    ).astype(jnp.bfloat16)
    send_ids = jnp.broadcast_to(send_ids.reshape(group_count, CAP, 1), (group_count, CAP, 128))
    send_ids = jnp.concatenate([send_ids, jnp.zeros_like(send_ids)], axis=1)
    got_tokens, got_ids = exchange((send_tokens, send_ids), "grp", group_count, 0)
    got_ids = jnp.repeat(got_ids[:, :CAP, 0].astype(jnp.int32), step_count, axis=1)
    owner_out, chip_pieces = owner_adapter_term(
        got_tokens, got_ids, token_rows, pooled_down_weights, pool_up
    )
    back, base_query_rows, key_base, value_base = exchange_project(
        owner_out, chip_pieces, w_query, w_key, w_value, "grp", group_count, "tp", 1
    )
    adapter_output = jnp.dot(
        jnp.transpose(place_tokens),
        back.reshape(group_count * CAP * step_count, query_width),
        preferred_element_type=jnp.float32,
    )
    base_query_rows = base_query_rows + adapter_output
    position = lengths[:, None] + jnp.arange(step_count, dtype=jnp.int32)[None, :]
    queries = rotate(base_query_rows.reshape(row_count, step_count, q_local, HD), position)
    queries = queries.astype(jnp.bfloat16).reshape(row_count, step_count, kv_local, group_size, HD)
    key_new = rotate(key_base.reshape(row_count, step_count, kv_local, HD), position).astype(
        jnp.bfloat16
    )
    value_new = value_base.reshape(row_count, step_count, kv_local, HD).astype(jnp.bfloat16)
    cache_keys = cache_key.reshape(row_count, cache_key.shape[1], kv_local, HD)
    cache_values = cache_value.reshape(row_count, cache_value.shape[1], kv_local, HD)
    combined = attend(queries, key_new, value_new, cache_keys, cache_values, lengths)
    return combined.reshape(row_count, step_count, query_width)


def solution(mesh):
    in_specs = (
        P("grp", None, "tp"),
        P("grp"),
        P(),
        P("grp"),
        P(None, "tp"),
        P(None, "tp"),
        P(None, "tp"),
        P("grp", "tp", None),
        P("grp", None, "tp"),
        P("grp", None, "tp"),
        P("grp", None, "tp"),
    )
    out_specs = P("grp", None, "tp")
    return jax.shard_map(body, mesh=mesh, in_specs=in_specs, out_specs=out_specs, check_vma=False)
```

```python
import math

import jax
import jax.numpy as jnp
from jax import lax
from jax.experimental import pallas as pl
from jax.experimental.pallas import tpu as pltpu
from jax.sharding import PartitionSpec as P

MESH = pl.DeviceIdType.MESH

HD = 128
CAP = 8


rope_base = 500000.0


def rotate(values, position):
    half_width = values.shape[-1] // 2
    inv_freq = jnp.exp(
        jnp.arange(half_width, dtype=jnp.float32) * (-2.0 * math.log(rope_base) / values.shape[-1])
    )
    angles = position.astype(jnp.float32)[:, :, None, None] * inv_freq
    cosine = jnp.cos(angles)
    sines = jnp.sin(angles)
    front_half = values[..., :half_width]
    back_half = values[..., half_width:]
    return jnp.concatenate(
        [front_half * cosine - back_half * sines, back_half * cosine + front_half * sines], axis=-1
    )


def attend(queries, key_new, value_new, cache_key, cache_value, lengths):
    score_scale = 1.0 / math.sqrt(queries.shape[-1])
    cached = (
        jnp.einsum("rskgd,rlkd->rskgl", queries, cache_key, preferred_element_type=jnp.float32)
        * score_scale
    )
    fresh_scores = (
        jnp.einsum("rskgd,rtkd->rskgt", queries, key_new, preferred_element_type=jnp.float32)
        * score_scale
    )
    live_mask = jnp.arange(cache_key.shape[1], dtype=jnp.int32)[None, :] < lengths[:, None]
    cached = jnp.where(live_mask[:, None, None, None, :], cached, -1e30)
    steps_here = key_new.shape[1]
    causal = (
        jnp.arange(steps_here, dtype=jnp.int32)[:, None]
        >= jnp.arange(steps_here, dtype=jnp.int32)[None, :]
    )
    fresh_scores = jnp.where(causal[None, :, None, None, :], fresh_scores, -1e30)
    row_max = jnp.maximum(jnp.max(cached, axis=-1), jnp.max(fresh_scores, axis=-1))
    cache_exp = jnp.exp(cached - row_max[..., None])
    fresh_exp = jnp.exp(fresh_scores - row_max[..., None])
    weight_sum = jnp.sum(cache_exp, axis=-1) + jnp.sum(fresh_exp, axis=-1)
    cache_weights = (cache_exp / weight_sum[..., None]).astype(jnp.bfloat16)
    fresh_weights = (fresh_exp / weight_sum[..., None]).astype(jnp.bfloat16)
    combined = jnp.einsum(
        "rskgl,rlkd->rskgd", cache_weights, cache_value, preferred_element_type=jnp.float32
    )
    combined = combined + jnp.einsum(
        "rskgt,rtkd->rskgd", fresh_weights, value_new, preferred_element_type=jnp.float32
    )
    return combined.astype(jnp.bfloat16)


TORUS_ORDER = (
    (0, 1), (1, 0), (0, 3), (3, 0), (1, 1), (3, 3), (1, 3), (3, 1),
    (0, 2), (2, 0), (2, 1), (1, 2), (2, 3), (3, 2), (2, 2),
)


def peer_offsets(count):
    if count == 16:
        def shifted(me, dz, dy):
            return lax.rem(me // 4 + dz, 4) * 4 + lax.rem(lax.rem(me, 4) + dy, 4)

        return [
            (lambda me, a=dz, b=dy: shifted(me, a, b), lambda me, a=dz, b=dy: shifted(me, 4 - a, 4 - b))
            for dz, dy in TORUS_ORDER
        ]
    return [
        (lambda me, d=offset: lax.rem(me + d, count), lambda me, d=offset: lax.rem(me + count - d, count))
        for offset in range(1, count)
    ]


def exchange_kernel(axis, count, arrays, *refs):
    send_refs = refs[:arrays]
    got_refs = refs[arrays : 2 * arrays]
    send_sem, recv_sem, local_sem = refs[2 * arrays :]
    me = lax.axis_index(axis)
    barrier = pltpu.get_barrier_semaphore()
    offsets = peer_offsets(count)
    for offset in range(1, count):
        peer = offsets[offset - 1][0](me)
        pl.semaphore_signal(barrier, inc=1, device_id={axis: peer}, device_id_type=MESH)
    pl.semaphore_wait(barrier, count - 1)
    locals_ = []
    for which in range(arrays):
        local = pltpu.make_async_copy(
            send_refs[which].at[me], got_refs[which].at[me], local_sem.at[which]
        )
        local.start()
        locals_.append(local)
    outgoing = []
    for offset in range(1, count):
        peer = offsets[offset - 1][0](me)
        for which in range(arrays):
            copy = pltpu.make_async_remote_copy(
                src_ref=send_refs[which].at[peer],
                dst_ref=got_refs[which].at[me],
                send_sem=send_sem.at[which, offset],
                recv_sem=recv_sem.at[which, offset],
                device_id={axis: peer},
                device_id_type=MESH,
            )
            copy.start()
            outgoing.append(copy)
    for offset in range(1, count):
        source = offsets[offset - 1][1](me)
        for which in range(arrays):
            outgoing[(offset - 1) * arrays + which].wait_send()
            incoming = pltpu.make_async_remote_copy(
                src_ref=send_refs[which].at[source],
                dst_ref=got_refs[which].at[source],
                send_sem=send_sem.at[which, offset],
                recv_sem=recv_sem.at[which, offset],
                device_id={axis: source},
                device_id_type=MESH,
            )
            incoming.wait_recv()
    for local in locals_:
        local.wait()


def exchange(values, axis, count, collective):
    arrays = len(values)
    vmem = pl.BlockSpec(memory_space=pltpu.VMEM)
    return pl.pallas_call(
        lambda *refs: exchange_kernel(axis, count, arrays, *refs),
        out_shape=tuple(jax.ShapeDtypeStruct(v.shape, v.dtype) for v in values),
        in_specs=[vmem] * arrays,
        out_specs=tuple([vmem] * arrays),
        scratch_shapes=[
            pltpu.SemaphoreType.DMA((arrays, count)),
            pltpu.SemaphoreType.DMA((arrays, count)),
            pltpu.SemaphoreType.DMA((arrays,)),
        ],
        compiler_params=pltpu.CompilerParams(collective_id=collective, has_side_effects=True),
    )(*values)


def exchange_ring_kernel(axis, count, gather_axis, arrays, *refs):
    send_refs = refs[:arrays]
    piece_ref = refs[arrays]
    got_refs = refs[arrays + 1 : 2 * arrays + 1]
    chip_pieces = refs[2 * arrays + 1]
    (send_sem, recv_sem, local_sem, near_send, near_recv, far_send, far_recv,
     piece_sem) = refs[2 * arrays + 2 :]
    chips = chip_pieces.shape[0]
    half = chip_pieces.shape[1] // 2
    me = lax.axis_index(axis)
    mine = lax.axis_index(gather_axis)
    chip = mine // 2
    core = lax.rem(mine, 2)
    right_chip = lax.rem(chip + 1, chips)
    left_chip = lax.rem(chip + chips - 1, chips)
    far_chip = lax.rem(chip + 2, chips)
    right = right_chip * 2 + core
    left = left_chip * 2 + core

    barrier = pltpu.get_barrier_semaphore()
    offsets = peer_offsets(count)
    for offset in range(1, count):
        peer = offsets[offset - 1][0](me)
        pl.semaphore_signal(barrier, inc=1, device_id={axis: peer}, device_id_type=MESH)
    pl.semaphore_signal(barrier, inc=1, device_id={gather_axis: right}, device_id_type=MESH)
    pl.semaphore_signal(barrier, inc=1, device_id={gather_axis: left}, device_id_type=MESH)
    pl.semaphore_wait(barrier, count + 1)

    near = []
    for side, target in ((0, right), (1, left)):
        copy = pltpu.make_async_remote_copy(
            src_ref=piece_ref,
            dst_ref=chip_pieces.at[chip],
            send_sem=near_send.at[side],
            recv_sem=near_recv.at[side],
            device_id={gather_axis: target},
            device_id_type=MESH,
        )
        copy.start()
        near.append(copy)
    own_piece = pltpu.make_async_copy(piece_ref, chip_pieces.at[chip], piece_sem)
    own_piece.start()

    locals_ = []
    for which in range(arrays):
        local = pltpu.make_async_copy(
            send_refs[which].at[me], got_refs[which].at[me], local_sem.at[which]
        )
        local.start()
        locals_.append(local)
    outgoing = []
    for offset in range(1, count):
        peer = offsets[offset - 1][0](me)
        for which in range(arrays):
            copy = pltpu.make_async_remote_copy(
                src_ref=send_refs[which].at[peer],
                dst_ref=got_refs[which].at[me],
                send_sem=send_sem.at[which, offset],
                recv_sem=recv_sem.at[which, offset],
                device_id={axis: peer},
                device_id_type=MESH,
            )
            copy.start()
            outgoing.append(copy)

    far = []
    for side, source_chip, source, target, rows in (
        (0, left_chip, left, right, pl.ds(0, half)),
        (1, right_chip, right, left, pl.ds(half, half)),
    ):
        near[side].wait_send()
        incoming = pltpu.make_async_remote_copy(
            src_ref=piece_ref,
            dst_ref=chip_pieces.at[source_chip],
            send_sem=near_send.at[side],
            recv_sem=near_recv.at[side],
            device_id={gather_axis: source},
            device_id_type=MESH,
        )
        incoming.wait_recv()
        copy = pltpu.make_async_remote_copy(
            src_ref=chip_pieces.at[source_chip, rows],
            dst_ref=chip_pieces.at[source_chip, rows],
            send_sem=far_send.at[side],
            recv_sem=far_recv.at[side],
            device_id={gather_axis: target},
            device_id_type=MESH,
        )
        copy.start()
        far.append(copy)
    for side, source, rows in ((0, left, pl.ds(0, half)), (1, right, pl.ds(half, half))):
        far[side].wait_send()
        incoming = pltpu.make_async_remote_copy(
            src_ref=chip_pieces.at[far_chip, rows],
            dst_ref=chip_pieces.at[far_chip, rows],
            send_sem=far_send.at[side],
            recv_sem=far_recv.at[side],
            device_id={gather_axis: source},
            device_id_type=MESH,
        )
        incoming.wait_recv()

    for offset in range(1, count):
        source = offsets[offset - 1][1](me)
        for which in range(arrays):
            outgoing[(offset - 1) * arrays + which].wait_send()
            incoming = pltpu.make_async_remote_copy(
                src_ref=send_refs[which].at[source],
                dst_ref=got_refs[which].at[source],
                send_sem=send_sem.at[which, offset],
                recv_sem=recv_sem.at[which, offset],
                device_id={axis: source},
                device_id_type=MESH,
            )
            incoming.wait_recv()
    for local in locals_:
        local.wait()
    own_piece.wait()


def exchange_ring(values, piece, axis, count, gather_axis, collective):
    arrays = len(values)
    chips = lax.axis_size(gather_axis) // 2
    vmem = pl.BlockSpec(memory_space=pltpu.VMEM)
    outs = pl.pallas_call(
        lambda *refs: exchange_ring_kernel(axis, count, gather_axis, arrays, *refs),
        out_shape=tuple(jax.ShapeDtypeStruct(v.shape, v.dtype) for v in values)
        + (jax.ShapeDtypeStruct((chips,) + piece.shape, piece.dtype),),
        in_specs=[vmem] * (arrays + 1),
        out_specs=tuple([vmem] * (arrays + 1)),
        scratch_shapes=[
            pltpu.SemaphoreType.DMA((arrays, count)),
            pltpu.SemaphoreType.DMA((arrays, count)),
            pltpu.SemaphoreType.DMA((arrays,)),
            pltpu.SemaphoreType.DMA((2,)),
            pltpu.SemaphoreType.DMA((2,)),
            pltpu.SemaphoreType.DMA((2,)),
            pltpu.SemaphoreType.DMA((2,)),
            pltpu.SemaphoreType.DMA(()),
        ],
        compiler_params=pltpu.CompilerParams(collective_id=collective, has_side_effects=True),
    )(*values, piece)
    return outs[:arrays], outs[arrays]


def exchange_project_kernel(
    axis, count, gather_axis, send_ref, chip_pieces, wq_hbm, wk_ref, wv_ref,
    got_ref, q_ref, k_ref, v_ref,
    partner_pieces, wq_buf, send_sem, recv_sem, local_sem, wq_sem, partner_send, partner_recv,
):
    me = lax.axis_index(axis)
    mine = lax.axis_index(gather_axis)
    core = lax.rem(mine, 2)
    partner = (mine // 2) * 2 + (1 - core)
    barrier = pltpu.get_barrier_semaphore()
    offsets = peer_offsets(count)
    for offset in range(1, count):
        peer = offsets[offset - 1][0](me)
        pl.semaphore_signal(barrier, inc=1, device_id={axis: peer}, device_id_type=MESH)
    pl.semaphore_signal(barrier, inc=1, device_id={gather_axis: partner}, device_id_type=MESH)
    pl.semaphore_wait(barrier, count)
    to_partner = pltpu.make_async_remote_copy(
        src_ref=chip_pieces,
        dst_ref=partner_pieces,
        send_sem=partner_send,
        recv_sem=partner_recv,
        device_id={gather_axis: partner},
        device_id_type=MESH,
    )
    to_partner.start()
    local = pltpu.make_async_copy(send_ref.at[me], got_ref.at[me], local_sem)
    local.start()
    outgoing = []
    for offset in range(1, count):
        peer = offsets[offset - 1][0](me)
        copy = pltpu.make_async_remote_copy(
            src_ref=send_ref.at[peer],
            dst_ref=got_ref.at[me],
            send_sem=send_sem.at[offset],
            recv_sem=recv_sem.at[offset],
            device_id={axis: peer},
            device_id_type=MESH,
        )
        copy.start()
        outgoing.append(copy)

    chips, unused_item, piece_width = chip_pieces.shape
    steps = 2 * chips

    def chunk_copy(step, slot):
        index = lax.rem(step, chips) * 2 + core + (step // chips) * (1 - 2 * core)
        return pltpu.make_async_copy(
            wq_hbm.at[pl.ds(pl.multiple_of(index * piece_width, piece_width), piece_width)],
            wq_buf.at[slot],
            wq_sem.at[slot],
        )

    chunk_copy(0, 0).start()
    q_ref[...] = jnp.zeros_like(q_ref)
    k_ref[...] = jnp.zeros_like(k_ref)
    v_ref[...] = jnp.zeros_like(v_ref)

    def project(step, piece):
        slot = lax.rem(step, 2)
        chunk_copy(step, slot).wait()

        @pl.when(step + 1 < steps)
        def _():
            chunk_copy(step + 1, 1 - slot).start()

        index = lax.rem(step, chips) * 2 + core + (step // chips) * (1 - 2 * core)
        rows = pl.ds(pl.multiple_of(index * piece_width, piece_width), piece_width)
        q_ref[...] += jnp.dot(piece, wq_buf[slot], preferred_element_type=jnp.float32)
        k_ref[...] += jnp.dot(piece, wk_ref[rows, :], preferred_element_type=jnp.float32)
        v_ref[...] += jnp.dot(piece, wv_ref[rows, :], preferred_element_type=jnp.float32)

    def own_step(step, carry):
        project(step, chip_pieces[step])
        return carry

    def partner_step(step, carry):
        project(step, partner_pieces[step - chips])
        return carry

    lax.fori_loop(0, chips, own_step, 0)
    to_partner.wait_send()
    to_partner.wait_recv()
    lax.fori_loop(chips, steps, partner_step, 0)

    for offset in range(1, count):
        outgoing[offset - 1].wait_send()
        source = offsets[offset - 1][1](me)
        incoming = pltpu.make_async_remote_copy(
            src_ref=send_ref.at[source],
            dst_ref=got_ref.at[source],
            send_sem=send_sem.at[offset],
            recv_sem=recv_sem.at[offset],
            device_id={axis: source},
            device_id_type=MESH,
        )
        incoming.wait_recv()
    local.wait()


def exchange_project(values, chip_pieces, w_query, w_key, w_value, axis, count, gather_axis, collective):
    chips, token_count, piece_width = chip_pieces.shape
    vmem = pl.BlockSpec(memory_space=pltpu.VMEM)
    return pl.pallas_call(
        lambda *refs: exchange_project_kernel(axis, count, gather_axis, *refs),
        out_shape=(
            jax.ShapeDtypeStruct(values.shape, values.dtype),
            jax.ShapeDtypeStruct((token_count, w_query.shape[1]), jnp.float32),
            jax.ShapeDtypeStruct((token_count, w_key.shape[1]), jnp.float32),
            jax.ShapeDtypeStruct((token_count, w_value.shape[1]), jnp.float32),
        ),
        in_specs=[vmem, vmem, pl.BlockSpec(memory_space=pl.ANY), vmem, vmem],
        out_specs=(vmem, vmem, vmem, vmem),
        scratch_shapes=[
            pltpu.VMEM(chip_pieces.shape, chip_pieces.dtype),
            pltpu.VMEM((2, piece_width, w_query.shape[1]), w_query.dtype),
            pltpu.SemaphoreType.DMA((count,)),
            pltpu.SemaphoreType.DMA((count,)),
            pltpu.SemaphoreType.DMA(()),
            pltpu.SemaphoreType.DMA((2,)),
            pltpu.SemaphoreType.DMA(()),
            pltpu.SemaphoreType.DMA(()),
        ],
        compiler_params=pltpu.CompilerParams(
            collective_id=collective, has_side_effects=True, vmem_limit_bytes=60 * 1024 * 1024
        ),
    )(values, chip_pieces, w_query, w_key, w_value)


def sum_kernel(axis, count, part_ref, total_ref, held, first_send, first_recv, second_send, second_recv):
    me = lax.axis_index(axis)
    barrier = pltpu.get_barrier_semaphore()
    for offset in range(1, count):
        peer = lax.rem(me + offset, count)
        pl.semaphore_signal(barrier, inc=1, device_id={axis: peer}, device_id_type=MESH)
    pl.semaphore_wait(barrier, count - 1)
    outgoing = []
    for offset in range(1, count):
        peer = lax.rem(me + offset, count)
        copy = pltpu.make_async_remote_copy(
            src_ref=part_ref.at[peer],
            dst_ref=held.at[me],
            send_sem=first_send.at[offset],
            recv_sem=first_recv.at[offset],
            device_id={axis: peer},
            device_id_type=MESH,
        )
        copy.start()
        outgoing.append(copy)
    held[me] = part_ref[me]
    for offset in range(1, count):
        outgoing[offset - 1].wait_send()
        source = lax.rem(me + count - offset, count)
        incoming = pltpu.make_async_remote_copy(
            src_ref=part_ref.at[source],
            dst_ref=held.at[source],
            send_sem=first_send.at[offset],
            recv_sem=first_recv.at[offset],
            device_id={axis: source},
            device_id_type=MESH,
        )
        incoming.wait_recv()
    total = held[0]
    for index in range(1, count):
        total = total + held[index]
    total_ref[me] = total.astype(total_ref.dtype)
    outgoing = []
    for offset in range(1, count):
        peer = lax.rem(me + offset, count)
        copy = pltpu.make_async_remote_copy(
            src_ref=total_ref.at[me],
            dst_ref=total_ref.at[me],
            send_sem=second_send.at[offset],
            recv_sem=second_recv.at[offset],
            device_id={axis: peer},
            device_id_type=MESH,
        )
        copy.start()
        outgoing.append(copy)
    for offset in range(1, count):
        outgoing[offset - 1].wait_send()
        source = lax.rem(me + count - offset, count)
        incoming = pltpu.make_async_remote_copy(
            src_ref=total_ref.at[source],
            dst_ref=total_ref.at[source],
            send_sem=second_send.at[offset],
            recv_sem=second_recv.at[offset],
            device_id={axis: source},
            device_id_type=MESH,
        )
        incoming.wait_recv()


def axis_sum(values, axis, count, collective, out_dtype):
    chunks = values.reshape(count, -1, 128)
    summed = pl.pallas_call(
        lambda *refs: sum_kernel(axis, count, *refs),
        out_shape=jax.ShapeDtypeStruct(chunks.shape, out_dtype),
        in_specs=[pl.BlockSpec(memory_space=pltpu.VMEM)],
        out_specs=pl.BlockSpec(memory_space=pltpu.VMEM),
        scratch_shapes=[
            pltpu.VMEM(chunks.shape, values.dtype),
            pltpu.SemaphoreType.DMA((count,)),
            pltpu.SemaphoreType.DMA((count,)),
            pltpu.SemaphoreType.DMA((count,)),
            pltpu.SemaphoreType.DMA((count,)),
        ],
        compiler_params=pltpu.CompilerParams(collective_id=collective, has_side_effects=True),
    )(chunks)
    return summed.reshape(values.shape)


def owner_adapter_term(received, slot_ids, down_local, up_local):
    sources, rows, part_width = received.shape
    local_adapters, unused_item, adapter_rank = down_local.shape
    query_width = up_local.shape[2]
    token_rows = received.reshape(sources * rows, part_width)
    every_down = jnp.einsum(
        "td,adr->tar", token_rows, down_local, preferred_element_type=jnp.float32
    )
    pick = slot_ids.reshape(sources * rows)[:, None] == jnp.arange(local_adapters, dtype=jnp.int32)[None, :]
    partial_value_sum = jnp.sum(jnp.where(pick[:, :, None], every_down, 0.0), axis=1)
    tp_count = lax.axis_size("tp")
    summed = axis_sum(partial_value_sum.reshape(-1, 128), "tp", tp_count, 2, jnp.bfloat16)
    adapter_middle = summed.reshape(sources * rows, adapter_rank)
    spread_rows = jnp.where(pick[:, :, None], adapter_middle[:, None, :], jnp.zeros((), jnp.bfloat16))
    spread_rows = spread_rows.reshape(sources * rows, local_adapters * adapter_rank)
    adapter_output = jnp.dot(
        spread_rows,
        up_local.reshape(local_adapters * adapter_rank, query_width),
        preferred_element_type=jnp.float32,
    ).astype(jnp.bfloat16)
    return adapter_output.reshape(sources, rows, query_width)


def body(
    tokens,
    adapter_id,
    pool_slot,
    lengths,
    w_query,
    w_key,
    w_value,
    pooled_down_weights,
    pool_up,
    cache_key,
    cache_value,
):
    group_count = lax.axis_size("grp")
    tp_count = lax.axis_size("tp")
    row_count, step_count, part_width = tokens.shape
    local_adapter_rows, unused_item, adapter_rank = pooled_down_weights.shape
    query_width = w_query.shape[1]
    kv_width = w_key.shape[1]
    kv_local = kv_width // HD
    q_local = query_width // HD
    group_size = q_local // kv_local
    count_of_tokens = row_count * step_count
    adapter_span = jnp.arange(pool_slot.shape[0], dtype=jnp.int32)
    pool_pos = jnp.sum(
        jnp.where(adapter_id[:, None] == adapter_span[None, :], pool_slot[None, :], 0), axis=1
    )
    owner_grp = pool_pos // local_adapter_rows
    local_slot = pool_pos % local_adapter_rows
    row_span = jnp.arange(row_count, dtype=jnp.int32)
    same_owner = (owner_grp[:, None] == owner_grp[None, :]) & (row_span[None, :] < row_span[:, None])
    owner_rank = jnp.sum(same_owner.astype(jnp.int32), axis=1)
    send_slot = owner_grp * CAP + owner_rank
    slot_span = jnp.arange(group_count * CAP, dtype=jnp.int32)
    place = (slot_span[:, None] == send_slot[None, :]).astype(jnp.bfloat16)
    token_slot = (send_slot[:, None] * step_count + jnp.arange(step_count, dtype=jnp.int32)[None, :]).reshape(-1)
    token_span = jnp.arange(group_count * CAP * step_count, dtype=jnp.int32)
    place_tokens = (token_span[:, None] == token_slot[None, :]).astype(jnp.bfloat16)
    token_rows = tokens.reshape(count_of_tokens, part_width)
    send_tokens = jnp.dot(place_tokens, token_rows, preferred_element_type=jnp.float32).astype(jnp.bfloat16)
    send_tokens = send_tokens.reshape(group_count, CAP * step_count, part_width)
    send_ids = jnp.dot(
        place, local_slot.astype(jnp.bfloat16)[:, None], preferred_element_type=jnp.float32
    ).astype(jnp.bfloat16)
    send_ids = jnp.broadcast_to(send_ids.reshape(group_count, CAP, 1), (group_count, CAP, 128))
    send_ids = jnp.concatenate([send_ids, jnp.zeros_like(send_ids)], axis=1)
    (got_tokens, got_ids), chip_pieces = exchange_ring(
        (send_tokens, send_ids), token_rows, "grp", group_count, "tp", 0
    )
    got_ids = jnp.repeat(got_ids[:, :CAP, 0].astype(jnp.int32), step_count, axis=1)
    owner_out = owner_adapter_term(got_tokens, got_ids, pooled_down_weights, pool_up)
    back, base_query_rows, key_base, value_base = exchange_project(
        owner_out, chip_pieces, w_query, w_key, w_value, "grp", group_count, "tp", 1
    )
    adapter_output = jnp.dot(
        jnp.transpose(place_tokens),
        back.reshape(group_count * CAP * step_count, query_width),
        preferred_element_type=jnp.float32,
    )
    base_query_rows = base_query_rows + adapter_output
    position = lengths[:, None] + jnp.arange(step_count, dtype=jnp.int32)[None, :]
    queries = rotate(base_query_rows.reshape(row_count, step_count, q_local, HD), position)
    queries = queries.astype(jnp.bfloat16).reshape(row_count, step_count, kv_local, group_size, HD)
    key_new = rotate(key_base.reshape(row_count, step_count, kv_local, HD), position).astype(
        jnp.bfloat16
    )
    value_new = value_base.reshape(row_count, step_count, kv_local, HD).astype(jnp.bfloat16)
    cache_keys = cache_key.reshape(row_count, cache_key.shape[1], kv_local, HD)
    cache_values = cache_value.reshape(row_count, cache_value.shape[1], kv_local, HD)
    combined = attend(queries, key_new, value_new, cache_keys, cache_values, lengths)
    return combined.reshape(row_count, step_count, query_width)


def solution(mesh):
    in_specs = (
        P("grp", None, "tp"),
        P("grp"),
        P(),
        P("grp"),
        P(None, "tp"),
        P(None, "tp"),
        P(None, "tp"),
        P("grp", "tp", None),
        P("grp", None, "tp"),
        P("grp", None, "tp"),
        P("grp", None, "tp"),
    )
    out_specs = P("grp", None, "tp")
    return jax.shard_map(body, mesh=mesh, in_specs=in_specs, out_specs=out_specs, check_vma=False)
```

```python
import math

import jax
import jax.numpy as jnp
from jax import lax
from jax.experimental import pallas as pl
from jax.experimental.pallas import tpu as pltpu
from jax.sharding import PartitionSpec as P

MESH = pl.DeviceIdType.MESH

HD = 128
CAP = 8


rope_base = 500000.0


def rotate(values, position):
    half_width = values.shape[-1] // 2
    inv_freq = jnp.exp(
        jnp.arange(half_width, dtype=jnp.float32) * (-2.0 * math.log(rope_base) / values.shape[-1])
    )
    angles = position.astype(jnp.float32)[:, :, None, None] * inv_freq
    cosine = jnp.cos(angles)
    sines = jnp.sin(angles)
    front_half = values[..., :half_width]
    back_half = values[..., half_width:]
    return jnp.concatenate(
        [front_half * cosine - back_half * sines, back_half * cosine + front_half * sines], axis=-1
    )


def attend(queries, key_new, value_new, cache_key, cache_value, lengths):
    score_scale = 1.0 / math.sqrt(queries.shape[-1])
    cached = (
        jnp.einsum("rskgd,rlkd->rskgl", queries, cache_key, preferred_element_type=jnp.float32)
        * score_scale
    )
    fresh_scores = (
        jnp.einsum("rskgd,rtkd->rskgt", queries, key_new, preferred_element_type=jnp.float32)
        * score_scale
    )
    live_mask = jnp.arange(cache_key.shape[1], dtype=jnp.int32)[None, :] < lengths[:, None]
    cached = jnp.where(live_mask[:, None, None, None, :], cached, -1e30)
    steps_here = key_new.shape[1]
    causal = (
        jnp.arange(steps_here, dtype=jnp.int32)[:, None]
        >= jnp.arange(steps_here, dtype=jnp.int32)[None, :]
    )
    fresh_scores = jnp.where(causal[None, :, None, None, :], fresh_scores, -1e30)
    row_max = jnp.maximum(jnp.max(cached, axis=-1), jnp.max(fresh_scores, axis=-1))
    cache_exp = jnp.exp(cached - row_max[..., None])
    fresh_exp = jnp.exp(fresh_scores - row_max[..., None])
    weight_sum = jnp.sum(cache_exp, axis=-1) + jnp.sum(fresh_exp, axis=-1)
    cache_weights = (cache_exp / weight_sum[..., None]).astype(jnp.bfloat16)
    fresh_weights = (fresh_exp / weight_sum[..., None]).astype(jnp.bfloat16)
    combined = jnp.einsum(
        "rskgl,rlkd->rskgd", cache_weights, cache_value, preferred_element_type=jnp.float32
    )
    combined = combined + jnp.einsum(
        "rskgt,rtkd->rskgd", fresh_weights, value_new, preferred_element_type=jnp.float32
    )
    return combined.astype(jnp.bfloat16)


TORUS_ORDER = (
    (0, 1), (1, 0), (0, 3), (3, 0), (1, 1), (3, 3), (1, 3), (3, 1),
    (0, 2), (2, 0), (2, 1), (1, 2), (2, 3), (3, 2), (2, 2),
)


def peer_offsets(count):
    if count == 16:
        def shifted(me, dz, dy):
            return lax.rem(me // 4 + dz, 4) * 4 + lax.rem(lax.rem(me, 4) + dy, 4)

        return [
            (lambda me, a=dz, b=dy: shifted(me, a, b), lambda me, a=dz, b=dy: shifted(me, 4 - a, 4 - b))
            for dz, dy in TORUS_ORDER
        ]
    return [
        (lambda me, d=offset: lax.rem(me + d, count), lambda me, d=offset: lax.rem(me + count - d, count))
        for offset in range(1, count)
    ]


def exchange_kernel(axis, count, arrays, *refs):
    send_refs = refs[:arrays]
    got_refs = refs[arrays : 2 * arrays]
    send_sem, recv_sem, local_sem = refs[2 * arrays :]
    me = lax.axis_index(axis)
    barrier = pltpu.get_barrier_semaphore()
    offsets = peer_offsets(count)
    for offset in range(1, count):
        peer = offsets[offset - 1][0](me)
        pl.semaphore_signal(barrier, inc=1, device_id={axis: peer}, device_id_type=MESH)
    pl.semaphore_wait(barrier, count - 1)
    locals_ = []
    for which in range(arrays):
        local = pltpu.make_async_copy(
            send_refs[which].at[me], got_refs[which].at[me], local_sem.at[which]
        )
        local.start()
        locals_.append(local)
    outgoing = []
    for offset in range(1, count):
        peer = offsets[offset - 1][0](me)
        for which in range(arrays):
            copy = pltpu.make_async_remote_copy(
                src_ref=send_refs[which].at[peer],
                dst_ref=got_refs[which].at[me],
                send_sem=send_sem.at[which, offset],
                recv_sem=recv_sem.at[which, offset],
                device_id={axis: peer},
                device_id_type=MESH,
            )
            copy.start()
            outgoing.append(copy)
    for offset in range(1, count):
        source = offsets[offset - 1][1](me)
        for which in range(arrays):
            outgoing[(offset - 1) * arrays + which].wait_send()
            incoming = pltpu.make_async_remote_copy(
                src_ref=send_refs[which].at[source],
                dst_ref=got_refs[which].at[source],
                send_sem=send_sem.at[which, offset],
                recv_sem=recv_sem.at[which, offset],
                device_id={axis: source},
                device_id_type=MESH,
            )
            incoming.wait_recv()
    for local in locals_:
        local.wait()


def exchange(values, axis, count, collective):
    arrays = len(values)
    vmem = pl.BlockSpec(memory_space=pltpu.VMEM)
    return pl.pallas_call(
        lambda *refs: exchange_kernel(axis, count, arrays, *refs),
        out_shape=tuple(jax.ShapeDtypeStruct(v.shape, v.dtype) for v in values),
        in_specs=[vmem] * arrays,
        out_specs=tuple([vmem] * arrays),
        scratch_shapes=[
            pltpu.SemaphoreType.DMA((arrays, count)),
            pltpu.SemaphoreType.DMA((arrays, count)),
            pltpu.SemaphoreType.DMA((arrays,)),
        ],
        compiler_params=pltpu.CompilerParams(collective_id=collective, has_side_effects=True),
    )(*values)


def exchange_ring_kernel(axis, count, gather_axis, arrays, *refs):
    send_refs = refs[:arrays]
    piece_ref = refs[arrays]
    got_refs = refs[arrays + 1 : 2 * arrays + 1]
    chip_pieces = refs[2 * arrays + 1]
    send_sem, recv_sem, local_sem, near_send, near_recv, piece_sem = refs[2 * arrays + 2 :]
    chips = lax.axis_size(gather_axis) // 2
    me = lax.axis_index(axis)
    mine = lax.axis_index(gather_axis)
    chip = mine // 2
    core = lax.rem(mine, 2)
    right_chip = lax.rem(chip + 1, chips)
    left_chip = lax.rem(chip + chips - 1, chips)
    right = right_chip * 2 + core
    left = left_chip * 2 + core

    barrier = pltpu.get_barrier_semaphore()
    offsets = peer_offsets(count)
    for offset in range(1, count):
        peer = offsets[offset - 1][0](me)
        pl.semaphore_signal(barrier, inc=1, device_id={axis: peer}, device_id_type=MESH)
    pl.semaphore_signal(barrier, inc=1, device_id={gather_axis: right}, device_id_type=MESH)
    pl.semaphore_signal(barrier, inc=1, device_id={gather_axis: left}, device_id_type=MESH)
    pl.semaphore_wait(barrier, count + 1)

    near = []
    for side, target in ((0, right), (1, left)):
        copy = pltpu.make_async_remote_copy(
            src_ref=piece_ref,
            dst_ref=chip_pieces.at[1 + side],
            send_sem=near_send.at[side],
            recv_sem=near_recv.at[side],
            device_id={gather_axis: target},
            device_id_type=MESH,
        )
        copy.start()
        near.append(copy)
    own_piece = pltpu.make_async_copy(piece_ref, chip_pieces.at[0], piece_sem)
    own_piece.start()

    locals_ = []
    for which in range(arrays):
        local = pltpu.make_async_copy(
            send_refs[which].at[me], got_refs[which].at[me], local_sem.at[which]
        )
        local.start()
        locals_.append(local)
    outgoing = []
    for offset in range(1, count):
        peer = offsets[offset - 1][0](me)
        for which in range(arrays):
            copy = pltpu.make_async_remote_copy(
                src_ref=send_refs[which].at[peer],
                dst_ref=got_refs[which].at[me],
                send_sem=send_sem.at[which, offset],
                recv_sem=recv_sem.at[which, offset],
                device_id={axis: peer},
                device_id_type=MESH,
            )
            copy.start()
            outgoing.append(copy)

    for side, source in ((0, left), (1, right)):
        near[side].wait_send()
        incoming = pltpu.make_async_remote_copy(
            src_ref=piece_ref,
            dst_ref=chip_pieces.at[1 + side],
            send_sem=near_send.at[side],
            recv_sem=near_recv.at[side],
            device_id={gather_axis: source},
            device_id_type=MESH,
        )
        incoming.wait_recv()

    for offset in range(1, count):
        source = offsets[offset - 1][1](me)
        for which in range(arrays):
            outgoing[(offset - 1) * arrays + which].wait_send()
            incoming = pltpu.make_async_remote_copy(
                src_ref=send_refs[which].at[source],
                dst_ref=got_refs[which].at[source],
                send_sem=send_sem.at[which, offset],
                recv_sem=recv_sem.at[which, offset],
                device_id={axis: source},
                device_id_type=MESH,
            )
            incoming.wait_recv()
    for local in locals_:
        local.wait()
    own_piece.wait()


def exchange_ring(values, piece, axis, count, gather_axis, collective):
    arrays = len(values)
    vmem = pl.BlockSpec(memory_space=pltpu.VMEM)
    outs = pl.pallas_call(
        lambda *refs: exchange_ring_kernel(axis, count, gather_axis, arrays, *refs),
        out_shape=tuple(jax.ShapeDtypeStruct(v.shape, v.dtype) for v in values)
        + (jax.ShapeDtypeStruct((3,) + piece.shape, piece.dtype),),
        in_specs=[vmem] * (arrays + 1),
        out_specs=tuple([vmem] * (arrays + 1)),
        scratch_shapes=[
            pltpu.SemaphoreType.DMA((arrays, count)),
            pltpu.SemaphoreType.DMA((arrays, count)),
            pltpu.SemaphoreType.DMA((arrays,)),
            pltpu.SemaphoreType.DMA((2,)),
            pltpu.SemaphoreType.DMA((2,)),
            pltpu.SemaphoreType.DMA(()),
        ],
        compiler_params=pltpu.CompilerParams(collective_id=collective, has_side_effects=True),
    )(*values, piece)
    return outs[:arrays], outs[arrays]


def exchange_project_kernel(
    axis, count, gather_axis, send_ref, near_pieces, wq_hbm, wk_ref, wv_ref,
    got_ref, q_ref, k_ref, v_ref,
    far_piece, partner_near, partner_far, wq_buf, send_sem, recv_sem, local_sem, wq_sem,
    far_send, far_recv, partner_send, partner_recv,
):
    me = lax.axis_index(axis)
    mine = lax.axis_index(gather_axis)
    chips = lax.axis_size(gather_axis) // 2
    chip = mine // 2
    core = lax.rem(mine, 2)
    partner = chip * 2 + (1 - core)
    right = lax.rem(chip + 1, chips) * 2 + core
    left = lax.rem(chip + chips - 1, chips) * 2 + core
    half = far_piece.shape[0] // 2
    barrier = pltpu.get_barrier_semaphore()
    offsets = peer_offsets(count)
    for offset in range(1, count):
        peer = offsets[offset - 1][0](me)
        pl.semaphore_signal(barrier, inc=1, device_id={axis: peer}, device_id_type=MESH)
    for neighbour in (partner, right, left):
        pl.semaphore_signal(barrier, inc=1, device_id={gather_axis: neighbour}, device_id_type=MESH)
    pl.semaphore_wait(barrier, count + 2)

    far_out = []
    for side, slot, target, rows in ((0, 1, right, pl.ds(0, half)), (1, 2, left, pl.ds(half, half))):
        copy = pltpu.make_async_remote_copy(
            src_ref=near_pieces.at[slot, rows],
            dst_ref=far_piece.at[rows],
            send_sem=far_send.at[side],
            recv_sem=far_recv.at[side],
            device_id={gather_axis: target},
            device_id_type=MESH,
        )
        copy.start()
        far_out.append(copy)
    to_partner = pltpu.make_async_remote_copy(
        src_ref=near_pieces,
        dst_ref=partner_near,
        send_sem=partner_send.at[0],
        recv_sem=partner_recv.at[0],
        device_id={gather_axis: partner},
        device_id_type=MESH,
    )
    to_partner.start()
    local = pltpu.make_async_copy(send_ref.at[me], got_ref.at[me], local_sem)
    local.start()
    outgoing = []
    for offset in range(1, count):
        peer = offsets[offset - 1][0](me)
        copy = pltpu.make_async_remote_copy(
            src_ref=send_ref.at[peer],
            dst_ref=got_ref.at[me],
            send_sem=send_sem.at[offset],
            recv_sem=recv_sem.at[offset],
            device_id={axis: peer},
            device_id_type=MESH,
        )
        copy.start()
        outgoing.append(copy)

    piece_width = near_pieces.shape[2]
    chip_shift = (0, chips - 1, 1, 2)

    def piece_index(step):
        piece_core = core if step < 4 else 1 - core
        return lax.rem(chip + chip_shift[step % 4], chips) * 2 + piece_core

    def chunk_copy(step):
        index = piece_index(step)
        return pltpu.make_async_copy(
            wq_hbm.at[pl.ds(pl.multiple_of(index * piece_width, piece_width), piece_width)],
            wq_buf.at[step % 2],
            wq_sem.at[step % 2],
        )

    chunk_copy(0).start()
    q_ref[...] = jnp.zeros_like(q_ref)
    k_ref[...] = jnp.zeros_like(k_ref)
    v_ref[...] = jnp.zeros_like(v_ref)

    def project(step, piece):
        chunk_copy(step).wait()
        if step + 1 < 8:
            chunk_copy(step + 1).start()
        index = piece_index(step)
        rows = pl.ds(pl.multiple_of(index * piece_width, piece_width), piece_width)
        q_ref[...] += jnp.dot(piece, wq_buf[step % 2], preferred_element_type=jnp.float32)
        k_ref[...] += jnp.dot(piece, wk_ref[rows, :], preferred_element_type=jnp.float32)
        v_ref[...] += jnp.dot(piece, wv_ref[rows, :], preferred_element_type=jnp.float32)

    for step in range(3):
        project(step, near_pieces[step])
    for side, source, rows in ((0, left, pl.ds(0, half)), (1, right, pl.ds(half, half))):
        far_out[side].wait_send()
        incoming = pltpu.make_async_remote_copy(
            src_ref=near_pieces.at[1, rows],
            dst_ref=far_piece.at[rows],
            send_sem=far_send.at[side],
            recv_sem=far_recv.at[side],
            device_id={gather_axis: source},
            device_id_type=MESH,
        )
        incoming.wait_recv()
    far_to_partner = pltpu.make_async_remote_copy(
        src_ref=far_piece,
        dst_ref=partner_far,
        send_sem=partner_send.at[1],
        recv_sem=partner_recv.at[1],
        device_id={gather_axis: partner},
        device_id_type=MESH,
    )
    far_to_partner.start()
    project(3, far_piece[...])
    to_partner.wait_send()
    to_partner.wait_recv()
    for step in range(3):
        project(4 + step, partner_near[step])
    far_to_partner.wait_send()
    far_to_partner.wait_recv()
    project(7, partner_far[...])

    for offset in range(1, count):
        outgoing[offset - 1].wait_send()
        source = offsets[offset - 1][1](me)
        incoming = pltpu.make_async_remote_copy(
            src_ref=send_ref.at[source],
            dst_ref=got_ref.at[source],
            send_sem=send_sem.at[offset],
            recv_sem=recv_sem.at[offset],
            device_id={axis: source},
            device_id_type=MESH,
        )
        incoming.wait_recv()
    local.wait()


def exchange_project(values, near_pieces, w_query, w_key, w_value, axis, count, gather_axis, collective):
    unused_item, token_count, piece_width = near_pieces.shape
    vmem = pl.BlockSpec(memory_space=pltpu.VMEM)
    return pl.pallas_call(
        lambda *refs: exchange_project_kernel(axis, count, gather_axis, *refs),
        out_shape=(
            jax.ShapeDtypeStruct(values.shape, values.dtype),
            jax.ShapeDtypeStruct((token_count, w_query.shape[1]), jnp.float32),
            jax.ShapeDtypeStruct((token_count, w_key.shape[1]), jnp.float32),
            jax.ShapeDtypeStruct((token_count, w_value.shape[1]), jnp.float32),
        ),
        in_specs=[vmem, vmem, pl.BlockSpec(memory_space=pl.ANY), vmem, vmem],
        out_specs=(vmem, vmem, vmem, vmem),
        scratch_shapes=[
            pltpu.VMEM((token_count, piece_width), near_pieces.dtype),
            pltpu.VMEM(near_pieces.shape, near_pieces.dtype),
            pltpu.VMEM((token_count, piece_width), near_pieces.dtype),
            pltpu.VMEM((2, piece_width, w_query.shape[1]), w_query.dtype),
            pltpu.SemaphoreType.DMA((count,)),
            pltpu.SemaphoreType.DMA((count,)),
            pltpu.SemaphoreType.DMA(()),
            pltpu.SemaphoreType.DMA((2,)),
            pltpu.SemaphoreType.DMA((2,)),
            pltpu.SemaphoreType.DMA((2,)),
            pltpu.SemaphoreType.DMA((2,)),
            pltpu.SemaphoreType.DMA((2,)),
        ],
        compiler_params=pltpu.CompilerParams(
            collective_id=collective, has_side_effects=True, vmem_limit_bytes=60 * 1024 * 1024
        ),
    )(values, near_pieces, w_query, w_key, w_value)


def sum_kernel(axis, count, part_ref, total_ref, held, first_send, first_recv, second_send, second_recv):
    me = lax.axis_index(axis)
    barrier = pltpu.get_barrier_semaphore()
    for offset in range(1, count):
        peer = lax.rem(me + offset, count)
        pl.semaphore_signal(barrier, inc=1, device_id={axis: peer}, device_id_type=MESH)
    pl.semaphore_wait(barrier, count - 1)
    outgoing = []
    for offset in range(1, count):
        peer = lax.rem(me + offset, count)
        copy = pltpu.make_async_remote_copy(
            src_ref=part_ref.at[peer],
            dst_ref=held.at[me],
            send_sem=first_send.at[offset],
            recv_sem=first_recv.at[offset],
            device_id={axis: peer},
            device_id_type=MESH,
        )
        copy.start()
        outgoing.append(copy)
    held[me] = part_ref[me]
    for offset in range(1, count):
        outgoing[offset - 1].wait_send()
        source = lax.rem(me + count - offset, count)
        incoming = pltpu.make_async_remote_copy(
            src_ref=part_ref.at[source],
            dst_ref=held.at[source],
            send_sem=first_send.at[offset],
            recv_sem=first_recv.at[offset],
            device_id={axis: source},
            device_id_type=MESH,
        )
        incoming.wait_recv()
    total = held[0]
    for index in range(1, count):
        total = total + held[index]
    total_ref[me] = total.astype(total_ref.dtype)
    outgoing = []
    for offset in range(1, count):
        peer = lax.rem(me + offset, count)
        copy = pltpu.make_async_remote_copy(
            src_ref=total_ref.at[me],
            dst_ref=total_ref.at[me],
            send_sem=second_send.at[offset],
            recv_sem=second_recv.at[offset],
            device_id={axis: peer},
            device_id_type=MESH,
        )
        copy.start()
        outgoing.append(copy)
    for offset in range(1, count):
        outgoing[offset - 1].wait_send()
        source = lax.rem(me + count - offset, count)
        incoming = pltpu.make_async_remote_copy(
            src_ref=total_ref.at[source],
            dst_ref=total_ref.at[source],
            send_sem=second_send.at[offset],
            recv_sem=second_recv.at[offset],
            device_id={axis: source},
            device_id_type=MESH,
        )
        incoming.wait_recv()


def axis_sum(values, axis, count, collective, out_dtype):
    chunks = values.reshape(count, -1, 128)
    summed = pl.pallas_call(
        lambda *refs: sum_kernel(axis, count, *refs),
        out_shape=jax.ShapeDtypeStruct(chunks.shape, out_dtype),
        in_specs=[pl.BlockSpec(memory_space=pltpu.VMEM)],
        out_specs=pl.BlockSpec(memory_space=pltpu.VMEM),
        scratch_shapes=[
            pltpu.VMEM(chunks.shape, values.dtype),
            pltpu.SemaphoreType.DMA((count,)),
            pltpu.SemaphoreType.DMA((count,)),
            pltpu.SemaphoreType.DMA((count,)),
            pltpu.SemaphoreType.DMA((count,)),
        ],
        compiler_params=pltpu.CompilerParams(collective_id=collective, has_side_effects=True),
    )(chunks)
    return summed.reshape(values.shape)


def owner_adapter_term(received, slot_ids, down_local, up_local):
    sources, rows, part_width = received.shape
    local_adapters, unused_item, adapter_rank = down_local.shape
    query_width = up_local.shape[2]
    token_rows = received.reshape(sources * rows, part_width)
    every_down = jnp.einsum(
        "td,adr->tar", token_rows, down_local, preferred_element_type=jnp.float32
    )
    pick = slot_ids.reshape(sources * rows)[:, None] == jnp.arange(local_adapters, dtype=jnp.int32)[None, :]
    partial_value_sum = jnp.sum(jnp.where(pick[:, :, None], every_down, 0.0), axis=1)
    tp_count = lax.axis_size("tp")
    summed = axis_sum(partial_value_sum.reshape(-1, 128), "tp", tp_count, 2, jnp.bfloat16)
    adapter_middle = summed.reshape(sources * rows, adapter_rank)
    spread_rows = jnp.where(pick[:, :, None], adapter_middle[:, None, :], jnp.zeros((), jnp.bfloat16))
    spread_rows = spread_rows.reshape(sources * rows, local_adapters * adapter_rank)
    adapter_output = jnp.dot(
        spread_rows,
        up_local.reshape(local_adapters * adapter_rank, query_width),
        preferred_element_type=jnp.float32,
    ).astype(jnp.bfloat16)
    return adapter_output.reshape(sources, rows, query_width)


def body(
    tokens,
    adapter_id,
    pool_slot,
    lengths,
    w_query,
    w_key,
    w_value,
    pooled_down_weights,
    pool_up,
    cache_key,
    cache_value,
):
    group_count = lax.axis_size("grp")
    tp_count = lax.axis_size("tp")
    row_count, step_count, part_width = tokens.shape
    local_adapter_rows, unused_item, adapter_rank = pooled_down_weights.shape
    query_width = w_query.shape[1]
    kv_width = w_key.shape[1]
    kv_local = kv_width // HD
    q_local = query_width // HD
    group_size = q_local // kv_local
    count_of_tokens = row_count * step_count
    adapter_span = jnp.arange(pool_slot.shape[0], dtype=jnp.int32)
    pool_pos = jnp.sum(
        jnp.where(adapter_id[:, None] == adapter_span[None, :], pool_slot[None, :], 0), axis=1
    )
    owner_grp = pool_pos // local_adapter_rows
    local_slot = pool_pos % local_adapter_rows
    row_span = jnp.arange(row_count, dtype=jnp.int32)
    same_owner = (owner_grp[:, None] == owner_grp[None, :]) & (row_span[None, :] < row_span[:, None])
    owner_rank = jnp.sum(same_owner.astype(jnp.int32), axis=1)
    send_slot = owner_grp * CAP + owner_rank
    slot_span = jnp.arange(group_count * CAP, dtype=jnp.int32)
    place = (slot_span[:, None] == send_slot[None, :]).astype(jnp.bfloat16)
    token_slot = (send_slot[:, None] * step_count + jnp.arange(step_count, dtype=jnp.int32)[None, :]).reshape(-1)
    token_span = jnp.arange(group_count * CAP * step_count, dtype=jnp.int32)
    place_tokens = (token_span[:, None] == token_slot[None, :]).astype(jnp.bfloat16)
    token_rows = tokens.reshape(count_of_tokens, part_width)
    send_tokens = jnp.dot(place_tokens, token_rows, preferred_element_type=jnp.float32).astype(jnp.bfloat16)
    send_tokens = send_tokens.reshape(group_count, CAP * step_count, part_width)
    send_ids = jnp.dot(
        place, local_slot.astype(jnp.bfloat16)[:, None], preferred_element_type=jnp.float32
    ).astype(jnp.bfloat16)
    send_ids = jnp.broadcast_to(send_ids.reshape(group_count, CAP, 1), (group_count, CAP, 128))
    send_ids = jnp.concatenate([send_ids, jnp.zeros_like(send_ids)], axis=1)
    (got_tokens, got_ids), chip_pieces = exchange_ring(
        (send_tokens, send_ids), token_rows, "grp", group_count, "tp", 0
    )
    got_ids = jnp.repeat(got_ids[:, :CAP, 0].astype(jnp.int32), step_count, axis=1)
    owner_out = owner_adapter_term(got_tokens, got_ids, pooled_down_weights, pool_up)
    back, base_query_rows, key_base, value_base = exchange_project(
        owner_out, chip_pieces, w_query, w_key, w_value, "grp", group_count, "tp", 1
    )
    adapter_output = jnp.dot(
        jnp.transpose(place_tokens),
        back.reshape(group_count * CAP * step_count, query_width),
        preferred_element_type=jnp.float32,
    )
    base_query_rows = base_query_rows + adapter_output
    position = lengths[:, None] + jnp.arange(step_count, dtype=jnp.int32)[None, :]
    queries = rotate(base_query_rows.reshape(row_count, step_count, q_local, HD), position)
    queries = queries.astype(jnp.bfloat16).reshape(row_count, step_count, kv_local, group_size, HD)
    key_new = rotate(key_base.reshape(row_count, step_count, kv_local, HD), position).astype(
        jnp.bfloat16
    )
    value_new = value_base.reshape(row_count, step_count, kv_local, HD).astype(jnp.bfloat16)
    cache_keys = cache_key.reshape(row_count, cache_key.shape[1], kv_local, HD)
    cache_values = cache_value.reshape(row_count, cache_value.shape[1], kv_local, HD)
    combined = attend(queries, key_new, value_new, cache_keys, cache_values, lengths)
    return combined.reshape(row_count, step_count, query_width)


def solution(mesh):
    in_specs = (
        P("grp", None, "tp"),
        P("grp"),
        P(),
        P("grp"),
        P(None, "tp"),
        P(None, "tp"),
        P(None, "tp"),
        P("grp", "tp", None),
        P("grp", None, "tp"),
        P("grp", None, "tp"),
        P("grp", None, "tp"),
    )
    out_specs = P("grp", None, "tp")
    return jax.shard_map(body, mesh=mesh, in_specs=in_specs, out_specs=out_specs, check_vma=False)
```

```python
import math

import jax
import jax.numpy as jnp
from jax import lax
from jax.experimental import pallas as pl
from jax.experimental.pallas import tpu as pltpu
from jax.sharding import PartitionSpec as P

MESH = pl.DeviceIdType.MESH

HD = 128
CAP = 8


rope_base = 500000.0


def rotate(values, position):
    half_width = values.shape[-1] // 2
    inv_freq = jnp.exp(
        jnp.arange(half_width, dtype=jnp.float32) * (-2.0 * math.log(rope_base) / values.shape[-1])
    )
    angles = position.astype(jnp.float32)[:, :, None, None] * inv_freq
    cosine = jnp.cos(angles)
    sines = jnp.sin(angles)
    front_half = values[..., :half_width]
    back_half = values[..., half_width:]
    return jnp.concatenate(
        [front_half * cosine - back_half * sines, back_half * cosine + front_half * sines], axis=-1
    )


def attend(queries, key_new, value_new, cache_key, cache_value, lengths):
    score_scale = 1.0 / math.sqrt(queries.shape[-1])
    cached = (
        jnp.einsum("rskgd,rlkd->rskgl", queries, cache_key, preferred_element_type=jnp.float32)
        * score_scale
    )
    fresh_scores = (
        jnp.einsum("rskgd,rtkd->rskgt", queries, key_new, preferred_element_type=jnp.float32)
        * score_scale
    )
    live_mask = jnp.arange(cache_key.shape[1], dtype=jnp.int32)[None, :] < lengths[:, None]
    cached = jnp.where(live_mask[:, None, None, None, :], cached, -1e30)
    steps_here = key_new.shape[1]
    causal = (
        jnp.arange(steps_here, dtype=jnp.int32)[:, None]
        >= jnp.arange(steps_here, dtype=jnp.int32)[None, :]
    )
    fresh_scores = jnp.where(causal[None, :, None, None, :], fresh_scores, -1e30)
    row_max = jnp.maximum(jnp.max(cached, axis=-1), jnp.max(fresh_scores, axis=-1))
    cache_exp = jnp.exp(cached - row_max[..., None])
    fresh_exp = jnp.exp(fresh_scores - row_max[..., None])
    weight_sum = jnp.sum(cache_exp, axis=-1) + jnp.sum(fresh_exp, axis=-1)
    cache_weights = (cache_exp / weight_sum[..., None]).astype(jnp.bfloat16)
    fresh_weights = (fresh_exp / weight_sum[..., None]).astype(jnp.bfloat16)
    combined = jnp.einsum(
        "rskgl,rlkd->rskgd", cache_weights, cache_value, preferred_element_type=jnp.float32
    )
    combined = combined + jnp.einsum(
        "rskgt,rtkd->rskgd", fresh_weights, value_new, preferred_element_type=jnp.float32
    )
    return combined.astype(jnp.bfloat16)


TORUS_ORDER = (
    (0, 1), (1, 0), (0, 3), (3, 0), (1, 1), (3, 3), (1, 3), (3, 1),
    (0, 2), (2, 0), (2, 1), (1, 2), (2, 3), (3, 2), (2, 2),
)


def peer_offsets(count):
    if count == 16:
        def shifted(me, dz, dy):
            return lax.rem(me // 4 + dz, 4) * 4 + lax.rem(lax.rem(me, 4) + dy, 4)

        return [
            (lambda me, a=dz, b=dy: shifted(me, a, b), lambda me, a=dz, b=dy: shifted(me, 4 - a, 4 - b))
            for dz, dy in TORUS_ORDER
        ]
    return [
        (lambda me, d=offset: lax.rem(me + d, count), lambda me, d=offset: lax.rem(me + count - d, count))
        for offset in range(1, count)
    ]


def exchange_kernel(axis, count, arrays, *refs):
    send_refs = refs[:arrays]
    got_refs = refs[arrays : 2 * arrays]
    send_sem, recv_sem, local_sem = refs[2 * arrays :]
    me = lax.axis_index(axis)
    barrier = pltpu.get_barrier_semaphore()
    offsets = peer_offsets(count)
    for offset in range(1, count):
        peer = offsets[offset - 1][0](me)
        pl.semaphore_signal(barrier, inc=1, device_id={axis: peer}, device_id_type=MESH)
    pl.semaphore_wait(barrier, count - 1)
    locals_ = []
    for which in range(arrays):
        local = pltpu.make_async_copy(
            send_refs[which].at[me], got_refs[which].at[me], local_sem.at[which]
        )
        local.start()
        locals_.append(local)
    outgoing = []
    for offset in range(1, count):
        peer = offsets[offset - 1][0](me)
        for which in range(arrays):
            copy = pltpu.make_async_remote_copy(
                src_ref=send_refs[which].at[peer],
                dst_ref=got_refs[which].at[me],
                send_sem=send_sem.at[which, offset],
                recv_sem=recv_sem.at[which, offset],
                device_id={axis: peer},
                device_id_type=MESH,
            )
            copy.start()
            outgoing.append(copy)
    for offset in range(1, count):
        source = offsets[offset - 1][1](me)
        for which in range(arrays):
            outgoing[(offset - 1) * arrays + which].wait_send()
            incoming = pltpu.make_async_remote_copy(
                src_ref=send_refs[which].at[source],
                dst_ref=got_refs[which].at[source],
                send_sem=send_sem.at[which, offset],
                recv_sem=recv_sem.at[which, offset],
                device_id={axis: source},
                device_id_type=MESH,
            )
            incoming.wait_recv()
    for local in locals_:
        local.wait()


def exchange(values, axis, count, collective):
    arrays = len(values)
    vmem = pl.BlockSpec(memory_space=pltpu.VMEM)
    return pl.pallas_call(
        lambda *refs: exchange_kernel(axis, count, arrays, *refs),
        out_shape=tuple(jax.ShapeDtypeStruct(v.shape, v.dtype) for v in values),
        in_specs=[vmem] * arrays,
        out_specs=tuple([vmem] * arrays),
        scratch_shapes=[
            pltpu.SemaphoreType.DMA((arrays, count)),
            pltpu.SemaphoreType.DMA((arrays, count)),
            pltpu.SemaphoreType.DMA((arrays,)),
        ],
        compiler_params=pltpu.CompilerParams(collective_id=collective, has_side_effects=True),
    )(*values)


def exchange_ring_kernel(axis, count, gather_axis, arrays, *refs):
    send_refs = refs[:arrays]
    piece_ref = refs[arrays]
    got_refs = refs[arrays + 1 : 2 * arrays + 1]
    chip_pieces = refs[2 * arrays + 1]
    send_sem, recv_sem, local_sem, near_send, near_recv, piece_sem = refs[2 * arrays + 2 :]
    chips = lax.axis_size(gather_axis) // 2
    me = lax.axis_index(axis)
    mine = lax.axis_index(gather_axis)
    chip = mine // 2
    core = lax.rem(mine, 2)
    right_chip = lax.rem(chip + 1, chips)
    left_chip = lax.rem(chip + chips - 1, chips)
    right = right_chip * 2 + core
    left = left_chip * 2 + core

    barrier = pltpu.get_barrier_semaphore()
    offsets = peer_offsets(count)
    for offset in range(1, count):
        peer = offsets[offset - 1][0](me)
        pl.semaphore_signal(barrier, inc=1, device_id={axis: peer}, device_id_type=MESH)
    pl.semaphore_signal(barrier, inc=1, device_id={gather_axis: right}, device_id_type=MESH)
    pl.semaphore_signal(barrier, inc=1, device_id={gather_axis: left}, device_id_type=MESH)
    pl.semaphore_wait(barrier, count + 1)

    near = []
    for side, target in ((0, right), (1, left)):
        copy = pltpu.make_async_remote_copy(
            src_ref=piece_ref,
            dst_ref=chip_pieces.at[1 + side],
            send_sem=near_send.at[side],
            recv_sem=near_recv.at[side],
            device_id={gather_axis: target},
            device_id_type=MESH,
        )
        copy.start()
        near.append(copy)
    own_piece = pltpu.make_async_copy(piece_ref, chip_pieces.at[0], piece_sem)
    own_piece.start()

    locals_ = []
    for which in range(arrays):
        local = pltpu.make_async_copy(
            send_refs[which].at[me], got_refs[which].at[me], local_sem.at[which]
        )
        local.start()
        locals_.append(local)
    outgoing = []
    for offset in range(1, count):
        peer = offsets[offset - 1][0](me)
        for which in range(arrays):
            copy = pltpu.make_async_remote_copy(
                src_ref=send_refs[which].at[peer],
                dst_ref=got_refs[which].at[me],
                send_sem=send_sem.at[which, offset],
                recv_sem=recv_sem.at[which, offset],
                device_id={axis: peer},
                device_id_type=MESH,
            )
            copy.start()
            outgoing.append(copy)

    for side, source in ((0, left), (1, right)):
        near[side].wait_send()
        incoming = pltpu.make_async_remote_copy(
            src_ref=piece_ref,
            dst_ref=chip_pieces.at[1 + side],
            send_sem=near_send.at[side],
            recv_sem=near_recv.at[side],
            device_id={gather_axis: source},
            device_id_type=MESH,
        )
        incoming.wait_recv()

    for offset in range(1, count):
        source = offsets[offset - 1][1](me)
        for which in range(arrays):
            outgoing[(offset - 1) * arrays + which].wait_send()
            incoming = pltpu.make_async_remote_copy(
                src_ref=send_refs[which].at[source],
                dst_ref=got_refs[which].at[source],
                send_sem=send_sem.at[which, offset],
                recv_sem=recv_sem.at[which, offset],
                device_id={axis: source},
                device_id_type=MESH,
            )
            incoming.wait_recv()
    for local in locals_:
        local.wait()
    own_piece.wait()


def exchange_ring(values, piece, axis, count, gather_axis, collective):
    arrays = len(values)
    vmem = pl.BlockSpec(memory_space=pltpu.VMEM)
    outs = pl.pallas_call(
        lambda *refs: exchange_ring_kernel(axis, count, gather_axis, arrays, *refs),
        out_shape=tuple(jax.ShapeDtypeStruct(v.shape, v.dtype) for v in values)
        + (jax.ShapeDtypeStruct((3,) + piece.shape, piece.dtype),),
        in_specs=[vmem] * (arrays + 1),
        out_specs=tuple([vmem] * (arrays + 1)),
        scratch_shapes=[
            pltpu.SemaphoreType.DMA((arrays, count)),
            pltpu.SemaphoreType.DMA((arrays, count)),
            pltpu.SemaphoreType.DMA((arrays,)),
            pltpu.SemaphoreType.DMA((2,)),
            pltpu.SemaphoreType.DMA((2,)),
            pltpu.SemaphoreType.DMA(()),
        ],
        compiler_params=pltpu.CompilerParams(collective_id=collective, has_side_effects=True),
    )(*values, piece)
    return outs[:arrays], outs[arrays]


def tail_kernel(
    axis, count, gather_axis, part_ref, ids_ref, up_ref, near_pieces, wq_hbm, wk_ref, wv_ref,
    got_ref, q_ref, k_ref, v_ref,
    held, total, send_buf, far_piece, partner_near, partner_far, wq_buf,
    first_send, first_recv, second_send, second_recv, send_sem, recv_sem, local_sem, wq_sem,
    far_send, far_recv, partner_send, partner_recv,
):
    me = lax.axis_index(axis)
    mine = lax.axis_index(gather_axis)
    members = lax.axis_size(gather_axis)
    chips = members // 2
    chip = mine // 2
    core = lax.rem(mine, 2)
    partner = chip * 2 + (1 - core)
    right = lax.rem(chip + 1, chips) * 2 + core
    left = lax.rem(chip + chips - 1, chips) * 2 + core
    half = far_piece.shape[0] // 2
    barrier = pltpu.get_barrier_semaphore()
    offsets = peer_offsets(count)
    for offset in range(1, count):
        peer = offsets[offset - 1][0](me)
        pl.semaphore_signal(barrier, inc=1, device_id={axis: peer}, device_id_type=MESH)
    for offset in range(1, members):
        peer = lax.rem(mine + offset, members)
        pl.semaphore_signal(barrier, inc=1, device_id={gather_axis: peer}, device_id_type=MESH)
    pl.semaphore_wait(barrier, count + members - 2)

    first_out = []
    for offset in range(1, members):
        peer = lax.rem(mine + offset, members)
        copy = pltpu.make_async_remote_copy(
            src_ref=part_ref.at[peer],
            dst_ref=held.at[mine],
            send_sem=first_send.at[offset],
            recv_sem=first_recv.at[offset],
            device_id={gather_axis: peer},
            device_id_type=MESH,
        )
        copy.start()
        first_out.append(copy)
    far_out = []
    for side, slot, target, rows in ((0, 1, right, pl.ds(0, half)), (1, 2, left, pl.ds(half, half))):
        copy = pltpu.make_async_remote_copy(
            src_ref=near_pieces.at[slot, rows],
            dst_ref=far_piece.at[rows],
            send_sem=far_send.at[side],
            recv_sem=far_recv.at[side],
            device_id={gather_axis: target},
            device_id_type=MESH,
        )
        copy.start()
        far_out.append(copy)
    to_partner = pltpu.make_async_remote_copy(
        src_ref=near_pieces,
        dst_ref=partner_near,
        send_sem=partner_send.at[0],
        recv_sem=partner_recv.at[0],
        device_id={gather_axis: partner},
        device_id_type=MESH,
    )
    to_partner.start()
    held[mine] = part_ref[mine]

    piece_width = near_pieces.shape[2]
    chip_shift = (0, chips - 1, 1, 2)

    def piece_index(step):
        piece_core = core if step < 4 else 1 - core
        return lax.rem(chip + chip_shift[step % 4], chips) * 2 + piece_core

    def chunk_copy(step):
        index = piece_index(step)
        return pltpu.make_async_copy(
            wq_hbm.at[pl.ds(pl.multiple_of(index * piece_width, piece_width), piece_width)],
            wq_buf.at[step % 2],
            wq_sem.at[step % 2],
        )

    chunk_copy(0).start()
    q_ref[...] = jnp.zeros_like(q_ref)
    k_ref[...] = jnp.zeros_like(k_ref)
    v_ref[...] = jnp.zeros_like(v_ref)

    def project(step, piece):
        chunk_copy(step).wait()
        if step + 1 < 8:
            chunk_copy(step + 1).start()
        index = piece_index(step)
        rows = pl.ds(pl.multiple_of(index * piece_width, piece_width), piece_width)
        q_ref[...] += jnp.dot(piece, wq_buf[step % 2], preferred_element_type=jnp.float32)
        k_ref[...] += jnp.dot(piece, wk_ref[rows, :], preferred_element_type=jnp.float32)
        v_ref[...] += jnp.dot(piece, wv_ref[rows, :], preferred_element_type=jnp.float32)

    for step in range(3):
        project(step, near_pieces[step])

    for offset in range(1, members):
        first_out[offset - 1].wait_send()
        source = lax.rem(mine + members - offset, members)
        incoming = pltpu.make_async_remote_copy(
            src_ref=part_ref.at[source],
            dst_ref=held.at[source],
            send_sem=first_send.at[offset],
            recv_sem=first_recv.at[offset],
            device_id={gather_axis: source},
            device_id_type=MESH,
        )
        incoming.wait_recv()
    summed = held[0]
    for index in range(1, members):
        summed = summed + held[index]
    total[mine] = summed.astype(total.dtype)
    second_out = []
    for offset in range(1, members):
        peer = lax.rem(mine + offset, members)
        copy = pltpu.make_async_remote_copy(
            src_ref=total.at[mine],
            dst_ref=total.at[mine],
            send_sem=second_send.at[offset],
            recv_sem=second_recv.at[offset],
            device_id={gather_axis: peer},
            device_id_type=MESH,
        )
        copy.start()
        second_out.append(copy)

    for side, source, rows in ((0, left, pl.ds(0, half)), (1, right, pl.ds(half, half))):
        far_out[side].wait_send()
        incoming = pltpu.make_async_remote_copy(
            src_ref=near_pieces.at[1, rows],
            dst_ref=far_piece.at[rows],
            send_sem=far_send.at[side],
            recv_sem=far_recv.at[side],
            device_id={gather_axis: source},
            device_id_type=MESH,
        )
        incoming.wait_recv()
    far_to_partner = pltpu.make_async_remote_copy(
        src_ref=far_piece,
        dst_ref=partner_far,
        send_sem=partner_send.at[1],
        recv_sem=partner_recv.at[1],
        device_id={gather_axis: partner},
        device_id_type=MESH,
    )
    far_to_partner.start()

    for offset in range(1, members):
        second_out[offset - 1].wait_send()
        source = lax.rem(mine + members - offset, members)
        incoming = pltpu.make_async_remote_copy(
            src_ref=total.at[source],
            dst_ref=total.at[source],
            send_sem=second_send.at[offset],
            recv_sem=second_recv.at[offset],
            device_id={gather_axis: source},
            device_id_type=MESH,
        )
        incoming.wait_recv()

    middle = total[...].reshape(ids_ref.shape[0], total.shape[2])
    slot_ids = ids_ref[...]
    upward = jnp.zeros((ids_ref.shape[0], up_ref.shape[2]), jnp.float32)
    for adapter in range(up_ref.shape[0]):
        chosen = jnp.where(slot_ids == adapter, middle, jnp.zeros_like(middle))
        upward = upward + jnp.dot(chosen, up_ref[adapter], preferred_element_type=jnp.float32)
    send_buf[...] = upward.astype(send_buf.dtype).reshape(send_buf.shape)

    local = pltpu.make_async_copy(send_buf.at[me], got_ref.at[me], local_sem)
    local.start()
    outgoing = []
    for offset in range(1, count):
        peer = offsets[offset - 1][0](me)
        copy = pltpu.make_async_remote_copy(
            src_ref=send_buf.at[peer],
            dst_ref=got_ref.at[me],
            send_sem=send_sem.at[offset],
            recv_sem=recv_sem.at[offset],
            device_id={axis: peer},
            device_id_type=MESH,
        )
        copy.start()
        outgoing.append(copy)

    project(3, far_piece[...])
    to_partner.wait_send()
    to_partner.wait_recv()
    for step in range(3):
        project(4 + step, partner_near[step])
    far_to_partner.wait_send()
    far_to_partner.wait_recv()
    project(7, partner_far[...])

    for offset in range(1, count):
        outgoing[offset - 1].wait_send()
        source = offsets[offset - 1][1](me)
        incoming = pltpu.make_async_remote_copy(
            src_ref=send_buf.at[source],
            dst_ref=got_ref.at[source],
            send_sem=send_sem.at[offset],
            recv_sem=recv_sem.at[offset],
            device_id={axis: source},
            device_id_type=MESH,
        )
        incoming.wait_recv()
    local.wait()


def tail(partial, slot_ids, up_local, near_pieces, w_query, w_key, w_value, axis, count, gather_axis, collective):
    members = lax.axis_size(gather_axis)
    token_rows, adapter_rank = partial.shape
    chunks = partial.reshape(members, token_rows // members, adapter_rank)
    query_width = up_local.shape[2]
    unused_item, token_count, piece_width = near_pieces.shape
    got_shape = (count, token_rows // count, query_width)
    vmem = pl.BlockSpec(memory_space=pltpu.VMEM)
    return pl.pallas_call(
        lambda *refs: tail_kernel(axis, count, gather_axis, *refs),
        out_shape=(
            jax.ShapeDtypeStruct(got_shape, jnp.bfloat16),
            jax.ShapeDtypeStruct((token_count, w_query.shape[1]), jnp.float32),
            jax.ShapeDtypeStruct((token_count, w_key.shape[1]), jnp.float32),
            jax.ShapeDtypeStruct((token_count, w_value.shape[1]), jnp.float32),
        ),
        in_specs=[vmem, vmem, vmem, vmem, pl.BlockSpec(memory_space=pl.ANY), vmem, vmem],
        out_specs=(vmem, vmem, vmem, vmem),
        scratch_shapes=[
            pltpu.VMEM(chunks.shape, jnp.float32),
            pltpu.VMEM(chunks.shape, jnp.bfloat16),
            pltpu.VMEM(got_shape, jnp.bfloat16),
            pltpu.VMEM((token_count, piece_width), near_pieces.dtype),
            pltpu.VMEM(near_pieces.shape, near_pieces.dtype),
            pltpu.VMEM((token_count, piece_width), near_pieces.dtype),
            pltpu.VMEM((2, piece_width, w_query.shape[1]), w_query.dtype),
            pltpu.SemaphoreType.DMA((members,)),
            pltpu.SemaphoreType.DMA((members,)),
            pltpu.SemaphoreType.DMA((members,)),
            pltpu.SemaphoreType.DMA((members,)),
            pltpu.SemaphoreType.DMA((count,)),
            pltpu.SemaphoreType.DMA((count,)),
            pltpu.SemaphoreType.DMA(()),
            pltpu.SemaphoreType.DMA((2,)),
            pltpu.SemaphoreType.DMA((2,)),
            pltpu.SemaphoreType.DMA((2,)),
            pltpu.SemaphoreType.DMA((2,)),
            pltpu.SemaphoreType.DMA((2,)),
        ],
        compiler_params=pltpu.CompilerParams(
            collective_id=collective, has_side_effects=True, vmem_limit_bytes=60 * 1024 * 1024
        ),
    )(chunks, slot_ids, up_local, near_pieces, w_query, w_key, w_value)


def down_partial(received, slot_ids, down_local):
    sources, rows, part_width = received.shape
    local_adapters, unused_item, adapter_rank = down_local.shape
    token_rows = received.reshape(sources * rows, part_width)
    every_down = jnp.einsum(
        "td,adr->tar", token_rows, down_local, preferred_element_type=jnp.float32
    )
    pick = slot_ids.reshape(sources * rows)[:, None] == jnp.arange(local_adapters, dtype=jnp.int32)[None, :]
    return jnp.sum(jnp.where(pick[:, :, None], every_down, 0.0), axis=1)


def body(
    tokens,
    adapter_id,
    pool_slot,
    lengths,
    w_query,
    w_key,
    w_value,
    pooled_down_weights,
    pool_up,
    cache_key,
    cache_value,
):
    group_count = lax.axis_size("grp")
    tp_count = lax.axis_size("tp")
    row_count, step_count, part_width = tokens.shape
    local_adapter_rows, unused_item, adapter_rank = pooled_down_weights.shape
    query_width = w_query.shape[1]
    kv_width = w_key.shape[1]
    kv_local = kv_width // HD
    q_local = query_width // HD
    group_size = q_local // kv_local
    count_of_tokens = row_count * step_count
    adapter_span = jnp.arange(pool_slot.shape[0], dtype=jnp.int32)
    pool_pos = jnp.sum(
        jnp.where(adapter_id[:, None] == adapter_span[None, :], pool_slot[None, :], 0), axis=1
    )
    owner_grp = pool_pos // local_adapter_rows
    local_slot = pool_pos % local_adapter_rows
    row_span = jnp.arange(row_count, dtype=jnp.int32)
    same_owner = (owner_grp[:, None] == owner_grp[None, :]) & (row_span[None, :] < row_span[:, None])
    owner_rank = jnp.sum(same_owner.astype(jnp.int32), axis=1)
    send_slot = owner_grp * CAP + owner_rank
    slot_span = jnp.arange(group_count * CAP, dtype=jnp.int32)
    place = (slot_span[:, None] == send_slot[None, :]).astype(jnp.bfloat16)
    token_slot = (send_slot[:, None] * step_count + jnp.arange(step_count, dtype=jnp.int32)[None, :]).reshape(-1)
    token_span = jnp.arange(group_count * CAP * step_count, dtype=jnp.int32)
    place_tokens = (token_span[:, None] == token_slot[None, :]).astype(jnp.bfloat16)
    token_rows = tokens.reshape(count_of_tokens, part_width)
    send_tokens = jnp.dot(place_tokens, token_rows, preferred_element_type=jnp.float32).astype(jnp.bfloat16)
    send_tokens = send_tokens.reshape(group_count, CAP * step_count, part_width)
    send_ids = jnp.dot(
        place, local_slot.astype(jnp.bfloat16)[:, None], preferred_element_type=jnp.float32
    ).astype(jnp.bfloat16)
    send_ids = jnp.broadcast_to(send_ids.reshape(group_count, CAP, 1), (group_count, CAP, 128))
    send_ids = jnp.concatenate([send_ids, jnp.zeros_like(send_ids)], axis=1)
    (got_tokens, got_ids), chip_pieces = exchange_ring(
        (send_tokens, send_ids), token_rows, "grp", group_count, "tp", 0
    )
    got_ids = jnp.repeat(got_ids[:, :CAP, 0].astype(jnp.int32), step_count, axis=1)
    partial = down_partial(got_tokens, got_ids, pooled_down_weights)
    back, base_query_rows, key_base, value_base = tail(
        partial, got_ids.reshape(-1, 1), pool_up, chip_pieces, w_query, w_key, w_value,
        "grp", group_count, "tp", 1
    )
    adapter_output = jnp.dot(
        jnp.transpose(place_tokens),
        back.reshape(group_count * CAP * step_count, query_width),
        preferred_element_type=jnp.float32,
    )
    base_query_rows = base_query_rows + adapter_output
    position = lengths[:, None] + jnp.arange(step_count, dtype=jnp.int32)[None, :]
    queries = rotate(base_query_rows.reshape(row_count, step_count, q_local, HD), position)
    queries = queries.astype(jnp.bfloat16).reshape(row_count, step_count, kv_local, group_size, HD)
    key_new = rotate(key_base.reshape(row_count, step_count, kv_local, HD), position).astype(
        jnp.bfloat16
    )
    value_new = value_base.reshape(row_count, step_count, kv_local, HD).astype(jnp.bfloat16)
    cache_keys = cache_key.reshape(row_count, cache_key.shape[1], kv_local, HD)
    cache_values = cache_value.reshape(row_count, cache_value.shape[1], kv_local, HD)
    combined = attend(queries, key_new, value_new, cache_keys, cache_values, lengths)
    return combined.reshape(row_count, step_count, query_width)


def solution(mesh):
    in_specs = (
        P("grp", None, "tp"),
        P("grp"),
        P(),
        P("grp"),
        P(None, "tp"),
        P(None, "tp"),
        P(None, "tp"),
        P("grp", "tp", None),
        P("grp", None, "tp"),
        P("grp", None, "tp"),
        P("grp", None, "tp"),
    )
    out_specs = P("grp", None, "tp")
    return jax.shard_map(body, mesh=mesh, in_specs=in_specs, out_specs=out_specs, check_vma=False)
```

```python
import math

import jax
import jax.numpy as jnp
from jax import lax
from jax.experimental import pallas as pl
from jax.experimental.pallas import tpu as pltpu
from jax.sharding import PartitionSpec as P

MESH = pl.DeviceIdType.MESH

HD = 128
CAP = 8


rope_base = 500000.0


def rotate(values, position):
    half_width = values.shape[-1] // 2
    inv_freq = jnp.exp(
        jnp.arange(half_width, dtype=jnp.float32) * (-2.0 * math.log(rope_base) / values.shape[-1])
    )
    angles = position.astype(jnp.float32)[:, :, None, None] * inv_freq
    cosine = jnp.cos(angles)
    sines = jnp.sin(angles)
    front_half = values[..., :half_width]
    back_half = values[..., half_width:]
    return jnp.concatenate(
        [front_half * cosine - back_half * sines, back_half * cosine + front_half * sines], axis=-1
    )


def attend(queries, key_new, value_new, cache_key, cache_value, lengths):
    score_scale = 1.0 / math.sqrt(queries.shape[-1])
    cached = (
        jnp.einsum("rskgd,rlkd->rskgl", queries, cache_key, preferred_element_type=jnp.float32)
        * score_scale
    )
    fresh_scores = (
        jnp.einsum("rskgd,rtkd->rskgt", queries, key_new, preferred_element_type=jnp.float32)
        * score_scale
    )
    live_mask = jnp.arange(cache_key.shape[1], dtype=jnp.int32)[None, :] < lengths[:, None]
    cached = jnp.where(live_mask[:, None, None, None, :], cached, -1e30)
    steps_here = key_new.shape[1]
    causal = (
        jnp.arange(steps_here, dtype=jnp.int32)[:, None]
        >= jnp.arange(steps_here, dtype=jnp.int32)[None, :]
    )
    fresh_scores = jnp.where(causal[None, :, None, None, :], fresh_scores, -1e30)
    row_max = jnp.maximum(jnp.max(cached, axis=-1), jnp.max(fresh_scores, axis=-1))
    cache_exp = jnp.exp(cached - row_max[..., None])
    fresh_exp = jnp.exp(fresh_scores - row_max[..., None])
    weight_sum = jnp.sum(cache_exp, axis=-1) + jnp.sum(fresh_exp, axis=-1)
    cache_weights = (cache_exp / weight_sum[..., None]).astype(jnp.bfloat16)
    fresh_weights = (fresh_exp / weight_sum[..., None]).astype(jnp.bfloat16)
    combined = jnp.einsum(
        "rskgl,rlkd->rskgd", cache_weights, cache_value, preferred_element_type=jnp.float32
    )
    combined = combined + jnp.einsum(
        "rskgt,rtkd->rskgd", fresh_weights, value_new, preferred_element_type=jnp.float32
    )
    return combined.astype(jnp.bfloat16)


TORUS_ORDER = (
    (0, 1), (1, 0), (0, 3), (3, 0), (1, 1), (3, 3), (1, 3), (3, 1),
    (0, 2), (2, 0), (2, 1), (1, 2), (2, 3), (3, 2), (2, 2),
)


def peer_offsets(count):
    if count == 16:
        def shifted(me, dz, dy):
            return lax.rem(me // 4 + dz, 4) * 4 + lax.rem(lax.rem(me, 4) + dy, 4)

        return [
            (lambda me, a=dz, b=dy: shifted(me, a, b), lambda me, a=dz, b=dy: shifted(me, 4 - a, 4 - b))
            for dz, dy in TORUS_ORDER
        ]
    return [
        (lambda me, d=offset: lax.rem(me + d, count), lambda me, d=offset: lax.rem(me + count - d, count))
        for offset in range(1, count)
    ]


def exchange_kernel(axis, count, arrays, *refs):
    send_refs = refs[:arrays]
    got_refs = refs[arrays : 2 * arrays]
    send_sem, recv_sem, local_sem = refs[2 * arrays :]
    me = lax.axis_index(axis)
    barrier = pltpu.get_barrier_semaphore()
    offsets = peer_offsets(count)
    for offset in range(1, count):
        peer = offsets[offset - 1][0](me)
        pl.semaphore_signal(barrier, inc=1, device_id={axis: peer}, device_id_type=MESH)
    pl.semaphore_wait(barrier, count - 1)
    locals_ = []
    for which in range(arrays):
        local = pltpu.make_async_copy(
            send_refs[which].at[me], got_refs[which].at[me], local_sem.at[which]
        )
        local.start()
        locals_.append(local)
    outgoing = []
    for offset in range(1, count):
        peer = offsets[offset - 1][0](me)
        for which in range(arrays):
            copy = pltpu.make_async_remote_copy(
                src_ref=send_refs[which].at[peer],
                dst_ref=got_refs[which].at[me],
                send_sem=send_sem.at[which, offset],
                recv_sem=recv_sem.at[which, offset],
                device_id={axis: peer},
                device_id_type=MESH,
            )
            copy.start()
            outgoing.append(copy)
    for offset in range(1, count):
        source = offsets[offset - 1][1](me)
        for which in range(arrays):
            outgoing[(offset - 1) * arrays + which].wait_send()
            incoming = pltpu.make_async_remote_copy(
                src_ref=send_refs[which].at[source],
                dst_ref=got_refs[which].at[source],
                send_sem=send_sem.at[which, offset],
                recv_sem=recv_sem.at[which, offset],
                device_id={axis: source},
                device_id_type=MESH,
            )
            incoming.wait_recv()
    for local in locals_:
        local.wait()


def exchange(values, axis, count, collective):
    arrays = len(values)
    vmem = pl.BlockSpec(memory_space=pltpu.VMEM)
    return pl.pallas_call(
        lambda *refs: exchange_kernel(axis, count, arrays, *refs),
        out_shape=tuple(jax.ShapeDtypeStruct(v.shape, v.dtype) for v in values),
        in_specs=[vmem] * arrays,
        out_specs=tuple([vmem] * arrays),
        scratch_shapes=[
            pltpu.SemaphoreType.DMA((arrays, count)),
            pltpu.SemaphoreType.DMA((arrays, count)),
            pltpu.SemaphoreType.DMA((arrays,)),
        ],
        compiler_params=pltpu.CompilerParams(collective_id=collective, has_side_effects=True),
    )(*values)


def exchange_ring_kernel(axis, count, gather_axis, arrays, *refs):
    send_refs = refs[:arrays]
    piece_ref = refs[arrays]
    got_refs = refs[arrays + 1 : 2 * arrays + 1]
    chip_pieces = refs[2 * arrays + 1]
    send_sem, recv_sem, local_sem, near_send, near_recv, piece_sem = refs[2 * arrays + 2 :]
    chips = lax.axis_size(gather_axis) // 2
    me = lax.axis_index(axis)
    mine = lax.axis_index(gather_axis)
    chip = mine // 2
    core = lax.rem(mine, 2)
    right_chip = lax.rem(chip + 1, chips)
    left_chip = lax.rem(chip + chips - 1, chips)
    right = right_chip * 2 + core
    left = left_chip * 2 + core

    barrier = pltpu.get_barrier_semaphore()
    offsets = peer_offsets(count)
    for offset in range(1, count):
        peer = offsets[offset - 1][0](me)
        pl.semaphore_signal(barrier, inc=1, device_id={axis: peer}, device_id_type=MESH)
    pl.semaphore_signal(barrier, inc=1, device_id={gather_axis: right}, device_id_type=MESH)
    pl.semaphore_signal(barrier, inc=1, device_id={gather_axis: left}, device_id_type=MESH)
    pl.semaphore_wait(barrier, count + 1)

    near = []
    for side, target in ((0, right), (1, left)):
        copy = pltpu.make_async_remote_copy(
            src_ref=piece_ref,
            dst_ref=chip_pieces.at[1 + side],
            send_sem=near_send.at[side],
            recv_sem=near_recv.at[side],
            device_id={gather_axis: target},
            device_id_type=MESH,
        )
        copy.start()
        near.append(copy)
    own_piece = pltpu.make_async_copy(piece_ref, chip_pieces.at[0], piece_sem)
    own_piece.start()

    locals_ = []
    for which in range(arrays):
        local = pltpu.make_async_copy(
            send_refs[which].at[me], got_refs[which].at[me], local_sem.at[which]
        )
        local.start()
        locals_.append(local)
    outgoing = []
    for offset in range(1, count):
        peer = offsets[offset - 1][0](me)
        for which in range(arrays):
            copy = pltpu.make_async_remote_copy(
                src_ref=send_refs[which].at[peer],
                dst_ref=got_refs[which].at[me],
                send_sem=send_sem.at[which, offset],
                recv_sem=recv_sem.at[which, offset],
                device_id={axis: peer},
                device_id_type=MESH,
            )
            copy.start()
            outgoing.append(copy)

    for side, source in ((0, left), (1, right)):
        near[side].wait_send()
        incoming = pltpu.make_async_remote_copy(
            src_ref=piece_ref,
            dst_ref=chip_pieces.at[1 + side],
            send_sem=near_send.at[side],
            recv_sem=near_recv.at[side],
            device_id={gather_axis: source},
            device_id_type=MESH,
        )
        incoming.wait_recv()

    for offset in range(1, count):
        source = offsets[offset - 1][1](me)
        for which in range(arrays):
            outgoing[(offset - 1) * arrays + which].wait_send()
            incoming = pltpu.make_async_remote_copy(
                src_ref=send_refs[which].at[source],
                dst_ref=got_refs[which].at[source],
                send_sem=send_sem.at[which, offset],
                recv_sem=recv_sem.at[which, offset],
                device_id={axis: source},
                device_id_type=MESH,
            )
            incoming.wait_recv()
    for local in locals_:
        local.wait()
    own_piece.wait()


def exchange_ring(values, piece, axis, count, gather_axis, collective):
    arrays = len(values)
    vmem = pl.BlockSpec(memory_space=pltpu.VMEM)
    outs = pl.pallas_call(
        lambda *refs: exchange_ring_kernel(axis, count, gather_axis, arrays, *refs),
        out_shape=tuple(jax.ShapeDtypeStruct(v.shape, v.dtype) for v in values)
        + (jax.ShapeDtypeStruct((3,) + piece.shape, piece.dtype),),
        in_specs=[vmem] * (arrays + 1),
        out_specs=tuple([vmem] * (arrays + 1)),
        scratch_shapes=[
            pltpu.SemaphoreType.DMA((arrays, count)),
            pltpu.SemaphoreType.DMA((arrays, count)),
            pltpu.SemaphoreType.DMA((arrays,)),
            pltpu.SemaphoreType.DMA((2,)),
            pltpu.SemaphoreType.DMA((2,)),
            pltpu.SemaphoreType.DMA(()),
        ],
        compiler_params=pltpu.CompilerParams(collective_id=collective, has_side_effects=True),
    )(*values, piece)
    return outs[:arrays], outs[arrays]


def tail_kernel(
    axis, count, gather_axis, part_ref, ids_ref, up_ref, near_pieces, wq_hbm, wk_ref, wv_ref,
    got_ref, q_ref, k_ref, v_ref,
    held, total, send_buf, far_piece, partner_near, partner_far, wq_buf,
    first_send, first_recv, second_send, second_recv, send_sem, recv_sem, local_sem, wq_sem,
    far_send, far_recv, partner_send, partner_recv,
):
    me = lax.axis_index(axis)
    mine = lax.axis_index(gather_axis)
    members = lax.axis_size(gather_axis)
    chips = members // 2
    chip = mine // 2
    core = lax.rem(mine, 2)
    partner = chip * 2 + (1 - core)
    right = lax.rem(chip + 1, chips) * 2 + core
    left = lax.rem(chip + chips - 1, chips) * 2 + core
    half = far_piece.shape[0] // 2
    barrier = pltpu.get_barrier_semaphore()
    offsets = peer_offsets(count)
    for offset in range(1, count):
        peer = offsets[offset - 1][0](me)
        pl.semaphore_signal(barrier, inc=1, device_id={axis: peer}, device_id_type=MESH)
    for offset in range(1, members):
        peer = lax.rem(mine + offset, members)
        pl.semaphore_signal(barrier, inc=1, device_id={gather_axis: peer}, device_id_type=MESH)
    pl.semaphore_wait(barrier, count + members - 2)

    first_out = []
    for offset in range(1, members):
        peer = lax.rem(mine + offset, members)
        copy = pltpu.make_async_remote_copy(
            src_ref=part_ref.at[peer],
            dst_ref=held.at[mine],
            send_sem=first_send.at[offset],
            recv_sem=first_recv.at[offset],
            device_id={gather_axis: peer},
            device_id_type=MESH,
        )
        copy.start()
        first_out.append(copy)
    far_out = []
    for side, slot, target, rows in ((0, 1, right, pl.ds(0, half)), (1, 2, left, pl.ds(half, half))):
        copy = pltpu.make_async_remote_copy(
            src_ref=near_pieces.at[slot, rows],
            dst_ref=far_piece.at[rows],
            send_sem=far_send.at[side],
            recv_sem=far_recv.at[side],
            device_id={gather_axis: target},
            device_id_type=MESH,
        )
        copy.start()
        far_out.append(copy)
    to_partner = pltpu.make_async_remote_copy(
        src_ref=near_pieces,
        dst_ref=partner_near,
        send_sem=partner_send.at[0],
        recv_sem=partner_recv.at[0],
        device_id={gather_axis: partner},
        device_id_type=MESH,
    )
    to_partner.start()
    held[mine] = part_ref[mine]

    piece_width = near_pieces.shape[2]
    chip_shift = (0, chips - 1, 1, 2)

    def piece_index(step):
        piece_core = core if step < 4 else 1 - core
        return lax.rem(chip + chip_shift[step % 4], chips) * 2 + piece_core

    def chunk_copy(step):
        index = piece_index(step)
        return pltpu.make_async_copy(
            wq_hbm.at[pl.ds(pl.multiple_of(index * piece_width, piece_width), piece_width)],
            wq_buf.at[step % 2],
            wq_sem.at[step % 2],
        )

    chunk_copy(0).start()
    q_ref[...] = jnp.zeros_like(q_ref)
    k_ref[...] = jnp.zeros_like(k_ref)
    v_ref[...] = jnp.zeros_like(v_ref)

    def project(step, piece):
        chunk_copy(step).wait()
        if step + 1 < 8:
            chunk_copy(step + 1).start()
        index = piece_index(step)
        rows = pl.ds(pl.multiple_of(index * piece_width, piece_width), piece_width)
        q_ref[...] += jnp.dot(piece, wq_buf[step % 2], preferred_element_type=jnp.float32)
        k_ref[...] += jnp.dot(piece, wk_ref[rows, :], preferred_element_type=jnp.float32)
        v_ref[...] += jnp.dot(piece, wv_ref[rows, :], preferred_element_type=jnp.float32)

    for offset in range(1, members):
        first_out[offset - 1].wait_send()
        source = lax.rem(mine + members - offset, members)
        incoming = pltpu.make_async_remote_copy(
            src_ref=part_ref.at[source],
            dst_ref=held.at[source],
            send_sem=first_send.at[offset],
            recv_sem=first_recv.at[offset],
            device_id={gather_axis: source},
            device_id_type=MESH,
        )
        incoming.wait_recv()
    summed = held[0]
    for index in range(1, members):
        summed = summed + held[index]
    total[mine] = summed.astype(total.dtype)
    second_out = []
    for offset in range(1, members):
        peer = lax.rem(mine + offset, members)
        copy = pltpu.make_async_remote_copy(
            src_ref=total.at[mine],
            dst_ref=total.at[mine],
            send_sem=second_send.at[offset],
            recv_sem=second_recv.at[offset],
            device_id={gather_axis: peer},
            device_id_type=MESH,
        )
        copy.start()
        second_out.append(copy)

    for side, source, rows in ((0, left, pl.ds(0, half)), (1, right, pl.ds(half, half))):
        far_out[side].wait_send()
        incoming = pltpu.make_async_remote_copy(
            src_ref=near_pieces.at[1, rows],
            dst_ref=far_piece.at[rows],
            send_sem=far_send.at[side],
            recv_sem=far_recv.at[side],
            device_id={gather_axis: source},
            device_id_type=MESH,
        )
        incoming.wait_recv()
    far_to_partner = pltpu.make_async_remote_copy(
        src_ref=far_piece,
        dst_ref=partner_far,
        send_sem=partner_send.at[1],
        recv_sem=partner_recv.at[1],
        device_id={gather_axis: partner},
        device_id_type=MESH,
    )
    far_to_partner.start()

    for offset in range(1, members):
        second_out[offset - 1].wait_send()
        source = lax.rem(mine + members - offset, members)
        incoming = pltpu.make_async_remote_copy(
            src_ref=total.at[source],
            dst_ref=total.at[source],
            send_sem=second_send.at[offset],
            recv_sem=second_recv.at[offset],
            device_id={gather_axis: source},
            device_id_type=MESH,
        )
        incoming.wait_recv()

    middle = total[...].reshape(ids_ref.shape[0], total.shape[2])
    slot_ids = ids_ref[...]
    upward = jnp.zeros((ids_ref.shape[0], up_ref.shape[2]), jnp.float32)
    for adapter in range(up_ref.shape[0]):
        chosen = jnp.where(slot_ids == adapter, middle, jnp.zeros_like(middle))
        upward = upward + jnp.dot(chosen, up_ref[adapter], preferred_element_type=jnp.float32)
    send_buf[...] = upward.astype(send_buf.dtype).reshape(send_buf.shape)

    local = pltpu.make_async_copy(send_buf.at[me], got_ref.at[me], local_sem)
    local.start()
    outgoing = []
    for offset in range(1, count):
        peer = offsets[offset - 1][0](me)
        copy = pltpu.make_async_remote_copy(
            src_ref=send_buf.at[peer],
            dst_ref=got_ref.at[me],
            send_sem=send_sem.at[offset],
            recv_sem=recv_sem.at[offset],
            device_id={axis: peer},
            device_id_type=MESH,
        )
        copy.start()
        outgoing.append(copy)

    for step in range(3):
        project(step, near_pieces[step])
    project(3, far_piece[...])
    to_partner.wait_send()
    to_partner.wait_recv()
    for step in range(3):
        project(4 + step, partner_near[step])
    far_to_partner.wait_send()
    far_to_partner.wait_recv()
    project(7, partner_far[...])

    for offset in range(1, count):
        outgoing[offset - 1].wait_send()
        source = offsets[offset - 1][1](me)
        incoming = pltpu.make_async_remote_copy(
            src_ref=send_buf.at[source],
            dst_ref=got_ref.at[source],
            send_sem=send_sem.at[offset],
            recv_sem=recv_sem.at[offset],
            device_id={axis: source},
            device_id_type=MESH,
        )
        incoming.wait_recv()
    local.wait()


def tail(partial, slot_ids, up_local, near_pieces, w_query, w_key, w_value, axis, count, gather_axis, collective):
    members = lax.axis_size(gather_axis)
    token_rows, adapter_rank = partial.shape
    chunks = partial.reshape(members, token_rows // members, adapter_rank)
    query_width = up_local.shape[2]
    unused_item, token_count, piece_width = near_pieces.shape
    got_shape = (count, token_rows // count, query_width)
    vmem = pl.BlockSpec(memory_space=pltpu.VMEM)
    return pl.pallas_call(
        lambda *refs: tail_kernel(axis, count, gather_axis, *refs),
        out_shape=(
            jax.ShapeDtypeStruct(got_shape, jnp.bfloat16),
            jax.ShapeDtypeStruct((token_count, w_query.shape[1]), jnp.float32),
            jax.ShapeDtypeStruct((token_count, w_key.shape[1]), jnp.float32),
            jax.ShapeDtypeStruct((token_count, w_value.shape[1]), jnp.float32),
        ),
        in_specs=[vmem, vmem, vmem, vmem, pl.BlockSpec(memory_space=pl.ANY), vmem, vmem],
        out_specs=(vmem, vmem, vmem, vmem),
        scratch_shapes=[
            pltpu.VMEM(chunks.shape, jnp.float32),
            pltpu.VMEM(chunks.shape, jnp.bfloat16),
            pltpu.VMEM(got_shape, jnp.bfloat16),
            pltpu.VMEM((token_count, piece_width), near_pieces.dtype),
            pltpu.VMEM(near_pieces.shape, near_pieces.dtype),
            pltpu.VMEM((token_count, piece_width), near_pieces.dtype),
            pltpu.VMEM((2, piece_width, w_query.shape[1]), w_query.dtype),
            pltpu.SemaphoreType.DMA((members,)),
            pltpu.SemaphoreType.DMA((members,)),
            pltpu.SemaphoreType.DMA((members,)),
            pltpu.SemaphoreType.DMA((members,)),
            pltpu.SemaphoreType.DMA((count,)),
            pltpu.SemaphoreType.DMA((count,)),
            pltpu.SemaphoreType.DMA(()),
            pltpu.SemaphoreType.DMA((2,)),
            pltpu.SemaphoreType.DMA((2,)),
            pltpu.SemaphoreType.DMA((2,)),
            pltpu.SemaphoreType.DMA((2,)),
            pltpu.SemaphoreType.DMA((2,)),
        ],
        compiler_params=pltpu.CompilerParams(
            collective_id=collective, has_side_effects=True, vmem_limit_bytes=60 * 1024 * 1024
        ),
    )(chunks, slot_ids, up_local, near_pieces, w_query, w_key, w_value)


def down_partial(received, slot_ids, down_local):
    sources, rows, part_width = received.shape
    local_adapters, unused_item, adapter_rank = down_local.shape
    token_rows = received.reshape(sources * rows, part_width)
    every_down = jnp.einsum(
        "td,adr->tar", token_rows, down_local, preferred_element_type=jnp.float32
    )
    pick = slot_ids.reshape(sources * rows)[:, None] == jnp.arange(local_adapters, dtype=jnp.int32)[None, :]
    return jnp.sum(jnp.where(pick[:, :, None], every_down, 0.0), axis=1)


def body(
    tokens,
    adapter_id,
    pool_slot,
    lengths,
    w_query,
    w_key,
    w_value,
    pooled_down_weights,
    pool_up,
    cache_key,
    cache_value,
):
    group_count = lax.axis_size("grp")
    tp_count = lax.axis_size("tp")
    row_count, step_count, part_width = tokens.shape
    local_adapter_rows, unused_item, adapter_rank = pooled_down_weights.shape
    query_width = w_query.shape[1]
    kv_width = w_key.shape[1]
    kv_local = kv_width // HD
    q_local = query_width // HD
    group_size = q_local // kv_local
    count_of_tokens = row_count * step_count
    adapter_span = jnp.arange(pool_slot.shape[0], dtype=jnp.int32)
    pool_pos = jnp.sum(
        jnp.where(adapter_id[:, None] == adapter_span[None, :], pool_slot[None, :], 0), axis=1
    )
    owner_grp = pool_pos // local_adapter_rows
    local_slot = pool_pos % local_adapter_rows
    row_span = jnp.arange(row_count, dtype=jnp.int32)
    same_owner = (owner_grp[:, None] == owner_grp[None, :]) & (row_span[None, :] < row_span[:, None])
    owner_rank = jnp.sum(same_owner.astype(jnp.int32), axis=1)
    send_slot = owner_grp * CAP + owner_rank
    slot_span = jnp.arange(group_count * CAP, dtype=jnp.int32)
    place = (slot_span[:, None] == send_slot[None, :]).astype(jnp.bfloat16)
    token_slot = (send_slot[:, None] * step_count + jnp.arange(step_count, dtype=jnp.int32)[None, :]).reshape(-1)
    token_span = jnp.arange(group_count * CAP * step_count, dtype=jnp.int32)
    place_tokens = (token_span[:, None] == token_slot[None, :]).astype(jnp.bfloat16)
    token_rows = tokens.reshape(count_of_tokens, part_width)
    send_tokens = jnp.dot(place_tokens, token_rows, preferred_element_type=jnp.float32).astype(jnp.bfloat16)
    send_tokens = send_tokens.reshape(group_count, CAP * step_count, part_width)
    send_ids = jnp.dot(
        place, local_slot.astype(jnp.bfloat16)[:, None], preferred_element_type=jnp.float32
    ).astype(jnp.bfloat16)
    send_ids = jnp.broadcast_to(send_ids.reshape(group_count, CAP, 1), (group_count, CAP, 128))
    send_ids = jnp.concatenate([send_ids, jnp.zeros_like(send_ids)], axis=1)
    (got_tokens, got_ids), chip_pieces = exchange_ring(
        (send_tokens, send_ids), token_rows, "grp", group_count, "tp", 0
    )
    got_ids = jnp.repeat(got_ids[:, :CAP, 0].astype(jnp.int32), step_count, axis=1)
    partial = down_partial(got_tokens, got_ids, pooled_down_weights)
    back, base_query_rows, key_base, value_base = tail(
        partial, got_ids.reshape(-1, 1), pool_up, chip_pieces, w_query, w_key, w_value,
        "grp", group_count, "tp", 1
    )
    adapter_output = jnp.dot(
        jnp.transpose(place_tokens),
        back.reshape(group_count * CAP * step_count, query_width),
        preferred_element_type=jnp.float32,
    )
    base_query_rows = base_query_rows + adapter_output
    position = lengths[:, None] + jnp.arange(step_count, dtype=jnp.int32)[None, :]
    queries = rotate(base_query_rows.reshape(row_count, step_count, q_local, HD), position)
    queries = queries.astype(jnp.bfloat16).reshape(row_count, step_count, kv_local, group_size, HD)
    key_new = rotate(key_base.reshape(row_count, step_count, kv_local, HD), position).astype(
        jnp.bfloat16
    )
    value_new = value_base.reshape(row_count, step_count, kv_local, HD).astype(jnp.bfloat16)
    cache_keys = cache_key.reshape(row_count, cache_key.shape[1], kv_local, HD)
    cache_values = cache_value.reshape(row_count, cache_value.shape[1], kv_local, HD)
    combined = attend(queries, key_new, value_new, cache_keys, cache_values, lengths)
    return combined.reshape(row_count, step_count, query_width)


def solution(mesh):
    in_specs = (
        P("grp", None, "tp"),
        P("grp"),
        P(),
        P("grp"),
        P(None, "tp"),
        P(None, "tp"),
        P(None, "tp"),
        P("grp", "tp", None),
        P("grp", None, "tp"),
        P("grp", None, "tp"),
        P("grp", None, "tp"),
    )
    out_specs = P("grp", None, "tp")
    return jax.shard_map(body, mesh=mesh, in_specs=in_specs, out_specs=out_specs, check_vma=False)
```

```python
import math

import jax
import jax.numpy as jnp
from jax import lax
from jax.experimental import pallas as pl
from jax.experimental.pallas import tpu as pltpu
from jax.sharding import PartitionSpec as P

MESH = pl.DeviceIdType.MESH

HD = 128
CAP = 8


rope_base = 500000.0


def rotate(values, position):
    half_width = values.shape[-1] // 2
    inv_freq = jnp.exp(
        jnp.arange(half_width, dtype=jnp.float32) * (-2.0 * math.log(rope_base) / values.shape[-1])
    )
    angles = position.astype(jnp.float32)[:, :, None, None] * inv_freq
    cosine = jnp.cos(angles)
    sines = jnp.sin(angles)
    front_half = values[..., :half_width]
    back_half = values[..., half_width:]
    return jnp.concatenate(
        [front_half * cosine - back_half * sines, back_half * cosine + front_half * sines], axis=-1
    )


def attend(queries, key_new, value_new, cache_key, cache_value, lengths):
    score_scale = 1.0 / math.sqrt(queries.shape[-1])
    cached = (
        jnp.einsum("rskgd,rlkd->rskgl", queries, cache_key, preferred_element_type=jnp.float32)
        * score_scale
    )
    fresh_scores = (
        jnp.einsum("rskgd,rtkd->rskgt", queries, key_new, preferred_element_type=jnp.float32)
        * score_scale
    )
    live_mask = jnp.arange(cache_key.shape[1], dtype=jnp.int32)[None, :] < lengths[:, None]
    cached = jnp.where(live_mask[:, None, None, None, :], cached, -1e30)
    steps_here = key_new.shape[1]
    causal = (
        jnp.arange(steps_here, dtype=jnp.int32)[:, None]
        >= jnp.arange(steps_here, dtype=jnp.int32)[None, :]
    )
    fresh_scores = jnp.where(causal[None, :, None, None, :], fresh_scores, -1e30)
    row_max = jnp.maximum(jnp.max(cached, axis=-1), jnp.max(fresh_scores, axis=-1))
    cache_exp = jnp.exp(cached - row_max[..., None])
    fresh_exp = jnp.exp(fresh_scores - row_max[..., None])
    weight_sum = jnp.sum(cache_exp, axis=-1) + jnp.sum(fresh_exp, axis=-1)
    cache_weights = (cache_exp / weight_sum[..., None]).astype(jnp.bfloat16)
    fresh_weights = (fresh_exp / weight_sum[..., None]).astype(jnp.bfloat16)
    combined = jnp.einsum(
        "rskgl,rlkd->rskgd", cache_weights, cache_value, preferred_element_type=jnp.float32
    )
    combined = combined + jnp.einsum(
        "rskgt,rtkd->rskgd", fresh_weights, value_new, preferred_element_type=jnp.float32
    )
    return combined.astype(jnp.bfloat16)


TORUS_ORDER = (
    (0, 1), (1, 0), (0, 3), (3, 0), (1, 1), (3, 3), (1, 3), (3, 1),
    (0, 2), (2, 0), (2, 1), (1, 2), (2, 3), (3, 2), (2, 2),
)


def peer_offsets(count):
    if count == 16:
        def shifted(me, dz, dy):
            return lax.rem(me // 4 + dz, 4) * 4 + lax.rem(lax.rem(me, 4) + dy, 4)

        return [
            (lambda me, a=dz, b=dy: shifted(me, a, b), lambda me, a=dz, b=dy: shifted(me, 4 - a, 4 - b))
            for dz, dy in TORUS_ORDER
        ]
    return [
        (lambda me, d=offset: lax.rem(me + d, count), lambda me, d=offset: lax.rem(me + count - d, count))
        for offset in range(1, count)
    ]


def exchange_kernel(axis, count, arrays, *refs):
    send_refs = refs[:arrays]
    got_refs = refs[arrays : 2 * arrays]
    send_sem, recv_sem, local_sem = refs[2 * arrays :]
    me = lax.axis_index(axis)
    barrier = pltpu.get_barrier_semaphore()
    offsets = peer_offsets(count)
    for offset in range(1, count):
        peer = offsets[offset - 1][0](me)
        pl.semaphore_signal(barrier, inc=1, device_id={axis: peer}, device_id_type=MESH)
    pl.semaphore_wait(barrier, count - 1)
    locals_ = []
    for which in range(arrays):
        local = pltpu.make_async_copy(
            send_refs[which].at[me], got_refs[which].at[me], local_sem.at[which]
        )
        local.start()
        locals_.append(local)
    outgoing = []
    for offset in range(1, count):
        peer = offsets[offset - 1][0](me)
        for which in range(arrays):
            copy = pltpu.make_async_remote_copy(
                src_ref=send_refs[which].at[peer],
                dst_ref=got_refs[which].at[me],
                send_sem=send_sem.at[which, offset],
                recv_sem=recv_sem.at[which, offset],
                device_id={axis: peer},
                device_id_type=MESH,
            )
            copy.start()
            outgoing.append(copy)
    for offset in range(1, count):
        source = offsets[offset - 1][1](me)
        for which in range(arrays):
            outgoing[(offset - 1) * arrays + which].wait_send()
            incoming = pltpu.make_async_remote_copy(
                src_ref=send_refs[which].at[source],
                dst_ref=got_refs[which].at[source],
                send_sem=send_sem.at[which, offset],
                recv_sem=recv_sem.at[which, offset],
                device_id={axis: source},
                device_id_type=MESH,
            )
            incoming.wait_recv()
    for local in locals_:
        local.wait()


def exchange(values, axis, count, collective):
    arrays = len(values)
    vmem = pl.BlockSpec(memory_space=pltpu.VMEM)
    return pl.pallas_call(
        lambda *refs: exchange_kernel(axis, count, arrays, *refs),
        out_shape=tuple(jax.ShapeDtypeStruct(v.shape, v.dtype) for v in values),
        in_specs=[vmem] * arrays,
        out_specs=tuple([vmem] * arrays),
        scratch_shapes=[
            pltpu.SemaphoreType.DMA((arrays, count)),
            pltpu.SemaphoreType.DMA((arrays, count)),
            pltpu.SemaphoreType.DMA((arrays,)),
        ],
        compiler_params=pltpu.CompilerParams(collective_id=collective, has_side_effects=True),
    )(*values)


def exchange_ring_kernel(axis, count, gather_axis, arrays, *refs):
    send_refs = refs[:arrays]
    piece_ref = refs[arrays]
    got_refs = refs[arrays + 1 : 2 * arrays + 1]
    chip_pieces = refs[2 * arrays + 1]
    send_sem, recv_sem, local_sem, near_send, near_recv, piece_sem = refs[2 * arrays + 2 :]
    chips = lax.axis_size(gather_axis) // 2
    me = lax.axis_index(axis)
    mine = lax.axis_index(gather_axis)
    chip = mine // 2
    core = lax.rem(mine, 2)
    right_chip = lax.rem(chip + 1, chips)
    left_chip = lax.rem(chip + chips - 1, chips)
    right = right_chip * 2 + core
    left = left_chip * 2 + core

    barrier = pltpu.get_barrier_semaphore()
    offsets = peer_offsets(count)
    for offset in range(1, count):
        peer = offsets[offset - 1][0](me)
        pl.semaphore_signal(barrier, inc=1, device_id={axis: peer}, device_id_type=MESH)
    pl.semaphore_signal(barrier, inc=1, device_id={gather_axis: right}, device_id_type=MESH)
    pl.semaphore_signal(barrier, inc=1, device_id={gather_axis: left}, device_id_type=MESH)
    pl.semaphore_wait(barrier, count + 1)

    near = []
    for side, target in ((0, right), (1, left)):
        copy = pltpu.make_async_remote_copy(
            src_ref=piece_ref,
            dst_ref=chip_pieces.at[1 + side],
            send_sem=near_send.at[side],
            recv_sem=near_recv.at[side],
            device_id={gather_axis: target},
            device_id_type=MESH,
        )
        copy.start()
        near.append(copy)
    own_piece = pltpu.make_async_copy(piece_ref, chip_pieces.at[0], piece_sem)
    own_piece.start()

    locals_ = []
    for which in range(arrays):
        local = pltpu.make_async_copy(
            send_refs[which].at[me], got_refs[which].at[me], local_sem.at[which]
        )
        local.start()
        locals_.append(local)
    outgoing = []
    for offset in range(1, count):
        peer = offsets[offset - 1][0](me)
        for which in range(arrays):
            copy = pltpu.make_async_remote_copy(
                src_ref=send_refs[which].at[peer],
                dst_ref=got_refs[which].at[me],
                send_sem=send_sem.at[which, offset],
                recv_sem=recv_sem.at[which, offset],
                device_id={axis: peer},
                device_id_type=MESH,
            )
            copy.start()
            outgoing.append(copy)

    for side, source in ((0, left), (1, right)):
        near[side].wait_send()
        incoming = pltpu.make_async_remote_copy(
            src_ref=piece_ref,
            dst_ref=chip_pieces.at[1 + side],
            send_sem=near_send.at[side],
            recv_sem=near_recv.at[side],
            device_id={gather_axis: source},
            device_id_type=MESH,
        )
        incoming.wait_recv()

    for offset in range(1, count):
        source = offsets[offset - 1][1](me)
        for which in range(arrays):
            outgoing[(offset - 1) * arrays + which].wait_send()
            incoming = pltpu.make_async_remote_copy(
                src_ref=send_refs[which].at[source],
                dst_ref=got_refs[which].at[source],
                send_sem=send_sem.at[which, offset],
                recv_sem=recv_sem.at[which, offset],
                device_id={axis: source},
                device_id_type=MESH,
            )
            incoming.wait_recv()
    for local in locals_:
        local.wait()
    own_piece.wait()


def exchange_ring(values, piece, axis, count, gather_axis, collective):
    arrays = len(values)
    vmem = pl.BlockSpec(memory_space=pltpu.VMEM)
    outs = pl.pallas_call(
        lambda *refs: exchange_ring_kernel(axis, count, gather_axis, arrays, *refs),
        out_shape=tuple(jax.ShapeDtypeStruct(v.shape, v.dtype) for v in values)
        + (jax.ShapeDtypeStruct((3,) + piece.shape, piece.dtype),),
        in_specs=[vmem] * (arrays + 1),
        out_specs=tuple([vmem] * (arrays + 1)),
        scratch_shapes=[
            pltpu.SemaphoreType.DMA((arrays, count)),
            pltpu.SemaphoreType.DMA((arrays, count)),
            pltpu.SemaphoreType.DMA((arrays,)),
            pltpu.SemaphoreType.DMA((2,)),
            pltpu.SemaphoreType.DMA((2,)),
            pltpu.SemaphoreType.DMA(()),
        ],
        compiler_params=pltpu.CompilerParams(collective_id=collective, has_side_effects=True),
    )(*values, piece)
    return outs[:arrays], outs[arrays]


def exchange_project_kernel(
    axis, count, gather_axis, send_ref, near_pieces, wq_hbm, wk_ref, wv_ref,
    place_ref, cos_ref, sin_ref,
    queries_ref, key_ref, value_ref,
    got_ref, q_ref, k_ref, v_ref,
    far_piece, partner_near, partner_far, wq_buf, send_sem, recv_sem, local_sem, wq_sem,
    far_send, far_recv, partner_send, partner_recv,
):
    me = lax.axis_index(axis)
    mine = lax.axis_index(gather_axis)
    chips = lax.axis_size(gather_axis) // 2
    chip = mine // 2
    core = lax.rem(mine, 2)
    partner = chip * 2 + (1 - core)
    right = lax.rem(chip + 1, chips) * 2 + core
    left = lax.rem(chip + chips - 1, chips) * 2 + core
    half = far_piece.shape[0] // 2
    barrier = pltpu.get_barrier_semaphore()
    offsets = peer_offsets(count)
    for offset in range(1, count):
        peer = offsets[offset - 1][0](me)
        pl.semaphore_signal(barrier, inc=1, device_id={axis: peer}, device_id_type=MESH)
    for neighbour in (partner, right, left):
        pl.semaphore_signal(barrier, inc=1, device_id={gather_axis: neighbour}, device_id_type=MESH)
    pl.semaphore_wait(barrier, count + 2)

    far_out = []
    for side, slot, target, rows in ((0, 1, right, pl.ds(0, half)), (1, 2, left, pl.ds(half, half))):
        copy = pltpu.make_async_remote_copy(
            src_ref=near_pieces.at[slot, rows],
            dst_ref=far_piece.at[rows],
            send_sem=far_send.at[side],
            recv_sem=far_recv.at[side],
            device_id={gather_axis: target},
            device_id_type=MESH,
        )
        copy.start()
        far_out.append(copy)
    to_partner = pltpu.make_async_remote_copy(
        src_ref=near_pieces,
        dst_ref=partner_near,
        send_sem=partner_send.at[0],
        recv_sem=partner_recv.at[0],
        device_id={gather_axis: partner},
        device_id_type=MESH,
    )
    to_partner.start()
    local = pltpu.make_async_copy(send_ref.at[me], got_ref.at[me], local_sem)
    local.start()
    outgoing = []
    for offset in range(1, count):
        peer = offsets[offset - 1][0](me)
        copy = pltpu.make_async_remote_copy(
            src_ref=send_ref.at[peer],
            dst_ref=got_ref.at[me],
            send_sem=send_sem.at[offset],
            recv_sem=recv_sem.at[offset],
            device_id={axis: peer},
            device_id_type=MESH,
        )
        copy.start()
        outgoing.append(copy)

    piece_width = near_pieces.shape[2]
    chip_shift = (0, chips - 1, 1, 2)

    def piece_index(step):
        piece_core = core if step < 4 else 1 - core
        return lax.rem(chip + chip_shift[step % 4], chips) * 2 + piece_core

    def chunk_copy(step):
        index = piece_index(step)
        return pltpu.make_async_copy(
            wq_hbm.at[pl.ds(pl.multiple_of(index * piece_width, piece_width), piece_width)],
            wq_buf.at[step % 2],
            wq_sem.at[step % 2],
        )

    chunk_copy(0).start()
    q_ref[...] = jnp.zeros_like(q_ref)
    k_ref[...] = jnp.zeros_like(k_ref)
    v_ref[...] = jnp.zeros_like(v_ref)

    def project(step, piece):
        chunk_copy(step).wait()
        if step + 1 < 8:
            chunk_copy(step + 1).start()
        index = piece_index(step)
        rows = pl.ds(pl.multiple_of(index * piece_width, piece_width), piece_width)
        q_ref[...] += jnp.dot(piece, wq_buf[step % 2], preferred_element_type=jnp.float32)
        k_ref[...] += jnp.dot(piece, wk_ref[rows, :], preferred_element_type=jnp.float32)
        v_ref[...] += jnp.dot(piece, wv_ref[rows, :], preferred_element_type=jnp.float32)

    for step in range(3):
        project(step, near_pieces[step])
    for side, source, rows in ((0, left, pl.ds(0, half)), (1, right, pl.ds(half, half))):
        far_out[side].wait_send()
        incoming = pltpu.make_async_remote_copy(
            src_ref=near_pieces.at[1, rows],
            dst_ref=far_piece.at[rows],
            send_sem=far_send.at[side],
            recv_sem=far_recv.at[side],
            device_id={gather_axis: source},
            device_id_type=MESH,
        )
        incoming.wait_recv()
    far_to_partner = pltpu.make_async_remote_copy(
        src_ref=far_piece,
        dst_ref=partner_far,
        send_sem=partner_send.at[1],
        recv_sem=partner_recv.at[1],
        device_id={gather_axis: partner},
        device_id_type=MESH,
    )
    far_to_partner.start()
    project(3, far_piece[...])
    to_partner.wait_send()
    to_partner.wait_recv()
    for step in range(3):
        project(4 + step, partner_near[step])
    far_to_partner.wait_send()
    far_to_partner.wait_recv()
    project(7, partner_far[...])

    for offset in range(1, count):
        outgoing[offset - 1].wait_send()
        source = offsets[offset - 1][1](me)
        incoming = pltpu.make_async_remote_copy(
            src_ref=send_ref.at[source],
            dst_ref=got_ref.at[source],
            send_sem=send_sem.at[offset],
            recv_sem=recv_sem.at[offset],
            device_id={axis: source},
            device_id_type=MESH,
        )
        incoming.wait_recv()
    local.wait()

    slots, slot_rows, width = got_ref.shape
    adapter_rows = jnp.dot(
        place_ref[...], got_ref[...].reshape(slots * slot_rows, width),
        preferred_element_type=jnp.float32,
    )
    cosine = cos_ref[...]
    sines = sin_ref[...]
    half_turn = HD // 2

    def rotated(values):
        return values * cosine + pltpu.roll(values, half_turn, 1) * sines

    for head in range(width // HD):
        lanes = slice(head * HD, (head + 1) * HD)
        summed = q_ref[:, lanes] + adapter_rows[:, lanes]
        queries_ref[:, lanes] = rotated(summed).astype(queries_ref.dtype)
    for head in range(key_ref.shape[1] // HD):
        lanes = slice(head * HD, (head + 1) * HD)
        key_ref[:, lanes] = rotated(k_ref[:, lanes]).astype(key_ref.dtype)
    value_ref[...] = v_ref[...].astype(value_ref.dtype)


def exchange_project(values, near_pieces, w_query, w_key, w_value, place_t, cosine, sines,
                     axis, count, gather_axis, collective):
    unused_item, token_count, piece_width = near_pieces.shape
    vmem = pl.BlockSpec(memory_space=pltpu.VMEM)
    return pl.pallas_call(
        lambda *refs: exchange_project_kernel(axis, count, gather_axis, *refs),
        out_shape=(
            jax.ShapeDtypeStruct((token_count, w_query.shape[1]), jnp.bfloat16),
            jax.ShapeDtypeStruct((token_count, w_key.shape[1]), jnp.bfloat16),
            jax.ShapeDtypeStruct((token_count, w_value.shape[1]), jnp.bfloat16),
        ),
        in_specs=[vmem, vmem, pl.BlockSpec(memory_space=pl.ANY), vmem, vmem, vmem, vmem, vmem],
        out_specs=(vmem, vmem, vmem),
        scratch_shapes=[
            pltpu.VMEM(values.shape, values.dtype),
            pltpu.VMEM((token_count, w_query.shape[1]), jnp.float32),
            pltpu.VMEM((token_count, w_key.shape[1]), jnp.float32),
            pltpu.VMEM((token_count, w_value.shape[1]), jnp.float32),
            pltpu.VMEM((token_count, piece_width), near_pieces.dtype),
            pltpu.VMEM(near_pieces.shape, near_pieces.dtype),
            pltpu.VMEM((token_count, piece_width), near_pieces.dtype),
            pltpu.VMEM((2, piece_width, w_query.shape[1]), w_query.dtype),
            pltpu.SemaphoreType.DMA((count,)),
            pltpu.SemaphoreType.DMA((count,)),
            pltpu.SemaphoreType.DMA(()),
            pltpu.SemaphoreType.DMA((2,)),
            pltpu.SemaphoreType.DMA((2,)),
            pltpu.SemaphoreType.DMA((2,)),
            pltpu.SemaphoreType.DMA((2,)),
            pltpu.SemaphoreType.DMA((2,)),
        ],
        compiler_params=pltpu.CompilerParams(
            collective_id=collective, has_side_effects=True, vmem_limit_bytes=60 * 1024 * 1024
        ),
    )(values, near_pieces, w_query, w_key, w_value, place_t, cosine, sines)


def sum_kernel(axis, count, part_ref, total_ref, held, first_send, first_recv, second_send, second_recv):
    me = lax.axis_index(axis)
    barrier = pltpu.get_barrier_semaphore()
    for offset in range(1, count):
        peer = lax.rem(me + offset, count)
        pl.semaphore_signal(barrier, inc=1, device_id={axis: peer}, device_id_type=MESH)
    pl.semaphore_wait(barrier, count - 1)
    outgoing = []
    for offset in range(1, count):
        peer = lax.rem(me + offset, count)
        copy = pltpu.make_async_remote_copy(
            src_ref=part_ref.at[peer],
            dst_ref=held.at[me],
            send_sem=first_send.at[offset],
            recv_sem=first_recv.at[offset],
            device_id={axis: peer},
            device_id_type=MESH,
        )
        copy.start()
        outgoing.append(copy)
    held[me] = part_ref[me]
    for offset in range(1, count):
        outgoing[offset - 1].wait_send()
        source = lax.rem(me + count - offset, count)
        incoming = pltpu.make_async_remote_copy(
            src_ref=part_ref.at[source],
            dst_ref=held.at[source],
            send_sem=first_send.at[offset],
            recv_sem=first_recv.at[offset],
            device_id={axis: source},
            device_id_type=MESH,
        )
        incoming.wait_recv()
    total = held[0]
    for index in range(1, count):
        total = total + held[index]
    total_ref[me] = total.astype(total_ref.dtype)
    outgoing = []
    for offset in range(1, count):
        peer = lax.rem(me + offset, count)
        copy = pltpu.make_async_remote_copy(
            src_ref=total_ref.at[me],
            dst_ref=total_ref.at[me],
            send_sem=second_send.at[offset],
            recv_sem=second_recv.at[offset],
            device_id={axis: peer},
            device_id_type=MESH,
        )
        copy.start()
        outgoing.append(copy)
    for offset in range(1, count):
        outgoing[offset - 1].wait_send()
        source = lax.rem(me + count - offset, count)
        incoming = pltpu.make_async_remote_copy(
            src_ref=total_ref.at[source],
            dst_ref=total_ref.at[source],
            send_sem=second_send.at[offset],
            recv_sem=second_recv.at[offset],
            device_id={axis: source},
            device_id_type=MESH,
        )
        incoming.wait_recv()


def axis_sum(values, axis, count, collective, out_dtype):
    chunks = values.reshape(count, -1, 128)
    summed = pl.pallas_call(
        lambda *refs: sum_kernel(axis, count, *refs),
        out_shape=jax.ShapeDtypeStruct(chunks.shape, out_dtype),
        in_specs=[pl.BlockSpec(memory_space=pltpu.VMEM)],
        out_specs=pl.BlockSpec(memory_space=pltpu.VMEM),
        scratch_shapes=[
            pltpu.VMEM(chunks.shape, values.dtype),
            pltpu.SemaphoreType.DMA((count,)),
            pltpu.SemaphoreType.DMA((count,)),
            pltpu.SemaphoreType.DMA((count,)),
            pltpu.SemaphoreType.DMA((count,)),
        ],
        compiler_params=pltpu.CompilerParams(collective_id=collective, has_side_effects=True),
    )(chunks)
    return summed.reshape(values.shape)


def owner_adapter_term(received, slot_ids, down_local, up_local):
    sources, rows, part_width = received.shape
    local_adapters, unused_item, adapter_rank = down_local.shape
    query_width = up_local.shape[2]
    token_rows = received.reshape(sources * rows, part_width)
    every_down = jnp.einsum(
        "td,adr->tar", token_rows, down_local, preferred_element_type=jnp.float32
    )
    pick = slot_ids.reshape(sources * rows)[:, None] == jnp.arange(local_adapters, dtype=jnp.int32)[None, :]
    partial_value_sum = jnp.sum(jnp.where(pick[:, :, None], every_down, 0.0), axis=1)
    tp_count = lax.axis_size("tp")
    summed = axis_sum(partial_value_sum.reshape(-1, 128), "tp", tp_count, 2, jnp.bfloat16)
    adapter_middle = summed.reshape(sources * rows, adapter_rank)
    spread_rows = jnp.where(pick[:, :, None], adapter_middle[:, None, :], jnp.zeros((), jnp.bfloat16))
    spread_rows = spread_rows.reshape(sources * rows, local_adapters * adapter_rank)
    adapter_output = jnp.dot(
        spread_rows,
        up_local.reshape(local_adapters * adapter_rank, query_width),
        preferred_element_type=jnp.float32,
    ).astype(jnp.bfloat16)
    return adapter_output.reshape(sources, rows, query_width)


def body(
    tokens,
    adapter_id,
    pool_slot,
    lengths,
    w_query,
    w_key,
    w_value,
    pooled_down_weights,
    pool_up,
    cache_key,
    cache_value,
):
    group_count = lax.axis_size("grp")
    tp_count = lax.axis_size("tp")
    row_count, step_count, part_width = tokens.shape
    local_adapter_rows, unused_item, adapter_rank = pooled_down_weights.shape
    query_width = w_query.shape[1]
    kv_width = w_key.shape[1]
    kv_local = kv_width // HD
    q_local = query_width // HD
    group_size = q_local // kv_local
    count_of_tokens = row_count * step_count
    adapter_span = jnp.arange(pool_slot.shape[0], dtype=jnp.int32)
    pool_pos = jnp.sum(
        jnp.where(adapter_id[:, None] == adapter_span[None, :], pool_slot[None, :], 0), axis=1
    )
    owner_grp = pool_pos // local_adapter_rows
    local_slot = pool_pos % local_adapter_rows
    row_span = jnp.arange(row_count, dtype=jnp.int32)
    same_owner = (owner_grp[:, None] == owner_grp[None, :]) & (row_span[None, :] < row_span[:, None])
    owner_rank = jnp.sum(same_owner.astype(jnp.int32), axis=1)
    send_slot = owner_grp * CAP + owner_rank
    slot_span = jnp.arange(group_count * CAP, dtype=jnp.int32)
    place = (slot_span[:, None] == send_slot[None, :]).astype(jnp.bfloat16)
    token_slot = (send_slot[:, None] * step_count + jnp.arange(step_count, dtype=jnp.int32)[None, :]).reshape(-1)
    token_span = jnp.arange(group_count * CAP * step_count, dtype=jnp.int32)
    place_tokens = (token_span[:, None] == token_slot[None, :]).astype(jnp.bfloat16)
    token_rows = tokens.reshape(count_of_tokens, part_width)
    send_tokens = jnp.dot(place_tokens, token_rows, preferred_element_type=jnp.float32).astype(jnp.bfloat16)
    send_tokens = send_tokens.reshape(group_count, CAP * step_count, part_width)
    send_ids = jnp.dot(
        place, local_slot.astype(jnp.bfloat16)[:, None], preferred_element_type=jnp.float32
    ).astype(jnp.bfloat16)
    send_ids = jnp.broadcast_to(send_ids.reshape(group_count, CAP, 1), (group_count, CAP, 128))
    send_ids = jnp.concatenate([send_ids, jnp.zeros_like(send_ids)], axis=1)
    (got_tokens, got_ids), chip_pieces = exchange_ring(
        (send_tokens, send_ids), token_rows, "grp", group_count, "tp", 0
    )
    got_ids = jnp.repeat(got_ids[:, :CAP, 0].astype(jnp.int32), step_count, axis=1)
    owner_out = owner_adapter_term(got_tokens, got_ids, pooled_down_weights, pool_up)
    position = lengths[:, None] + jnp.arange(step_count, dtype=jnp.int32)[None, :]
    half_width = HD // 2
    inv_freq = jnp.exp(
        jnp.arange(half_width, dtype=jnp.float32) * (-2.0 * math.log(rope_base) / HD)
    )
    angles = position.reshape(count_of_tokens).astype(jnp.float32)[:, None] * inv_freq
    cosine = jnp.concatenate([jnp.cos(angles), jnp.cos(angles)], axis=1)
    sines = jnp.concatenate([-jnp.sin(angles), jnp.sin(angles)], axis=1)
    queries, key_new, value_new = exchange_project(
        owner_out, chip_pieces, w_query, w_key, w_value, jnp.transpose(place_tokens), cosine, sines,
        "grp", group_count, "tp", 1
    )
    queries = queries.reshape(row_count, step_count, kv_local, group_size, HD)
    key_new = key_new.reshape(row_count, step_count, kv_local, HD)
    value_new = value_new.reshape(row_count, step_count, kv_local, HD)
    cache_keys = cache_key.reshape(row_count, cache_key.shape[1], kv_local, HD)
    cache_values = cache_value.reshape(row_count, cache_value.shape[1], kv_local, HD)
    combined = attend(queries, key_new, value_new, cache_keys, cache_values, lengths)
    return combined.reshape(row_count, step_count, query_width)


def solution(mesh):
    in_specs = (
        P("grp", None, "tp"),
        P("grp"),
        P(),
        P("grp"),
        P(None, "tp"),
        P(None, "tp"),
        P(None, "tp"),
        P("grp", "tp", None),
        P("grp", None, "tp"),
        P("grp", None, "tp"),
        P("grp", None, "tp"),
    )
    out_specs = P("grp", None, "tp")
    return jax.shard_map(body, mesh=mesh, in_specs=in_specs, out_specs=out_specs, check_vma=False)
```

```python
import math

import jax
import jax.numpy as jnp
from jax import lax
from jax.experimental import pallas as pl
from jax.experimental.pallas import tpu as pltpu
from jax.sharding import PartitionSpec as P

MESH = pl.DeviceIdType.MESH

HD = 128
CAP = 8


rope_base = 500000.0


def rotate(values, position):
    half_width = values.shape[-1] // 2
    inv_freq = jnp.exp(
        jnp.arange(half_width, dtype=jnp.float32) * (-2.0 * math.log(rope_base) / values.shape[-1])
    )
    angles = position.astype(jnp.float32)[:, :, None, None] * inv_freq
    cosine = jnp.cos(angles)
    sines = jnp.sin(angles)
    front_half = values[..., :half_width]
    back_half = values[..., half_width:]
    return jnp.concatenate(
        [front_half * cosine - back_half * sines, back_half * cosine + front_half * sines], axis=-1
    )


def attend(queries, key_new, value_new, cache_key, cache_value, lengths):
    score_scale = 1.0 / math.sqrt(queries.shape[-1])
    cached = (
        jnp.einsum("rskgd,rlkd->rskgl", queries, cache_key, preferred_element_type=jnp.float32)
        * score_scale
    )
    fresh_scores = (
        jnp.einsum("rskgd,rtkd->rskgt", queries, key_new, preferred_element_type=jnp.float32)
        * score_scale
    )
    live_mask = jnp.arange(cache_key.shape[1], dtype=jnp.int32)[None, :] < lengths[:, None]
    cached = jnp.where(live_mask[:, None, None, None, :], cached, -1e30)
    steps_here = key_new.shape[1]
    causal = (
        jnp.arange(steps_here, dtype=jnp.int32)[:, None]
        >= jnp.arange(steps_here, dtype=jnp.int32)[None, :]
    )
    fresh_scores = jnp.where(causal[None, :, None, None, :], fresh_scores, -1e30)
    row_max = jnp.maximum(jnp.max(cached, axis=-1), jnp.max(fresh_scores, axis=-1))
    cache_exp = jnp.exp(cached - row_max[..., None])
    fresh_exp = jnp.exp(fresh_scores - row_max[..., None])
    weight_sum = jnp.sum(cache_exp, axis=-1) + jnp.sum(fresh_exp, axis=-1)
    cache_weights = (cache_exp / weight_sum[..., None]).astype(jnp.bfloat16)
    fresh_weights = (fresh_exp / weight_sum[..., None]).astype(jnp.bfloat16)
    combined = jnp.einsum(
        "rskgl,rlkd->rskgd", cache_weights, cache_value, preferred_element_type=jnp.float32
    )
    combined = combined + jnp.einsum(
        "rskgt,rtkd->rskgd", fresh_weights, value_new, preferred_element_type=jnp.float32
    )
    return combined.astype(jnp.bfloat16)


TORUS_ORDER = (
    (0, 1), (1, 0), (0, 3), (3, 0), (1, 1), (3, 3), (1, 3), (3, 1),
    (0, 2), (2, 0), (2, 1), (1, 2), (2, 3), (3, 2), (2, 2),
)


def peer_offsets(count):
    if count == 16:
        def shifted(me, dz, dy):
            return lax.rem(me // 4 + dz, 4) * 4 + lax.rem(lax.rem(me, 4) + dy, 4)

        return [
            (lambda me, a=dz, b=dy: shifted(me, a, b), lambda me, a=dz, b=dy: shifted(me, 4 - a, 4 - b))
            for dz, dy in TORUS_ORDER
        ]
    return [
        (lambda me, d=offset: lax.rem(me + d, count), lambda me, d=offset: lax.rem(me + count - d, count))
        for offset in range(1, count)
    ]


def exchange_kernel(axis, count, arrays, *refs):
    send_refs = refs[:arrays]
    got_refs = refs[arrays : 2 * arrays]
    send_sem, recv_sem, local_sem = refs[2 * arrays :]
    me = lax.axis_index(axis)
    barrier = pltpu.get_barrier_semaphore()
    offsets = peer_offsets(count)
    for offset in range(1, count):
        peer = offsets[offset - 1][0](me)
        pl.semaphore_signal(barrier, inc=1, device_id={axis: peer}, device_id_type=MESH)
    pl.semaphore_wait(barrier, count - 1)
    locals_ = []
    for which in range(arrays):
        local = pltpu.make_async_copy(
            send_refs[which].at[me], got_refs[which].at[me], local_sem.at[which]
        )
        local.start()
        locals_.append(local)
    outgoing = []
    for offset in range(1, count):
        peer = offsets[offset - 1][0](me)
        for which in range(arrays):
            copy = pltpu.make_async_remote_copy(
                src_ref=send_refs[which].at[peer],
                dst_ref=got_refs[which].at[me],
                send_sem=send_sem.at[which, offset],
                recv_sem=recv_sem.at[which, offset],
                device_id={axis: peer},
                device_id_type=MESH,
            )
            copy.start()
            outgoing.append(copy)
    for offset in range(1, count):
        source = offsets[offset - 1][1](me)
        for which in range(arrays):
            outgoing[(offset - 1) * arrays + which].wait_send()
            incoming = pltpu.make_async_remote_copy(
                src_ref=send_refs[which].at[source],
                dst_ref=got_refs[which].at[source],
                send_sem=send_sem.at[which, offset],
                recv_sem=recv_sem.at[which, offset],
                device_id={axis: source},
                device_id_type=MESH,
            )
            incoming.wait_recv()
    for local in locals_:
        local.wait()


def exchange(values, axis, count, collective):
    arrays = len(values)
    vmem = pl.BlockSpec(memory_space=pltpu.VMEM)
    return pl.pallas_call(
        lambda *refs: exchange_kernel(axis, count, arrays, *refs),
        out_shape=tuple(jax.ShapeDtypeStruct(v.shape, v.dtype) for v in values),
        in_specs=[vmem] * arrays,
        out_specs=tuple([vmem] * arrays),
        scratch_shapes=[
            pltpu.SemaphoreType.DMA((arrays, count)),
            pltpu.SemaphoreType.DMA((arrays, count)),
            pltpu.SemaphoreType.DMA((arrays,)),
        ],
        compiler_params=pltpu.CompilerParams(collective_id=collective, has_side_effects=True),
    )(*values)


def exchange_ring_kernel(axis, count, gather_axis, arrays, *refs):
    send_refs = refs[:arrays]
    piece_ref = refs[arrays]
    got_refs = refs[arrays + 1 : 2 * arrays + 1]
    chip_pieces = refs[2 * arrays + 1]
    send_sem, recv_sem, local_sem, near_send, near_recv, piece_sem = refs[2 * arrays + 2 :]
    chips = lax.axis_size(gather_axis) // 2
    me = lax.axis_index(axis)
    mine = lax.axis_index(gather_axis)
    chip = mine // 2
    core = lax.rem(mine, 2)
    right_chip = lax.rem(chip + 1, chips)
    left_chip = lax.rem(chip + chips - 1, chips)
    right = right_chip * 2 + core
    left = left_chip * 2 + core

    barrier = pltpu.get_barrier_semaphore()
    offsets = peer_offsets(count)
    for offset in range(1, count):
        peer = offsets[offset - 1][0](me)
        pl.semaphore_signal(barrier, inc=1, device_id={axis: peer}, device_id_type=MESH)
    pl.semaphore_signal(barrier, inc=1, device_id={gather_axis: right}, device_id_type=MESH)
    pl.semaphore_signal(barrier, inc=1, device_id={gather_axis: left}, device_id_type=MESH)
    pl.semaphore_wait(barrier, count + 1)

    near = []
    for side, target in ((0, right), (1, left)):
        copy = pltpu.make_async_remote_copy(
            src_ref=piece_ref,
            dst_ref=chip_pieces.at[1 + side],
            send_sem=near_send.at[side],
            recv_sem=near_recv.at[side],
            device_id={gather_axis: target},
            device_id_type=MESH,
        )
        copy.start()
        near.append(copy)
    own_piece = pltpu.make_async_copy(piece_ref, chip_pieces.at[0], piece_sem)
    own_piece.start()

    locals_ = []
    for which in range(arrays):
        local = pltpu.make_async_copy(
            send_refs[which].at[me], got_refs[which].at[me], local_sem.at[which]
        )
        local.start()
        locals_.append(local)
    outgoing = []
    for offset in range(1, count):
        peer = offsets[offset - 1][0](me)
        for which in range(arrays):
            copy = pltpu.make_async_remote_copy(
                src_ref=send_refs[which].at[peer],
                dst_ref=got_refs[which].at[me],
                send_sem=send_sem.at[which, offset],
                recv_sem=recv_sem.at[which, offset],
                device_id={axis: peer},
                device_id_type=MESH,
            )
            copy.start()
            outgoing.append(copy)

    for side, source in ((0, left), (1, right)):
        near[side].wait_send()
        incoming = pltpu.make_async_remote_copy(
            src_ref=piece_ref,
            dst_ref=chip_pieces.at[1 + side],
            send_sem=near_send.at[side],
            recv_sem=near_recv.at[side],
            device_id={gather_axis: source},
            device_id_type=MESH,
        )
        incoming.wait_recv()

    for offset in range(1, count):
        source = offsets[offset - 1][1](me)
        for which in range(arrays):
            outgoing[(offset - 1) * arrays + which].wait_send()
            incoming = pltpu.make_async_remote_copy(
                src_ref=send_refs[which].at[source],
                dst_ref=got_refs[which].at[source],
                send_sem=send_sem.at[which, offset],
                recv_sem=recv_sem.at[which, offset],
                device_id={axis: source},
                device_id_type=MESH,
            )
            incoming.wait_recv()
    for local in locals_:
        local.wait()
    own_piece.wait()


def exchange_ring(values, piece, axis, count, gather_axis, collective):
    arrays = len(values)
    vmem = pl.BlockSpec(memory_space=pltpu.VMEM)
    outs = pl.pallas_call(
        lambda *refs: exchange_ring_kernel(axis, count, gather_axis, arrays, *refs),
        out_shape=tuple(jax.ShapeDtypeStruct(v.shape, v.dtype) for v in values)
        + (jax.ShapeDtypeStruct((3,) + piece.shape, piece.dtype),),
        in_specs=[vmem] * (arrays + 1),
        out_specs=tuple([vmem] * (arrays + 1)),
        scratch_shapes=[
            pltpu.SemaphoreType.DMA((arrays, count)),
            pltpu.SemaphoreType.DMA((arrays, count)),
            pltpu.SemaphoreType.DMA((arrays,)),
            pltpu.SemaphoreType.DMA((2,)),
            pltpu.SemaphoreType.DMA((2,)),
            pltpu.SemaphoreType.DMA(()),
        ],
        compiler_params=pltpu.CompilerParams(collective_id=collective, has_side_effects=True),
    )(*values, piece)
    return outs[:arrays], outs[arrays]


def exchange_project_kernel(
    axis, count, gather_axis, send_ref, near_pieces, wq_hbm, wk_ref, wv_ref,
    place_ref, cos_ref, sin_ref,
    queries_ref, key_ref, value_ref,
    got_ref, q_ref, k_ref, v_ref,
    far_piece, partner_near, partner_far, wq_buf, send_sem, recv_sem, local_sem, wq_sem,
    far_send, far_recv, partner_send, partner_recv,
):
    me = lax.axis_index(axis)
    mine = lax.axis_index(gather_axis)
    chips = lax.axis_size(gather_axis) // 2
    chip = mine // 2
    core = lax.rem(mine, 2)
    partner = chip * 2 + (1 - core)
    right = lax.rem(chip + 1, chips) * 2 + core
    left = lax.rem(chip + chips - 1, chips) * 2 + core
    half = far_piece.shape[0] // 2
    barrier = pltpu.get_barrier_semaphore()
    offsets = peer_offsets(count)
    for offset in range(1, count):
        peer = offsets[offset - 1][0](me)
        pl.semaphore_signal(barrier, inc=1, device_id={axis: peer}, device_id_type=MESH)
    for neighbour in (partner, right, left):
        pl.semaphore_signal(barrier, inc=1, device_id={gather_axis: neighbour}, device_id_type=MESH)
    pl.semaphore_wait(barrier, count + 2)

    far_out = []
    for side, slot, target, rows in ((0, 1, right, pl.ds(0, half)), (1, 2, left, pl.ds(half, half))):
        copy = pltpu.make_async_remote_copy(
            src_ref=near_pieces.at[slot, rows],
            dst_ref=far_piece.at[rows],
            send_sem=far_send.at[side],
            recv_sem=far_recv.at[side],
            device_id={gather_axis: target},
            device_id_type=MESH,
        )
        copy.start()
        far_out.append(copy)
    to_partner = pltpu.make_async_remote_copy(
        src_ref=near_pieces,
        dst_ref=partner_near,
        send_sem=partner_send.at[0],
        recv_sem=partner_recv.at[0],
        device_id={gather_axis: partner},
        device_id_type=MESH,
    )
    to_partner.start()
    local = pltpu.make_async_copy(send_ref.at[me], got_ref.at[me], local_sem)
    local.start()
    outgoing = []
    for offset in range(1, count):
        peer = offsets[offset - 1][0](me)
        copy = pltpu.make_async_remote_copy(
            src_ref=send_ref.at[peer],
            dst_ref=got_ref.at[me],
            send_sem=send_sem.at[offset],
            recv_sem=recv_sem.at[offset],
            device_id={axis: peer},
            device_id_type=MESH,
        )
        copy.start()
        outgoing.append(copy)

    piece_width = near_pieces.shape[2]
    chip_shift = (0, chips - 1, 1, 2)

    def piece_index(step):
        piece_core = core if step < 4 else 1 - core
        return lax.rem(chip + chip_shift[step % 4], chips) * 2 + piece_core

    def chunk_copy(step):
        index = piece_index(step)
        return pltpu.make_async_copy(
            wq_hbm.at[pl.ds(pl.multiple_of(index * piece_width, piece_width), piece_width)],
            wq_buf.at[step % 2],
            wq_sem.at[step % 2],
        )

    chunk_copy(0).start()
    q_ref[...] = jnp.zeros_like(q_ref)
    k_ref[...] = jnp.zeros_like(k_ref)
    v_ref[...] = jnp.zeros_like(v_ref)

    def project(step, piece):
        chunk_copy(step).wait()
        if step + 1 < 8:
            chunk_copy(step + 1).start()
        index = piece_index(step)
        rows = pl.ds(pl.multiple_of(index * piece_width, piece_width), piece_width)
        q_ref[...] += jnp.dot(piece, wq_buf[step % 2], preferred_element_type=jnp.float32)
        k_ref[...] += jnp.dot(piece, wk_ref[rows, :], preferred_element_type=jnp.float32)
        v_ref[...] += jnp.dot(piece, wv_ref[rows, :], preferred_element_type=jnp.float32)

    for step in range(3):
        project(step, near_pieces[step])
    for side, source, rows in ((0, left, pl.ds(0, half)), (1, right, pl.ds(half, half))):
        far_out[side].wait_send()
        incoming = pltpu.make_async_remote_copy(
            src_ref=near_pieces.at[1, rows],
            dst_ref=far_piece.at[rows],
            send_sem=far_send.at[side],
            recv_sem=far_recv.at[side],
            device_id={gather_axis: source},
            device_id_type=MESH,
        )
        incoming.wait_recv()
    far_to_partner = pltpu.make_async_remote_copy(
        src_ref=far_piece,
        dst_ref=partner_far,
        send_sem=partner_send.at[1],
        recv_sem=partner_recv.at[1],
        device_id={gather_axis: partner},
        device_id_type=MESH,
    )
    far_to_partner.start()
    project(3, far_piece[...])
    to_partner.wait_send()
    to_partner.wait_recv()
    for step in range(3):
        project(4 + step, partner_near[step])
    far_to_partner.wait_send()
    far_to_partner.wait_recv()
    project(7, partner_far[...])

    for offset in range(1, count):
        outgoing[offset - 1].wait_send()
        source = offsets[offset - 1][1](me)
        incoming = pltpu.make_async_remote_copy(
            src_ref=send_ref.at[source],
            dst_ref=got_ref.at[source],
            send_sem=send_sem.at[offset],
            recv_sem=recv_sem.at[offset],
            device_id={axis: source},
            device_id_type=MESH,
        )
        incoming.wait_recv()
    local.wait()

    slots, slot_rows, width = got_ref.shape
    adapter_rows = jnp.dot(
        place_ref[...], got_ref[...].reshape(slots * slot_rows, width),
        preferred_element_type=jnp.float32,
    )
    cosine = cos_ref[...]
    sines = sin_ref[...]
    half_turn = HD // 2

    def rotated(values):
        return values * cosine + pltpu.roll(values, half_turn, 1) * sines

    for head in range(width // HD):
        lanes = slice(head * HD, (head + 1) * HD)
        summed = q_ref[:, lanes] + adapter_rows[:, lanes]
        queries_ref[:, lanes] = rotated(summed).astype(queries_ref.dtype)
    for head in range(key_ref.shape[1] // HD):
        lanes = slice(head * HD, (head + 1) * HD)
        key_ref[:, lanes] = rotated(k_ref[:, lanes]).astype(key_ref.dtype)
    value_ref[...] = v_ref[...].astype(value_ref.dtype)


def exchange_project(values, near_pieces, w_query, w_key, w_value, place_t, cosine, sines,
                     axis, count, gather_axis, collective):
    unused_item, token_count, piece_width = near_pieces.shape
    vmem = pl.BlockSpec(memory_space=pltpu.VMEM)
    return pl.pallas_call(
        lambda *refs: exchange_project_kernel(axis, count, gather_axis, *refs),
        out_shape=(
            jax.ShapeDtypeStruct((token_count, w_query.shape[1]), jnp.bfloat16),
            jax.ShapeDtypeStruct((token_count, w_key.shape[1]), jnp.bfloat16),
            jax.ShapeDtypeStruct((token_count, w_value.shape[1]), jnp.bfloat16),
        ),
        in_specs=[vmem, vmem, pl.BlockSpec(memory_space=pl.ANY), vmem, vmem, vmem, vmem, vmem],
        out_specs=(vmem, vmem, vmem),
        scratch_shapes=[
            pltpu.VMEM(values.shape, values.dtype),
            pltpu.VMEM((token_count, w_query.shape[1]), jnp.float32),
            pltpu.VMEM((token_count, w_key.shape[1]), jnp.float32),
            pltpu.VMEM((token_count, w_value.shape[1]), jnp.float32),
            pltpu.VMEM((token_count, piece_width), near_pieces.dtype),
            pltpu.VMEM(near_pieces.shape, near_pieces.dtype),
            pltpu.VMEM((token_count, piece_width), near_pieces.dtype),
            pltpu.VMEM((2, piece_width, w_query.shape[1]), w_query.dtype),
            pltpu.SemaphoreType.DMA((count,)),
            pltpu.SemaphoreType.DMA((count,)),
            pltpu.SemaphoreType.DMA(()),
            pltpu.SemaphoreType.DMA((2,)),
            pltpu.SemaphoreType.DMA((2,)),
            pltpu.SemaphoreType.DMA((2,)),
            pltpu.SemaphoreType.DMA((2,)),
            pltpu.SemaphoreType.DMA((2,)),
        ],
        compiler_params=pltpu.CompilerParams(
            collective_id=collective, has_side_effects=True, vmem_limit_bytes=60 * 1024 * 1024
        ),
    )(values, near_pieces, w_query, w_key, w_value, place_t, cosine, sines)


def sum_kernel(axis, count, part_ref, total_ref, held, first_send, first_recv, second_send, second_recv):
    me = lax.axis_index(axis)
    barrier = pltpu.get_barrier_semaphore()
    for offset in range(1, count):
        peer = lax.rem(me + offset, count)
        pl.semaphore_signal(barrier, inc=1, device_id={axis: peer}, device_id_type=MESH)
    pl.semaphore_wait(barrier, count - 1)
    outgoing = []
    for offset in range(1, count):
        peer = lax.rem(me + offset, count)
        copy = pltpu.make_async_remote_copy(
            src_ref=part_ref.at[peer],
            dst_ref=held.at[me],
            send_sem=first_send.at[offset],
            recv_sem=first_recv.at[offset],
            device_id={axis: peer},
            device_id_type=MESH,
        )
        copy.start()
        outgoing.append(copy)
    held[me] = part_ref[me]
    for offset in range(1, count):
        outgoing[offset - 1].wait_send()
        source = lax.rem(me + count - offset, count)
        incoming = pltpu.make_async_remote_copy(
            src_ref=part_ref.at[source],
            dst_ref=held.at[source],
            send_sem=first_send.at[offset],
            recv_sem=first_recv.at[offset],
            device_id={axis: source},
            device_id_type=MESH,
        )
        incoming.wait_recv()
    total = held[0]
    for index in range(1, count):
        total = total + held[index]
    total_ref[me] = total.astype(total_ref.dtype)
    outgoing = []
    for offset in range(1, count):
        peer = lax.rem(me + offset, count)
        copy = pltpu.make_async_remote_copy(
            src_ref=total_ref.at[me],
            dst_ref=total_ref.at[me],
            send_sem=second_send.at[offset],
            recv_sem=second_recv.at[offset],
            device_id={axis: peer},
            device_id_type=MESH,
        )
        copy.start()
        outgoing.append(copy)
    for offset in range(1, count):
        outgoing[offset - 1].wait_send()
        source = lax.rem(me + count - offset, count)
        incoming = pltpu.make_async_remote_copy(
            src_ref=total_ref.at[source],
            dst_ref=total_ref.at[source],
            send_sem=second_send.at[offset],
            recv_sem=second_recv.at[offset],
            device_id={axis: source},
            device_id_type=MESH,
        )
        incoming.wait_recv()


def axis_sum(values, axis, count, collective, out_dtype):
    chunks = values.reshape(count, -1, 128)
    summed = pl.pallas_call(
        lambda *refs: sum_kernel(axis, count, *refs),
        out_shape=jax.ShapeDtypeStruct(chunks.shape, out_dtype),
        in_specs=[pl.BlockSpec(memory_space=pltpu.VMEM)],
        out_specs=pl.BlockSpec(memory_space=pltpu.VMEM),
        scratch_shapes=[
            pltpu.VMEM(chunks.shape, values.dtype),
            pltpu.SemaphoreType.DMA((count,)),
            pltpu.SemaphoreType.DMA((count,)),
            pltpu.SemaphoreType.DMA((count,)),
            pltpu.SemaphoreType.DMA((count,)),
        ],
        compiler_params=pltpu.CompilerParams(collective_id=collective, has_side_effects=True),
    )(chunks)
    return summed.reshape(values.shape)


def owner_adapter_term(received, slot_ids, down_local, up_local):
    sources, rows, part_width = received.shape
    local_adapters, unused_item, adapter_rank = down_local.shape
    query_width = up_local.shape[2]
    token_rows = received.reshape(sources * rows, part_width)
    every_down = jnp.einsum(
        "td,adr->tar", token_rows, down_local, preferred_element_type=jnp.float32
    )
    pick = slot_ids.reshape(sources * rows)[:, None] == jnp.arange(local_adapters, dtype=jnp.int32)[None, :]
    partial_value_sum = jnp.sum(jnp.where(pick[:, :, None], every_down, 0.0), axis=1)
    tp_count = lax.axis_size("tp")
    summed = axis_sum(partial_value_sum.reshape(-1, 128), "tp", tp_count, 2, jnp.bfloat16)
    adapter_middle = summed.reshape(sources * rows, adapter_rank)
    spread_rows = jnp.where(pick[:, :, None], adapter_middle[:, None, :], jnp.zeros((), jnp.bfloat16))
    spread_rows = spread_rows.reshape(sources * rows, local_adapters * adapter_rank)
    adapter_output = jnp.dot(
        spread_rows,
        up_local.reshape(local_adapters * adapter_rank, query_width),
        preferred_element_type=jnp.float32,
    ).astype(jnp.bfloat16)
    return adapter_output.reshape(sources, rows, query_width)


def body(
    tokens,
    adapter_id,
    pool_slot,
    lengths,
    w_query,
    w_key,
    w_value,
    pooled_down_weights,
    pool_up,
    cache_key,
    cache_value,
):
    group_count = lax.axis_size("grp")
    tp_count = lax.axis_size("tp")
    row_count, step_count, part_width = tokens.shape
    local_adapter_rows, unused_item, adapter_rank = pooled_down_weights.shape
    query_width = w_query.shape[1]
    kv_width = w_key.shape[1]
    kv_local = kv_width // HD
    q_local = query_width // HD
    group_size = q_local // kv_local
    count_of_tokens = row_count * step_count
    adapter_span = jnp.arange(pool_slot.shape[0], dtype=jnp.int32)
    pool_pos = jnp.sum(
        jnp.where(adapter_id[:, None] == adapter_span[None, :], pool_slot[None, :], 0), axis=1
    )
    owner_grp = pool_pos // local_adapter_rows
    local_slot = pool_pos % local_adapter_rows
    row_span = jnp.arange(row_count, dtype=jnp.int32)
    same_owner = (owner_grp[:, None] == owner_grp[None, :]) & (row_span[None, :] < row_span[:, None])
    owner_rank = jnp.sum(same_owner.astype(jnp.int32), axis=1)
    send_slot = owner_grp * CAP + owner_rank
    slot_span = jnp.arange(group_count * CAP, dtype=jnp.int32)
    place = (slot_span[:, None] == send_slot[None, :]).astype(jnp.bfloat16)
    token_slot = (send_slot[:, None] * step_count + jnp.arange(step_count, dtype=jnp.int32)[None, :]).reshape(-1)
    token_span = jnp.arange(group_count * CAP * step_count, dtype=jnp.int32)
    place_tokens = (token_span[:, None] == token_slot[None, :]).astype(jnp.bfloat16)
    token_rows = tokens.reshape(count_of_tokens, part_width)
    send_tokens = jnp.dot(place_tokens, token_rows, preferred_element_type=jnp.float32).astype(jnp.bfloat16)
    send_tokens = send_tokens.reshape(group_count, CAP * step_count, part_width)
    send_ids = jnp.dot(
        place, local_slot.astype(jnp.bfloat16)[:, None], preferred_element_type=jnp.float32
    ).astype(jnp.bfloat16)
    send_ids = jnp.broadcast_to(send_ids.reshape(group_count, CAP, 1), (group_count, CAP, 128))
    send_ids = jnp.concatenate([send_ids, jnp.zeros_like(send_ids)], axis=1)
    (got_tokens, got_ids), chip_pieces = exchange_ring(
        (send_tokens, send_ids), token_rows, "grp", group_count, "tp", 0
    )
    got_ids = jnp.repeat(got_ids[:, :CAP, 0].astype(jnp.int32), step_count, axis=1)
    owner_out = owner_adapter_term(got_tokens, got_ids, pooled_down_weights, pool_up)
    position = lengths[:, None] + jnp.arange(step_count, dtype=jnp.int32)[None, :]
    half_width = HD // 2
    inv_freq = jnp.exp(
        jnp.arange(half_width, dtype=jnp.float32) * (-2.0 * math.log(rope_base) / HD)
    )
    both_halves = jnp.concatenate([inv_freq, inv_freq])
    turn_sign = jnp.where(jnp.arange(HD, dtype=jnp.int32) < half_width, -1.0, 1.0).astype(jnp.float32)
    angles = position.reshape(count_of_tokens).astype(jnp.float32)[:, None] * both_halves[None, :]
    cosine = jnp.cos(angles)
    sines = jnp.sin(angles) * turn_sign[None, :]
    place_back = (token_slot[:, None] == token_span[None, :]).astype(jnp.bfloat16)
    queries, key_new, value_new = exchange_project(
        owner_out, chip_pieces, w_query, w_key, w_value, place_back, cosine, sines,
        "grp", group_count, "tp", 1
    )
    queries = queries.reshape(row_count, step_count, kv_local, group_size, HD)
    key_new = key_new.reshape(row_count, step_count, kv_local, HD)
    value_new = value_new.reshape(row_count, step_count, kv_local, HD)
    cache_keys = cache_key.reshape(row_count, cache_key.shape[1], kv_local, HD)
    cache_values = cache_value.reshape(row_count, cache_value.shape[1], kv_local, HD)
    combined = attend(queries, key_new, value_new, cache_keys, cache_values, lengths)
    return combined.reshape(row_count, step_count, query_width)


def solution(mesh):
    in_specs = (
        P("grp", None, "tp"),
        P("grp"),
        P(),
        P("grp"),
        P(None, "tp"),
        P(None, "tp"),
        P(None, "tp"),
        P("grp", "tp", None),
        P("grp", None, "tp"),
        P("grp", None, "tp"),
        P("grp", None, "tp"),
    )
    out_specs = P("grp", None, "tp")
    return jax.shard_map(body, mesh=mesh, in_specs=in_specs, out_specs=out_specs, check_vma=False)
```

```python
import math

import jax
import jax.numpy as jnp
from jax import lax
from jax.experimental import pallas as pl
from jax.experimental.pallas import tpu as pltpu
from jax.sharding import PartitionSpec as P

MESH = pl.DeviceIdType.MESH

HD = 128
CAP = 8


rope_base = 500000.0


def rotate(values, position):
    half_width = values.shape[-1] // 2
    inv_freq = jnp.exp(
        jnp.arange(half_width, dtype=jnp.float32) * (-2.0 * math.log(rope_base) / values.shape[-1])
    )
    angles = position.astype(jnp.float32)[:, :, None, None] * inv_freq
    cosine = jnp.cos(angles)
    sines = jnp.sin(angles)
    front_half = values[..., :half_width]
    back_half = values[..., half_width:]
    return jnp.concatenate(
        [front_half * cosine - back_half * sines, back_half * cosine + front_half * sines], axis=-1
    )


def attend(queries, key_new, value_new, cache_key, cache_value, lengths):
    score_scale = 1.0 / math.sqrt(queries.shape[-1])
    cached = (
        jnp.einsum("rskgd,rlkd->rskgl", queries, cache_key, preferred_element_type=jnp.float32)
        * score_scale
    )
    fresh_scores = (
        jnp.einsum("rskgd,rtkd->rskgt", queries, key_new, preferred_element_type=jnp.float32)
        * score_scale
    )
    live_mask = jnp.arange(cache_key.shape[1], dtype=jnp.int32)[None, :] < lengths[:, None]
    cached = jnp.where(live_mask[:, None, None, None, :], cached, -1e30)
    steps_here = key_new.shape[1]
    causal = (
        jnp.arange(steps_here, dtype=jnp.int32)[:, None]
        >= jnp.arange(steps_here, dtype=jnp.int32)[None, :]
    )
    fresh_scores = jnp.where(causal[None, :, None, None, :], fresh_scores, -1e30)
    row_max = jnp.maximum(jnp.max(cached, axis=-1), jnp.max(fresh_scores, axis=-1))
    cache_exp = jnp.exp(cached - row_max[..., None])
    fresh_exp = jnp.exp(fresh_scores - row_max[..., None])
    weight_sum = jnp.sum(cache_exp, axis=-1) + jnp.sum(fresh_exp, axis=-1)
    cache_weights = (cache_exp / weight_sum[..., None]).astype(jnp.bfloat16)
    fresh_weights = (fresh_exp / weight_sum[..., None]).astype(jnp.bfloat16)
    combined = jnp.einsum(
        "rskgl,rlkd->rskgd", cache_weights, cache_value, preferred_element_type=jnp.float32
    )
    combined = combined + jnp.einsum(
        "rskgt,rtkd->rskgd", fresh_weights, value_new, preferred_element_type=jnp.float32
    )
    return combined.astype(jnp.bfloat16)


TORUS_ORDER = (
    (0, 1), (1, 0), (0, 3), (3, 0), (1, 1), (3, 3), (1, 3), (3, 1),
    (0, 2), (2, 0), (2, 1), (1, 2), (2, 3), (3, 2), (2, 2),
)


def peer_offsets(count):
    if count == 16:
        def shifted(me, dz, dy):
            return lax.rem(me // 4 + dz, 4) * 4 + lax.rem(lax.rem(me, 4) + dy, 4)

        return [
            (lambda me, a=dz, b=dy: shifted(me, a, b), lambda me, a=dz, b=dy: shifted(me, 4 - a, 4 - b))
            for dz, dy in TORUS_ORDER
        ]
    return [
        (lambda me, d=offset: lax.rem(me + d, count), lambda me, d=offset: lax.rem(me + count - d, count))
        for offset in range(1, count)
    ]


def exchange_kernel(axis, count, arrays, *refs):
    send_refs = refs[:arrays]
    got_refs = refs[arrays : 2 * arrays]
    send_sem, recv_sem, local_sem = refs[2 * arrays :]
    me = lax.axis_index(axis)
    barrier = pltpu.get_barrier_semaphore()
    offsets = peer_offsets(count)
    for offset in range(1, count):
        peer = offsets[offset - 1][0](me)
        pl.semaphore_signal(barrier, inc=1, device_id={axis: peer}, device_id_type=MESH)
    pl.semaphore_wait(barrier, count - 1)
    locals_ = []
    for which in range(arrays):
        local = pltpu.make_async_copy(
            send_refs[which].at[me], got_refs[which].at[me], local_sem.at[which]
        )
        local.start()
        locals_.append(local)
    outgoing = []
    for offset in range(1, count):
        peer = offsets[offset - 1][0](me)
        for which in range(arrays):
            copy = pltpu.make_async_remote_copy(
                src_ref=send_refs[which].at[peer],
                dst_ref=got_refs[which].at[me],
                send_sem=send_sem.at[which, offset],
                recv_sem=recv_sem.at[which, offset],
                device_id={axis: peer},
                device_id_type=MESH,
            )
            copy.start()
            outgoing.append(copy)
    for offset in range(1, count):
        source = offsets[offset - 1][1](me)
        for which in range(arrays):
            outgoing[(offset - 1) * arrays + which].wait_send()
            incoming = pltpu.make_async_remote_copy(
                src_ref=send_refs[which].at[source],
                dst_ref=got_refs[which].at[source],
                send_sem=send_sem.at[which, offset],
                recv_sem=recv_sem.at[which, offset],
                device_id={axis: source},
                device_id_type=MESH,
            )
            incoming.wait_recv()
    for local in locals_:
        local.wait()


def exchange(values, axis, count, collective):
    arrays = len(values)
    vmem = pl.BlockSpec(memory_space=pltpu.VMEM)
    return pl.pallas_call(
        lambda *refs: exchange_kernel(axis, count, arrays, *refs),
        out_shape=tuple(jax.ShapeDtypeStruct(v.shape, v.dtype) for v in values),
        in_specs=[vmem] * arrays,
        out_specs=tuple([vmem] * arrays),
        scratch_shapes=[
            pltpu.SemaphoreType.DMA((arrays, count)),
            pltpu.SemaphoreType.DMA((arrays, count)),
            pltpu.SemaphoreType.DMA((arrays,)),
        ],
        compiler_params=pltpu.CompilerParams(collective_id=collective, has_side_effects=True),
    )(*values)


def exchange_ring_kernel(axis, count, gather_axis, arrays, *refs):
    send_refs = refs[:arrays]
    piece_ref = refs[arrays]
    down_ref = refs[arrays + 1]
    total = refs[arrays + 2]
    chip_pieces = refs[arrays + 3]
    got_refs = (refs[arrays + 5], refs[arrays + 4])
    (part, held, send_sem, recv_sem, local_sem, near_send, near_recv, piece_sem,
     first_send, first_recv, second_send, second_recv) = refs[arrays + 6 :]
    members = lax.axis_size(gather_axis)
    chips = lax.axis_size(gather_axis) // 2
    me = lax.axis_index(axis)
    mine = lax.axis_index(gather_axis)
    chip = mine // 2
    core = lax.rem(mine, 2)
    right_chip = lax.rem(chip + 1, chips)
    left_chip = lax.rem(chip + chips - 1, chips)
    right = right_chip * 2 + core
    left = left_chip * 2 + core

    barrier = pltpu.get_barrier_semaphore()
    offsets = peer_offsets(count)
    for offset in range(1, count):
        peer = offsets[offset - 1][0](me)
        pl.semaphore_signal(barrier, inc=1, device_id={axis: peer}, device_id_type=MESH)
    for offset in range(1, members):
        peer = lax.rem(mine + offset, members)
        pl.semaphore_signal(barrier, inc=1, device_id={gather_axis: peer}, device_id_type=MESH)
    pl.semaphore_wait(barrier, count + members - 2)

    near = []
    for side, target in ((0, right), (1, left)):
        copy = pltpu.make_async_remote_copy(
            src_ref=piece_ref,
            dst_ref=chip_pieces.at[1 + side],
            send_sem=near_send.at[side],
            recv_sem=near_recv.at[side],
            device_id={gather_axis: target},
            device_id_type=MESH,
        )
        copy.start()
        near.append(copy)
    own_piece = pltpu.make_async_copy(piece_ref, chip_pieces.at[0], piece_sem)
    own_piece.start()

    locals_ = []
    for which in range(arrays):
        local = pltpu.make_async_copy(
            send_refs[which].at[me], got_refs[which].at[me], local_sem.at[which]
        )
        local.start()
        locals_.append(local)
    outgoing = []
    for offset in range(1, count):
        peer = offsets[offset - 1][0](me)
        for which in range(arrays):
            copy = pltpu.make_async_remote_copy(
                src_ref=send_refs[which].at[peer],
                dst_ref=got_refs[which].at[me],
                send_sem=send_sem.at[which, offset],
                recv_sem=recv_sem.at[which, offset],
                device_id={axis: peer},
                device_id_type=MESH,
            )
            copy.start()
            outgoing.append(copy)

    for side, source in ((0, left), (1, right)):
        near[side].wait_send()
        incoming = pltpu.make_async_remote_copy(
            src_ref=piece_ref,
            dst_ref=chip_pieces.at[1 + side],
            send_sem=near_send.at[side],
            recv_sem=near_recv.at[side],
            device_id={gather_axis: source},
            device_id_type=MESH,
        )
        incoming.wait_recv()

    for offset in range(1, count):
        source = offsets[offset - 1][1](me)
        for which in range(arrays):
            outgoing[(offset - 1) * arrays + which].wait_send()
            incoming = pltpu.make_async_remote_copy(
                src_ref=send_refs[which].at[source],
                dst_ref=got_refs[which].at[source],
                send_sem=send_sem.at[which, offset],
                recv_sem=recv_sem.at[which, offset],
                device_id={axis: source},
                device_id_type=MESH,
            )
            incoming.wait_recv()
    for local in locals_:
        local.wait()

    sources, slot_rows, part_width = got_refs[0].shape
    token_count = sources * slot_rows
    tokens_here = got_refs[0][...].reshape(token_count, part_width)
    adapter_of = got_refs[1][...].reshape(token_count, got_refs[1].shape[2])[:, 0:1].astype(jnp.int32)
    partial = jnp.zeros((token_count, down_ref.shape[2]), jnp.float32)
    for adapter in range(down_ref.shape[0]):
        product = jnp.dot(tokens_here, down_ref[adapter], preferred_element_type=jnp.float32)
        partial = partial + jnp.where(adapter_of == adapter, product, jnp.zeros_like(product))
    part[...] = partial.reshape(part.shape)

    first_out = []
    for offset in range(1, members):
        peer = lax.rem(mine + offset, members)
        copy = pltpu.make_async_remote_copy(
            src_ref=part.at[peer],
            dst_ref=held.at[mine],
            send_sem=first_send.at[offset],
            recv_sem=first_recv.at[offset],
            device_id={gather_axis: peer},
            device_id_type=MESH,
        )
        copy.start()
        first_out.append(copy)
    held[mine] = part[mine]
    for offset in range(1, members):
        first_out[offset - 1].wait_send()
        source = lax.rem(mine + members - offset, members)
        incoming = pltpu.make_async_remote_copy(
            src_ref=part.at[source],
            dst_ref=held.at[source],
            send_sem=first_send.at[offset],
            recv_sem=first_recv.at[offset],
            device_id={gather_axis: source},
            device_id_type=MESH,
        )
        incoming.wait_recv()
    summed = held[0]
    for index in range(1, members):
        summed = summed + held[index]
    total[mine] = summed.astype(total.dtype)
    second_out = []
    for offset in range(1, members):
        peer = lax.rem(mine + offset, members)
        copy = pltpu.make_async_remote_copy(
            src_ref=total.at[mine],
            dst_ref=total.at[mine],
            send_sem=second_send.at[offset],
            recv_sem=second_recv.at[offset],
            device_id={gather_axis: peer},
            device_id_type=MESH,
        )
        copy.start()
        second_out.append(copy)
    for offset in range(1, members):
        second_out[offset - 1].wait_send()
        source = lax.rem(mine + members - offset, members)
        incoming = pltpu.make_async_remote_copy(
            src_ref=total.at[source],
            dst_ref=total.at[source],
            send_sem=second_send.at[offset],
            recv_sem=second_recv.at[offset],
            device_id={gather_axis: source},
            device_id_type=MESH,
        )
        incoming.wait_recv()
    own_piece.wait()


def exchange_ring(values, piece, down_local, axis, count, gather_axis, collective):
    arrays = len(values)
    members = lax.axis_size(gather_axis)
    sources, slot_rows, unused_item = values[0].shape
    adapter_rank = down_local.shape[2]
    chunk_shape = (members, sources * slot_rows // members, adapter_rank)
    vmem = pl.BlockSpec(memory_space=pltpu.VMEM)
    outs = pl.pallas_call(
        lambda *refs: exchange_ring_kernel(axis, count, gather_axis, arrays, *refs),
        out_shape=(jax.ShapeDtypeStruct(chunk_shape, jnp.bfloat16),
                   jax.ShapeDtypeStruct((3,) + piece.shape, piece.dtype),
                   jax.ShapeDtypeStruct(values[1].shape, values[1].dtype)),
        in_specs=[vmem] * (arrays + 2),
        out_specs=(vmem, vmem, vmem),
        scratch_shapes=[pltpu.VMEM(values[0].shape, values[0].dtype)]
        + [
            pltpu.VMEM(chunk_shape, jnp.float32),
            pltpu.VMEM(chunk_shape, jnp.float32),
            pltpu.SemaphoreType.DMA((arrays, count)),
            pltpu.SemaphoreType.DMA((arrays, count)),
            pltpu.SemaphoreType.DMA((arrays,)),
            pltpu.SemaphoreType.DMA((2,)),
            pltpu.SemaphoreType.DMA((2,)),
            pltpu.SemaphoreType.DMA(()),
            pltpu.SemaphoreType.DMA((members,)),
            pltpu.SemaphoreType.DMA((members,)),
            pltpu.SemaphoreType.DMA((members,)),
            pltpu.SemaphoreType.DMA((members,)),
        ],
        compiler_params=pltpu.CompilerParams(collective_id=collective, has_side_effects=True),
    )(*values, piece, down_local)
    return outs


def exchange_project_kernel(
    axis, count, gather_axis, send_ref, near_pieces, wq_hbm, wk_ref, wv_ref,
    place_ref, cos_ref, sin_ref,
    queries_ref, key_ref, value_ref,
    got_ref, q_ref, k_ref, v_ref,
    far_piece, partner_near, partner_far, wq_buf, send_sem, recv_sem, local_sem, wq_sem,
    far_send, far_recv, partner_send, partner_recv,
):
    me = lax.axis_index(axis)
    mine = lax.axis_index(gather_axis)
    chips = lax.axis_size(gather_axis) // 2
    chip = mine // 2
    core = lax.rem(mine, 2)
    partner = chip * 2 + (1 - core)
    right = lax.rem(chip + 1, chips) * 2 + core
    left = lax.rem(chip + chips - 1, chips) * 2 + core
    half = far_piece.shape[0] // 2
    barrier = pltpu.get_barrier_semaphore()
    offsets = peer_offsets(count)
    for offset in range(1, count):
        peer = offsets[offset - 1][0](me)
        pl.semaphore_signal(barrier, inc=1, device_id={axis: peer}, device_id_type=MESH)
    for neighbour in (partner, right, left):
        pl.semaphore_signal(barrier, inc=1, device_id={gather_axis: neighbour}, device_id_type=MESH)
    pl.semaphore_wait(barrier, count + 2)

    far_out = []
    for side, slot, target, rows in ((0, 1, right, pl.ds(0, half)), (1, 2, left, pl.ds(half, half))):
        copy = pltpu.make_async_remote_copy(
            src_ref=near_pieces.at[slot, rows],
            dst_ref=far_piece.at[rows],
            send_sem=far_send.at[side],
            recv_sem=far_recv.at[side],
            device_id={gather_axis: target},
            device_id_type=MESH,
        )
        copy.start()
        far_out.append(copy)
    to_partner = pltpu.make_async_remote_copy(
        src_ref=near_pieces,
        dst_ref=partner_near,
        send_sem=partner_send.at[0],
        recv_sem=partner_recv.at[0],
        device_id={gather_axis: partner},
        device_id_type=MESH,
    )
    to_partner.start()
    local = pltpu.make_async_copy(send_ref.at[me], got_ref.at[me], local_sem)
    local.start()
    outgoing = []
    for offset in range(1, count):
        peer = offsets[offset - 1][0](me)
        copy = pltpu.make_async_remote_copy(
            src_ref=send_ref.at[peer],
            dst_ref=got_ref.at[me],
            send_sem=send_sem.at[offset],
            recv_sem=recv_sem.at[offset],
            device_id={axis: peer},
            device_id_type=MESH,
        )
        copy.start()
        outgoing.append(copy)

    piece_width = near_pieces.shape[2]
    chip_shift = (0, chips - 1, 1, 2)

    def piece_index(step):
        piece_core = core if step < 4 else 1 - core
        return lax.rem(chip + chip_shift[step % 4], chips) * 2 + piece_core

    def chunk_copy(step):
        index = piece_index(step)
        return pltpu.make_async_copy(
            wq_hbm.at[pl.ds(pl.multiple_of(index * piece_width, piece_width), piece_width)],
            wq_buf.at[step % 2],
            wq_sem.at[step % 2],
        )

    chunk_copy(0).start()
    q_ref[...] = jnp.zeros_like(q_ref)
    k_ref[...] = jnp.zeros_like(k_ref)
    v_ref[...] = jnp.zeros_like(v_ref)

    def project(step, piece):
        chunk_copy(step).wait()
        if step + 1 < 8:
            chunk_copy(step + 1).start()
        index = piece_index(step)
        rows = pl.ds(pl.multiple_of(index * piece_width, piece_width), piece_width)
        q_ref[...] += jnp.dot(piece, wq_buf[step % 2], preferred_element_type=jnp.float32)
        k_ref[...] += jnp.dot(piece, wk_ref[rows, :], preferred_element_type=jnp.float32)
        v_ref[...] += jnp.dot(piece, wv_ref[rows, :], preferred_element_type=jnp.float32)

    for step in range(3):
        project(step, near_pieces[step])
    for side, source, rows in ((0, left, pl.ds(0, half)), (1, right, pl.ds(half, half))):
        far_out[side].wait_send()
        incoming = pltpu.make_async_remote_copy(
            src_ref=near_pieces.at[1, rows],
            dst_ref=far_piece.at[rows],
            send_sem=far_send.at[side],
            recv_sem=far_recv.at[side],
            device_id={gather_axis: source},
            device_id_type=MESH,
        )
        incoming.wait_recv()
    far_to_partner = pltpu.make_async_remote_copy(
        src_ref=far_piece,
        dst_ref=partner_far,
        send_sem=partner_send.at[1],
        recv_sem=partner_recv.at[1],
        device_id={gather_axis: partner},
        device_id_type=MESH,
    )
    far_to_partner.start()
    project(3, far_piece[...])
    to_partner.wait_send()
    to_partner.wait_recv()
    for step in range(3):
        project(4 + step, partner_near[step])
    far_to_partner.wait_send()
    far_to_partner.wait_recv()
    project(7, partner_far[...])

    for offset in range(1, count):
        outgoing[offset - 1].wait_send()
        source = offsets[offset - 1][1](me)
        incoming = pltpu.make_async_remote_copy(
            src_ref=send_ref.at[source],
            dst_ref=got_ref.at[source],
            send_sem=send_sem.at[offset],
            recv_sem=recv_sem.at[offset],
            device_id={axis: source},
            device_id_type=MESH,
        )
        incoming.wait_recv()
    local.wait()

    slots, slot_rows, width = got_ref.shape
    adapter_rows = jnp.dot(
        place_ref[...], got_ref[...].reshape(slots * slot_rows, width),
        preferred_element_type=jnp.float32,
    )
    cosine = cos_ref[...]
    sines = sin_ref[...]
    half_turn = HD // 2

    def rotated(values):
        return values * cosine + pltpu.roll(values, half_turn, 1) * sines

    for head in range(width // HD):
        lanes = slice(head * HD, (head + 1) * HD)
        summed = q_ref[:, lanes] + adapter_rows[:, lanes]
        queries_ref[:, lanes] = rotated(summed).astype(queries_ref.dtype)
    for head in range(key_ref.shape[1] // HD):
        lanes = slice(head * HD, (head + 1) * HD)
        key_ref[:, lanes] = rotated(k_ref[:, lanes]).astype(key_ref.dtype)
    value_ref[...] = v_ref[...].astype(value_ref.dtype)


def exchange_project(values, near_pieces, w_query, w_key, w_value, place_t, cosine, sines,
                     axis, count, gather_axis, collective):
    unused_item, token_count, piece_width = near_pieces.shape
    vmem = pl.BlockSpec(memory_space=pltpu.VMEM)
    return pl.pallas_call(
        lambda *refs: exchange_project_kernel(axis, count, gather_axis, *refs),
        out_shape=(
            jax.ShapeDtypeStruct((token_count, w_query.shape[1]), jnp.bfloat16),
            jax.ShapeDtypeStruct((token_count, w_key.shape[1]), jnp.bfloat16),
            jax.ShapeDtypeStruct((token_count, w_value.shape[1]), jnp.bfloat16),
        ),
        in_specs=[vmem, vmem, pl.BlockSpec(memory_space=pl.ANY), vmem, vmem, vmem, vmem, vmem],
        out_specs=(vmem, vmem, vmem),
        scratch_shapes=[
            pltpu.VMEM(values.shape, values.dtype),
            pltpu.VMEM((token_count, w_query.shape[1]), jnp.float32),
            pltpu.VMEM((token_count, w_key.shape[1]), jnp.float32),
            pltpu.VMEM((token_count, w_value.shape[1]), jnp.float32),
            pltpu.VMEM((token_count, piece_width), near_pieces.dtype),
            pltpu.VMEM(near_pieces.shape, near_pieces.dtype),
            pltpu.VMEM((token_count, piece_width), near_pieces.dtype),
            pltpu.VMEM((2, piece_width, w_query.shape[1]), w_query.dtype),
            pltpu.SemaphoreType.DMA((count,)),
            pltpu.SemaphoreType.DMA((count,)),
            pltpu.SemaphoreType.DMA(()),
            pltpu.SemaphoreType.DMA((2,)),
            pltpu.SemaphoreType.DMA((2,)),
            pltpu.SemaphoreType.DMA((2,)),
            pltpu.SemaphoreType.DMA((2,)),
            pltpu.SemaphoreType.DMA((2,)),
        ],
        compiler_params=pltpu.CompilerParams(
            collective_id=collective, has_side_effects=True, vmem_limit_bytes=60 * 1024 * 1024
        ),
    )(values, near_pieces, w_query, w_key, w_value, place_t, cosine, sines)


def sum_kernel(axis, count, part_ref, total_ref, held, first_send, first_recv, second_send, second_recv):
    me = lax.axis_index(axis)
    barrier = pltpu.get_barrier_semaphore()
    for offset in range(1, count):
        peer = lax.rem(me + offset, count)
        pl.semaphore_signal(barrier, inc=1, device_id={axis: peer}, device_id_type=MESH)
    pl.semaphore_wait(barrier, count - 1)
    outgoing = []
    for offset in range(1, count):
        peer = lax.rem(me + offset, count)
        copy = pltpu.make_async_remote_copy(
            src_ref=part_ref.at[peer],
            dst_ref=held.at[me],
            send_sem=first_send.at[offset],
            recv_sem=first_recv.at[offset],
            device_id={axis: peer},
            device_id_type=MESH,
        )
        copy.start()
        outgoing.append(copy)
    held[me] = part_ref[me]
    for offset in range(1, count):
        outgoing[offset - 1].wait_send()
        source = lax.rem(me + count - offset, count)
        incoming = pltpu.make_async_remote_copy(
            src_ref=part_ref.at[source],
            dst_ref=held.at[source],
            send_sem=first_send.at[offset],
            recv_sem=first_recv.at[offset],
            device_id={axis: source},
            device_id_type=MESH,
        )
        incoming.wait_recv()
    total = held[0]
    for index in range(1, count):
        total = total + held[index]
    total_ref[me] = total.astype(total_ref.dtype)
    outgoing = []
    for offset in range(1, count):
        peer = lax.rem(me + offset, count)
        copy = pltpu.make_async_remote_copy(
            src_ref=total_ref.at[me],
            dst_ref=total_ref.at[me],
            send_sem=second_send.at[offset],
            recv_sem=second_recv.at[offset],
            device_id={axis: peer},
            device_id_type=MESH,
        )
        copy.start()
        outgoing.append(copy)
    for offset in range(1, count):
        outgoing[offset - 1].wait_send()
        source = lax.rem(me + count - offset, count)
        incoming = pltpu.make_async_remote_copy(
            src_ref=total_ref.at[source],
            dst_ref=total_ref.at[source],
            send_sem=second_send.at[offset],
            recv_sem=second_recv.at[offset],
            device_id={axis: source},
            device_id_type=MESH,
        )
        incoming.wait_recv()


def axis_sum(values, axis, count, collective, out_dtype):
    chunks = values.reshape(count, -1, 128)
    summed = pl.pallas_call(
        lambda *refs: sum_kernel(axis, count, *refs),
        out_shape=jax.ShapeDtypeStruct(chunks.shape, out_dtype),
        in_specs=[pl.BlockSpec(memory_space=pltpu.VMEM)],
        out_specs=pl.BlockSpec(memory_space=pltpu.VMEM),
        scratch_shapes=[
            pltpu.VMEM(chunks.shape, values.dtype),
            pltpu.SemaphoreType.DMA((count,)),
            pltpu.SemaphoreType.DMA((count,)),
            pltpu.SemaphoreType.DMA((count,)),
            pltpu.SemaphoreType.DMA((count,)),
        ],
        compiler_params=pltpu.CompilerParams(collective_id=collective, has_side_effects=True),
    )(chunks)
    return summed.reshape(values.shape)


def adapter_up(adapter_middle, slot_ids, up_local):
    sources, rows = slot_ids.shape
    local_adapters, adapter_rank, query_width = up_local.shape
    pick = slot_ids.reshape(sources * rows)[:, None] == jnp.arange(local_adapters, dtype=jnp.int32)[None, :]
    spread_rows = jnp.where(pick[:, :, None], adapter_middle[:, None, :], jnp.zeros((), jnp.bfloat16))
    spread_rows = spread_rows.reshape(sources * rows, local_adapters * adapter_rank)
    adapter_output = jnp.dot(
        spread_rows,
        up_local.reshape(local_adapters * adapter_rank, query_width),
        preferred_element_type=jnp.float32,
    ).astype(jnp.bfloat16)
    return adapter_output.reshape(sources, rows, query_width)


def body(
    tokens,
    adapter_id,
    pool_slot,
    lengths,
    w_query,
    w_key,
    w_value,
    pooled_down_weights,
    pool_up,
    cache_key,
    cache_value,
):
    group_count = lax.axis_size("grp")
    tp_count = lax.axis_size("tp")
    row_count, step_count, part_width = tokens.shape
    local_adapter_rows, unused_item, adapter_rank = pooled_down_weights.shape
    query_width = w_query.shape[1]
    kv_width = w_key.shape[1]
    kv_local = kv_width // HD
    q_local = query_width // HD
    group_size = q_local // kv_local
    count_of_tokens = row_count * step_count
    adapter_span = jnp.arange(pool_slot.shape[0], dtype=jnp.int32)
    pool_pos = jnp.sum(
        jnp.where(adapter_id[:, None] == adapter_span[None, :], pool_slot[None, :], 0), axis=1
    )
    owner_grp = pool_pos // local_adapter_rows
    local_slot = pool_pos % local_adapter_rows
    row_span = jnp.arange(row_count, dtype=jnp.int32)
    same_owner = (owner_grp[:, None] == owner_grp[None, :]) & (row_span[None, :] < row_span[:, None])
    owner_rank = jnp.sum(same_owner.astype(jnp.int32), axis=1)
    send_slot = owner_grp * CAP + owner_rank
    slot_span = jnp.arange(group_count * CAP, dtype=jnp.int32)
    place = (slot_span[:, None] == send_slot[None, :]).astype(jnp.bfloat16)
    token_slot = (send_slot[:, None] * step_count + jnp.arange(step_count, dtype=jnp.int32)[None, :]).reshape(-1)
    token_span = jnp.arange(group_count * CAP * step_count, dtype=jnp.int32)
    place_tokens = (token_span[:, None] == token_slot[None, :]).astype(jnp.bfloat16)
    token_rows = tokens.reshape(count_of_tokens, part_width)
    send_tokens = jnp.dot(place_tokens, token_rows, preferred_element_type=jnp.float32).astype(jnp.bfloat16)
    send_tokens = send_tokens.reshape(group_count, CAP * step_count, part_width)
    send_ids = jnp.dot(
        place_tokens, local_slot.astype(jnp.bfloat16)[:, None].repeat(step_count, axis=0),
        preferred_element_type=jnp.float32,
    ).astype(jnp.bfloat16)
    send_ids = jnp.broadcast_to(
        send_ids.reshape(group_count, CAP * step_count, 1), (group_count, CAP * step_count, 128)
    )
    total, chip_pieces, got_ids = exchange_ring(
        (send_tokens, send_ids), token_rows, pooled_down_weights, "grp", group_count, "tp", 0
    )
    adapter_middle = total.reshape(group_count * CAP * step_count, adapter_rank)
    owner_out = adapter_up(adapter_middle, got_ids[:, :, 0].astype(jnp.int32), pool_up)
    position = lengths[:, None] + jnp.arange(step_count, dtype=jnp.int32)[None, :]
    half_width = HD // 2
    inv_freq = jnp.exp(
        jnp.arange(half_width, dtype=jnp.float32) * (-2.0 * math.log(rope_base) / HD)
    )
    both_halves = jnp.concatenate([inv_freq, inv_freq])
    turn_sign = jnp.where(jnp.arange(HD, dtype=jnp.int32) < half_width, -1.0, 1.0).astype(jnp.float32)
    angles = position.reshape(count_of_tokens).astype(jnp.float32)[:, None] * both_halves[None, :]
    cosine = jnp.cos(angles)
    sines = jnp.sin(angles) * turn_sign[None, :]
    place_back = (token_slot[:, None] == token_span[None, :]).astype(jnp.bfloat16)
    queries, key_new, value_new = exchange_project(
        owner_out, chip_pieces, w_query, w_key, w_value, place_back, cosine, sines,
        "grp", group_count, "tp", 1
    )
    queries = queries.reshape(row_count, step_count, kv_local, group_size, HD)
    key_new = key_new.reshape(row_count, step_count, kv_local, HD)
    value_new = value_new.reshape(row_count, step_count, kv_local, HD)
    cache_keys = cache_key.reshape(row_count, cache_key.shape[1], kv_local, HD)
    cache_values = cache_value.reshape(row_count, cache_value.shape[1], kv_local, HD)
    combined = attend(queries, key_new, value_new, cache_keys, cache_values, lengths)
    return combined.reshape(row_count, step_count, query_width)


def solution(mesh):
    in_specs = (
        P("grp", None, "tp"),
        P("grp"),
        P(),
        P("grp"),
        P(None, "tp"),
        P(None, "tp"),
        P(None, "tp"),
        P("grp", "tp", None),
        P("grp", None, "tp"),
        P("grp", None, "tp"),
        P("grp", None, "tp"),
    )
    out_specs = P("grp", None, "tp")
    return jax.shard_map(body, mesh=mesh, in_specs=in_specs, out_specs=out_specs, check_vma=False)
```

```python
import math

import jax
import jax.numpy as jnp
from jax import lax
from jax.experimental import pallas as pl
from jax.experimental.pallas import tpu as pltpu
from jax.sharding import PartitionSpec as P

MESH = pl.DeviceIdType.MESH

HD = 128
CAP = 8


rope_base = 500000.0


def rotate(values, position):
    half_width = values.shape[-1] // 2
    inv_freq = jnp.exp(
        jnp.arange(half_width, dtype=jnp.float32) * (-2.0 * math.log(rope_base) / values.shape[-1])
    )
    angles = position.astype(jnp.float32)[:, :, None, None] * inv_freq
    cosine = jnp.cos(angles)
    sines = jnp.sin(angles)
    front_half = values[..., :half_width]
    back_half = values[..., half_width:]
    return jnp.concatenate(
        [front_half * cosine - back_half * sines, back_half * cosine + front_half * sines], axis=-1
    )


def attend(queries, key_new, value_new, cache_key, cache_value, lengths):
    score_scale = 1.0 / math.sqrt(queries.shape[-1])
    cached = (
        jnp.einsum("rskgd,rlkd->rskgl", queries, cache_key, preferred_element_type=jnp.float32)
        * score_scale
    )
    fresh_keys = jnp.transpose(key_new, (0, 2, 1, 3)).astype(jnp.float32)
    fresh_scores = (
        jnp.sum(
            queries.astype(jnp.float32)[:, :, :, :, None, :] * fresh_keys[:, None, :, None, :, :],
            axis=-1,
        )
        * score_scale
    )
    live_mask = jnp.arange(cache_key.shape[1], dtype=jnp.int32)[None, :] < lengths[:, None]
    cached = jnp.where(live_mask[:, None, None, None, :], cached, -1e30)
    steps_here = key_new.shape[1]
    causal = (
        jnp.arange(steps_here, dtype=jnp.int32)[:, None]
        >= jnp.arange(steps_here, dtype=jnp.int32)[None, :]
    )
    fresh_scores = jnp.where(causal[None, :, None, None, :], fresh_scores, -1e30)
    row_max = jnp.maximum(jnp.max(cached, axis=-1), jnp.max(fresh_scores, axis=-1))
    cache_exp = jnp.exp(cached - row_max[..., None])
    fresh_exp = jnp.exp(fresh_scores - row_max[..., None])
    weight_sum = jnp.sum(cache_exp, axis=-1) + jnp.sum(fresh_exp, axis=-1)
    cache_weights = (cache_exp / weight_sum[..., None]).astype(jnp.bfloat16)
    fresh_weights = (fresh_exp / weight_sum[..., None]).astype(jnp.bfloat16)
    combined = jnp.einsum(
        "rskgl,rlkd->rskgd", cache_weights, cache_value, preferred_element_type=jnp.float32
    )
    combined = combined + jnp.einsum(
        "rskgt,rtkd->rskgd", fresh_weights, value_new, preferred_element_type=jnp.float32
    )
    return combined.astype(jnp.bfloat16)


TORUS_ORDER = (
    (0, 1), (1, 0), (0, 3), (3, 0), (1, 1), (3, 3), (1, 3), (3, 1),
    (0, 2), (2, 0), (2, 1), (1, 2), (2, 3), (3, 2), (2, 2),
)


def peer_offsets(count):
    if count == 16:
        def shifted(me, dz, dy):
            return lax.rem(me // 4 + dz, 4) * 4 + lax.rem(lax.rem(me, 4) + dy, 4)

        return [
            (lambda me, a=dz, b=dy: shifted(me, a, b), lambda me, a=dz, b=dy: shifted(me, 4 - a, 4 - b))
            for dz, dy in TORUS_ORDER
        ]
    return [
        (lambda me, d=offset: lax.rem(me + d, count), lambda me, d=offset: lax.rem(me + count - d, count))
        for offset in range(1, count)
    ]


def exchange_kernel(axis, count, arrays, *refs):
    send_refs = refs[:arrays]
    got_refs = refs[arrays : 2 * arrays]
    send_sem, recv_sem, local_sem = refs[2 * arrays :]
    me = lax.axis_index(axis)
    barrier = pltpu.get_barrier_semaphore()
    offsets = peer_offsets(count)
    for offset in range(1, count):
        peer = offsets[offset - 1][0](me)
        pl.semaphore_signal(barrier, inc=1, device_id={axis: peer}, device_id_type=MESH)
    pl.semaphore_wait(barrier, count - 1)
    locals_ = []
    for which in range(arrays):
        local = pltpu.make_async_copy(
            send_refs[which].at[me], got_refs[which].at[me], local_sem.at[which]
        )
        local.start()
        locals_.append(local)
    outgoing = []
    for offset in range(1, count):
        peer = offsets[offset - 1][0](me)
        for which in range(arrays):
            copy = pltpu.make_async_remote_copy(
                src_ref=send_refs[which].at[peer],
                dst_ref=got_refs[which].at[me],
                send_sem=send_sem.at[which, offset],
                recv_sem=recv_sem.at[which, offset],
                device_id={axis: peer},
                device_id_type=MESH,
            )
            copy.start()
            outgoing.append(copy)
    for offset in range(1, count):
        source = offsets[offset - 1][1](me)
        for which in range(arrays):
            outgoing[(offset - 1) * arrays + which].wait_send()
            incoming = pltpu.make_async_remote_copy(
                src_ref=send_refs[which].at[source],
                dst_ref=got_refs[which].at[source],
                send_sem=send_sem.at[which, offset],
                recv_sem=recv_sem.at[which, offset],
                device_id={axis: source},
                device_id_type=MESH,
            )
            incoming.wait_recv()
    for local in locals_:
        local.wait()


def exchange(values, axis, count, collective):
    arrays = len(values)
    vmem = pl.BlockSpec(memory_space=pltpu.VMEM)
    return pl.pallas_call(
        lambda *refs: exchange_kernel(axis, count, arrays, *refs),
        out_shape=tuple(jax.ShapeDtypeStruct(v.shape, v.dtype) for v in values),
        in_specs=[vmem] * arrays,
        out_specs=tuple([vmem] * arrays),
        scratch_shapes=[
            pltpu.SemaphoreType.DMA((arrays, count)),
            pltpu.SemaphoreType.DMA((arrays, count)),
            pltpu.SemaphoreType.DMA((arrays,)),
        ],
        compiler_params=pltpu.CompilerParams(collective_id=collective, has_side_effects=True),
    )(*values)


def exchange_ring_kernel(axis, count, gather_axis, arrays, *refs):
    send_refs = refs[:arrays]
    piece_ref = refs[arrays]
    got_refs = refs[arrays + 1 : 2 * arrays + 1]
    chip_pieces = refs[2 * arrays + 1]
    send_sem, recv_sem, local_sem, near_send, near_recv, piece_sem = refs[2 * arrays + 2 :]
    chips = lax.axis_size(gather_axis) // 2
    me = lax.axis_index(axis)
    mine = lax.axis_index(gather_axis)
    chip = mine // 2
    core = lax.rem(mine, 2)
    right_chip = lax.rem(chip + 1, chips)
    left_chip = lax.rem(chip + chips - 1, chips)
    right = right_chip * 2 + core
    left = left_chip * 2 + core

    barrier = pltpu.get_barrier_semaphore()
    offsets = peer_offsets(count)
    for offset in range(1, count):
        peer = offsets[offset - 1][0](me)
        pl.semaphore_signal(barrier, inc=1, device_id={axis: peer}, device_id_type=MESH)
    pl.semaphore_signal(barrier, inc=1, device_id={gather_axis: right}, device_id_type=MESH)
    pl.semaphore_signal(barrier, inc=1, device_id={gather_axis: left}, device_id_type=MESH)
    pl.semaphore_wait(barrier, count + 1)

    near = []
    for side, target in ((0, right), (1, left)):
        copy = pltpu.make_async_remote_copy(
            src_ref=piece_ref,
            dst_ref=chip_pieces.at[1 + side],
            send_sem=near_send.at[side],
            recv_sem=near_recv.at[side],
            device_id={gather_axis: target},
            device_id_type=MESH,
        )
        copy.start()
        near.append(copy)
    own_piece = pltpu.make_async_copy(piece_ref, chip_pieces.at[0], piece_sem)
    own_piece.start()

    locals_ = []
    for which in range(arrays):
        local = pltpu.make_async_copy(
            send_refs[which].at[me], got_refs[which].at[me], local_sem.at[which]
        )
        local.start()
        locals_.append(local)
    outgoing = []
    for offset in range(1, count):
        peer = offsets[offset - 1][0](me)
        for which in range(arrays):
            copy = pltpu.make_async_remote_copy(
                src_ref=send_refs[which].at[peer],
                dst_ref=got_refs[which].at[me],
                send_sem=send_sem.at[which, offset],
                recv_sem=recv_sem.at[which, offset],
                device_id={axis: peer},
                device_id_type=MESH,
            )
            copy.start()
            outgoing.append(copy)

    for side, source in ((0, left), (1, right)):
        near[side].wait_send()
        incoming = pltpu.make_async_remote_copy(
            src_ref=piece_ref,
            dst_ref=chip_pieces.at[1 + side],
            send_sem=near_send.at[side],
            recv_sem=near_recv.at[side],
            device_id={gather_axis: source},
            device_id_type=MESH,
        )
        incoming.wait_recv()

    for offset in range(1, count):
        source = offsets[offset - 1][1](me)
        for which in range(arrays):
            outgoing[(offset - 1) * arrays + which].wait_send()
            incoming = pltpu.make_async_remote_copy(
                src_ref=send_refs[which].at[source],
                dst_ref=got_refs[which].at[source],
                send_sem=send_sem.at[which, offset],
                recv_sem=recv_sem.at[which, offset],
                device_id={axis: source},
                device_id_type=MESH,
            )
            incoming.wait_recv()
    for local in locals_:
        local.wait()
    own_piece.wait()


def exchange_ring(values, piece, axis, count, gather_axis, collective):
    arrays = len(values)
    vmem = pl.BlockSpec(memory_space=pltpu.VMEM)
    outs = pl.pallas_call(
        lambda *refs: exchange_ring_kernel(axis, count, gather_axis, arrays, *refs),
        out_shape=tuple(jax.ShapeDtypeStruct(v.shape, v.dtype) for v in values)
        + (jax.ShapeDtypeStruct((3,) + piece.shape, piece.dtype),),
        in_specs=[vmem] * (arrays + 1),
        out_specs=tuple([vmem] * (arrays + 1)),
        scratch_shapes=[
            pltpu.SemaphoreType.DMA((arrays, count)),
            pltpu.SemaphoreType.DMA((arrays, count)),
            pltpu.SemaphoreType.DMA((arrays,)),
            pltpu.SemaphoreType.DMA((2,)),
            pltpu.SemaphoreType.DMA((2,)),
            pltpu.SemaphoreType.DMA(()),
        ],
        compiler_params=pltpu.CompilerParams(collective_id=collective, has_side_effects=True),
    )(*values, piece)
    return outs[:arrays], outs[arrays]


def exchange_project_kernel(
    axis, count, gather_axis, send_ref, near_pieces, wq_hbm, wk_ref, wv_ref,
    place_ref, cos_ref, sin_ref,
    queries_ref, key_ref, value_ref,
    got_ref, q_ref, k_ref, v_ref,
    far_piece, partner_near, partner_far, wq_buf, send_sem, recv_sem, local_sem, wq_sem,
    far_send, far_recv, partner_send, partner_recv,
):
    me = lax.axis_index(axis)
    mine = lax.axis_index(gather_axis)
    chips = lax.axis_size(gather_axis) // 2
    chip = mine // 2
    core = lax.rem(mine, 2)
    partner = chip * 2 + (1 - core)
    right = lax.rem(chip + 1, chips) * 2 + core
    left = lax.rem(chip + chips - 1, chips) * 2 + core
    half = far_piece.shape[0] // 2
    barrier = pltpu.get_barrier_semaphore()
    offsets = peer_offsets(count)
    for offset in range(1, count):
        peer = offsets[offset - 1][0](me)
        pl.semaphore_signal(barrier, inc=1, device_id={axis: peer}, device_id_type=MESH)
    for neighbour in (partner, right, left):
        pl.semaphore_signal(barrier, inc=1, device_id={gather_axis: neighbour}, device_id_type=MESH)
    pl.semaphore_wait(barrier, count + 2)

    far_out = []
    for side, slot, target, rows in ((0, 1, right, pl.ds(0, half)), (1, 2, left, pl.ds(half, half))):
        copy = pltpu.make_async_remote_copy(
            src_ref=near_pieces.at[slot, rows],
            dst_ref=far_piece.at[rows],
            send_sem=far_send.at[side],
            recv_sem=far_recv.at[side],
            device_id={gather_axis: target},
            device_id_type=MESH,
        )
        copy.start()
        far_out.append(copy)
    to_partner = pltpu.make_async_remote_copy(
        src_ref=near_pieces,
        dst_ref=partner_near,
        send_sem=partner_send.at[0],
        recv_sem=partner_recv.at[0],
        device_id={gather_axis: partner},
        device_id_type=MESH,
    )
    to_partner.start()
    local = pltpu.make_async_copy(send_ref.at[me], got_ref.at[me], local_sem)
    local.start()
    outgoing = []
    for offset in range(1, count):
        peer = offsets[offset - 1][0](me)
        copy = pltpu.make_async_remote_copy(
            src_ref=send_ref.at[peer],
            dst_ref=got_ref.at[me],
            send_sem=send_sem.at[offset],
            recv_sem=recv_sem.at[offset],
            device_id={axis: peer},
            device_id_type=MESH,
        )
        copy.start()
        outgoing.append(copy)

    piece_width = near_pieces.shape[2]
    chip_shift = (0, chips - 1, 1, 2)

    def piece_index(step):
        piece_core = core if step < 4 else 1 - core
        return lax.rem(chip + chip_shift[step % 4], chips) * 2 + piece_core

    def chunk_copy(step):
        index = piece_index(step)
        return pltpu.make_async_copy(
            wq_hbm.at[pl.ds(pl.multiple_of(index * piece_width, piece_width), piece_width)],
            wq_buf.at[step % 2],
            wq_sem.at[step % 2],
        )

    chunk_copy(0).start()
    q_ref[...] = jnp.zeros_like(q_ref)
    k_ref[...] = jnp.zeros_like(k_ref)
    v_ref[...] = jnp.zeros_like(v_ref)

    def project(step, piece):
        chunk_copy(step).wait()
        if step + 1 < 8:
            chunk_copy(step + 1).start()
        index = piece_index(step)
        rows = pl.ds(pl.multiple_of(index * piece_width, piece_width), piece_width)
        q_ref[...] += jnp.dot(piece, wq_buf[step % 2], preferred_element_type=jnp.float32)
        k_ref[...] += jnp.dot(piece, wk_ref[rows, :], preferred_element_type=jnp.float32)
        v_ref[...] += jnp.dot(piece, wv_ref[rows, :], preferred_element_type=jnp.float32)

    for step in range(3):
        project(step, near_pieces[step])
    for side, source, rows in ((0, left, pl.ds(0, half)), (1, right, pl.ds(half, half))):
        far_out[side].wait_send()
        incoming = pltpu.make_async_remote_copy(
            src_ref=near_pieces.at[1, rows],
            dst_ref=far_piece.at[rows],
            send_sem=far_send.at[side],
            recv_sem=far_recv.at[side],
            device_id={gather_axis: source},
            device_id_type=MESH,
        )
        incoming.wait_recv()
    far_to_partner = pltpu.make_async_remote_copy(
        src_ref=far_piece,
        dst_ref=partner_far,
        send_sem=partner_send.at[1],
        recv_sem=partner_recv.at[1],
        device_id={gather_axis: partner},
        device_id_type=MESH,
    )
    far_to_partner.start()
    project(3, far_piece[...])
    to_partner.wait_send()
    to_partner.wait_recv()
    for step in range(3):
        project(4 + step, partner_near[step])
    far_to_partner.wait_send()
    far_to_partner.wait_recv()
    project(7, partner_far[...])

    for offset in range(1, count):
        outgoing[offset - 1].wait_send()
        source = offsets[offset - 1][1](me)
        incoming = pltpu.make_async_remote_copy(
            src_ref=send_ref.at[source],
            dst_ref=got_ref.at[source],
            send_sem=send_sem.at[offset],
            recv_sem=recv_sem.at[offset],
            device_id={axis: source},
            device_id_type=MESH,
        )
        incoming.wait_recv()
    local.wait()

    slots, slot_rows, width = got_ref.shape
    adapter_rows = jnp.dot(
        place_ref[...], got_ref[...].reshape(slots * slot_rows, width),
        preferred_element_type=jnp.float32,
    )
    cosine = cos_ref[...]
    sines = sin_ref[...]
    half_turn = HD // 2

    def rotated(values):
        return values * cosine + pltpu.roll(values, half_turn, 1) * sines

    for head in range(width // HD):
        lanes = slice(head * HD, (head + 1) * HD)
        summed = q_ref[:, lanes] + adapter_rows[:, lanes]
        queries_ref[:, lanes] = rotated(summed).astype(queries_ref.dtype)
    for head in range(key_ref.shape[1] // HD):
        lanes = slice(head * HD, (head + 1) * HD)
        key_ref[:, lanes] = rotated(k_ref[:, lanes]).astype(key_ref.dtype)
    value_ref[...] = v_ref[...].astype(value_ref.dtype)


def exchange_project(values, near_pieces, w_query, w_key, w_value, place_t, cosine, sines,
                     axis, count, gather_axis, collective):
    unused_item, token_count, piece_width = near_pieces.shape
    vmem = pl.BlockSpec(memory_space=pltpu.VMEM)
    return pl.pallas_call(
        lambda *refs: exchange_project_kernel(axis, count, gather_axis, *refs),
        out_shape=(
            jax.ShapeDtypeStruct((token_count, w_query.shape[1]), jnp.bfloat16),
            jax.ShapeDtypeStruct((token_count, w_key.shape[1]), jnp.bfloat16),
            jax.ShapeDtypeStruct((token_count, w_value.shape[1]), jnp.bfloat16),
        ),
        in_specs=[vmem, vmem, pl.BlockSpec(memory_space=pl.ANY), vmem, vmem, vmem, vmem, vmem],
        out_specs=(vmem, vmem, vmem),
        scratch_shapes=[
            pltpu.VMEM(values.shape, values.dtype),
            pltpu.VMEM((token_count, w_query.shape[1]), jnp.float32),
            pltpu.VMEM((token_count, w_key.shape[1]), jnp.float32),
            pltpu.VMEM((token_count, w_value.shape[1]), jnp.float32),
            pltpu.VMEM((token_count, piece_width), near_pieces.dtype),
            pltpu.VMEM(near_pieces.shape, near_pieces.dtype),
            pltpu.VMEM((token_count, piece_width), near_pieces.dtype),
            pltpu.VMEM((2, piece_width, w_query.shape[1]), w_query.dtype),
            pltpu.SemaphoreType.DMA((count,)),
            pltpu.SemaphoreType.DMA((count,)),
            pltpu.SemaphoreType.DMA(()),
            pltpu.SemaphoreType.DMA((2,)),
            pltpu.SemaphoreType.DMA((2,)),
            pltpu.SemaphoreType.DMA((2,)),
            pltpu.SemaphoreType.DMA((2,)),
            pltpu.SemaphoreType.DMA((2,)),
        ],
        compiler_params=pltpu.CompilerParams(
            collective_id=collective, has_side_effects=True, vmem_limit_bytes=60 * 1024 * 1024
        ),
    )(values, near_pieces, w_query, w_key, w_value, place_t, cosine, sines)


def sum_kernel(axis, count, part_ref, total_ref, held, first_send, first_recv, second_send, second_recv):
    me = lax.axis_index(axis)
    barrier = pltpu.get_barrier_semaphore()
    for offset in range(1, count):
        peer = lax.rem(me + offset, count)
        pl.semaphore_signal(barrier, inc=1, device_id={axis: peer}, device_id_type=MESH)
    pl.semaphore_wait(barrier, count - 1)
    outgoing = []
    for offset in range(1, count):
        peer = lax.rem(me + offset, count)
        copy = pltpu.make_async_remote_copy(
            src_ref=part_ref.at[peer],
            dst_ref=held.at[me],
            send_sem=first_send.at[offset],
            recv_sem=first_recv.at[offset],
            device_id={axis: peer},
            device_id_type=MESH,
        )
        copy.start()
        outgoing.append(copy)
    held[me] = part_ref[me]
    for offset in range(1, count):
        outgoing[offset - 1].wait_send()
        source = lax.rem(me + count - offset, count)
        incoming = pltpu.make_async_remote_copy(
            src_ref=part_ref.at[source],
            dst_ref=held.at[source],
            send_sem=first_send.at[offset],
            recv_sem=first_recv.at[offset],
            device_id={axis: source},
            device_id_type=MESH,
        )
        incoming.wait_recv()
    total = held[0]
    for index in range(1, count):
        total = total + held[index]
    total_ref[me] = total.astype(total_ref.dtype)
    outgoing = []
    for offset in range(1, count):
        peer = lax.rem(me + offset, count)
        copy = pltpu.make_async_remote_copy(
            src_ref=total_ref.at[me],
            dst_ref=total_ref.at[me],
            send_sem=second_send.at[offset],
            recv_sem=second_recv.at[offset],
            device_id={axis: peer},
            device_id_type=MESH,
        )
        copy.start()
        outgoing.append(copy)
    for offset in range(1, count):
        outgoing[offset - 1].wait_send()
        source = lax.rem(me + count - offset, count)
        incoming = pltpu.make_async_remote_copy(
            src_ref=total_ref.at[source],
            dst_ref=total_ref.at[source],
            send_sem=second_send.at[offset],
            recv_sem=second_recv.at[offset],
            device_id={axis: source},
            device_id_type=MESH,
        )
        incoming.wait_recv()


def axis_sum(values, axis, count, collective, out_dtype):
    chunks = values.reshape(count, -1, 128)
    summed = pl.pallas_call(
        lambda *refs: sum_kernel(axis, count, *refs),
        out_shape=jax.ShapeDtypeStruct(chunks.shape, out_dtype),
        in_specs=[pl.BlockSpec(memory_space=pltpu.VMEM)],
        out_specs=pl.BlockSpec(memory_space=pltpu.VMEM),
        scratch_shapes=[
            pltpu.VMEM(chunks.shape, values.dtype),
            pltpu.SemaphoreType.DMA((count,)),
            pltpu.SemaphoreType.DMA((count,)),
            pltpu.SemaphoreType.DMA((count,)),
            pltpu.SemaphoreType.DMA((count,)),
        ],
        compiler_params=pltpu.CompilerParams(collective_id=collective, has_side_effects=True),
    )(chunks)
    return summed.reshape(values.shape)


def owner_adapter_term(received, slot_ids, down_local, up_local):
    sources, rows, part_width = received.shape
    local_adapters, unused_item, adapter_rank = down_local.shape
    query_width = up_local.shape[2]
    token_rows = received.reshape(sources * rows, part_width)
    every_down = jnp.einsum(
        "td,adr->tar", token_rows, down_local, preferred_element_type=jnp.float32
    )
    pick = slot_ids.reshape(sources * rows)[:, None] == jnp.arange(local_adapters, dtype=jnp.int32)[None, :]
    partial_value_sum = jnp.sum(jnp.where(pick[:, :, None], every_down, 0.0), axis=1)
    tp_count = lax.axis_size("tp")
    summed = axis_sum(partial_value_sum.reshape(-1, 128), "tp", tp_count, 2, jnp.bfloat16)
    adapter_middle = summed.reshape(sources * rows, adapter_rank)
    spread_rows = jnp.where(pick[:, :, None], adapter_middle[:, None, :], jnp.zeros((), jnp.bfloat16))
    spread_rows = spread_rows.reshape(sources * rows, local_adapters * adapter_rank)
    adapter_output = jnp.dot(
        spread_rows,
        up_local.reshape(local_adapters * adapter_rank, query_width),
        preferred_element_type=jnp.float32,
    ).astype(jnp.bfloat16)
    return adapter_output.reshape(sources, rows, query_width)


def body(
    tokens,
    adapter_id,
    pool_slot,
    lengths,
    w_query,
    w_key,
    w_value,
    pooled_down_weights,
    pool_up,
    cache_key,
    cache_value,
):
    group_count = lax.axis_size("grp")
    tp_count = lax.axis_size("tp")
    row_count, step_count, part_width = tokens.shape
    local_adapter_rows, unused_item, adapter_rank = pooled_down_weights.shape
    query_width = w_query.shape[1]
    kv_width = w_key.shape[1]
    kv_local = kv_width // HD
    q_local = query_width // HD
    group_size = q_local // kv_local
    count_of_tokens = row_count * step_count
    adapter_span = jnp.arange(pool_slot.shape[0], dtype=jnp.int32)
    pool_pos = jnp.sum(
        jnp.where(adapter_id[:, None] == adapter_span[None, :], pool_slot[None, :], 0), axis=1
    )
    owner_grp = pool_pos // local_adapter_rows
    local_slot = pool_pos % local_adapter_rows
    row_span = jnp.arange(row_count, dtype=jnp.int32)
    same_owner = (owner_grp[:, None] == owner_grp[None, :]) & (row_span[None, :] < row_span[:, None])
    owner_rank = jnp.sum(same_owner.astype(jnp.int32), axis=1)
    send_slot = owner_grp * CAP + owner_rank
    slot_span = jnp.arange(group_count * CAP, dtype=jnp.int32)
    place = (slot_span[:, None] == send_slot[None, :]).astype(jnp.bfloat16)
    token_slot = (send_slot[:, None] * step_count + jnp.arange(step_count, dtype=jnp.int32)[None, :]).reshape(-1)
    token_span = jnp.arange(group_count * CAP * step_count, dtype=jnp.int32)
    place_tokens = (token_span[:, None] == token_slot[None, :]).astype(jnp.bfloat16)
    token_rows = tokens.reshape(count_of_tokens, part_width)
    send_tokens = jnp.dot(place_tokens, token_rows, preferred_element_type=jnp.float32).astype(jnp.bfloat16)
    send_tokens = send_tokens.reshape(group_count, CAP * step_count, part_width)
    send_ids = jnp.dot(
        place, local_slot.astype(jnp.bfloat16)[:, None], preferred_element_type=jnp.float32
    ).astype(jnp.bfloat16)
    send_ids = jnp.broadcast_to(send_ids.reshape(group_count, CAP, 1), (group_count, CAP, 128))
    send_ids = jnp.concatenate([send_ids, jnp.zeros_like(send_ids)], axis=1)
    (got_tokens, got_ids), chip_pieces = exchange_ring(
        (send_tokens, send_ids), token_rows, "grp", group_count, "tp", 0
    )
    got_ids = jnp.repeat(got_ids[:, :CAP, 0].astype(jnp.int32), step_count, axis=1)
    owner_out = owner_adapter_term(got_tokens, got_ids, pooled_down_weights, pool_up)
    position = lengths[:, None] + jnp.arange(step_count, dtype=jnp.int32)[None, :]
    half_width = HD // 2
    inv_freq = jnp.exp(
        jnp.arange(half_width, dtype=jnp.float32) * (-2.0 * math.log(rope_base) / HD)
    )
    angles = position.reshape(count_of_tokens).astype(jnp.float32)[:, None] * inv_freq
    cosine = jnp.concatenate([jnp.cos(angles), jnp.cos(angles)], axis=1)
    sines = jnp.concatenate([-jnp.sin(angles), jnp.sin(angles)], axis=1)
    queries, key_new, value_new = exchange_project(
        owner_out, chip_pieces, w_query, w_key, w_value, jnp.transpose(place_tokens), cosine, sines,
        "grp", group_count, "tp", 1
    )
    queries = queries.reshape(row_count, step_count, kv_local, group_size, HD)
    key_new = key_new.reshape(row_count, step_count, kv_local, HD)
    value_new = value_new.reshape(row_count, step_count, kv_local, HD)
    cache_keys = cache_key.reshape(row_count, cache_key.shape[1], kv_local, HD)
    cache_values = cache_value.reshape(row_count, cache_value.shape[1], kv_local, HD)
    combined = attend(queries, key_new, value_new, cache_keys, cache_values, lengths)
    return combined.reshape(row_count, step_count, query_width)


def solution(mesh):
    in_specs = (
        P("grp", None, "tp"),
        P("grp"),
        P(),
        P("grp"),
        P(None, "tp"),
        P(None, "tp"),
        P(None, "tp"),
        P("grp", "tp", None),
        P("grp", None, "tp"),
        P("grp", None, "tp"),
        P("grp", None, "tp"),
    )
    out_specs = P("grp", None, "tp")
    return jax.shard_map(body, mesh=mesh, in_specs=in_specs, out_specs=out_specs, check_vma=False)
```

```python
import math

import jax
import jax.numpy as jnp
from jax import lax
from jax.experimental import pallas as pl
from jax.experimental.pallas import tpu as pltpu
from jax.sharding import PartitionSpec as P

MESH = pl.DeviceIdType.MESH

HD = 128
CAP = 8


rope_base = 500000.0


def rotate(values, position):
    half_width = values.shape[-1] // 2
    inv_freq = jnp.exp(
        jnp.arange(half_width, dtype=jnp.float32) * (-2.0 * math.log(rope_base) / values.shape[-1])
    )
    angles = position.astype(jnp.float32)[:, :, None, None] * inv_freq
    cosine = jnp.cos(angles)
    sines = jnp.sin(angles)
    front_half = values[..., :half_width]
    back_half = values[..., half_width:]
    return jnp.concatenate(
        [front_half * cosine - back_half * sines, back_half * cosine + front_half * sines], axis=-1
    )


def attend(queries, key_new, value_new, cache_key, cache_value, lengths):
    score_scale = 1.0 / math.sqrt(queries.shape[-1])
    cached = (
        jnp.einsum("rskgd,rlkd->rskgl", queries, cache_key, preferred_element_type=jnp.float32)
        * score_scale
    )
    fresh_keys = jnp.transpose(key_new, (0, 2, 1, 3)).astype(jnp.float32)
    fresh_scores = (
        jnp.sum(
            queries.astype(jnp.float32)[:, :, :, :, None, :] * fresh_keys[:, None, :, None, :, :],
            axis=-1,
        )
        * score_scale
    )
    live_mask = jnp.arange(cache_key.shape[1], dtype=jnp.int32)[None, :] < lengths[:, None]
    cached = jnp.where(live_mask[:, None, None, None, :], cached, -1e30)
    steps_here = key_new.shape[1]
    causal = (
        jnp.arange(steps_here, dtype=jnp.int32)[:, None]
        >= jnp.arange(steps_here, dtype=jnp.int32)[None, :]
    )
    fresh_scores = jnp.where(causal[None, :, None, None, :], fresh_scores, -1e30)
    row_max = jnp.maximum(jnp.max(cached, axis=-1), jnp.max(fresh_scores, axis=-1))
    cache_exp = jnp.exp(cached - row_max[..., None])
    fresh_exp = jnp.exp(fresh_scores - row_max[..., None])
    weight_sum = jnp.sum(cache_exp, axis=-1) + jnp.sum(fresh_exp, axis=-1)
    cache_weights = (cache_exp / weight_sum[..., None]).astype(jnp.bfloat16)
    fresh_weights = (fresh_exp / weight_sum[..., None]).astype(jnp.bfloat16)
    combined = jnp.einsum(
        "rskgl,rlkd->rskgd", cache_weights, cache_value, preferred_element_type=jnp.float32
    )
    fresh_values = jnp.transpose(value_new, (0, 2, 1, 3)).astype(jnp.float32)
    combined = combined + jnp.sum(
        fresh_weights.astype(jnp.float32)[..., None] * fresh_values[:, None, :, None, :, :],
        axis=4,
    )
    return combined.astype(jnp.bfloat16)


TORUS_ORDER = (
    (0, 1), (1, 0), (0, 3), (3, 0), (1, 1), (3, 3), (1, 3), (3, 1),
    (0, 2), (2, 0), (2, 1), (1, 2), (2, 3), (3, 2), (2, 2),
)


def peer_offsets(count):
    if count == 16:
        def shifted(me, dz, dy):
            return lax.rem(me // 4 + dz, 4) * 4 + lax.rem(lax.rem(me, 4) + dy, 4)

        return [
            (lambda me, a=dz, b=dy: shifted(me, a, b), lambda me, a=dz, b=dy: shifted(me, 4 - a, 4 - b))
            for dz, dy in TORUS_ORDER
        ]
    return [
        (lambda me, d=offset: lax.rem(me + d, count), lambda me, d=offset: lax.rem(me + count - d, count))
        for offset in range(1, count)
    ]


def exchange_kernel(axis, count, arrays, *refs):
    send_refs = refs[:arrays]
    got_refs = refs[arrays : 2 * arrays]
    send_sem, recv_sem, local_sem = refs[2 * arrays :]
    me = lax.axis_index(axis)
    barrier = pltpu.get_barrier_semaphore()
    offsets = peer_offsets(count)
    for offset in range(1, count):
        peer = offsets[offset - 1][0](me)
        pl.semaphore_signal(barrier, inc=1, device_id={axis: peer}, device_id_type=MESH)
    pl.semaphore_wait(barrier, count - 1)
    locals_ = []
    for which in range(arrays):
        local = pltpu.make_async_copy(
            send_refs[which].at[me], got_refs[which].at[me], local_sem.at[which]
        )
        local.start()
        locals_.append(local)
    outgoing = []
    for offset in range(1, count):
        peer = offsets[offset - 1][0](me)
        for which in range(arrays):
            copy = pltpu.make_async_remote_copy(
                src_ref=send_refs[which].at[peer],
                dst_ref=got_refs[which].at[me],
                send_sem=send_sem.at[which, offset],
                recv_sem=recv_sem.at[which, offset],
                device_id={axis: peer},
                device_id_type=MESH,
            )
            copy.start()
            outgoing.append(copy)
    for offset in range(1, count):
        source = offsets[offset - 1][1](me)
        for which in range(arrays):
            outgoing[(offset - 1) * arrays + which].wait_send()
            incoming = pltpu.make_async_remote_copy(
                src_ref=send_refs[which].at[source],
                dst_ref=got_refs[which].at[source],
                send_sem=send_sem.at[which, offset],
                recv_sem=recv_sem.at[which, offset],
                device_id={axis: source},
                device_id_type=MESH,
            )
            incoming.wait_recv()
    for local in locals_:
        local.wait()


def exchange(values, axis, count, collective):
    arrays = len(values)
    vmem = pl.BlockSpec(memory_space=pltpu.VMEM)
    return pl.pallas_call(
        lambda *refs: exchange_kernel(axis, count, arrays, *refs),
        out_shape=tuple(jax.ShapeDtypeStruct(v.shape, v.dtype) for v in values),
        in_specs=[vmem] * arrays,
        out_specs=tuple([vmem] * arrays),
        scratch_shapes=[
            pltpu.SemaphoreType.DMA((arrays, count)),
            pltpu.SemaphoreType.DMA((arrays, count)),
            pltpu.SemaphoreType.DMA((arrays,)),
        ],
        compiler_params=pltpu.CompilerParams(collective_id=collective, has_side_effects=True),
    )(*values)


def exchange_ring_kernel(axis, count, gather_axis, arrays, *refs):
    send_refs = refs[:arrays]
    piece_ref = refs[arrays]
    got_refs = refs[arrays + 1 : 2 * arrays + 1]
    chip_pieces = refs[2 * arrays + 1]
    send_sem, recv_sem, local_sem, near_send, near_recv, piece_sem = refs[2 * arrays + 2 :]
    chips = lax.axis_size(gather_axis) // 2
    me = lax.axis_index(axis)
    mine = lax.axis_index(gather_axis)
    chip = mine // 2
    core = lax.rem(mine, 2)
    right_chip = lax.rem(chip + 1, chips)
    left_chip = lax.rem(chip + chips - 1, chips)
    right = right_chip * 2 + core
    left = left_chip * 2 + core

    barrier = pltpu.get_barrier_semaphore()
    offsets = peer_offsets(count)
    for offset in range(1, count):
        peer = offsets[offset - 1][0](me)
        pl.semaphore_signal(barrier, inc=1, device_id={axis: peer}, device_id_type=MESH)
    pl.semaphore_signal(barrier, inc=1, device_id={gather_axis: right}, device_id_type=MESH)
    pl.semaphore_signal(barrier, inc=1, device_id={gather_axis: left}, device_id_type=MESH)
    pl.semaphore_wait(barrier, count + 1)

    near = []
    for side, target in ((0, right), (1, left)):
        copy = pltpu.make_async_remote_copy(
            src_ref=piece_ref,
            dst_ref=chip_pieces.at[1 + side],
            send_sem=near_send.at[side],
            recv_sem=near_recv.at[side],
            device_id={gather_axis: target},
            device_id_type=MESH,
        )
        copy.start()
        near.append(copy)
    own_piece = pltpu.make_async_copy(piece_ref, chip_pieces.at[0], piece_sem)
    own_piece.start()

    locals_ = []
    for which in range(arrays):
        local = pltpu.make_async_copy(
            send_refs[which].at[me], got_refs[which].at[me], local_sem.at[which]
        )
        local.start()
        locals_.append(local)
    outgoing = []
    for offset in range(1, count):
        peer = offsets[offset - 1][0](me)
        for which in range(arrays):
            copy = pltpu.make_async_remote_copy(
                src_ref=send_refs[which].at[peer],
                dst_ref=got_refs[which].at[me],
                send_sem=send_sem.at[which, offset],
                recv_sem=recv_sem.at[which, offset],
                device_id={axis: peer},
                device_id_type=MESH,
            )
            copy.start()
            outgoing.append(copy)

    for side, source in ((0, left), (1, right)):
        near[side].wait_send()
        incoming = pltpu.make_async_remote_copy(
            src_ref=piece_ref,
            dst_ref=chip_pieces.at[1 + side],
            send_sem=near_send.at[side],
            recv_sem=near_recv.at[side],
            device_id={gather_axis: source},
            device_id_type=MESH,
        )
        incoming.wait_recv()

    for offset in range(1, count):
        source = offsets[offset - 1][1](me)
        for which in range(arrays):
            outgoing[(offset - 1) * arrays + which].wait_send()
            incoming = pltpu.make_async_remote_copy(
                src_ref=send_refs[which].at[source],
                dst_ref=got_refs[which].at[source],
                send_sem=send_sem.at[which, offset],
                recv_sem=recv_sem.at[which, offset],
                device_id={axis: source},
                device_id_type=MESH,
            )
            incoming.wait_recv()
    for local in locals_:
        local.wait()
    own_piece.wait()


def exchange_ring(values, piece, axis, count, gather_axis, collective):
    arrays = len(values)
    vmem = pl.BlockSpec(memory_space=pltpu.VMEM)
    outs = pl.pallas_call(
        lambda *refs: exchange_ring_kernel(axis, count, gather_axis, arrays, *refs),
        out_shape=tuple(jax.ShapeDtypeStruct(v.shape, v.dtype) for v in values)
        + (jax.ShapeDtypeStruct((3,) + piece.shape, piece.dtype),),
        in_specs=[vmem] * (arrays + 1),
        out_specs=tuple([vmem] * (arrays + 1)),
        scratch_shapes=[
            pltpu.SemaphoreType.DMA((arrays, count)),
            pltpu.SemaphoreType.DMA((arrays, count)),
            pltpu.SemaphoreType.DMA((arrays,)),
            pltpu.SemaphoreType.DMA((2,)),
            pltpu.SemaphoreType.DMA((2,)),
            pltpu.SemaphoreType.DMA(()),
        ],
        compiler_params=pltpu.CompilerParams(collective_id=collective, has_side_effects=True),
    )(*values, piece)
    return outs[:arrays], outs[arrays]


def exchange_project_kernel(
    axis, count, gather_axis, send_ref, near_pieces, wq_hbm, wk_ref, wv_ref,
    place_ref, cos_ref, sin_ref,
    queries_ref, key_ref, value_ref,
    got_ref, q_ref, k_ref, v_ref,
    far_piece, partner_near, partner_far, wq_buf, send_sem, recv_sem, local_sem, wq_sem,
    far_send, far_recv, partner_send, partner_recv,
):
    me = lax.axis_index(axis)
    mine = lax.axis_index(gather_axis)
    chips = lax.axis_size(gather_axis) // 2
    chip = mine // 2
    core = lax.rem(mine, 2)
    partner = chip * 2 + (1 - core)
    right = lax.rem(chip + 1, chips) * 2 + core
    left = lax.rem(chip + chips - 1, chips) * 2 + core
    half = far_piece.shape[0] // 2
    barrier = pltpu.get_barrier_semaphore()
    offsets = peer_offsets(count)
    for offset in range(1, count):
        peer = offsets[offset - 1][0](me)
        pl.semaphore_signal(barrier, inc=1, device_id={axis: peer}, device_id_type=MESH)
    for neighbour in (partner, right, left):
        pl.semaphore_signal(barrier, inc=1, device_id={gather_axis: neighbour}, device_id_type=MESH)
    pl.semaphore_wait(barrier, count + 2)

    far_out = []
    for side, slot, target, rows in ((0, 1, right, pl.ds(0, half)), (1, 2, left, pl.ds(half, half))):
        copy = pltpu.make_async_remote_copy(
            src_ref=near_pieces.at[slot, rows],
            dst_ref=far_piece.at[rows],
            send_sem=far_send.at[side],
            recv_sem=far_recv.at[side],
            device_id={gather_axis: target},
            device_id_type=MESH,
        )
        copy.start()
        far_out.append(copy)
    to_partner = pltpu.make_async_remote_copy(
        src_ref=near_pieces,
        dst_ref=partner_near,
        send_sem=partner_send.at[0],
        recv_sem=partner_recv.at[0],
        device_id={gather_axis: partner},
        device_id_type=MESH,
    )
    to_partner.start()
    local = pltpu.make_async_copy(send_ref.at[me], got_ref.at[me], local_sem)
    local.start()
    outgoing = []
    for offset in range(1, count):
        peer = offsets[offset - 1][0](me)
        copy = pltpu.make_async_remote_copy(
            src_ref=send_ref.at[peer],
            dst_ref=got_ref.at[me],
            send_sem=send_sem.at[offset],
            recv_sem=recv_sem.at[offset],
            device_id={axis: peer},
            device_id_type=MESH,
        )
        copy.start()
        outgoing.append(copy)

    piece_width = near_pieces.shape[2]
    chip_shift = (0, chips - 1, 1, 2)

    def piece_index(step):
        piece_core = core if step < 4 else 1 - core
        return lax.rem(chip + chip_shift[step % 4], chips) * 2 + piece_core

    def chunk_copy(step):
        index = piece_index(step)
        return pltpu.make_async_copy(
            wq_hbm.at[pl.ds(pl.multiple_of(index * piece_width, piece_width), piece_width)],
            wq_buf.at[step % 2],
            wq_sem.at[step % 2],
        )

    chunk_copy(0).start()
    q_ref[...] = jnp.zeros_like(q_ref)
    k_ref[...] = jnp.zeros_like(k_ref)
    v_ref[...] = jnp.zeros_like(v_ref)

    def project(step, piece):
        chunk_copy(step).wait()
        if step + 1 < 8:
            chunk_copy(step + 1).start()
        index = piece_index(step)
        rows = pl.ds(pl.multiple_of(index * piece_width, piece_width), piece_width)
        q_ref[...] += jnp.dot(piece, wq_buf[step % 2], preferred_element_type=jnp.float32)
        k_ref[...] += jnp.dot(piece, wk_ref[rows, :], preferred_element_type=jnp.float32)
        v_ref[...] += jnp.dot(piece, wv_ref[rows, :], preferred_element_type=jnp.float32)

    for step in range(3):
        project(step, near_pieces[step])
    for side, source, rows in ((0, left, pl.ds(0, half)), (1, right, pl.ds(half, half))):
        far_out[side].wait_send()
        incoming = pltpu.make_async_remote_copy(
            src_ref=near_pieces.at[1, rows],
            dst_ref=far_piece.at[rows],
            send_sem=far_send.at[side],
            recv_sem=far_recv.at[side],
            device_id={gather_axis: source},
            device_id_type=MESH,
        )
        incoming.wait_recv()
    far_to_partner = pltpu.make_async_remote_copy(
        src_ref=far_piece,
        dst_ref=partner_far,
        send_sem=partner_send.at[1],
        recv_sem=partner_recv.at[1],
        device_id={gather_axis: partner},
        device_id_type=MESH,
    )
    far_to_partner.start()
    project(3, far_piece[...])
    to_partner.wait_send()
    to_partner.wait_recv()
    for step in range(3):
        project(4 + step, partner_near[step])
    far_to_partner.wait_send()
    far_to_partner.wait_recv()
    project(7, partner_far[...])

    for offset in range(1, count):
        outgoing[offset - 1].wait_send()
        source = offsets[offset - 1][1](me)
        incoming = pltpu.make_async_remote_copy(
            src_ref=send_ref.at[source],
            dst_ref=got_ref.at[source],
            send_sem=send_sem.at[offset],
            recv_sem=recv_sem.at[offset],
            device_id={axis: source},
            device_id_type=MESH,
        )
        incoming.wait_recv()
    local.wait()

    slots, slot_rows, width = got_ref.shape
    adapter_rows = jnp.dot(
        place_ref[...], got_ref[...].reshape(slots * slot_rows, width),
        preferred_element_type=jnp.float32,
    )
    cosine = cos_ref[...]
    sines = sin_ref[...]
    half_turn = HD // 2

    def rotated(values):
        return values * cosine + pltpu.roll(values, half_turn, 1) * sines

    for head in range(width // HD):
        lanes = slice(head * HD, (head + 1) * HD)
        summed = q_ref[:, lanes] + adapter_rows[:, lanes]
        queries_ref[:, lanes] = rotated(summed).astype(queries_ref.dtype)
    for head in range(key_ref.shape[1] // HD):
        lanes = slice(head * HD, (head + 1) * HD)
        key_ref[:, lanes] = rotated(k_ref[:, lanes]).astype(key_ref.dtype)
    value_ref[...] = v_ref[...].astype(value_ref.dtype)


def exchange_project(values, near_pieces, w_query, w_key, w_value, place_t, cosine, sines,
                     axis, count, gather_axis, collective):
    unused_item, token_count, piece_width = near_pieces.shape
    vmem = pl.BlockSpec(memory_space=pltpu.VMEM)
    return pl.pallas_call(
        lambda *refs: exchange_project_kernel(axis, count, gather_axis, *refs),
        out_shape=(
            jax.ShapeDtypeStruct((token_count, w_query.shape[1]), jnp.bfloat16),
            jax.ShapeDtypeStruct((token_count, w_key.shape[1]), jnp.bfloat16),
            jax.ShapeDtypeStruct((token_count, w_value.shape[1]), jnp.bfloat16),
        ),
        in_specs=[vmem, vmem, pl.BlockSpec(memory_space=pl.ANY), vmem, vmem, vmem, vmem, vmem],
        out_specs=(vmem, vmem, vmem),
        scratch_shapes=[
            pltpu.VMEM(values.shape, values.dtype),
            pltpu.VMEM((token_count, w_query.shape[1]), jnp.float32),
            pltpu.VMEM((token_count, w_key.shape[1]), jnp.float32),
            pltpu.VMEM((token_count, w_value.shape[1]), jnp.float32),
            pltpu.VMEM((token_count, piece_width), near_pieces.dtype),
            pltpu.VMEM(near_pieces.shape, near_pieces.dtype),
            pltpu.VMEM((token_count, piece_width), near_pieces.dtype),
            pltpu.VMEM((2, piece_width, w_query.shape[1]), w_query.dtype),
            pltpu.SemaphoreType.DMA((count,)),
            pltpu.SemaphoreType.DMA((count,)),
            pltpu.SemaphoreType.DMA(()),
            pltpu.SemaphoreType.DMA((2,)),
            pltpu.SemaphoreType.DMA((2,)),
            pltpu.SemaphoreType.DMA((2,)),
            pltpu.SemaphoreType.DMA((2,)),
            pltpu.SemaphoreType.DMA((2,)),
        ],
        compiler_params=pltpu.CompilerParams(
            collective_id=collective, has_side_effects=True, vmem_limit_bytes=60 * 1024 * 1024
        ),
    )(values, near_pieces, w_query, w_key, w_value, place_t, cosine, sines)


def sum_kernel(axis, count, part_ref, total_ref, held, first_send, first_recv, second_send, second_recv):
    me = lax.axis_index(axis)
    barrier = pltpu.get_barrier_semaphore()
    for offset in range(1, count):
        peer = lax.rem(me + offset, count)
        pl.semaphore_signal(barrier, inc=1, device_id={axis: peer}, device_id_type=MESH)
    pl.semaphore_wait(barrier, count - 1)
    outgoing = []
    for offset in range(1, count):
        peer = lax.rem(me + offset, count)
        copy = pltpu.make_async_remote_copy(
            src_ref=part_ref.at[peer],
            dst_ref=held.at[me],
            send_sem=first_send.at[offset],
            recv_sem=first_recv.at[offset],
            device_id={axis: peer},
            device_id_type=MESH,
        )
        copy.start()
        outgoing.append(copy)
    held[me] = part_ref[me]
    for offset in range(1, count):
        outgoing[offset - 1].wait_send()
        source = lax.rem(me + count - offset, count)
        incoming = pltpu.make_async_remote_copy(
            src_ref=part_ref.at[source],
            dst_ref=held.at[source],
            send_sem=first_send.at[offset],
            recv_sem=first_recv.at[offset],
            device_id={axis: source},
            device_id_type=MESH,
        )
        incoming.wait_recv()
    total = held[0]
    for index in range(1, count):
        total = total + held[index]
    total_ref[me] = total.astype(total_ref.dtype)
    outgoing = []
    for offset in range(1, count):
        peer = lax.rem(me + offset, count)
        copy = pltpu.make_async_remote_copy(
            src_ref=total_ref.at[me],
            dst_ref=total_ref.at[me],
            send_sem=second_send.at[offset],
            recv_sem=second_recv.at[offset],
            device_id={axis: peer},
            device_id_type=MESH,
        )
        copy.start()
        outgoing.append(copy)
    for offset in range(1, count):
        outgoing[offset - 1].wait_send()
        source = lax.rem(me + count - offset, count)
        incoming = pltpu.make_async_remote_copy(
            src_ref=total_ref.at[source],
            dst_ref=total_ref.at[source],
            send_sem=second_send.at[offset],
            recv_sem=second_recv.at[offset],
            device_id={axis: source},
            device_id_type=MESH,
        )
        incoming.wait_recv()


def axis_sum(values, axis, count, collective, out_dtype):
    chunks = values.reshape(count, -1, 128)
    summed = pl.pallas_call(
        lambda *refs: sum_kernel(axis, count, *refs),
        out_shape=jax.ShapeDtypeStruct(chunks.shape, out_dtype),
        in_specs=[pl.BlockSpec(memory_space=pltpu.VMEM)],
        out_specs=pl.BlockSpec(memory_space=pltpu.VMEM),
        scratch_shapes=[
            pltpu.VMEM(chunks.shape, values.dtype),
            pltpu.SemaphoreType.DMA((count,)),
            pltpu.SemaphoreType.DMA((count,)),
            pltpu.SemaphoreType.DMA((count,)),
            pltpu.SemaphoreType.DMA((count,)),
        ],
        compiler_params=pltpu.CompilerParams(collective_id=collective, has_side_effects=True),
    )(chunks)
    return summed.reshape(values.shape)


def owner_adapter_term(received, slot_ids, down_local, up_local):
    sources, rows, part_width = received.shape
    local_adapters, unused_item, adapter_rank = down_local.shape
    query_width = up_local.shape[2]
    token_rows = received.reshape(sources * rows, part_width)
    every_down = jnp.einsum(
        "td,adr->tar", token_rows, down_local, preferred_element_type=jnp.float32
    )
    pick = slot_ids.reshape(sources * rows)[:, None] == jnp.arange(local_adapters, dtype=jnp.int32)[None, :]
    partial_value_sum = jnp.sum(jnp.where(pick[:, :, None], every_down, 0.0), axis=1)
    tp_count = lax.axis_size("tp")
    summed = axis_sum(partial_value_sum.reshape(-1, 128), "tp", tp_count, 2, jnp.bfloat16)
    adapter_middle = summed.reshape(sources * rows, adapter_rank)
    spread_rows = jnp.where(pick[:, :, None], adapter_middle[:, None, :], jnp.zeros((), jnp.bfloat16))
    spread_rows = spread_rows.reshape(sources * rows, local_adapters * adapter_rank)
    adapter_output = jnp.dot(
        spread_rows,
        up_local.reshape(local_adapters * adapter_rank, query_width),
        preferred_element_type=jnp.float32,
    ).astype(jnp.bfloat16)
    return adapter_output.reshape(sources, rows, query_width)


def body(
    tokens,
    adapter_id,
    pool_slot,
    lengths,
    w_query,
    w_key,
    w_value,
    pooled_down_weights,
    pool_up,
    cache_key,
    cache_value,
):
    group_count = lax.axis_size("grp")
    tp_count = lax.axis_size("tp")
    row_count, step_count, part_width = tokens.shape
    local_adapter_rows, unused_item, adapter_rank = pooled_down_weights.shape
    query_width = w_query.shape[1]
    kv_width = w_key.shape[1]
    kv_local = kv_width // HD
    q_local = query_width // HD
    group_size = q_local // kv_local
    count_of_tokens = row_count * step_count
    adapter_span = jnp.arange(pool_slot.shape[0], dtype=jnp.int32)
    pool_pos = jnp.sum(
        jnp.where(adapter_id[:, None] == adapter_span[None, :], pool_slot[None, :], 0), axis=1
    )
    owner_grp = pool_pos // local_adapter_rows
    local_slot = pool_pos % local_adapter_rows
    row_span = jnp.arange(row_count, dtype=jnp.int32)
    same_owner = (owner_grp[:, None] == owner_grp[None, :]) & (row_span[None, :] < row_span[:, None])
    owner_rank = jnp.sum(same_owner.astype(jnp.int32), axis=1)
    send_slot = owner_grp * CAP + owner_rank
    slot_span = jnp.arange(group_count * CAP, dtype=jnp.int32)
    place = (slot_span[:, None] == send_slot[None, :]).astype(jnp.bfloat16)
    token_slot = (send_slot[:, None] * step_count + jnp.arange(step_count, dtype=jnp.int32)[None, :]).reshape(-1)
    token_span = jnp.arange(group_count * CAP * step_count, dtype=jnp.int32)
    place_tokens = (token_span[:, None] == token_slot[None, :]).astype(jnp.bfloat16)
    token_rows = tokens.reshape(count_of_tokens, part_width)
    send_tokens = jnp.dot(place_tokens, token_rows, preferred_element_type=jnp.float32).astype(jnp.bfloat16)
    send_tokens = send_tokens.reshape(group_count, CAP * step_count, part_width)
    send_ids = jnp.dot(
        place, local_slot.astype(jnp.bfloat16)[:, None], preferred_element_type=jnp.float32
    ).astype(jnp.bfloat16)
    send_ids = jnp.broadcast_to(send_ids.reshape(group_count, CAP, 1), (group_count, CAP, 128))
    send_ids = jnp.concatenate([send_ids, jnp.zeros_like(send_ids)], axis=1)
    (got_tokens, got_ids), chip_pieces = exchange_ring(
        (send_tokens, send_ids), token_rows, "grp", group_count, "tp", 0
    )
    got_ids = jnp.repeat(got_ids[:, :CAP, 0].astype(jnp.int32), step_count, axis=1)
    owner_out = owner_adapter_term(got_tokens, got_ids, pooled_down_weights, pool_up)
    position = lengths[:, None] + jnp.arange(step_count, dtype=jnp.int32)[None, :]
    half_width = HD // 2
    inv_freq = jnp.exp(
        jnp.arange(half_width, dtype=jnp.float32) * (-2.0 * math.log(rope_base) / HD)
    )
    angles = position.reshape(count_of_tokens).astype(jnp.float32)[:, None] * inv_freq
    cosine = jnp.concatenate([jnp.cos(angles), jnp.cos(angles)], axis=1)
    sines = jnp.concatenate([-jnp.sin(angles), jnp.sin(angles)], axis=1)
    queries, key_new, value_new = exchange_project(
        owner_out, chip_pieces, w_query, w_key, w_value, jnp.transpose(place_tokens), cosine, sines,
        "grp", group_count, "tp", 1
    )
    queries = queries.reshape(row_count, step_count, kv_local, group_size, HD)
    key_new = key_new.reshape(row_count, step_count, kv_local, HD)
    value_new = value_new.reshape(row_count, step_count, kv_local, HD)
    cache_keys = cache_key.reshape(row_count, cache_key.shape[1], kv_local, HD)
    cache_values = cache_value.reshape(row_count, cache_value.shape[1], kv_local, HD)
    combined = attend(queries, key_new, value_new, cache_keys, cache_values, lengths)
    return combined.reshape(row_count, step_count, query_width)


def solution(mesh):
    in_specs = (
        P("grp", None, "tp"),
        P("grp"),
        P(),
        P("grp"),
        P(None, "tp"),
        P(None, "tp"),
        P(None, "tp"),
        P("grp", "tp", None),
        P("grp", None, "tp"),
        P("grp", None, "tp"),
        P("grp", None, "tp"),
    )
    out_specs = P("grp", None, "tp")
    return jax.shard_map(body, mesh=mesh, in_specs=in_specs, out_specs=out_specs, check_vma=False)
```

```python
import math

import jax
import jax.numpy as jnp
from jax import lax
from jax.experimental import pallas as pl
from jax.experimental.pallas import tpu as pltpu
from jax.sharding import PartitionSpec as P

MESH = pl.DeviceIdType.MESH

HD = 128
CAP = 8


rope_base = 500000.0


def rotate(values, position):
    half_width = values.shape[-1] // 2
    inv_freq = jnp.exp(
        jnp.arange(half_width, dtype=jnp.float32) * (-2.0 * math.log(rope_base) / values.shape[-1])
    )
    angles = position.astype(jnp.float32)[:, :, None, None] * inv_freq
    cosine = jnp.cos(angles)
    sines = jnp.sin(angles)
    front_half = values[..., :half_width]
    back_half = values[..., half_width:]
    return jnp.concatenate(
        [front_half * cosine - back_half * sines, back_half * cosine + front_half * sines], axis=-1
    )


def attend(queries, key_new, value_new, cache_key, cache_value, lengths):
    score_scale = 1.0 / math.sqrt(queries.shape[-1])
    cached = (
        jnp.einsum("rskgd,rlkd->rskgl", queries, cache_key, preferred_element_type=jnp.float32)
        * score_scale
    )
    fresh_keys = jnp.transpose(key_new, (0, 2, 1, 3)).astype(jnp.float32)
    fresh_scores = (
        jnp.sum(
            queries.astype(jnp.float32)[:, :, :, :, None, :] * fresh_keys[:, None, :, None, :, :],
            axis=-1,
        )
        * score_scale
    )
    live_mask = jnp.arange(cache_key.shape[1], dtype=jnp.int32)[None, :] < lengths[:, None]
    cached = jnp.where(live_mask[:, None, None, None, :], cached, -1e30)
    steps_here = key_new.shape[1]
    causal = (
        jnp.arange(steps_here, dtype=jnp.int32)[:, None]
        >= jnp.arange(steps_here, dtype=jnp.int32)[None, :]
    )
    fresh_scores = jnp.where(causal[None, :, None, None, :], fresh_scores, -1e30)
    row_max = jnp.maximum(jnp.max(cached, axis=-1), jnp.max(fresh_scores, axis=-1))
    cache_exp = jnp.exp(cached - row_max[..., None])
    fresh_exp = jnp.exp(fresh_scores - row_max[..., None])
    weight_sum = jnp.sum(cache_exp, axis=-1) + jnp.sum(fresh_exp, axis=-1)
    cache_weights = (cache_exp / weight_sum[..., None]).astype(jnp.bfloat16)
    fresh_weights = (fresh_exp / weight_sum[..., None]).astype(jnp.bfloat16)
    combined = jnp.einsum(
        "rskgl,rlkd->rskgd", cache_weights, cache_value, preferred_element_type=jnp.float32
    )
    combined = combined + jnp.einsum(
        "rskgt,rtkd->rskgd", fresh_weights, value_new, preferred_element_type=jnp.float32
    )
    return combined.astype(jnp.bfloat16)


TORUS_ORDER = (
    (0, 1), (1, 0), (0, 3), (3, 0), (1, 1), (3, 3), (1, 3), (3, 1),
    (0, 2), (2, 0), (2, 1), (1, 2), (2, 3), (3, 2), (2, 2),
)


def peer_offsets(count):
    if count == 16:
        def shifted(me, dz, dy):
            return lax.rem(me // 4 + dz, 4) * 4 + lax.rem(lax.rem(me, 4) + dy, 4)

        return [
            (lambda me, a=dz, b=dy: shifted(me, a, b), lambda me, a=dz, b=dy: shifted(me, 4 - a, 4 - b))
            for dz, dy in TORUS_ORDER
        ]
    return [
        (lambda me, d=offset: lax.rem(me + d, count), lambda me, d=offset: lax.rem(me + count - d, count))
        for offset in range(1, count)
    ]


def exchange_kernel(axis, count, arrays, *refs):
    send_refs = refs[:arrays]
    got_refs = refs[arrays : 2 * arrays]
    send_sem, recv_sem, local_sem = refs[2 * arrays :]
    me = lax.axis_index(axis)
    barrier = pltpu.get_barrier_semaphore()
    offsets = peer_offsets(count)
    for offset in range(1, count):
        peer = offsets[offset - 1][0](me)
        pl.semaphore_signal(barrier, inc=1, device_id={axis: peer}, device_id_type=MESH)
    pl.semaphore_wait(barrier, count - 1)
    locals_ = []
    for which in range(arrays):
        local = pltpu.make_async_copy(
            send_refs[which].at[me], got_refs[which].at[me], local_sem.at[which]
        )
        local.start()
        locals_.append(local)
    outgoing = []
    for offset in range(1, count):
        peer = offsets[offset - 1][0](me)
        for which in range(arrays):
            copy = pltpu.make_async_remote_copy(
                src_ref=send_refs[which].at[peer],
                dst_ref=got_refs[which].at[me],
                send_sem=send_sem.at[which, offset],
                recv_sem=recv_sem.at[which, offset],
                device_id={axis: peer},
                device_id_type=MESH,
            )
            copy.start()
            outgoing.append(copy)
    for offset in range(1, count):
        source = offsets[offset - 1][1](me)
        for which in range(arrays):
            outgoing[(offset - 1) * arrays + which].wait_send()
            incoming = pltpu.make_async_remote_copy(
                src_ref=send_refs[which].at[source],
                dst_ref=got_refs[which].at[source],
                send_sem=send_sem.at[which, offset],
                recv_sem=recv_sem.at[which, offset],
                device_id={axis: source},
                device_id_type=MESH,
            )
            incoming.wait_recv()
    for local in locals_:
        local.wait()


def exchange(values, axis, count, collective):
    arrays = len(values)
    vmem = pl.BlockSpec(memory_space=pltpu.VMEM)
    return pl.pallas_call(
        lambda *refs: exchange_kernel(axis, count, arrays, *refs),
        out_shape=tuple(jax.ShapeDtypeStruct(v.shape, v.dtype) for v in values),
        in_specs=[vmem] * arrays,
        out_specs=tuple([vmem] * arrays),
        scratch_shapes=[
            pltpu.SemaphoreType.DMA((arrays, count)),
            pltpu.SemaphoreType.DMA((arrays, count)),
            pltpu.SemaphoreType.DMA((arrays,)),
        ],
        compiler_params=pltpu.CompilerParams(collective_id=collective, has_side_effects=True),
    )(*values)


def exchange_ring_kernel(axis, count, gather_axis, arrays, *refs):
    send_refs = refs[:arrays]
    piece_ref = refs[arrays]
    got_refs = refs[arrays + 1 : 2 * arrays + 1]
    chip_pieces = refs[2 * arrays + 1]
    send_sem, recv_sem, local_sem, near_send, near_recv, piece_sem = refs[2 * arrays + 2 :]
    chips = lax.axis_size(gather_axis) // 2
    me = lax.axis_index(axis)
    mine = lax.axis_index(gather_axis)
    chip = mine // 2
    core = lax.rem(mine, 2)
    right_chip = lax.rem(chip + 1, chips)
    left_chip = lax.rem(chip + chips - 1, chips)
    right = right_chip * 2 + core
    left = left_chip * 2 + core

    barrier = pltpu.get_barrier_semaphore()
    offsets = peer_offsets(count)
    for offset in range(1, count):
        peer = offsets[offset - 1][0](me)
        pl.semaphore_signal(barrier, inc=1, device_id={axis: peer}, device_id_type=MESH)
    pl.semaphore_signal(barrier, inc=1, device_id={gather_axis: right}, device_id_type=MESH)
    pl.semaphore_signal(barrier, inc=1, device_id={gather_axis: left}, device_id_type=MESH)
    pl.semaphore_wait(barrier, count + 1)

    near = []
    for side, target in ((0, right), (1, left)):
        copy = pltpu.make_async_remote_copy(
            src_ref=piece_ref,
            dst_ref=chip_pieces.at[1 + side],
            send_sem=near_send.at[side],
            recv_sem=near_recv.at[side],
            device_id={gather_axis: target},
            device_id_type=MESH,
        )
        copy.start()
        near.append(copy)
    own_piece = pltpu.make_async_copy(piece_ref, chip_pieces.at[0], piece_sem)
    own_piece.start()

    locals_ = []
    for which in range(arrays):
        local = pltpu.make_async_copy(
            send_refs[which].at[me], got_refs[which].at[me], local_sem.at[which]
        )
        local.start()
        locals_.append(local)
    outgoing = []
    for offset in range(1, count):
        peer = offsets[offset - 1][0](me)
        for which in range(arrays):
            copy = pltpu.make_async_remote_copy(
                src_ref=send_refs[which].at[peer],
                dst_ref=got_refs[which].at[me],
                send_sem=send_sem.at[which, offset],
                recv_sem=recv_sem.at[which, offset],
                device_id={axis: peer},
                device_id_type=MESH,
            )
            copy.start()
            outgoing.append(copy)

    for side, source in ((0, left), (1, right)):
        near[side].wait_send()
        incoming = pltpu.make_async_remote_copy(
            src_ref=piece_ref,
            dst_ref=chip_pieces.at[1 + side],
            send_sem=near_send.at[side],
            recv_sem=near_recv.at[side],
            device_id={gather_axis: source},
            device_id_type=MESH,
        )
        incoming.wait_recv()

    for offset in range(1, count):
        source = offsets[offset - 1][1](me)
        for which in range(arrays):
            outgoing[(offset - 1) * arrays + which].wait_send()
            incoming = pltpu.make_async_remote_copy(
                src_ref=send_refs[which].at[source],
                dst_ref=got_refs[which].at[source],
                send_sem=send_sem.at[which, offset],
                recv_sem=recv_sem.at[which, offset],
                device_id={axis: source},
                device_id_type=MESH,
            )
            incoming.wait_recv()
    for local in locals_:
        local.wait()
    own_piece.wait()


def exchange_ring(values, piece, axis, count, gather_axis, collective):
    arrays = len(values)
    vmem = pl.BlockSpec(memory_space=pltpu.VMEM)
    outs = pl.pallas_call(
        lambda *refs: exchange_ring_kernel(axis, count, gather_axis, arrays, *refs),
        out_shape=tuple(jax.ShapeDtypeStruct(v.shape, v.dtype) for v in values)
        + (jax.ShapeDtypeStruct((3,) + piece.shape, piece.dtype),),
        in_specs=[vmem] * (arrays + 1),
        out_specs=tuple([vmem] * (arrays + 1)),
        scratch_shapes=[
            pltpu.SemaphoreType.DMA((arrays, count)),
            pltpu.SemaphoreType.DMA((arrays, count)),
            pltpu.SemaphoreType.DMA((arrays,)),
            pltpu.SemaphoreType.DMA((2,)),
            pltpu.SemaphoreType.DMA((2,)),
            pltpu.SemaphoreType.DMA(()),
        ],
        compiler_params=pltpu.CompilerParams(collective_id=collective, has_side_effects=True),
    )(*values, piece)
    return outs[:arrays], outs[arrays]


def exchange_project_kernel(
    axis, count, gather_axis, send_ref, near_pieces, wq_hbm, wk_ref, wv_ref,
    place_ref, cos_ref, sin_ref,
    queries_ref, key_ref, value_ref,
    got_ref, q_ref, k_ref, v_ref,
    far_piece, partner_near, partner_far, wq_buf, send_sem, recv_sem, local_sem, wq_sem,
    far_send, far_recv, partner_send, partner_recv,
):
    me = lax.axis_index(axis)
    mine = lax.axis_index(gather_axis)
    chips = lax.axis_size(gather_axis) // 2
    chip = mine // 2
    core = lax.rem(mine, 2)
    partner = chip * 2 + (1 - core)
    right = lax.rem(chip + 1, chips) * 2 + core
    left = lax.rem(chip + chips - 1, chips) * 2 + core
    half = far_piece.shape[0] // 2
    barrier = pltpu.get_barrier_semaphore()
    offsets = peer_offsets(count)
    for offset in range(1, count):
        peer = offsets[offset - 1][0](me)
        pl.semaphore_signal(barrier, inc=1, device_id={axis: peer}, device_id_type=MESH)
    for neighbour in (partner, right, left):
        pl.semaphore_signal(barrier, inc=1, device_id={gather_axis: neighbour}, device_id_type=MESH)
    pl.semaphore_wait(barrier, count + 2)

    far_out = []
    for side, slot, target, rows in ((0, 1, right, pl.ds(0, half)), (1, 2, left, pl.ds(half, half))):
        copy = pltpu.make_async_remote_copy(
            src_ref=near_pieces.at[slot, rows],
            dst_ref=far_piece.at[rows],
            send_sem=far_send.at[side],
            recv_sem=far_recv.at[side],
            device_id={gather_axis: target},
            device_id_type=MESH,
        )
        copy.start()
        far_out.append(copy)
    to_partner = pltpu.make_async_remote_copy(
        src_ref=near_pieces,
        dst_ref=partner_near,
        send_sem=partner_send.at[0],
        recv_sem=partner_recv.at[0],
        device_id={gather_axis: partner},
        device_id_type=MESH,
    )
    to_partner.start()
    local = pltpu.make_async_copy(send_ref.at[me], got_ref.at[me], local_sem)
    local.start()
    outgoing = []
    for offset in range(1, count):
        peer = offsets[offset - 1][0](me)
        copy = pltpu.make_async_remote_copy(
            src_ref=send_ref.at[peer],
            dst_ref=got_ref.at[me],
            send_sem=send_sem.at[offset],
            recv_sem=recv_sem.at[offset],
            device_id={axis: peer},
            device_id_type=MESH,
        )
        copy.start()
        outgoing.append(copy)

    piece_width = near_pieces.shape[2]
    chip_shift = (0, chips - 1, 1, 2)

    def piece_index(step):
        piece_core = core if step < 4 else 1 - core
        return lax.rem(chip + chip_shift[step % 4], chips) * 2 + piece_core

    def chunk_copy(step):
        index = piece_index(step)
        return pltpu.make_async_copy(
            wq_hbm.at[pl.ds(pl.multiple_of(index * piece_width, piece_width), piece_width)],
            wq_buf.at[step % 2],
            wq_sem.at[step % 2],
        )

    chunk_copy(0).start()
    q_ref[...] = jnp.zeros_like(q_ref)
    k_ref[...] = jnp.zeros_like(k_ref)
    v_ref[...] = jnp.zeros_like(v_ref)

    def project(step, piece):
        chunk_copy(step).wait()
        if step + 1 < 8:
            chunk_copy(step + 1).start()
        index = piece_index(step)
        rows = pl.ds(pl.multiple_of(index * piece_width, piece_width), piece_width)
        q_ref[...] += jnp.dot(piece, wq_buf[step % 2], preferred_element_type=jnp.float32)
        k_ref[...] += jnp.dot(piece, wk_ref[rows, :], preferred_element_type=jnp.float32)
        v_ref[...] += jnp.dot(piece, wv_ref[rows, :], preferred_element_type=jnp.float32)

    for step in range(3):
        project(step, near_pieces[step])
    for side, source, rows in ((0, left, pl.ds(0, half)), (1, right, pl.ds(half, half))):
        far_out[side].wait_send()
        incoming = pltpu.make_async_remote_copy(
            src_ref=near_pieces.at[1, rows],
            dst_ref=far_piece.at[rows],
            send_sem=far_send.at[side],
            recv_sem=far_recv.at[side],
            device_id={gather_axis: source},
            device_id_type=MESH,
        )
        incoming.wait_recv()
    far_to_partner = pltpu.make_async_remote_copy(
        src_ref=far_piece,
        dst_ref=partner_far,
        send_sem=partner_send.at[1],
        recv_sem=partner_recv.at[1],
        device_id={gather_axis: partner},
        device_id_type=MESH,
    )
    far_to_partner.start()
    project(3, far_piece[...])
    to_partner.wait_send()
    to_partner.wait_recv()
    for step in range(3):
        project(4 + step, partner_near[step])
    far_to_partner.wait_send()
    far_to_partner.wait_recv()
    project(7, partner_far[...])

    for offset in range(1, count):
        outgoing[offset - 1].wait_send()
        source = offsets[offset - 1][1](me)
        incoming = pltpu.make_async_remote_copy(
            src_ref=send_ref.at[source],
            dst_ref=got_ref.at[source],
            send_sem=send_sem.at[offset],
            recv_sem=recv_sem.at[offset],
            device_id={axis: source},
            device_id_type=MESH,
        )
        incoming.wait_recv()
    local.wait()

    slots, slot_rows, width = got_ref.shape
    adapter_rows = jnp.dot(
        place_ref[...], got_ref[...].reshape(slots * slot_rows, width),
        preferred_element_type=jnp.float32,
    )
    cosine = cos_ref[...]
    sines = sin_ref[...]
    half_turn = HD // 2

    def rotated(values):
        return values * cosine + pltpu.roll(values, half_turn, 1) * sines

    for head in range(width // HD):
        lanes = slice(head * HD, (head + 1) * HD)
        summed = q_ref[:, lanes] + adapter_rows[:, lanes]
        queries_ref[:, lanes] = rotated(summed).astype(queries_ref.dtype)
    for head in range(key_ref.shape[1] // HD):
        lanes = slice(head * HD, (head + 1) * HD)
        key_ref[:, lanes] = rotated(k_ref[:, lanes]).astype(key_ref.dtype)
    value_ref[...] = v_ref[...].astype(value_ref.dtype)


def exchange_project(values, near_pieces, w_query, w_key, w_value, place_t, cosine, sines,
                     axis, count, gather_axis, collective):
    unused_item, token_count, piece_width = near_pieces.shape
    vmem = pl.BlockSpec(memory_space=pltpu.VMEM)
    return pl.pallas_call(
        lambda *refs: exchange_project_kernel(axis, count, gather_axis, *refs),
        out_shape=(
            jax.ShapeDtypeStruct((token_count, w_query.shape[1]), jnp.bfloat16),
            jax.ShapeDtypeStruct((token_count, w_key.shape[1]), jnp.bfloat16),
            jax.ShapeDtypeStruct((token_count, w_value.shape[1]), jnp.bfloat16),
        ),
        in_specs=[vmem, vmem, pl.BlockSpec(memory_space=pl.ANY), vmem, vmem, vmem, vmem, vmem],
        out_specs=(vmem, vmem, vmem),
        scratch_shapes=[
            pltpu.VMEM(values.shape, values.dtype),
            pltpu.VMEM((token_count, w_query.shape[1]), jnp.float32),
            pltpu.VMEM((token_count, w_key.shape[1]), jnp.float32),
            pltpu.VMEM((token_count, w_value.shape[1]), jnp.float32),
            pltpu.VMEM((token_count, piece_width), near_pieces.dtype),
            pltpu.VMEM(near_pieces.shape, near_pieces.dtype),
            pltpu.VMEM((token_count, piece_width), near_pieces.dtype),
            pltpu.VMEM((2, piece_width, w_query.shape[1]), w_query.dtype),
            pltpu.SemaphoreType.DMA((count,)),
            pltpu.SemaphoreType.DMA((count,)),
            pltpu.SemaphoreType.DMA(()),
            pltpu.SemaphoreType.DMA((2,)),
            pltpu.SemaphoreType.DMA((2,)),
            pltpu.SemaphoreType.DMA((2,)),
            pltpu.SemaphoreType.DMA((2,)),
            pltpu.SemaphoreType.DMA((2,)),
        ],
        compiler_params=pltpu.CompilerParams(
            collective_id=collective, has_side_effects=True, vmem_limit_bytes=60 * 1024 * 1024
        ),
    )(values, near_pieces, w_query, w_key, w_value, place_t, cosine, sines)


def sum_kernel(axis, count, part_ref, total_ref, held, first_send, first_recv, second_send, second_recv):
    me = lax.axis_index(axis)
    barrier = pltpu.get_barrier_semaphore()
    for offset in range(1, count):
        peer = lax.rem(me + offset, count)
        pl.semaphore_signal(barrier, inc=1, device_id={axis: peer}, device_id_type=MESH)
    pl.semaphore_wait(barrier, count - 1)
    outgoing = []
    for offset in range(1, count):
        peer = lax.rem(me + offset, count)
        copy = pltpu.make_async_remote_copy(
            src_ref=part_ref.at[peer],
            dst_ref=held.at[me],
            send_sem=first_send.at[offset],
            recv_sem=first_recv.at[offset],
            device_id={axis: peer},
            device_id_type=MESH,
        )
        copy.start()
        outgoing.append(copy)
    held[me] = part_ref[me]
    for offset in range(1, count):
        outgoing[offset - 1].wait_send()
        source = lax.rem(me + count - offset, count)
        incoming = pltpu.make_async_remote_copy(
            src_ref=part_ref.at[source],
            dst_ref=held.at[source],
            send_sem=first_send.at[offset],
            recv_sem=first_recv.at[offset],
            device_id={axis: source},
            device_id_type=MESH,
        )
        incoming.wait_recv()
    total = held[0]
    for index in range(1, count):
        total = total + held[index]
    total_ref[me] = total.astype(total_ref.dtype)
    outgoing = []
    for offset in range(1, count):
        peer = lax.rem(me + offset, count)
        copy = pltpu.make_async_remote_copy(
            src_ref=total_ref.at[me],
            dst_ref=total_ref.at[me],
            send_sem=second_send.at[offset],
            recv_sem=second_recv.at[offset],
            device_id={axis: peer},
            device_id_type=MESH,
        )
        copy.start()
        outgoing.append(copy)
    for offset in range(1, count):
        outgoing[offset - 1].wait_send()
        source = lax.rem(me + count - offset, count)
        incoming = pltpu.make_async_remote_copy(
            src_ref=total_ref.at[source],
            dst_ref=total_ref.at[source],
            send_sem=second_send.at[offset],
            recv_sem=second_recv.at[offset],
            device_id={axis: source},
            device_id_type=MESH,
        )
        incoming.wait_recv()


def axis_sum(values, axis, count, collective, out_dtype):
    chunks = values.reshape(count, -1, values.shape[-1])
    summed = pl.pallas_call(
        lambda *refs: sum_kernel(axis, count, *refs),
        out_shape=jax.ShapeDtypeStruct(chunks.shape, out_dtype),
        in_specs=[pl.BlockSpec(memory_space=pltpu.VMEM)],
        out_specs=pl.BlockSpec(memory_space=pltpu.VMEM),
        scratch_shapes=[
            pltpu.VMEM(chunks.shape, values.dtype),
            pltpu.SemaphoreType.DMA((count,)),
            pltpu.SemaphoreType.DMA((count,)),
            pltpu.SemaphoreType.DMA((count,)),
            pltpu.SemaphoreType.DMA((count,)),
        ],
        compiler_params=pltpu.CompilerParams(collective_id=collective, has_side_effects=True),
    )(chunks)
    return summed.reshape(values.shape)


def owner_adapter_term(received, slot_ids, down_local, up_local):
    sources, rows, part_width = received.shape
    local_adapters, unused_item, adapter_rank = down_local.shape
    query_width = up_local.shape[2]
    token_rows = received.reshape(sources * rows, part_width)
    every_down = jnp.einsum(
        "td,adr->tar", token_rows, down_local, preferred_element_type=jnp.float32
    )
    pick = slot_ids.reshape(sources * rows)[:, None] == jnp.arange(local_adapters, dtype=jnp.int32)[None, :]
    partial_value_sum = jnp.sum(jnp.where(pick[:, :, None], every_down, 0.0), axis=1)
    tp_count = lax.axis_size("tp")
    summed = axis_sum(partial_value_sum, "tp", tp_count, 2, jnp.bfloat16)
    adapter_middle = summed.reshape(sources * rows, adapter_rank)
    spread_rows = jnp.where(pick[:, :, None], adapter_middle[:, None, :], jnp.zeros((), jnp.bfloat16))
    spread_rows = spread_rows.reshape(sources * rows, local_adapters * adapter_rank)
    adapter_output = jnp.dot(
        spread_rows,
        up_local.reshape(local_adapters * adapter_rank, query_width),
        preferred_element_type=jnp.float32,
    ).astype(jnp.bfloat16)
    return adapter_output.reshape(sources, rows, query_width)


def body(
    tokens,
    adapter_id,
    pool_slot,
    lengths,
    w_query,
    w_key,
    w_value,
    pooled_down_weights,
    pool_up,
    cache_key,
    cache_value,
):
    group_count = lax.axis_size("grp")
    tp_count = lax.axis_size("tp")
    row_count, step_count, part_width = tokens.shape
    local_adapter_rows, unused_item, adapter_rank = pooled_down_weights.shape
    query_width = w_query.shape[1]
    kv_width = w_key.shape[1]
    kv_local = kv_width // HD
    q_local = query_width // HD
    group_size = q_local // kv_local
    count_of_tokens = row_count * step_count
    adapter_span = jnp.arange(pool_slot.shape[0], dtype=jnp.int32)
    pool_pos = jnp.sum(
        jnp.where(adapter_id[:, None] == adapter_span[None, :], pool_slot[None, :], 0), axis=1
    )
    owner_grp = pool_pos // local_adapter_rows
    local_slot = pool_pos % local_adapter_rows
    row_span = jnp.arange(row_count, dtype=jnp.int32)
    same_owner = (owner_grp[:, None] == owner_grp[None, :]) & (row_span[None, :] < row_span[:, None])
    owner_rank = jnp.sum(same_owner.astype(jnp.int32), axis=1)
    send_slot = owner_grp * CAP + owner_rank
    slot_span = jnp.arange(group_count * CAP, dtype=jnp.int32)
    place = (slot_span[:, None] == send_slot[None, :]).astype(jnp.bfloat16)
    token_slot = (send_slot[:, None] * step_count + jnp.arange(step_count, dtype=jnp.int32)[None, :]).reshape(-1)
    token_span = jnp.arange(group_count * CAP * step_count, dtype=jnp.int32)
    place_tokens = (token_span[:, None] == token_slot[None, :]).astype(jnp.bfloat16)
    token_rows = tokens.reshape(count_of_tokens, part_width)
    send_tokens = jnp.dot(place_tokens, token_rows, preferred_element_type=jnp.float32).astype(jnp.bfloat16)
    send_tokens = send_tokens.reshape(group_count, CAP * step_count, part_width)
    send_ids = jnp.dot(
        place, local_slot.astype(jnp.bfloat16)[:, None], preferred_element_type=jnp.float32
    ).astype(jnp.bfloat16)
    send_ids = jnp.broadcast_to(send_ids.reshape(group_count, CAP, 1), (group_count, CAP, 128))
    send_ids = jnp.concatenate([send_ids, jnp.zeros_like(send_ids)], axis=1)
    (got_tokens, got_ids), chip_pieces = exchange_ring(
        (send_tokens, send_ids), token_rows, "grp", group_count, "tp", 0
    )
    got_ids = jnp.repeat(got_ids[:, :CAP, 0].astype(jnp.int32), step_count, axis=1)
    owner_out = owner_adapter_term(got_tokens, got_ids, pooled_down_weights, pool_up)
    position = lengths[:, None] + jnp.arange(step_count, dtype=jnp.int32)[None, :]
    half_width = HD // 2
    inv_freq = jnp.exp(
        jnp.arange(half_width, dtype=jnp.float32) * (-2.0 * math.log(rope_base) / HD)
    )
    angles = position.reshape(count_of_tokens).astype(jnp.float32)[:, None] * inv_freq
    cosine = jnp.concatenate([jnp.cos(angles), jnp.cos(angles)], axis=1)
    sines = jnp.concatenate([-jnp.sin(angles), jnp.sin(angles)], axis=1)
    queries, key_new, value_new = exchange_project(
        owner_out, chip_pieces, w_query, w_key, w_value, jnp.transpose(place_tokens), cosine, sines,
        "grp", group_count, "tp", 1
    )
    queries = queries.reshape(row_count, step_count, kv_local, group_size, HD)
    key_new = key_new.reshape(row_count, step_count, kv_local, HD)
    value_new = value_new.reshape(row_count, step_count, kv_local, HD)
    cache_keys = cache_key.reshape(row_count, cache_key.shape[1], kv_local, HD)
    cache_values = cache_value.reshape(row_count, cache_value.shape[1], kv_local, HD)
    combined = attend(queries, key_new, value_new, cache_keys, cache_values, lengths)
    return combined.reshape(row_count, step_count, query_width)


def solution(mesh):
    in_specs = (
        P("grp", None, "tp"),
        P("grp"),
        P(),
        P("grp"),
        P(None, "tp"),
        P(None, "tp"),
        P(None, "tp"),
        P("grp", "tp", None),
        P("grp", None, "tp"),
        P("grp", None, "tp"),
        P("grp", None, "tp"),
    )
    out_specs = P("grp", None, "tp")
    return jax.shard_map(body, mesh=mesh, in_specs=in_specs, out_specs=out_specs, check_vma=False)
```

```python
import math

import jax
import jax.numpy as jnp
from jax import lax
from jax.experimental import pallas as pl
from jax.experimental.pallas import tpu as pltpu
from jax.sharding import PartitionSpec as P

MESH = pl.DeviceIdType.MESH

HD = 128
CAP = 8


rope_base = 500000.0


def rotate(values, position):
    half_width = values.shape[-1] // 2
    inv_freq = jnp.exp(
        jnp.arange(half_width, dtype=jnp.float32) * (-2.0 * math.log(rope_base) / values.shape[-1])
    )
    angles = position.astype(jnp.float32)[:, :, None, None] * inv_freq
    cosine = jnp.cos(angles)
    sines = jnp.sin(angles)
    front_half = values[..., :half_width]
    back_half = values[..., half_width:]
    return jnp.concatenate(
        [front_half * cosine - back_half * sines, back_half * cosine + front_half * sines], axis=-1
    )


def attend(queries, key_new, value_new, cache_key, cache_value, lengths):
    score_scale = 1.0 / math.sqrt(queries.shape[-1])
    cached = (
        jnp.einsum("rskgd,rlkd->rskgl", queries, cache_key, preferred_element_type=jnp.float32)
        * score_scale
    )
    fresh_keys = jnp.transpose(key_new, (0, 2, 1, 3)).astype(jnp.float32)
    fresh_scores = (
        jnp.sum(
            queries.astype(jnp.float32)[:, :, :, :, None, :] * fresh_keys[:, None, :, None, :, :],
            axis=-1,
        )
        * score_scale
    )
    live_mask = jnp.arange(cache_key.shape[1], dtype=jnp.int32)[None, :] < lengths[:, None]
    cached = jnp.where(live_mask[:, None, None, None, :], cached, -1e30)
    steps_here = key_new.shape[1]
    causal = (
        jnp.arange(steps_here, dtype=jnp.int32)[:, None]
        >= jnp.arange(steps_here, dtype=jnp.int32)[None, :]
    )
    fresh_scores = jnp.where(causal[None, :, None, None, :], fresh_scores, -1e30)
    row_max = jnp.maximum(jnp.max(cached, axis=-1), jnp.max(fresh_scores, axis=-1))
    cache_exp = jnp.exp(cached - row_max[..., None])
    fresh_exp = jnp.exp(fresh_scores - row_max[..., None])
    weight_sum = jnp.sum(cache_exp, axis=-1) + jnp.sum(fresh_exp, axis=-1)
    cache_weights = (cache_exp / weight_sum[..., None]).astype(jnp.bfloat16)
    fresh_weights = (fresh_exp / weight_sum[..., None]).astype(jnp.bfloat16)
    combined = jnp.einsum(
        "rskgl,rlkd->rskgd", cache_weights, cache_value, preferred_element_type=jnp.float32
    )
    combined = combined + jnp.einsum(
        "rskgt,rtkd->rskgd", fresh_weights, value_new, preferred_element_type=jnp.float32
    )
    return combined.astype(jnp.bfloat16)


TORUS_ORDER = (
    (0, 1), (1, 0), (0, 3), (3, 0), (1, 1), (3, 3), (1, 3), (3, 1),
    (0, 2), (2, 0), (2, 1), (1, 2), (2, 3), (3, 2), (2, 2),
)


def peer_offsets(count):
    if count == 16:
        def shifted(me, dz, dy):
            return lax.rem(me // 4 + dz, 4) * 4 + lax.rem(lax.rem(me, 4) + dy, 4)

        return [
            (lambda me, a=dz, b=dy: shifted(me, a, b), lambda me, a=dz, b=dy: shifted(me, 4 - a, 4 - b))
            for dz, dy in TORUS_ORDER
        ]
    return [
        (lambda me, d=offset: lax.rem(me + d, count), lambda me, d=offset: lax.rem(me + count - d, count))
        for offset in range(1, count)
    ]


def exchange_kernel(axis, count, arrays, *refs):
    send_refs = refs[:arrays]
    got_refs = refs[arrays : 2 * arrays]
    send_sem, recv_sem, local_sem = refs[2 * arrays :]
    me = lax.axis_index(axis)
    barrier = pltpu.get_barrier_semaphore()
    offsets = peer_offsets(count)
    for offset in range(1, count):
        peer = offsets[offset - 1][0](me)
        pl.semaphore_signal(barrier, inc=1, device_id={axis: peer}, device_id_type=MESH)
    pl.semaphore_wait(barrier, count - 1)
    locals_ = []
    for which in range(arrays):
        local = pltpu.make_async_copy(
            send_refs[which].at[me], got_refs[which].at[me], local_sem.at[which]
        )
        local.start()
        locals_.append(local)
    outgoing = []
    for offset in range(1, count):
        peer = offsets[offset - 1][0](me)
        for which in range(arrays):
            copy = pltpu.make_async_remote_copy(
                src_ref=send_refs[which].at[peer],
                dst_ref=got_refs[which].at[me],
                send_sem=send_sem.at[which, offset],
                recv_sem=recv_sem.at[which, offset],
                device_id={axis: peer},
                device_id_type=MESH,
            )
            copy.start()
            outgoing.append(copy)
    for offset in range(1, count):
        source = offsets[offset - 1][1](me)
        for which in range(arrays):
            outgoing[(offset - 1) * arrays + which].wait_send()
            incoming = pltpu.make_async_remote_copy(
                src_ref=send_refs[which].at[source],
                dst_ref=got_refs[which].at[source],
                send_sem=send_sem.at[which, offset],
                recv_sem=recv_sem.at[which, offset],
                device_id={axis: source},
                device_id_type=MESH,
            )
            incoming.wait_recv()
    for local in locals_:
        local.wait()


def exchange(values, axis, count, collective):
    arrays = len(values)
    vmem = pl.BlockSpec(memory_space=pltpu.VMEM)
    return pl.pallas_call(
        lambda *refs: exchange_kernel(axis, count, arrays, *refs),
        out_shape=tuple(jax.ShapeDtypeStruct(v.shape, v.dtype) for v in values),
        in_specs=[vmem] * arrays,
        out_specs=tuple([vmem] * arrays),
        scratch_shapes=[
            pltpu.SemaphoreType.DMA((arrays, count)),
            pltpu.SemaphoreType.DMA((arrays, count)),
            pltpu.SemaphoreType.DMA((arrays,)),
        ],
        compiler_params=pltpu.CompilerParams(collective_id=collective, has_side_effects=True),
    )(*values)


def exchange_ring_kernel(axis, count, gather_axis, arrays, *refs):
    send_refs = refs[:arrays]
    piece_ref = refs[arrays]
    got_refs = refs[arrays + 1 : 2 * arrays + 1]
    chip_pieces = refs[2 * arrays + 1]
    send_sem, recv_sem, local_sem, near_send, near_recv, piece_sem = refs[2 * arrays + 2 :]
    chips = lax.axis_size(gather_axis) // 2
    me = lax.axis_index(axis)
    mine = lax.axis_index(gather_axis)
    chip = mine // 2
    core = lax.rem(mine, 2)
    right_chip = lax.rem(chip + 1, chips)
    left_chip = lax.rem(chip + chips - 1, chips)
    right = right_chip * 2 + core
    left = left_chip * 2 + core

    barrier = pltpu.get_barrier_semaphore()
    offsets = peer_offsets(count)
    for offset in range(1, count):
        peer = offsets[offset - 1][0](me)
        pl.semaphore_signal(barrier, inc=1, device_id={axis: peer}, device_id_type=MESH)
    pl.semaphore_signal(barrier, inc=1, device_id={gather_axis: right}, device_id_type=MESH)
    pl.semaphore_signal(barrier, inc=1, device_id={gather_axis: left}, device_id_type=MESH)
    pl.semaphore_wait(barrier, count + 1)

    locals_ = []
    for which in range(arrays):
        local = pltpu.make_async_copy(
            send_refs[which].at[me], got_refs[which].at[me], local_sem.at[which]
        )
        local.start()
        locals_.append(local)
    outgoing = []
    for offset in range(1, count):
        peer = offsets[offset - 1][0](me)
        for which in range(arrays):
            copy = pltpu.make_async_remote_copy(
                src_ref=send_refs[which].at[peer],
                dst_ref=got_refs[which].at[me],
                send_sem=send_sem.at[which, offset],
                recv_sem=recv_sem.at[which, offset],
                device_id={axis: peer},
                device_id_type=MESH,
            )
            copy.start()
            outgoing.append(copy)

    near = []
    for side, target in ((0, right), (1, left)):
        copy = pltpu.make_async_remote_copy(
            src_ref=piece_ref,
            dst_ref=chip_pieces.at[1 + side],
            send_sem=near_send.at[side],
            recv_sem=near_recv.at[side],
            device_id={gather_axis: target},
            device_id_type=MESH,
        )
        copy.start()
        near.append(copy)
    own_piece = pltpu.make_async_copy(piece_ref, chip_pieces.at[0], piece_sem)
    own_piece.start()


    for side, source in ((0, left), (1, right)):
        near[side].wait_send()
        incoming = pltpu.make_async_remote_copy(
            src_ref=piece_ref,
            dst_ref=chip_pieces.at[1 + side],
            send_sem=near_send.at[side],
            recv_sem=near_recv.at[side],
            device_id={gather_axis: source},
            device_id_type=MESH,
        )
        incoming.wait_recv()

    for offset in range(1, count):
        source = offsets[offset - 1][1](me)
        for which in range(arrays):
            outgoing[(offset - 1) * arrays + which].wait_send()
            incoming = pltpu.make_async_remote_copy(
                src_ref=send_refs[which].at[source],
                dst_ref=got_refs[which].at[source],
                send_sem=send_sem.at[which, offset],
                recv_sem=recv_sem.at[which, offset],
                device_id={axis: source},
                device_id_type=MESH,
            )
            incoming.wait_recv()
    for local in locals_:
        local.wait()
    own_piece.wait()


def exchange_ring(values, piece, axis, count, gather_axis, collective):
    arrays = len(values)
    vmem = pl.BlockSpec(memory_space=pltpu.VMEM)
    outs = pl.pallas_call(
        lambda *refs: exchange_ring_kernel(axis, count, gather_axis, arrays, *refs),
        out_shape=tuple(jax.ShapeDtypeStruct(v.shape, v.dtype) for v in values)
        + (jax.ShapeDtypeStruct((3,) + piece.shape, piece.dtype),),
        in_specs=[vmem] * (arrays + 1),
        out_specs=tuple([vmem] * (arrays + 1)),
        scratch_shapes=[
            pltpu.SemaphoreType.DMA((arrays, count)),
            pltpu.SemaphoreType.DMA((arrays, count)),
            pltpu.SemaphoreType.DMA((arrays,)),
            pltpu.SemaphoreType.DMA((2,)),
            pltpu.SemaphoreType.DMA((2,)),
            pltpu.SemaphoreType.DMA(()),
        ],
        compiler_params=pltpu.CompilerParams(collective_id=collective, has_side_effects=True),
    )(*values, piece)
    return outs[:arrays], outs[arrays]


def exchange_project_kernel(
    axis, count, gather_axis, send_ref, near_pieces, wq_hbm, wk_ref, wv_ref,
    place_ref, cos_ref, sin_ref,
    queries_ref, key_ref, value_ref,
    got_ref, q_ref, k_ref, v_ref,
    far_piece, partner_near, partner_far, wq_buf, send_sem, recv_sem, local_sem, wq_sem,
    far_send, far_recv, partner_send, partner_recv,
):
    me = lax.axis_index(axis)
    mine = lax.axis_index(gather_axis)
    chips = lax.axis_size(gather_axis) // 2
    chip = mine // 2
    core = lax.rem(mine, 2)
    partner = chip * 2 + (1 - core)
    right = lax.rem(chip + 1, chips) * 2 + core
    left = lax.rem(chip + chips - 1, chips) * 2 + core
    half = far_piece.shape[0] // 2
    barrier = pltpu.get_barrier_semaphore()
    offsets = peer_offsets(count)
    for offset in range(1, count):
        peer = offsets[offset - 1][0](me)
        pl.semaphore_signal(barrier, inc=1, device_id={axis: peer}, device_id_type=MESH)
    for neighbour in (partner, right, left):
        pl.semaphore_signal(barrier, inc=1, device_id={gather_axis: neighbour}, device_id_type=MESH)
    pl.semaphore_wait(barrier, count + 2)

    local = pltpu.make_async_copy(send_ref.at[me], got_ref.at[me], local_sem)
    local.start()
    outgoing = []
    for offset in range(1, count):
        peer = offsets[offset - 1][0](me)
        copy = pltpu.make_async_remote_copy(
            src_ref=send_ref.at[peer],
            dst_ref=got_ref.at[me],
            send_sem=send_sem.at[offset],
            recv_sem=recv_sem.at[offset],
            device_id={axis: peer},
            device_id_type=MESH,
        )
        copy.start()
        outgoing.append(copy)
    far_out = []
    for side, slot, target, rows in ((0, 1, right, pl.ds(0, half)), (1, 2, left, pl.ds(half, half))):
        copy = pltpu.make_async_remote_copy(
            src_ref=near_pieces.at[slot, rows],
            dst_ref=far_piece.at[rows],
            send_sem=far_send.at[side],
            recv_sem=far_recv.at[side],
            device_id={gather_axis: target},
            device_id_type=MESH,
        )
        copy.start()
        far_out.append(copy)
    to_partner = pltpu.make_async_remote_copy(
        src_ref=near_pieces,
        dst_ref=partner_near,
        send_sem=partner_send.at[0],
        recv_sem=partner_recv.at[0],
        device_id={gather_axis: partner},
        device_id_type=MESH,
    )
    to_partner.start()

    piece_width = near_pieces.shape[2]
    chip_shift = (0, chips - 1, 1, 2)

    def piece_index(step):
        piece_core = core if step < 4 else 1 - core
        return lax.rem(chip + chip_shift[step % 4], chips) * 2 + piece_core

    def chunk_copy(step):
        index = piece_index(step)
        return pltpu.make_async_copy(
            wq_hbm.at[pl.ds(pl.multiple_of(index * piece_width, piece_width), piece_width)],
            wq_buf.at[step % 2],
            wq_sem.at[step % 2],
        )

    chunk_copy(0).start()
    q_ref[...] = jnp.zeros_like(q_ref)
    k_ref[...] = jnp.zeros_like(k_ref)
    v_ref[...] = jnp.zeros_like(v_ref)

    def project(step, piece):
        chunk_copy(step).wait()
        if step + 1 < 8:
            chunk_copy(step + 1).start()
        index = piece_index(step)
        rows = pl.ds(pl.multiple_of(index * piece_width, piece_width), piece_width)
        q_ref[...] += jnp.dot(piece, wq_buf[step % 2], preferred_element_type=jnp.float32)
        k_ref[...] += jnp.dot(piece, wk_ref[rows, :], preferred_element_type=jnp.float32)
        v_ref[...] += jnp.dot(piece, wv_ref[rows, :], preferred_element_type=jnp.float32)

    for step in range(3):
        project(step, near_pieces[step])
    for side, source, rows in ((0, left, pl.ds(0, half)), (1, right, pl.ds(half, half))):
        far_out[side].wait_send()
        incoming = pltpu.make_async_remote_copy(
            src_ref=near_pieces.at[1, rows],
            dst_ref=far_piece.at[rows],
            send_sem=far_send.at[side],
            recv_sem=far_recv.at[side],
            device_id={gather_axis: source},
            device_id_type=MESH,
        )
        incoming.wait_recv()
    far_to_partner = pltpu.make_async_remote_copy(
        src_ref=far_piece,
        dst_ref=partner_far,
        send_sem=partner_send.at[1],
        recv_sem=partner_recv.at[1],
        device_id={gather_axis: partner},
        device_id_type=MESH,
    )
    far_to_partner.start()
    project(3, far_piece[...])
    to_partner.wait_send()
    to_partner.wait_recv()
    for step in range(3):
        project(4 + step, partner_near[step])
    far_to_partner.wait_send()
    far_to_partner.wait_recv()
    project(7, partner_far[...])

    for offset in range(1, count):
        outgoing[offset - 1].wait_send()
        source = offsets[offset - 1][1](me)
        incoming = pltpu.make_async_remote_copy(
            src_ref=send_ref.at[source],
            dst_ref=got_ref.at[source],
            send_sem=send_sem.at[offset],
            recv_sem=recv_sem.at[offset],
            device_id={axis: source},
            device_id_type=MESH,
        )
        incoming.wait_recv()
    local.wait()

    slots, slot_rows, width = got_ref.shape
    adapter_rows = jnp.dot(
        place_ref[...], got_ref[...].reshape(slots * slot_rows, width),
        preferred_element_type=jnp.float32,
    )
    cosine = cos_ref[...]
    sines = sin_ref[...]
    half_turn = HD // 2

    def rotated(values):
        return values * cosine + pltpu.roll(values, half_turn, 1) * sines

    for head in range(width // HD):
        lanes = slice(head * HD, (head + 1) * HD)
        summed = q_ref[:, lanes] + adapter_rows[:, lanes]
        queries_ref[:, lanes] = rotated(summed).astype(queries_ref.dtype)
    for head in range(key_ref.shape[1] // HD):
        lanes = slice(head * HD, (head + 1) * HD)
        key_ref[:, lanes] = rotated(k_ref[:, lanes]).astype(key_ref.dtype)
    value_ref[...] = v_ref[...].astype(value_ref.dtype)


def exchange_project(values, near_pieces, w_query, w_key, w_value, place_t, cosine, sines,
                     axis, count, gather_axis, collective):
    unused_item, token_count, piece_width = near_pieces.shape
    vmem = pl.BlockSpec(memory_space=pltpu.VMEM)
    return pl.pallas_call(
        lambda *refs: exchange_project_kernel(axis, count, gather_axis, *refs),
        out_shape=(
            jax.ShapeDtypeStruct((token_count, w_query.shape[1]), jnp.bfloat16),
            jax.ShapeDtypeStruct((token_count, w_key.shape[1]), jnp.bfloat16),
            jax.ShapeDtypeStruct((token_count, w_value.shape[1]), jnp.bfloat16),
        ),
        in_specs=[vmem, vmem, pl.BlockSpec(memory_space=pl.ANY), vmem, vmem, vmem, vmem, vmem],
        out_specs=(vmem, vmem, vmem),
        scratch_shapes=[
            pltpu.VMEM(values.shape, values.dtype),
            pltpu.VMEM((token_count, w_query.shape[1]), jnp.float32),
            pltpu.VMEM((token_count, w_key.shape[1]), jnp.float32),
            pltpu.VMEM((token_count, w_value.shape[1]), jnp.float32),
            pltpu.VMEM((token_count, piece_width), near_pieces.dtype),
            pltpu.VMEM(near_pieces.shape, near_pieces.dtype),
            pltpu.VMEM((token_count, piece_width), near_pieces.dtype),
            pltpu.VMEM((2, piece_width, w_query.shape[1]), w_query.dtype),
            pltpu.SemaphoreType.DMA((count,)),
            pltpu.SemaphoreType.DMA((count,)),
            pltpu.SemaphoreType.DMA(()),
            pltpu.SemaphoreType.DMA((2,)),
            pltpu.SemaphoreType.DMA((2,)),
            pltpu.SemaphoreType.DMA((2,)),
            pltpu.SemaphoreType.DMA((2,)),
            pltpu.SemaphoreType.DMA((2,)),
        ],
        compiler_params=pltpu.CompilerParams(
            collective_id=collective, has_side_effects=True, vmem_limit_bytes=60 * 1024 * 1024
        ),
    )(values, near_pieces, w_query, w_key, w_value, place_t, cosine, sines)


def sum_kernel(axis, count, part_ref, total_ref, held, first_send, first_recv, second_send, second_recv):
    me = lax.axis_index(axis)
    barrier = pltpu.get_barrier_semaphore()
    for offset in range(1, count):
        peer = lax.rem(me + offset, count)
        pl.semaphore_signal(barrier, inc=1, device_id={axis: peer}, device_id_type=MESH)
    pl.semaphore_wait(barrier, count - 1)
    outgoing = []
    for offset in range(1, count):
        peer = lax.rem(me + offset, count)
        copy = pltpu.make_async_remote_copy(
            src_ref=part_ref.at[peer],
            dst_ref=held.at[me],
            send_sem=first_send.at[offset],
            recv_sem=first_recv.at[offset],
            device_id={axis: peer},
            device_id_type=MESH,
        )
        copy.start()
        outgoing.append(copy)
    held[me] = part_ref[me]
    for offset in range(1, count):
        outgoing[offset - 1].wait_send()
        source = lax.rem(me + count - offset, count)
        incoming = pltpu.make_async_remote_copy(
            src_ref=part_ref.at[source],
            dst_ref=held.at[source],
            send_sem=first_send.at[offset],
            recv_sem=first_recv.at[offset],
            device_id={axis: source},
            device_id_type=MESH,
        )
        incoming.wait_recv()
    total = held[0]
    for index in range(1, count):
        total = total + held[index]
    total_ref[me] = total.astype(total_ref.dtype)
    outgoing = []
    for offset in range(1, count):
        peer = lax.rem(me + offset, count)
        copy = pltpu.make_async_remote_copy(
            src_ref=total_ref.at[me],
            dst_ref=total_ref.at[me],
            send_sem=second_send.at[offset],
            recv_sem=second_recv.at[offset],
            device_id={axis: peer},
            device_id_type=MESH,
        )
        copy.start()
        outgoing.append(copy)
    for offset in range(1, count):
        outgoing[offset - 1].wait_send()
        source = lax.rem(me + count - offset, count)
        incoming = pltpu.make_async_remote_copy(
            src_ref=total_ref.at[source],
            dst_ref=total_ref.at[source],
            send_sem=second_send.at[offset],
            recv_sem=second_recv.at[offset],
            device_id={axis: source},
            device_id_type=MESH,
        )
        incoming.wait_recv()


def axis_sum(values, axis, count, collective, out_dtype):
    chunks = values.reshape(count, -1, 128)
    summed = pl.pallas_call(
        lambda *refs: sum_kernel(axis, count, *refs),
        out_shape=jax.ShapeDtypeStruct(chunks.shape, out_dtype),
        in_specs=[pl.BlockSpec(memory_space=pltpu.VMEM)],
        out_specs=pl.BlockSpec(memory_space=pltpu.VMEM),
        scratch_shapes=[
            pltpu.VMEM(chunks.shape, values.dtype),
            pltpu.SemaphoreType.DMA((count,)),
            pltpu.SemaphoreType.DMA((count,)),
            pltpu.SemaphoreType.DMA((count,)),
            pltpu.SemaphoreType.DMA((count,)),
        ],
        compiler_params=pltpu.CompilerParams(collective_id=collective, has_side_effects=True),
    )(chunks)
    return summed.reshape(values.shape)


def owner_adapter_term(received, slot_ids, down_local, up_local):
    sources, rows, part_width = received.shape
    local_adapters, unused_item, adapter_rank = down_local.shape
    query_width = up_local.shape[2]
    token_rows = received.reshape(sources * rows, part_width)
    every_down = jnp.einsum(
        "td,adr->tar", token_rows, down_local, preferred_element_type=jnp.float32
    )
    pick = slot_ids.reshape(sources * rows)[:, None] == jnp.arange(local_adapters, dtype=jnp.int32)[None, :]
    partial_value_sum = jnp.sum(jnp.where(pick[:, :, None], every_down, 0.0), axis=1)
    tp_count = lax.axis_size("tp")
    summed = axis_sum(partial_value_sum.reshape(-1, 128), "tp", tp_count, 2, jnp.bfloat16)
    adapter_middle = summed.reshape(sources * rows, adapter_rank)
    spread_rows = jnp.where(pick[:, :, None], adapter_middle[:, None, :], jnp.zeros((), jnp.bfloat16))
    spread_rows = spread_rows.reshape(sources * rows, local_adapters * adapter_rank)
    adapter_output = jnp.dot(
        spread_rows,
        up_local.reshape(local_adapters * adapter_rank, query_width),
        preferred_element_type=jnp.float32,
    ).astype(jnp.bfloat16)
    return adapter_output.reshape(sources, rows, query_width)


def body(
    tokens,
    adapter_id,
    pool_slot,
    lengths,
    w_query,
    w_key,
    w_value,
    pooled_down_weights,
    pool_up,
    cache_key,
    cache_value,
):
    group_count = lax.axis_size("grp")
    tp_count = lax.axis_size("tp")
    row_count, step_count, part_width = tokens.shape
    local_adapter_rows, unused_item, adapter_rank = pooled_down_weights.shape
    query_width = w_query.shape[1]
    kv_width = w_key.shape[1]
    kv_local = kv_width // HD
    q_local = query_width // HD
    group_size = q_local // kv_local
    count_of_tokens = row_count * step_count
    adapter_span = jnp.arange(pool_slot.shape[0], dtype=jnp.int32)
    pool_pos = jnp.sum(
        jnp.where(adapter_id[:, None] == adapter_span[None, :], pool_slot[None, :], 0), axis=1
    )
    owner_grp = pool_pos // local_adapter_rows
    local_slot = pool_pos % local_adapter_rows
    row_span = jnp.arange(row_count, dtype=jnp.int32)
    same_owner = (owner_grp[:, None] == owner_grp[None, :]) & (row_span[None, :] < row_span[:, None])
    owner_rank = jnp.sum(same_owner.astype(jnp.int32), axis=1)
    send_slot = owner_grp * CAP + owner_rank
    slot_span = jnp.arange(group_count * CAP, dtype=jnp.int32)
    place = (slot_span[:, None] == send_slot[None, :]).astype(jnp.bfloat16)
    token_slot = (send_slot[:, None] * step_count + jnp.arange(step_count, dtype=jnp.int32)[None, :]).reshape(-1)
    token_span = jnp.arange(group_count * CAP * step_count, dtype=jnp.int32)
    place_tokens = (token_span[:, None] == token_slot[None, :]).astype(jnp.bfloat16)
    token_rows = tokens.reshape(count_of_tokens, part_width)
    send_tokens = jnp.dot(place_tokens, token_rows, preferred_element_type=jnp.float32).astype(jnp.bfloat16)
    send_tokens = send_tokens.reshape(group_count, CAP * step_count, part_width)
    send_ids = jnp.dot(
        place, local_slot.astype(jnp.bfloat16)[:, None], preferred_element_type=jnp.float32
    ).astype(jnp.bfloat16)
    send_ids = jnp.broadcast_to(send_ids.reshape(group_count, CAP, 1), (group_count, CAP, 128))
    send_ids = jnp.concatenate([send_ids, jnp.zeros_like(send_ids)], axis=1)
    (got_tokens, got_ids), chip_pieces = exchange_ring(
        (send_tokens, send_ids), token_rows, "grp", group_count, "tp", 0
    )
    got_ids = jnp.repeat(got_ids[:, :CAP, 0].astype(jnp.int32), step_count, axis=1)
    owner_out = owner_adapter_term(got_tokens, got_ids, pooled_down_weights, pool_up)
    position = lengths[:, None] + jnp.arange(step_count, dtype=jnp.int32)[None, :]
    half_width = HD // 2
    inv_freq = jnp.exp(
        jnp.arange(half_width, dtype=jnp.float32) * (-2.0 * math.log(rope_base) / HD)
    )
    angles = position.reshape(count_of_tokens).astype(jnp.float32)[:, None] * inv_freq
    cosine = jnp.concatenate([jnp.cos(angles), jnp.cos(angles)], axis=1)
    sines = jnp.concatenate([-jnp.sin(angles), jnp.sin(angles)], axis=1)
    queries, key_new, value_new = exchange_project(
        owner_out, chip_pieces, w_query, w_key, w_value, jnp.transpose(place_tokens), cosine, sines,
        "grp", group_count, "tp", 1
    )
    queries = queries.reshape(row_count, step_count, kv_local, group_size, HD)
    key_new = key_new.reshape(row_count, step_count, kv_local, HD)
    value_new = value_new.reshape(row_count, step_count, kv_local, HD)
    cache_keys = cache_key.reshape(row_count, cache_key.shape[1], kv_local, HD)
    cache_values = cache_value.reshape(row_count, cache_value.shape[1], kv_local, HD)
    combined = attend(queries, key_new, value_new, cache_keys, cache_values, lengths)
    return combined.reshape(row_count, step_count, query_width)


def solution(mesh):
    in_specs = (
        P("grp", None, "tp"),
        P("grp"),
        P(),
        P("grp"),
        P(None, "tp"),
        P(None, "tp"),
        P(None, "tp"),
        P("grp", "tp", None),
        P("grp", None, "tp"),
        P("grp", None, "tp"),
        P("grp", None, "tp"),
    )
    out_specs = P("grp", None, "tp")
    return jax.shard_map(body, mesh=mesh, in_specs=in_specs, out_specs=out_specs, check_vma=False)
```

```python
import math

import jax
import jax.numpy as jnp
from jax import lax
from jax.experimental import pallas as pl
from jax.experimental.pallas import tpu as pltpu
from jax.sharding import PartitionSpec as P

MESH = pl.DeviceIdType.MESH

HD = 128
CAP = 8


rope_base = 500000.0


def rotate(values, position):
    half_width = values.shape[-1] // 2
    inv_freq = jnp.exp(
        jnp.arange(half_width, dtype=jnp.float32) * (-2.0 * math.log(rope_base) / values.shape[-1])
    )
    angles = position.astype(jnp.float32)[:, :, None, None] * inv_freq
    cosine = jnp.cos(angles)
    sines = jnp.sin(angles)
    front_half = values[..., :half_width]
    back_half = values[..., half_width:]
    return jnp.concatenate(
        [front_half * cosine - back_half * sines, back_half * cosine + front_half * sines], axis=-1
    )


def attend(queries, key_new, value_new, cache_key, cache_value, lengths):
    score_scale = 1.0 / math.sqrt(queries.shape[-1])
    cached = (
        jnp.einsum("rskgd,rlkd->rskgl", queries, cache_key, preferred_element_type=jnp.float32)
        * score_scale
    )
    fresh_keys = jnp.transpose(key_new, (0, 2, 1, 3)).astype(jnp.float32)
    fresh_scores = (
        jnp.sum(
            queries.astype(jnp.float32)[:, :, :, :, None, :] * fresh_keys[:, None, :, None, :, :],
            axis=-1,
        )
        * score_scale
    )
    live_mask = jnp.arange(cache_key.shape[1], dtype=jnp.int32)[None, :] < lengths[:, None]
    cached = jnp.where(live_mask[:, None, None, None, :], cached, -1e30)
    steps_here = key_new.shape[1]
    causal = (
        jnp.arange(steps_here, dtype=jnp.int32)[:, None]
        >= jnp.arange(steps_here, dtype=jnp.int32)[None, :]
    )
    fresh_scores = jnp.where(causal[None, :, None, None, :], fresh_scores, -1e30)
    row_max = jnp.maximum(jnp.max(cached, axis=-1), jnp.max(fresh_scores, axis=-1))
    cache_exp = jnp.exp(cached - row_max[..., None])
    fresh_exp = jnp.exp(fresh_scores - row_max[..., None])
    weight_sum = jnp.sum(cache_exp, axis=-1) + jnp.sum(fresh_exp, axis=-1)
    cache_weights = (cache_exp / weight_sum[..., None]).astype(jnp.bfloat16)
    fresh_weights = (fresh_exp / weight_sum[..., None]).astype(jnp.bfloat16)
    combined = jnp.einsum(
        "rskgl,rlkd->rskgd", cache_weights, cache_value, preferred_element_type=jnp.float32
    )
    combined = combined + jnp.einsum(
        "rskgt,rtkd->rskgd", fresh_weights, value_new, preferred_element_type=jnp.float32
    )
    return combined.astype(jnp.bfloat16)


TORUS_ORDER = (
    (0, 1), (1, 0), (0, 3), (3, 0), (1, 1), (3, 3), (1, 3), (3, 1),
    (0, 2), (2, 0), (2, 1), (1, 2), (2, 3), (3, 2), (2, 2),
)


def peer_offsets(count):
    if count == 16:
        def shifted(me, dz, dy):
            return lax.rem(me // 4 + dz, 4) * 4 + lax.rem(lax.rem(me, 4) + dy, 4)

        return [
            (lambda me, a=dz, b=dy: shifted(me, a, b), lambda me, a=dz, b=dy: shifted(me, 4 - a, 4 - b))
            for dz, dy in TORUS_ORDER
        ]
    return [
        (lambda me, d=offset: lax.rem(me + d, count), lambda me, d=offset: lax.rem(me + count - d, count))
        for offset in range(1, count)
    ]


def exchange_kernel(axis, count, arrays, *refs):
    send_refs = refs[:arrays]
    got_refs = refs[arrays : 2 * arrays]
    send_sem, recv_sem, local_sem = refs[2 * arrays :]
    me = lax.axis_index(axis)
    barrier = pltpu.get_barrier_semaphore()
    offsets = peer_offsets(count)
    for offset in range(1, count):
        peer = offsets[offset - 1][0](me)
        pl.semaphore_signal(barrier, inc=1, device_id={axis: peer}, device_id_type=MESH)
    pl.semaphore_wait(barrier, count - 1)
    locals_ = []
    for which in range(arrays):
        local = pltpu.make_async_copy(
            send_refs[which].at[me], got_refs[which].at[me], local_sem.at[which]
        )
        local.start()
        locals_.append(local)
    outgoing = []
    for offset in range(1, count):
        peer = offsets[offset - 1][0](me)
        for which in range(arrays):
            copy = pltpu.make_async_remote_copy(
                src_ref=send_refs[which].at[peer],
                dst_ref=got_refs[which].at[me],
                send_sem=send_sem.at[which, offset],
                recv_sem=recv_sem.at[which, offset],
                device_id={axis: peer},
                device_id_type=MESH,
            )
            copy.start()
            outgoing.append(copy)
    for offset in range(1, count):
        source = offsets[offset - 1][1](me)
        for which in range(arrays):
            outgoing[(offset - 1) * arrays + which].wait_send()
            incoming = pltpu.make_async_remote_copy(
                src_ref=send_refs[which].at[source],
                dst_ref=got_refs[which].at[source],
                send_sem=send_sem.at[which, offset],
                recv_sem=recv_sem.at[which, offset],
                device_id={axis: source},
                device_id_type=MESH,
            )
            incoming.wait_recv()
    for local in locals_:
        local.wait()


def exchange(values, axis, count, collective):
    arrays = len(values)
    vmem = pl.BlockSpec(memory_space=pltpu.VMEM)
    return pl.pallas_call(
        lambda *refs: exchange_kernel(axis, count, arrays, *refs),
        out_shape=tuple(jax.ShapeDtypeStruct(v.shape, v.dtype) for v in values),
        in_specs=[vmem] * arrays,
        out_specs=tuple([vmem] * arrays),
        scratch_shapes=[
            pltpu.SemaphoreType.DMA((arrays, count)),
            pltpu.SemaphoreType.DMA((arrays, count)),
            pltpu.SemaphoreType.DMA((arrays,)),
        ],
        compiler_params=pltpu.CompilerParams(collective_id=collective, has_side_effects=True),
    )(*values)


def exchange_ring_kernel(axis, count, gather_axis, arrays, *refs):
    send_refs = refs[:arrays]
    piece_ref = refs[arrays]
    got_refs = refs[arrays + 1 : 2 * arrays + 1]
    chip_pieces = refs[2 * arrays + 1]
    send_sem, recv_sem, local_sem, near_send, near_recv, piece_sem = refs[2 * arrays + 2 :]
    chips = lax.axis_size(gather_axis) // 2
    me = lax.axis_index(axis)
    mine = lax.axis_index(gather_axis)
    chip = mine // 2
    core = lax.rem(mine, 2)
    right_chip = lax.rem(chip + 1, chips)
    left_chip = lax.rem(chip + chips - 1, chips)
    right = right_chip * 2 + core
    left = left_chip * 2 + core

    barrier = pltpu.get_barrier_semaphore()
    offsets = peer_offsets(count)
    for offset in range(1, count):
        peer = offsets[offset - 1][0](me)
        pl.semaphore_signal(barrier, inc=1, device_id={axis: peer}, device_id_type=MESH)
    pl.semaphore_signal(barrier, inc=1, device_id={gather_axis: right}, device_id_type=MESH)
    pl.semaphore_signal(barrier, inc=1, device_id={gather_axis: left}, device_id_type=MESH)
    pl.semaphore_wait(barrier, count + 1)

    near = []
    for side, target in ((0, right), (1, left)):
        copy = pltpu.make_async_remote_copy(
            src_ref=piece_ref,
            dst_ref=chip_pieces.at[1 + side],
            send_sem=near_send.at[side],
            recv_sem=near_recv.at[side],
            device_id={gather_axis: target},
            device_id_type=MESH,
        )
        copy.start()
        near.append(copy)
    own_piece = pltpu.make_async_copy(piece_ref, chip_pieces.at[0], piece_sem)
    own_piece.start()

    locals_ = []
    for which in range(arrays):
        local = pltpu.make_async_copy(
            send_refs[which].at[me], got_refs[which].at[me], local_sem.at[which]
        )
        local.start()
        locals_.append(local)
    outgoing = []
    for offset in range(1, count):
        peer = offsets[offset - 1][0](me)
        for which in range(arrays):
            copy = pltpu.make_async_remote_copy(
                src_ref=send_refs[which].at[peer],
                dst_ref=got_refs[which].at[me],
                send_sem=send_sem.at[which, offset],
                recv_sem=recv_sem.at[which, offset],
                device_id={axis: peer},
                device_id_type=MESH,
            )
            copy.start()
            outgoing.append(copy)

    for side, source in ((0, left), (1, right)):
        near[side].wait_send()
        incoming = pltpu.make_async_remote_copy(
            src_ref=piece_ref,
            dst_ref=chip_pieces.at[1 + side],
            send_sem=near_send.at[side],
            recv_sem=near_recv.at[side],
            device_id={gather_axis: source},
            device_id_type=MESH,
        )
        incoming.wait_recv()

    for offset in range(1, count):
        source = offsets[offset - 1][1](me)
        for which in range(arrays):
            outgoing[(offset - 1) * arrays + which].wait_send()
            incoming = pltpu.make_async_remote_copy(
                src_ref=send_refs[which].at[source],
                dst_ref=got_refs[which].at[source],
                send_sem=send_sem.at[which, offset],
                recv_sem=recv_sem.at[which, offset],
                device_id={axis: source},
                device_id_type=MESH,
            )
            incoming.wait_recv()
    for local in locals_:
        local.wait()
    own_piece.wait()


def exchange_ring(values, piece, axis, count, gather_axis, collective):
    arrays = len(values)
    vmem = pl.BlockSpec(memory_space=pltpu.VMEM)
    outs = pl.pallas_call(
        lambda *refs: exchange_ring_kernel(axis, count, gather_axis, arrays, *refs),
        out_shape=tuple(jax.ShapeDtypeStruct(v.shape, v.dtype) for v in values)
        + (jax.ShapeDtypeStruct((3,) + piece.shape, piece.dtype),),
        in_specs=[vmem] * (arrays + 1),
        out_specs=tuple([vmem] * (arrays + 1)),
        scratch_shapes=[
            pltpu.SemaphoreType.DMA((arrays, count)),
            pltpu.SemaphoreType.DMA((arrays, count)),
            pltpu.SemaphoreType.DMA((arrays,)),
            pltpu.SemaphoreType.DMA((2,)),
            pltpu.SemaphoreType.DMA((2,)),
            pltpu.SemaphoreType.DMA(()),
        ],
        compiler_params=pltpu.CompilerParams(collective_id=collective, has_side_effects=True),
    )(*values, piece)
    return outs[:arrays], outs[arrays]


def exchange_project_kernel(
    axis, count, gather_axis, send_ref, near_pieces, wq_hbm, wk_ref, wv_ref,
    place_ref, cos_ref, sin_ref,
    queries_ref, key_ref, value_ref,
    got_ref, q_ref, k_ref, v_ref,
    far_piece, partner_near, partner_far, wq_buf, send_sem, recv_sem, local_sem, wq_sem,
    far_send, far_recv, partner_send, partner_recv,
):
    me = lax.axis_index(axis)
    mine = lax.axis_index(gather_axis)
    chips = lax.axis_size(gather_axis) // 2
    chip = mine // 2
    core = lax.rem(mine, 2)
    partner = chip * 2 + (1 - core)
    right = lax.rem(chip + 1, chips) * 2 + core
    left = lax.rem(chip + chips - 1, chips) * 2 + core
    half = far_piece.shape[0] // 2
    barrier = pltpu.get_barrier_semaphore()
    offsets = peer_offsets(count)
    for offset in range(1, count):
        peer = offsets[offset - 1][0](me)
        pl.semaphore_signal(barrier, inc=1, device_id={axis: peer}, device_id_type=MESH)
    for neighbour in (partner, right, left):
        pl.semaphore_signal(barrier, inc=1, device_id={gather_axis: neighbour}, device_id_type=MESH)
    pl.semaphore_wait(barrier, count + 2)

    far_out = []
    for side, slot, target, rows in ((0, 1, right, pl.ds(0, half)), (1, 2, left, pl.ds(half, half))):
        copy = pltpu.make_async_remote_copy(
            src_ref=near_pieces.at[slot, rows],
            dst_ref=far_piece.at[rows],
            send_sem=far_send.at[side],
            recv_sem=far_recv.at[side],
            device_id={gather_axis: target},
            device_id_type=MESH,
        )
        copy.start()
        far_out.append(copy)
    to_partner = pltpu.make_async_remote_copy(
        src_ref=near_pieces,
        dst_ref=partner_near,
        send_sem=partner_send.at[0],
        recv_sem=partner_recv.at[0],
        device_id={gather_axis: partner},
        device_id_type=MESH,
    )
    to_partner.start()
    local = pltpu.make_async_copy(send_ref.at[me], got_ref.at[me], local_sem)
    local.start()
    outgoing = []
    for offset in range(1, count):
        peer = offsets[offset - 1][0](me)
        copy = pltpu.make_async_remote_copy(
            src_ref=send_ref.at[peer],
            dst_ref=got_ref.at[me],
            send_sem=send_sem.at[offset],
            recv_sem=recv_sem.at[offset],
            device_id={axis: peer},
            device_id_type=MESH,
        )
        copy.start()
        outgoing.append(copy)

    piece_width = near_pieces.shape[2]
    chip_shift = (0, chips - 1, 1, 2)

    def piece_index(step):
        piece_core = core if step < 4 else 1 - core
        return lax.rem(chip + chip_shift[step % 4], chips) * 2 + piece_core

    def chunk_copy(step):
        index = piece_index(step)
        return pltpu.make_async_copy(
            wq_hbm.at[pl.ds(pl.multiple_of(index * piece_width, piece_width), piece_width)],
            wq_buf.at[step % 2],
            wq_sem.at[step % 2],
        )

    chunk_copy(0).start()
    q_ref[...] = jnp.zeros_like(q_ref)
    k_ref[...] = jnp.zeros_like(k_ref)
    v_ref[...] = jnp.zeros_like(v_ref)

    def project(step, piece):
        chunk_copy(step).wait()
        if step + 1 < 8:
            chunk_copy(step + 1).start()
        index = piece_index(step)
        rows = pl.ds(pl.multiple_of(index * piece_width, piece_width), piece_width)
        q_ref[...] += jnp.dot(piece, wq_buf[step % 2], preferred_element_type=jnp.float32)
        k_ref[...] += jnp.dot(piece, wk_ref[rows, :], preferred_element_type=jnp.float32)
        v_ref[...] += jnp.dot(piece, wv_ref[rows, :], preferred_element_type=jnp.float32)

    for step in range(3):
        project(step, near_pieces[step])
    for side, source, rows in ((0, left, pl.ds(0, half)), (1, right, pl.ds(half, half))):
        far_out[side].wait_send()
        incoming = pltpu.make_async_remote_copy(
            src_ref=near_pieces.at[1, rows],
            dst_ref=far_piece.at[rows],
            send_sem=far_send.at[side],
            recv_sem=far_recv.at[side],
            device_id={gather_axis: source},
            device_id_type=MESH,
        )
        incoming.wait_recv()
    far_to_partner = pltpu.make_async_remote_copy(
        src_ref=far_piece,
        dst_ref=partner_far,
        send_sem=partner_send.at[1],
        recv_sem=partner_recv.at[1],
        device_id={gather_axis: partner},
        device_id_type=MESH,
    )
    far_to_partner.start()
    project(3, far_piece[...])
    to_partner.wait_send()
    to_partner.wait_recv()
    for step in range(3):
        project(4 + step, partner_near[step])
    far_to_partner.wait_send()
    far_to_partner.wait_recv()
    project(7, partner_far[...])

    for offset in range(1, count):
        outgoing[offset - 1].wait_send()
        source = offsets[offset - 1][1](me)
        incoming = pltpu.make_async_remote_copy(
            src_ref=send_ref.at[source],
            dst_ref=got_ref.at[source],
            send_sem=send_sem.at[offset],
            recv_sem=recv_sem.at[offset],
            device_id={axis: source},
            device_id_type=MESH,
        )
        incoming.wait_recv()
    local.wait()

    slots, slot_rows, width = got_ref.shape
    adapter_rows = jnp.dot(
        place_ref[...], got_ref[...].reshape(slots * slot_rows, width),
        preferred_element_type=jnp.float32,
    )
    cosine = cos_ref[...]
    sines = sin_ref[...]
    half_turn = HD // 2

    def rotated(values):
        return values * cosine + pltpu.roll(values, half_turn, 1) * sines

    for head in range(width // HD):
        lanes = slice(head * HD, (head + 1) * HD)
        summed = q_ref[:, lanes] + adapter_rows[:, lanes]
        queries_ref[:, lanes] = rotated(summed).astype(queries_ref.dtype)
    for head in range(key_ref.shape[1] // HD):
        lanes = slice(head * HD, (head + 1) * HD)
        key_ref[:, lanes] = rotated(k_ref[:, lanes]).astype(key_ref.dtype)
    value_ref[...] = v_ref[...].astype(value_ref.dtype)


def exchange_project(values, near_pieces, w_query, w_key, w_value, place_t, cosine, sines,
                     axis, count, gather_axis, collective):
    unused_item, token_count, piece_width = near_pieces.shape
    vmem = pl.BlockSpec(memory_space=pltpu.VMEM)
    return pl.pallas_call(
        lambda *refs: exchange_project_kernel(axis, count, gather_axis, *refs),
        out_shape=(
            jax.ShapeDtypeStruct((token_count, w_query.shape[1]), jnp.bfloat16),
            jax.ShapeDtypeStruct((token_count, w_key.shape[1]), jnp.bfloat16),
            jax.ShapeDtypeStruct((token_count, w_value.shape[1]), jnp.bfloat16),
        ),
        in_specs=[vmem, vmem, pl.BlockSpec(memory_space=pl.ANY), vmem, vmem, vmem, vmem, vmem],
        out_specs=(vmem, vmem, vmem),
        scratch_shapes=[
            pltpu.VMEM(values.shape, values.dtype),
            pltpu.VMEM((token_count, w_query.shape[1]), jnp.float32),
            pltpu.VMEM((token_count, w_key.shape[1]), jnp.float32),
            pltpu.VMEM((token_count, w_value.shape[1]), jnp.float32),
            pltpu.VMEM((token_count, piece_width), near_pieces.dtype),
            pltpu.VMEM(near_pieces.shape, near_pieces.dtype),
            pltpu.VMEM((token_count, piece_width), near_pieces.dtype),
            pltpu.VMEM((2, piece_width, w_query.shape[1]), w_query.dtype),
            pltpu.SemaphoreType.DMA((count,)),
            pltpu.SemaphoreType.DMA((count,)),
            pltpu.SemaphoreType.DMA(()),
            pltpu.SemaphoreType.DMA((2,)),
            pltpu.SemaphoreType.DMA((2,)),
            pltpu.SemaphoreType.DMA((2,)),
            pltpu.SemaphoreType.DMA((2,)),
            pltpu.SemaphoreType.DMA((2,)),
        ],
        compiler_params=pltpu.CompilerParams(
            collective_id=collective, has_side_effects=True, vmem_limit_bytes=60 * 1024 * 1024
        ),
    )(values, near_pieces, w_query, w_key, w_value, place_t, cosine, sines)


def sum_kernel(axis, count, part_ref, total_ref, held, first_send, first_recv, second_send, second_recv):
    me = lax.axis_index(axis)
    barrier = pltpu.get_barrier_semaphore()
    for offset in range(1, count):
        peer = lax.rem(me + offset, count)
        pl.semaphore_signal(barrier, inc=1, device_id={axis: peer}, device_id_type=MESH)
    pl.semaphore_wait(barrier, count - 1)
    outgoing = []
    for offset in range(1, count):
        peer = lax.rem(me + offset, count)
        copy = pltpu.make_async_remote_copy(
            src_ref=part_ref.at[peer],
            dst_ref=held.at[me],
            send_sem=first_send.at[offset],
            recv_sem=first_recv.at[offset],
            device_id={axis: peer},
            device_id_type=MESH,
        )
        copy.start()
        outgoing.append(copy)
    held[me] = part_ref[me]
    for offset in range(1, count):
        outgoing[offset - 1].wait_send()
        source = lax.rem(me + count - offset, count)
        incoming = pltpu.make_async_remote_copy(
            src_ref=part_ref.at[source],
            dst_ref=held.at[source],
            send_sem=first_send.at[offset],
            recv_sem=first_recv.at[offset],
            device_id={axis: source},
            device_id_type=MESH,
        )
        incoming.wait_recv()
    total = held[0]
    for index in range(1, count):
        total = total + held[index]
    total_ref[me] = total.astype(total_ref.dtype)
    outgoing = []
    for offset in range(1, count):
        peer = lax.rem(me + offset, count)
        copy = pltpu.make_async_remote_copy(
            src_ref=total_ref.at[me],
            dst_ref=total_ref.at[me],
            send_sem=second_send.at[offset],
            recv_sem=second_recv.at[offset],
            device_id={axis: peer},
            device_id_type=MESH,
        )
        copy.start()
        outgoing.append(copy)
    for offset in range(1, count):
        outgoing[offset - 1].wait_send()
        source = lax.rem(me + count - offset, count)
        incoming = pltpu.make_async_remote_copy(
            src_ref=total_ref.at[source],
            dst_ref=total_ref.at[source],
            send_sem=second_send.at[offset],
            recv_sem=second_recv.at[offset],
            device_id={axis: source},
            device_id_type=MESH,
        )
        incoming.wait_recv()


def axis_sum(values, axis, count, collective, out_dtype):
    chunks = values.reshape(count, -1, 128)
    summed = pl.pallas_call(
        lambda *refs: sum_kernel(axis, count, *refs),
        out_shape=jax.ShapeDtypeStruct(chunks.shape, out_dtype),
        in_specs=[pl.BlockSpec(memory_space=pltpu.VMEM)],
        out_specs=pl.BlockSpec(memory_space=pltpu.VMEM),
        scratch_shapes=[
            pltpu.VMEM(chunks.shape, values.dtype),
            pltpu.SemaphoreType.DMA((count,)),
            pltpu.SemaphoreType.DMA((count,)),
            pltpu.SemaphoreType.DMA((count,)),
            pltpu.SemaphoreType.DMA((count,)),
        ],
        compiler_params=pltpu.CompilerParams(collective_id=collective, has_side_effects=True),
    )(chunks)
    return summed.reshape(values.shape)


def owner_adapter_term(received, slot_ids, down_local, up_local):
    sources, rows, part_width = received.shape
    local_adapters, unused_item, adapter_rank = down_local.shape
    query_width = up_local.shape[2]
    token_rows = received.reshape(sources * rows, part_width)
    every_down = jnp.einsum(
        "td,adr->tar", token_rows, down_local, preferred_element_type=jnp.float32
    )
    pick = slot_ids.reshape(sources * rows)[:, None] == jnp.arange(local_adapters, dtype=jnp.int32)[None, :]
    partial_value_sum = jnp.sum(jnp.where(pick[:, :, None], every_down, 0.0), axis=1)
    tp_count = lax.axis_size("tp")
    summed = axis_sum(partial_value_sum.reshape(-1, 128), "tp", tp_count, 2, jnp.bfloat16)
    adapter_middle = summed.reshape(sources * rows, adapter_rank)
    spread_rows = jnp.where(pick[:, :, None], adapter_middle[:, None, :], jnp.zeros((), jnp.bfloat16))
    spread_rows = spread_rows.reshape(sources * rows, local_adapters * adapter_rank)
    adapter_output = jnp.dot(
        spread_rows,
        up_local.reshape(local_adapters * adapter_rank, query_width),
        preferred_element_type=jnp.float32,
    ).astype(jnp.bfloat16)
    return adapter_output.reshape(sources, rows, query_width)


def body(
    tokens,
    adapter_id,
    pool_slot,
    lengths,
    w_query,
    w_key,
    w_value,
    pooled_down_weights,
    pool_up,
    cache_key,
    cache_value,
):
    group_count = lax.axis_size("grp")
    tp_count = lax.axis_size("tp")
    row_count, step_count, part_width = tokens.shape
    local_adapter_rows, unused_item, adapter_rank = pooled_down_weights.shape
    query_width = w_query.shape[1]
    kv_width = w_key.shape[1]
    kv_local = kv_width // HD
    q_local = query_width // HD
    group_size = q_local // kv_local
    count_of_tokens = row_count * step_count
    adapter_span = jnp.arange(pool_slot.shape[0], dtype=jnp.int32)
    pool_pos = jnp.sum(
        jnp.where(adapter_id[:, None] == adapter_span[None, :], pool_slot[None, :], 0), axis=1
    )
    owner_grp = pool_pos // local_adapter_rows
    local_slot = pool_pos % local_adapter_rows
    row_span = jnp.arange(row_count, dtype=jnp.int32)
    same_owner = (owner_grp[:, None] == owner_grp[None, :]) & (row_span[None, :] < row_span[:, None])
    owner_rank = jnp.sum(same_owner.astype(jnp.int32), axis=1)
    send_slot = owner_grp * CAP + owner_rank
    slot_span = jnp.arange(group_count * CAP, dtype=jnp.int32)
    place = (slot_span[:, None] == send_slot[None, :]).astype(jnp.bfloat16)
    token_slot = (send_slot[:, None] * step_count + jnp.arange(step_count, dtype=jnp.int32)[None, :]).reshape(-1)
    token_span = jnp.arange(group_count * CAP * step_count, dtype=jnp.int32)
    place_tokens = (token_span[:, None] == token_slot[None, :]).astype(jnp.bfloat16)
    token_rows = tokens.reshape(count_of_tokens, part_width)
    send_tokens = jnp.dot(place_tokens, token_rows, preferred_element_type=jnp.float32).astype(jnp.bfloat16)
    send_tokens = send_tokens.reshape(group_count, CAP * step_count, part_width)
    send_ids = jnp.dot(
        place, local_slot.astype(jnp.bfloat16)[:, None], preferred_element_type=jnp.float32
    ).astype(jnp.bfloat16)
    send_ids = jnp.broadcast_to(send_ids.reshape(group_count, CAP, 1), (group_count, CAP, 128))
    send_ids = jnp.concatenate([send_ids, jnp.zeros_like(send_ids)], axis=1)
    (got_tokens, got_ids), chip_pieces = exchange_ring(
        (send_tokens, send_ids), token_rows, "grp", group_count, "tp", 0
    )
    got_ids = jnp.repeat(got_ids[:, :CAP, 0].astype(jnp.int32), step_count, axis=1)
    owner_out = owner_adapter_term(got_tokens, got_ids, pooled_down_weights, pool_up)
    position = lengths[:, None] + jnp.arange(step_count, dtype=jnp.int32)[None, :]
    half_width = HD // 2
    inv_freq = jnp.exp(
        jnp.arange(half_width, dtype=jnp.float32) * (-2.0 * math.log(rope_base) / HD)
    )
    both_halves = jnp.concatenate([inv_freq, inv_freq])
    turn_sign = jnp.where(jnp.arange(HD, dtype=jnp.int32) < half_width, -1.0, 1.0).astype(jnp.float32)
    angles = position.reshape(count_of_tokens).astype(jnp.float32)[:, None] * both_halves[None, :]
    cosine = jnp.cos(angles)
    sines = jnp.sin(angles) * turn_sign[None, :]
    place_back = (token_slot[:, None] == token_span[None, :]).astype(jnp.bfloat16)
    queries, key_new, value_new = exchange_project(
        owner_out, chip_pieces, w_query, w_key, w_value, place_back, cosine, sines,
        "grp", group_count, "tp", 1
    )
    queries = queries.reshape(row_count, step_count, kv_local, group_size, HD)
    key_new = key_new.reshape(row_count, step_count, kv_local, HD)
    value_new = value_new.reshape(row_count, step_count, kv_local, HD)
    cache_keys = cache_key.reshape(row_count, cache_key.shape[1], kv_local, HD)
    cache_values = cache_value.reshape(row_count, cache_value.shape[1], kv_local, HD)
    combined = attend(queries, key_new, value_new, cache_keys, cache_values, lengths)
    return combined.reshape(row_count, step_count, query_width)


def solution(mesh):
    in_specs = (
        P("grp", None, "tp"),
        P("grp"),
        P(),
        P("grp"),
        P(None, "tp"),
        P(None, "tp"),
        P(None, "tp"),
        P("grp", "tp", None),
        P("grp", None, "tp"),
        P("grp", None, "tp"),
        P("grp", None, "tp"),
    )
    out_specs = P("grp", None, "tp")
    return jax.shard_map(body, mesh=mesh, in_specs=in_specs, out_specs=out_specs, check_vma=False)
```

```python
import math

import jax
import jax.numpy as jnp
from jax import lax
from jax.experimental import pallas as pl
from jax.experimental.pallas import tpu as pltpu
from jax.sharding import PartitionSpec as P

MESH = pl.DeviceIdType.MESH

HD = 128
CAP = 8


rope_base = 500000.0


def rotate(values, position):
    half_width = values.shape[-1] // 2
    inv_freq = jnp.exp(
        jnp.arange(half_width, dtype=jnp.float32) * (-2.0 * math.log(rope_base) / values.shape[-1])
    )
    angles = position.astype(jnp.float32)[:, :, None, None] * inv_freq
    cosine = jnp.cos(angles)
    sines = jnp.sin(angles)
    front_half = values[..., :half_width]
    back_half = values[..., half_width:]
    return jnp.concatenate(
        [front_half * cosine - back_half * sines, back_half * cosine + front_half * sines], axis=-1
    )


def attend(queries, key_new, value_new, cache_key, cache_value, lengths):
    score_scale = 1.0 / math.sqrt(queries.shape[-1])
    cached = (
        jnp.einsum("rskgd,rlkd->rskgl", queries, cache_key, preferred_element_type=jnp.float32)
        * score_scale
    )
    fresh_keys = jnp.transpose(key_new, (0, 2, 1, 3)).astype(jnp.float32)
    fresh_scores = (
        jnp.sum(
            queries.astype(jnp.float32)[:, :, :, :, None, :] * fresh_keys[:, None, :, None, :, :],
            axis=-1,
        )
        * score_scale
    )
    live_mask = jnp.arange(cache_key.shape[1], dtype=jnp.int32)[None, :] < lengths[:, None]
    cached = jnp.where(live_mask[:, None, None, None, :], cached, -1e30)
    steps_here = key_new.shape[1]
    causal = (
        jnp.arange(steps_here, dtype=jnp.int32)[:, None]
        >= jnp.arange(steps_here, dtype=jnp.int32)[None, :]
    )
    fresh_scores = jnp.where(causal[None, :, None, None, :], fresh_scores, -1e30)
    row_max = jnp.maximum(jnp.max(cached, axis=-1), jnp.max(fresh_scores, axis=-1))
    cache_exp = jnp.exp(cached - row_max[..., None])
    fresh_exp = jnp.exp(fresh_scores - row_max[..., None])
    weight_sum = jnp.sum(cache_exp, axis=-1) + jnp.sum(fresh_exp, axis=-1)
    cache_weights = (cache_exp / weight_sum[..., None]).astype(jnp.bfloat16)
    fresh_weights = (fresh_exp / weight_sum[..., None]).astype(jnp.bfloat16)
    combined = jnp.einsum(
        "rskgl,rlkd->rskgd", cache_weights, cache_value, preferred_element_type=jnp.float32
    )
    combined = combined + jnp.einsum(
        "rskgt,rtkd->rskgd", fresh_weights, value_new, preferred_element_type=jnp.float32
    )
    return combined.astype(jnp.bfloat16)


TORUS_ORDER = (
    (0, 1), (1, 0), (0, 3), (3, 0), (1, 1), (3, 3), (1, 3), (3, 1),
    (0, 2), (2, 0), (2, 1), (1, 2), (2, 3), (3, 2), (2, 2),
)


def peer_offsets(count):
    if count == 16:
        def shifted(me, dz, dy):
            return lax.rem(me // 4 + dz, 4) * 4 + lax.rem(lax.rem(me, 4) + dy, 4)

        return [
            (lambda me, a=dz, b=dy: shifted(me, a, b), lambda me, a=dz, b=dy: shifted(me, 4 - a, 4 - b))
            for dz, dy in TORUS_ORDER
        ]
    return [
        (lambda me, d=offset: lax.rem(me + d, count), lambda me, d=offset: lax.rem(me + count - d, count))
        for offset in range(1, count)
    ]


def exchange_kernel(axis, count, arrays, *refs):
    send_refs = refs[:arrays]
    got_refs = refs[arrays : 2 * arrays]
    send_sem, recv_sem, local_sem = refs[2 * arrays :]
    me = lax.axis_index(axis)
    barrier = pltpu.get_barrier_semaphore()
    offsets = peer_offsets(count)
    for offset in range(1, count):
        peer = offsets[offset - 1][0](me)
        pl.semaphore_signal(barrier, inc=1, device_id={axis: peer}, device_id_type=MESH)
    pl.semaphore_wait(barrier, count - 1)
    locals_ = []
    for which in range(arrays):
        local = pltpu.make_async_copy(
            send_refs[which].at[me], got_refs[which].at[me], local_sem.at[which]
        )
        local.start()
        locals_.append(local)
    outgoing = []
    for offset in range(1, count):
        peer = offsets[offset - 1][0](me)
        for which in range(arrays):
            copy = pltpu.make_async_remote_copy(
                src_ref=send_refs[which].at[peer],
                dst_ref=got_refs[which].at[me],
                send_sem=send_sem.at[which, offset],
                recv_sem=recv_sem.at[which, offset],
                device_id={axis: peer},
                device_id_type=MESH,
            )
            copy.start()
            outgoing.append(copy)
    for offset in range(1, count):
        source = offsets[offset - 1][1](me)
        for which in range(arrays):
            outgoing[(offset - 1) * arrays + which].wait_send()
            incoming = pltpu.make_async_remote_copy(
                src_ref=send_refs[which].at[source],
                dst_ref=got_refs[which].at[source],
                send_sem=send_sem.at[which, offset],
                recv_sem=recv_sem.at[which, offset],
                device_id={axis: source},
                device_id_type=MESH,
            )
            incoming.wait_recv()
    for local in locals_:
        local.wait()


def exchange(values, axis, count, collective):
    arrays = len(values)
    vmem = pl.BlockSpec(memory_space=pltpu.VMEM)
    return pl.pallas_call(
        lambda *refs: exchange_kernel(axis, count, arrays, *refs),
        out_shape=tuple(jax.ShapeDtypeStruct(v.shape, v.dtype) for v in values),
        in_specs=[vmem] * arrays,
        out_specs=tuple([vmem] * arrays),
        scratch_shapes=[
            pltpu.SemaphoreType.DMA((arrays, count)),
            pltpu.SemaphoreType.DMA((arrays, count)),
            pltpu.SemaphoreType.DMA((arrays,)),
        ],
        compiler_params=pltpu.CompilerParams(collective_id=collective, has_side_effects=True),
    )(*values)


def exchange_ring_kernel(axis, count, gather_axis, arrays, *refs):
    send_refs = refs[:arrays]
    piece_ref = refs[arrays]
    got_refs = refs[arrays + 1 : 2 * arrays + 1]
    chip_pieces = refs[2 * arrays + 1]
    send_sem, recv_sem, local_sem, near_send, near_recv, piece_sem = refs[2 * arrays + 2 :]
    chips = lax.axis_size(gather_axis) // 2
    me = lax.axis_index(axis)
    mine = lax.axis_index(gather_axis)
    chip = mine // 2
    core = lax.rem(mine, 2)
    right_chip = lax.rem(chip + 1, chips)
    left_chip = lax.rem(chip + chips - 1, chips)
    right = right_chip * 2 + core
    left = left_chip * 2 + core

    barrier = pltpu.get_barrier_semaphore()
    offsets = peer_offsets(count)
    for offset in range(1, count):
        peer = offsets[offset - 1][0](me)
        pl.semaphore_signal(barrier, inc=1, device_id={axis: peer}, device_id_type=MESH)
    pl.semaphore_signal(barrier, inc=1, device_id={gather_axis: right}, device_id_type=MESH)
    pl.semaphore_signal(barrier, inc=1, device_id={gather_axis: left}, device_id_type=MESH)
    pl.semaphore_wait(barrier, count + 1)

    near = []
    for side, target in ((0, right), (1, left)):
        copy = pltpu.make_async_remote_copy(
            src_ref=piece_ref,
            dst_ref=chip_pieces.at[1 + side],
            send_sem=near_send.at[side],
            recv_sem=near_recv.at[side],
            device_id={gather_axis: target},
            device_id_type=MESH,
        )
        copy.start()
        near.append(copy)
    own_piece = pltpu.make_async_copy(piece_ref, chip_pieces.at[0], piece_sem)
    own_piece.start()

    locals_ = []
    for which in range(arrays):
        local = pltpu.make_async_copy(
            send_refs[which].at[me], got_refs[which].at[me], local_sem.at[which]
        )
        local.start()
        locals_.append(local)
    outgoing = []
    for offset in range(1, count):
        peer = offsets[offset - 1][0](me)
        for which in range(arrays):
            copy = pltpu.make_async_remote_copy(
                src_ref=send_refs[which].at[peer],
                dst_ref=got_refs[which].at[me],
                send_sem=send_sem.at[which, offset],
                recv_sem=recv_sem.at[which, offset],
                device_id={axis: peer},
                device_id_type=MESH,
            )
            copy.start()
            outgoing.append(copy)

    for side, source in ((0, left), (1, right)):
        near[side].wait_send()
        incoming = pltpu.make_async_remote_copy(
            src_ref=piece_ref,
            dst_ref=chip_pieces.at[1 + side],
            send_sem=near_send.at[side],
            recv_sem=near_recv.at[side],
            device_id={gather_axis: source},
            device_id_type=MESH,
        )
        incoming.wait_recv()

    for offset in range(1, count):
        source = offsets[offset - 1][1](me)
        for which in range(arrays):
            outgoing[(offset - 1) * arrays + which].wait_send()
            incoming = pltpu.make_async_remote_copy(
                src_ref=send_refs[which].at[source],
                dst_ref=got_refs[which].at[source],
                send_sem=send_sem.at[which, offset],
                recv_sem=recv_sem.at[which, offset],
                device_id={axis: source},
                device_id_type=MESH,
            )
            incoming.wait_recv()
    for local in locals_:
        local.wait()
    own_piece.wait()


def exchange_ring(values, piece, axis, count, gather_axis, collective):
    arrays = len(values)
    vmem = pl.BlockSpec(memory_space=pltpu.VMEM)
    outs = pl.pallas_call(
        lambda *refs: exchange_ring_kernel(axis, count, gather_axis, arrays, *refs),
        out_shape=tuple(jax.ShapeDtypeStruct(v.shape, v.dtype) for v in values)
        + (jax.ShapeDtypeStruct((3,) + piece.shape, piece.dtype),),
        in_specs=[vmem] * (arrays + 1),
        out_specs=tuple([vmem] * (arrays + 1)),
        scratch_shapes=[
            pltpu.SemaphoreType.DMA((arrays, count)),
            pltpu.SemaphoreType.DMA((arrays, count)),
            pltpu.SemaphoreType.DMA((arrays,)),
            pltpu.SemaphoreType.DMA((2,)),
            pltpu.SemaphoreType.DMA((2,)),
            pltpu.SemaphoreType.DMA(()),
        ],
        compiler_params=pltpu.CompilerParams(collective_id=collective, has_side_effects=True),
    )(*values, piece)
    return outs[:arrays], outs[arrays]


def exchange_project_kernel(
    axis, count, gather_axis, send_ref, near_pieces, wq_hbm, wk_ref, wv_ref,
    place_ref, cos_ref, sin_ref,
    queries_ref, key_ref, value_ref,
    got_ref, q_ref, k_ref, v_ref,
    far_piece, partner_near, partner_far, wq_buf, send_sem, recv_sem, local_sem, wq_sem,
    far_send, far_recv, partner_send, partner_recv,
):
    me = lax.axis_index(axis)
    mine = lax.axis_index(gather_axis)
    chips = lax.axis_size(gather_axis) // 2
    chip = mine // 2
    core = lax.rem(mine, 2)
    partner = chip * 2 + (1 - core)
    right = lax.rem(chip + 1, chips) * 2 + core
    left = lax.rem(chip + chips - 1, chips) * 2 + core
    half = far_piece.shape[0] // 2
    barrier = pltpu.get_barrier_semaphore()
    offsets = peer_offsets(count)
    for offset in range(1, count):
        peer = offsets[offset - 1][0](me)
        pl.semaphore_signal(barrier, inc=1, device_id={axis: peer}, device_id_type=MESH)
    for neighbour in (partner, right, left):
        pl.semaphore_signal(barrier, inc=1, device_id={gather_axis: neighbour}, device_id_type=MESH)
    pl.semaphore_wait(barrier, count + 2)

    far_out = []
    for side, slot, target, rows in ((0, 1, right, pl.ds(0, half)), (1, 2, left, pl.ds(half, half))):
        copy = pltpu.make_async_remote_copy(
            src_ref=near_pieces.at[slot, rows],
            dst_ref=far_piece.at[rows],
            send_sem=far_send.at[side],
            recv_sem=far_recv.at[side],
            device_id={gather_axis: target},
            device_id_type=MESH,
        )
        copy.start()
        far_out.append(copy)
    to_partner = pltpu.make_async_remote_copy(
        src_ref=near_pieces,
        dst_ref=partner_near,
        send_sem=partner_send.at[0],
        recv_sem=partner_recv.at[0],
        device_id={gather_axis: partner},
        device_id_type=MESH,
    )
    to_partner.start()
    local = pltpu.make_async_copy(send_ref.at[me], got_ref.at[me], local_sem)
    local.start()
    outgoing = []
    for offset in range(1, count):
        peer = offsets[offset - 1][0](me)
        copy = pltpu.make_async_remote_copy(
            src_ref=send_ref.at[peer],
            dst_ref=got_ref.at[me],
            send_sem=send_sem.at[offset],
            recv_sem=recv_sem.at[offset],
            device_id={axis: peer},
            device_id_type=MESH,
        )
        copy.start()
        outgoing.append(copy)

    piece_width = near_pieces.shape[2]
    chip_shift = (0, chips - 1, 1, 2)

    def piece_index(step):
        piece_core = core if step < 4 else 1 - core
        return lax.rem(chip + chip_shift[step % 4], chips) * 2 + piece_core

    def chunk_copy(step):
        index = piece_index(step)
        return pltpu.make_async_copy(
            wq_hbm.at[pl.ds(pl.multiple_of(index * piece_width, piece_width), piece_width)],
            wq_buf.at[step % 2],
            wq_sem.at[step % 2],
        )

    chunk_copy(0).start()
    q_ref[...] = jnp.zeros_like(q_ref)
    k_ref[...] = jnp.zeros_like(k_ref)
    v_ref[...] = jnp.zeros_like(v_ref)

    def project(step, piece):
        chunk_copy(step).wait()
        if step + 1 < 8:
            chunk_copy(step + 1).start()
        index = piece_index(step)
        rows = pl.ds(pl.multiple_of(index * piece_width, piece_width), piece_width)
        q_ref[...] += jnp.dot(piece, wq_buf[step % 2], preferred_element_type=jnp.float32)
        k_ref[...] += jnp.dot(piece, wk_ref[rows, :], preferred_element_type=jnp.float32)
        v_ref[...] += jnp.dot(piece, wv_ref[rows, :], preferred_element_type=jnp.float32)

    for step in range(3):
        project(step, near_pieces[step])
    for side, source, rows in ((0, left, pl.ds(0, half)), (1, right, pl.ds(half, half))):
        far_out[side].wait_send()
        incoming = pltpu.make_async_remote_copy(
            src_ref=near_pieces.at[1, rows],
            dst_ref=far_piece.at[rows],
            send_sem=far_send.at[side],
            recv_sem=far_recv.at[side],
            device_id={gather_axis: source},
            device_id_type=MESH,
        )
        incoming.wait_recv()
    far_to_partner = pltpu.make_async_remote_copy(
        src_ref=far_piece,
        dst_ref=partner_far,
        send_sem=partner_send.at[1],
        recv_sem=partner_recv.at[1],
        device_id={gather_axis: partner},
        device_id_type=MESH,
    )
    far_to_partner.start()
    project(3, far_piece[...])
    to_partner.wait_send()
    to_partner.wait_recv()
    for step in range(3):
        project(4 + step, partner_near[step])
    far_to_partner.wait_send()
    far_to_partner.wait_recv()
    project(7, partner_far[...])

    for offset in range(1, count):
        outgoing[offset - 1].wait_send()
        source = offsets[offset - 1][1](me)
        incoming = pltpu.make_async_remote_copy(
            src_ref=send_ref.at[source],
            dst_ref=got_ref.at[source],
            send_sem=send_sem.at[offset],
            recv_sem=recv_sem.at[offset],
            device_id={axis: source},
            device_id_type=MESH,
        )
        incoming.wait_recv()
    local.wait()

    slots, slot_rows, width = got_ref.shape
    adapter_rows = jnp.dot(
        place_ref[...], got_ref[...].reshape(slots * slot_rows, width),
        preferred_element_type=jnp.float32,
    )
    cosine = cos_ref[...]
    sines = sin_ref[...]
    half_turn = HD // 2

    def rotated(values):
        return values * cosine + pltpu.roll(values, half_turn, 1) * sines

    for head in range(width // HD):
        lanes = slice(head * HD, (head + 1) * HD)
        summed = q_ref[:, lanes] + adapter_rows[:, lanes]
        queries_ref[:, lanes] = rotated(summed).astype(queries_ref.dtype)
    for head in range(key_ref.shape[1] // HD):
        lanes = slice(head * HD, (head + 1) * HD)
        key_ref[:, lanes] = rotated(k_ref[:, lanes]).astype(key_ref.dtype)
    value_ref[...] = v_ref[...].astype(value_ref.dtype)


def exchange_project(values, near_pieces, w_query, w_key, w_value, place_t, cosine, sines,
                     axis, count, gather_axis, collective):
    unused_item, token_count, piece_width = near_pieces.shape
    vmem = pl.BlockSpec(memory_space=pltpu.VMEM)
    return pl.pallas_call(
        lambda *refs: exchange_project_kernel(axis, count, gather_axis, *refs),
        out_shape=(
            jax.ShapeDtypeStruct((token_count, w_query.shape[1]), jnp.bfloat16),
            jax.ShapeDtypeStruct((token_count, w_key.shape[1]), jnp.bfloat16),
            jax.ShapeDtypeStruct((token_count, w_value.shape[1]), jnp.bfloat16),
        ),
        in_specs=[vmem, vmem, pl.BlockSpec(memory_space=pl.ANY), vmem, vmem, vmem, vmem, vmem],
        out_specs=(vmem, vmem, vmem),
        scratch_shapes=[
            pltpu.VMEM(values.shape, values.dtype),
            pltpu.VMEM((token_count, w_query.shape[1]), jnp.float32),
            pltpu.VMEM((token_count, w_key.shape[1]), jnp.float32),
            pltpu.VMEM((token_count, w_value.shape[1]), jnp.float32),
            pltpu.VMEM((token_count, piece_width), near_pieces.dtype),
            pltpu.VMEM(near_pieces.shape, near_pieces.dtype),
            pltpu.VMEM((token_count, piece_width), near_pieces.dtype),
            pltpu.VMEM((2, piece_width, w_query.shape[1]), w_query.dtype),
            pltpu.SemaphoreType.DMA((count,)),
            pltpu.SemaphoreType.DMA((count,)),
            pltpu.SemaphoreType.DMA(()),
            pltpu.SemaphoreType.DMA((2,)),
            pltpu.SemaphoreType.DMA((2,)),
            pltpu.SemaphoreType.DMA((2,)),
            pltpu.SemaphoreType.DMA((2,)),
            pltpu.SemaphoreType.DMA((2,)),
        ],
        compiler_params=pltpu.CompilerParams(
            collective_id=collective, has_side_effects=True, vmem_limit_bytes=60 * 1024 * 1024
        ),
    )(values, near_pieces, w_query, w_key, w_value, place_t, cosine, sines)


def sum_kernel(axis, count, part_ref, total_ref, held, first_send, first_recv, second_send, second_recv):
    me = lax.axis_index(axis)
    barrier = pltpu.get_barrier_semaphore()
    for offset in range(1, count):
        peer = lax.rem(me + offset, count)
        pl.semaphore_signal(barrier, inc=1, device_id={axis: peer}, device_id_type=MESH)
    pl.semaphore_wait(barrier, count - 1)
    outgoing = []
    for offset in range(1, count):
        peer = lax.rem(me + offset, count)
        copy = pltpu.make_async_remote_copy(
            src_ref=part_ref.at[peer],
            dst_ref=held.at[me],
            send_sem=first_send.at[offset],
            recv_sem=first_recv.at[offset],
            device_id={axis: peer},
            device_id_type=MESH,
        )
        copy.start()
        outgoing.append(copy)
    held[me] = part_ref[me]
    for offset in range(1, count):
        outgoing[offset - 1].wait_send()
        source = lax.rem(me + count - offset, count)
        incoming = pltpu.make_async_remote_copy(
            src_ref=part_ref.at[source],
            dst_ref=held.at[source],
            send_sem=first_send.at[offset],
            recv_sem=first_recv.at[offset],
            device_id={axis: source},
            device_id_type=MESH,
        )
        incoming.wait_recv()
    total = held[0]
    for index in range(1, count):
        total = total + held[index]
    total_ref[me] = total.astype(total_ref.dtype)
    outgoing = []
    for offset in range(1, count):
        peer = lax.rem(me + offset, count)
        copy = pltpu.make_async_remote_copy(
            src_ref=total_ref.at[me],
            dst_ref=total_ref.at[me],
            send_sem=second_send.at[offset],
            recv_sem=second_recv.at[offset],
            device_id={axis: peer},
            device_id_type=MESH,
        )
        copy.start()
        outgoing.append(copy)
    for offset in range(1, count):
        outgoing[offset - 1].wait_send()
        source = lax.rem(me + count - offset, count)
        incoming = pltpu.make_async_remote_copy(
            src_ref=total_ref.at[source],
            dst_ref=total_ref.at[source],
            send_sem=second_send.at[offset],
            recv_sem=second_recv.at[offset],
            device_id={axis: source},
            device_id_type=MESH,
        )
        incoming.wait_recv()


def axis_sum(values, axis, count, collective, out_dtype):
    chunks = values.reshape(count, -1, 128)
    summed = pl.pallas_call(
        lambda *refs: sum_kernel(axis, count, *refs),
        out_shape=jax.ShapeDtypeStruct(chunks.shape, out_dtype),
        in_specs=[pl.BlockSpec(memory_space=pltpu.VMEM)],
        out_specs=pl.BlockSpec(memory_space=pltpu.VMEM),
        scratch_shapes=[
            pltpu.VMEM(chunks.shape, values.dtype),
            pltpu.SemaphoreType.DMA((count,)),
            pltpu.SemaphoreType.DMA((count,)),
            pltpu.SemaphoreType.DMA((count,)),
            pltpu.SemaphoreType.DMA((count,)),
        ],
        compiler_params=pltpu.CompilerParams(collective_id=collective, has_side_effects=True),
    )(chunks)
    return summed.reshape(values.shape)


def owner_adapter_term(received, slot_ids, down_local, up_local):
    sources, rows, part_width = received.shape
    local_adapters, unused_item, adapter_rank = down_local.shape
    query_width = up_local.shape[2]
    token_rows = received.reshape(sources * rows, part_width)
    every_down = jnp.einsum(
        "td,adr->tar", token_rows, down_local, preferred_element_type=jnp.float32
    )
    pick = slot_ids.reshape(sources * rows)[:, None] == jnp.arange(local_adapters, dtype=jnp.int32)[None, :]
    partial_value_sum = jnp.sum(jnp.where(pick[:, :, None], every_down, 0.0), axis=1)
    tp_count = lax.axis_size("tp")
    summed = axis_sum(partial_value_sum.reshape(-1, 128), "tp", tp_count, 2, jnp.bfloat16)
    adapter_middle = summed.reshape(sources * rows, adapter_rank)
    spread_rows = jnp.where(pick[:, :, None], adapter_middle[:, None, :], jnp.zeros((), jnp.bfloat16))
    spread_rows = spread_rows.reshape(sources * rows, local_adapters * adapter_rank)
    adapter_output = jnp.dot(
        spread_rows,
        up_local.reshape(local_adapters * adapter_rank, query_width),
        preferred_element_type=jnp.float32,
    ).astype(jnp.bfloat16)
    return adapter_output.reshape(sources, rows, query_width)


def body(
    tokens,
    adapter_id,
    pool_slot,
    lengths,
    w_query,
    w_key,
    w_value,
    pooled_down_weights,
    pool_up,
    cache_key,
    cache_value,
):
    group_count = lax.axis_size("grp")
    tp_count = lax.axis_size("tp")
    row_count, step_count, part_width = tokens.shape
    local_adapter_rows, unused_item, adapter_rank = pooled_down_weights.shape
    query_width = w_query.shape[1]
    kv_width = w_key.shape[1]
    kv_local = kv_width // HD
    q_local = query_width // HD
    group_size = q_local // kv_local
    count_of_tokens = row_count * step_count
    adapter_span = jnp.arange(pool_slot.shape[0], dtype=jnp.int32)
    pool_pos = jnp.take(pool_slot, adapter_id, axis=0, mode="clip")
    owner_grp = pool_pos // local_adapter_rows
    local_slot = pool_pos % local_adapter_rows
    row_span = jnp.arange(row_count, dtype=jnp.int32)
    same_owner = (owner_grp[:, None] == owner_grp[None, :]) & (row_span[None, :] < row_span[:, None])
    owner_rank = jnp.sum(same_owner.astype(jnp.int32), axis=1)
    send_slot = owner_grp * CAP + owner_rank
    slot_span = jnp.arange(group_count * CAP, dtype=jnp.int32)
    place = (slot_span[:, None] == send_slot[None, :]).astype(jnp.bfloat16)
    token_slot = (send_slot[:, None] * step_count + jnp.arange(step_count, dtype=jnp.int32)[None, :]).reshape(-1)
    token_span = jnp.arange(group_count * CAP * step_count, dtype=jnp.int32)
    place_tokens = (token_span[:, None] == token_slot[None, :]).astype(jnp.bfloat16)
    token_rows = tokens.reshape(count_of_tokens, part_width)
    send_tokens = jnp.dot(place_tokens, token_rows, preferred_element_type=jnp.float32).astype(jnp.bfloat16)
    send_tokens = send_tokens.reshape(group_count, CAP * step_count, part_width)
    send_ids = jnp.dot(
        place, local_slot.astype(jnp.bfloat16)[:, None], preferred_element_type=jnp.float32
    ).astype(jnp.bfloat16)
    send_ids = jnp.broadcast_to(send_ids.reshape(group_count, CAP, 1), (group_count, CAP, 128))
    send_ids = jnp.concatenate([send_ids, jnp.zeros_like(send_ids)], axis=1)
    (got_tokens, got_ids), chip_pieces = exchange_ring(
        (send_tokens, send_ids), token_rows, "grp", group_count, "tp", 0
    )
    got_ids = jnp.repeat(got_ids[:, :CAP, 0].astype(jnp.int32), step_count, axis=1)
    owner_out = owner_adapter_term(got_tokens, got_ids, pooled_down_weights, pool_up)
    position = lengths[:, None] + jnp.arange(step_count, dtype=jnp.int32)[None, :]
    half_width = HD // 2
    inv_freq = jnp.exp(
        jnp.arange(half_width, dtype=jnp.float32) * (-2.0 * math.log(rope_base) / HD)
    )
    both_halves = jnp.concatenate([inv_freq, inv_freq])
    turn_sign = jnp.where(jnp.arange(HD, dtype=jnp.int32) < half_width, -1.0, 1.0).astype(jnp.float32)
    angles = position.reshape(count_of_tokens).astype(jnp.float32)[:, None] * both_halves[None, :]
    cosine = jnp.cos(angles)
    sines = jnp.sin(angles) * turn_sign[None, :]
    place_back = (token_slot[:, None] == token_span[None, :]).astype(jnp.bfloat16)
    queries, key_new, value_new = exchange_project(
        owner_out, chip_pieces, w_query, w_key, w_value, place_back, cosine, sines,
        "grp", group_count, "tp", 1
    )
    queries = queries.reshape(row_count, step_count, kv_local, group_size, HD)
    key_new = key_new.reshape(row_count, step_count, kv_local, HD)
    value_new = value_new.reshape(row_count, step_count, kv_local, HD)
    cache_keys = cache_key.reshape(row_count, cache_key.shape[1], kv_local, HD)
    cache_values = cache_value.reshape(row_count, cache_value.shape[1], kv_local, HD)
    combined = attend(queries, key_new, value_new, cache_keys, cache_values, lengths)
    return combined.reshape(row_count, step_count, query_width)


def solution(mesh):
    in_specs = (
        P("grp", None, "tp"),
        P("grp"),
        P(),
        P("grp"),
        P(None, "tp"),
        P(None, "tp"),
        P(None, "tp"),
        P("grp", "tp", None),
        P("grp", None, "tp"),
        P("grp", None, "tp"),
        P("grp", None, "tp"),
    )
    out_specs = P("grp", None, "tp")
    return jax.shard_map(body, mesh=mesh, in_specs=in_specs, out_specs=out_specs, check_vma=False)
```

```python
import math

import jax
import jax.numpy as jnp
from jax import lax
from jax.experimental import pallas as pl
from jax.experimental.pallas import tpu as pltpu
from jax.sharding import PartitionSpec as P

MESH = pl.DeviceIdType.MESH

HD = 128
CAP = 8


rope_base = 500000.0


def rotate(values, position):
    half_width = values.shape[-1] // 2
    inv_freq = jnp.exp(
        jnp.arange(half_width, dtype=jnp.float32) * (-2.0 * math.log(rope_base) / values.shape[-1])
    )
    angles = position.astype(jnp.float32)[:, :, None, None] * inv_freq
    cosine = jnp.cos(angles)
    sines = jnp.sin(angles)
    front_half = values[..., :half_width]
    back_half = values[..., half_width:]
    return jnp.concatenate(
        [front_half * cosine - back_half * sines, back_half * cosine + front_half * sines], axis=-1
    )


def attend(queries, key_new, value_new, cache_key, cache_value, lengths):
    score_scale = 1.0 / math.sqrt(queries.shape[-1])
    cached = (
        jnp.einsum("rskgd,rlkd->rskgl", queries, cache_key, preferred_element_type=jnp.float32)
        * score_scale
    )
    fresh_keys = jnp.transpose(key_new, (0, 2, 1, 3)).astype(jnp.float32)
    fresh_scores = (
        jnp.sum(
            queries.astype(jnp.float32)[:, :, :, :, None, :] * fresh_keys[:, None, :, None, :, :],
            axis=-1,
        )
        * score_scale
    )
    live_mask = jnp.arange(cache_key.shape[1], dtype=jnp.int32)[None, :] < lengths[:, None]
    cached = jnp.where(live_mask[:, None, None, None, :], cached, -1e30)
    steps_here = key_new.shape[1]
    causal = (
        jnp.arange(steps_here, dtype=jnp.int32)[:, None]
        >= jnp.arange(steps_here, dtype=jnp.int32)[None, :]
    )
    fresh_scores = jnp.where(causal[None, :, None, None, :], fresh_scores, -1e30)
    row_max = jnp.maximum(jnp.max(cached, axis=-1), jnp.max(fresh_scores, axis=-1))
    cache_exp = jnp.exp(cached - row_max[..., None])
    fresh_exp = jnp.exp(fresh_scores - row_max[..., None])
    weight_sum = jnp.sum(cache_exp, axis=-1) + jnp.sum(fresh_exp, axis=-1)
    cache_weights = (cache_exp / weight_sum[..., None]).astype(jnp.bfloat16)
    fresh_weights = (fresh_exp / weight_sum[..., None]).astype(jnp.bfloat16)
    combined = jnp.einsum(
        "rskgl,rlkd->rskgd", cache_weights, cache_value, preferred_element_type=jnp.float32
    )
    combined = combined + jnp.einsum(
        "rskgt,rtkd->rskgd", fresh_weights, value_new, preferred_element_type=jnp.float32
    )
    return combined.astype(jnp.bfloat16)


TORUS_ORDER = (
    (0, 1), (1, 0), (0, 3), (3, 0), (1, 1), (3, 3), (1, 3), (3, 1),
    (0, 2), (2, 0), (2, 1), (1, 2), (2, 3), (3, 2), (2, 2),
)


def peer_offsets(count):
    if count == 16:
        def shifted(me, dz, dy):
            return lax.rem(me // 4 + dz, 4) * 4 + lax.rem(lax.rem(me, 4) + dy, 4)

        return [
            (lambda me, a=dz, b=dy: shifted(me, a, b), lambda me, a=dz, b=dy: shifted(me, 4 - a, 4 - b))
            for dz, dy in TORUS_ORDER
        ]
    return [
        (lambda me, d=offset: lax.rem(me + d, count), lambda me, d=offset: lax.rem(me + count - d, count))
        for offset in range(1, count)
    ]


def exchange_kernel(axis, count, arrays, *refs):
    send_refs = refs[:arrays]
    got_refs = refs[arrays : 2 * arrays]
    send_sem, recv_sem, local_sem = refs[2 * arrays :]
    me = lax.axis_index(axis)
    barrier = pltpu.get_barrier_semaphore()
    offsets = peer_offsets(count)
    for offset in range(1, count):
        peer = offsets[offset - 1][0](me)
        pl.semaphore_signal(barrier, inc=1, device_id={axis: peer}, device_id_type=MESH)
    pl.semaphore_wait(barrier, count - 1)
    locals_ = []
    for which in range(arrays):
        local = pltpu.make_async_copy(
            send_refs[which].at[me], got_refs[which].at[me], local_sem.at[which]
        )
        local.start()
        locals_.append(local)
    outgoing = []
    for offset in range(1, count):
        peer = offsets[offset - 1][0](me)
        for which in range(arrays):
            copy = pltpu.make_async_remote_copy(
                src_ref=send_refs[which].at[peer],
                dst_ref=got_refs[which].at[me],
                send_sem=send_sem.at[which, offset],
                recv_sem=recv_sem.at[which, offset],
                device_id={axis: peer},
                device_id_type=MESH,
            )
            copy.start()
            outgoing.append(copy)
    for offset in range(1, count):
        source = offsets[offset - 1][1](me)
        for which in range(arrays):
            outgoing[(offset - 1) * arrays + which].wait_send()
            incoming = pltpu.make_async_remote_copy(
                src_ref=send_refs[which].at[source],
                dst_ref=got_refs[which].at[source],
                send_sem=send_sem.at[which, offset],
                recv_sem=recv_sem.at[which, offset],
                device_id={axis: source},
                device_id_type=MESH,
            )
            incoming.wait_recv()
    for local in locals_:
        local.wait()


def exchange(values, axis, count, collective):
    arrays = len(values)
    vmem = pl.BlockSpec(memory_space=pltpu.VMEM)
    return pl.pallas_call(
        lambda *refs: exchange_kernel(axis, count, arrays, *refs),
        out_shape=tuple(jax.ShapeDtypeStruct(v.shape, v.dtype) for v in values),
        in_specs=[vmem] * arrays,
        out_specs=tuple([vmem] * arrays),
        scratch_shapes=[
            pltpu.SemaphoreType.DMA((arrays, count)),
            pltpu.SemaphoreType.DMA((arrays, count)),
            pltpu.SemaphoreType.DMA((arrays,)),
        ],
        compiler_params=pltpu.CompilerParams(collective_id=collective, has_side_effects=True),
    )(*values)


def exchange_ring_kernel(axis, count, gather_axis, arrays, *refs):
    send_refs = refs[:arrays]
    piece_ref = refs[arrays]
    got_refs = refs[arrays + 1 : 2 * arrays + 1]
    chip_pieces = refs[2 * arrays + 1]
    send_sem, recv_sem, local_sem, near_send, near_recv, piece_sem = refs[2 * arrays + 2 :]
    chips = lax.axis_size(gather_axis) // 2
    me = lax.axis_index(axis)
    mine = lax.axis_index(gather_axis)
    chip = mine // 2
    core = lax.rem(mine, 2)
    right_chip = lax.rem(chip + 1, chips)
    left_chip = lax.rem(chip + chips - 1, chips)
    right = right_chip * 2 + core
    left = left_chip * 2 + core

    barrier = pltpu.get_barrier_semaphore()
    offsets = peer_offsets(count)
    for offset in range(1, count):
        peer = offsets[offset - 1][0](me)
        pl.semaphore_signal(barrier, inc=1, device_id={axis: peer}, device_id_type=MESH)
    pl.semaphore_signal(barrier, inc=1, device_id={gather_axis: right}, device_id_type=MESH)
    pl.semaphore_signal(barrier, inc=1, device_id={gather_axis: left}, device_id_type=MESH)
    pl.semaphore_wait(barrier, count + 1)

    near = []
    for side, target in ((0, right), (1, left)):
        copy = pltpu.make_async_remote_copy(
            src_ref=piece_ref,
            dst_ref=chip_pieces.at[1 + side],
            send_sem=near_send.at[side],
            recv_sem=near_recv.at[side],
            device_id={gather_axis: target},
            device_id_type=MESH,
        )
        copy.start()
        near.append(copy)
    own_piece = pltpu.make_async_copy(piece_ref, chip_pieces.at[0], piece_sem)
    own_piece.start()

    locals_ = []
    for which in range(arrays):
        local = pltpu.make_async_copy(
            send_refs[which].at[me], got_refs[which].at[me], local_sem.at[which]
        )
        local.start()
        locals_.append(local)
    outgoing = []
    for offset in range(1, count):
        peer = offsets[offset - 1][0](me)
        for which in range(arrays):
            copy = pltpu.make_async_remote_copy(
                src_ref=send_refs[which].at[peer],
                dst_ref=got_refs[which].at[me],
                send_sem=send_sem.at[which, offset],
                recv_sem=recv_sem.at[which, offset],
                device_id={axis: peer},
                device_id_type=MESH,
            )
            copy.start()
            outgoing.append(copy)

    for side, source in ((0, left), (1, right)):
        near[side].wait_send()
        incoming = pltpu.make_async_remote_copy(
            src_ref=piece_ref,
            dst_ref=chip_pieces.at[1 + side],
            send_sem=near_send.at[side],
            recv_sem=near_recv.at[side],
            device_id={gather_axis: source},
            device_id_type=MESH,
        )
        incoming.wait_recv()

    for offset in range(1, count):
        source = offsets[offset - 1][1](me)
        for which in range(arrays):
            outgoing[(offset - 1) * arrays + which].wait_send()
            incoming = pltpu.make_async_remote_copy(
                src_ref=send_refs[which].at[source],
                dst_ref=got_refs[which].at[source],
                send_sem=send_sem.at[which, offset],
                recv_sem=recv_sem.at[which, offset],
                device_id={axis: source},
                device_id_type=MESH,
            )
            incoming.wait_recv()
    for local in locals_:
        local.wait()
    own_piece.wait()


def exchange_ring(values, piece, axis, count, gather_axis, collective):
    arrays = len(values)
    vmem = pl.BlockSpec(memory_space=pltpu.VMEM)
    outs = pl.pallas_call(
        lambda *refs: exchange_ring_kernel(axis, count, gather_axis, arrays, *refs),
        out_shape=tuple(jax.ShapeDtypeStruct(v.shape, v.dtype) for v in values)
        + (jax.ShapeDtypeStruct((3,) + piece.shape, piece.dtype),),
        in_specs=[vmem] * (arrays + 1),
        out_specs=tuple([vmem] * (arrays + 1)),
        scratch_shapes=[
            pltpu.SemaphoreType.DMA((arrays, count)),
            pltpu.SemaphoreType.DMA((arrays, count)),
            pltpu.SemaphoreType.DMA((arrays,)),
            pltpu.SemaphoreType.DMA((2,)),
            pltpu.SemaphoreType.DMA((2,)),
            pltpu.SemaphoreType.DMA(()),
        ],
        compiler_params=pltpu.CompilerParams(collective_id=collective, has_side_effects=True),
    )(*values, piece)
    return outs[:arrays], outs[arrays]


def exchange_project_kernel(
    axis, count, gather_axis, send_ref, near_pieces, wq_hbm, wk_ref, wv_ref,
    place_ref, cos_ref, sin_ref,
    queries_ref, key_ref, value_ref,
    got_ref, q_ref, k_ref, v_ref,
    far_piece, partner_near, partner_far, wq_buf, send_sem, recv_sem, local_sem, wq_sem,
    far_send, far_recv, partner_send, partner_recv,
):
    me = lax.axis_index(axis)
    mine = lax.axis_index(gather_axis)
    chips = lax.axis_size(gather_axis) // 2
    chip = mine // 2
    core = lax.rem(mine, 2)
    partner = chip * 2 + (1 - core)
    right = lax.rem(chip + 1, chips) * 2 + core
    left = lax.rem(chip + chips - 1, chips) * 2 + core
    half = far_piece.shape[0] // 2
    barrier = pltpu.get_barrier_semaphore()
    offsets = peer_offsets(count)
    for offset in range(1, count):
        peer = offsets[offset - 1][0](me)
        pl.semaphore_signal(barrier, inc=1, device_id={axis: peer}, device_id_type=MESH)
    for neighbour in (partner, right, left):
        pl.semaphore_signal(barrier, inc=1, device_id={gather_axis: neighbour}, device_id_type=MESH)
    pl.semaphore_wait(barrier, count + 2)

    far_out = []
    for side, slot, target, rows in ((0, 1, right, pl.ds(0, half)), (1, 2, left, pl.ds(half, half))):
        copy = pltpu.make_async_remote_copy(
            src_ref=near_pieces.at[slot, rows],
            dst_ref=far_piece.at[rows],
            send_sem=far_send.at[side],
            recv_sem=far_recv.at[side],
            device_id={gather_axis: target},
            device_id_type=MESH,
        )
        copy.start()
        far_out.append(copy)
    to_partner = pltpu.make_async_remote_copy(
        src_ref=near_pieces,
        dst_ref=partner_near,
        send_sem=partner_send.at[0],
        recv_sem=partner_recv.at[0],
        device_id={gather_axis: partner},
        device_id_type=MESH,
    )
    to_partner.start()
    local = pltpu.make_async_copy(send_ref.at[me], got_ref.at[me], local_sem)
    local.start()
    outgoing = []
    for offset in range(1, count):
        peer = offsets[offset - 1][0](me)
        copy = pltpu.make_async_remote_copy(
            src_ref=send_ref.at[peer],
            dst_ref=got_ref.at[me],
            send_sem=send_sem.at[offset],
            recv_sem=recv_sem.at[offset],
            device_id={axis: peer},
            device_id_type=MESH,
        )
        copy.start()
        outgoing.append(copy)

    piece_width = near_pieces.shape[2]
    chip_shift = (0, chips - 1, 1, 2)

    def piece_index(step):
        piece_core = core if step < 4 else 1 - core
        return lax.rem(chip + chip_shift[step % 4], chips) * 2 + piece_core

    def chunk_copy(step):
        index = piece_index(step)
        return pltpu.make_async_copy(
            wq_hbm.at[pl.ds(pl.multiple_of(index * piece_width, piece_width), piece_width)],
            wq_buf.at[step % 2],
            wq_sem.at[step % 2],
        )

    chunk_copy(0).start()
    q_ref[...] = jnp.zeros_like(q_ref)
    k_ref[...] = jnp.zeros_like(k_ref)
    v_ref[...] = jnp.zeros_like(v_ref)

    def project(step, piece):
        chunk_copy(step).wait()
        if step + 1 < 8:
            chunk_copy(step + 1).start()
        index = piece_index(step)
        rows = pl.ds(pl.multiple_of(index * piece_width, piece_width), piece_width)
        q_ref[...] += jnp.dot(piece, wq_buf[step % 2], preferred_element_type=jnp.float32)
        k_ref[...] += jnp.dot(piece, wk_ref[rows, :], preferred_element_type=jnp.float32)
        v_ref[...] += jnp.dot(piece, wv_ref[rows, :], preferred_element_type=jnp.float32)

    for step in range(3):
        project(step, near_pieces[step])
    for side, source, rows in ((0, left, pl.ds(0, half)), (1, right, pl.ds(half, half))):
        far_out[side].wait_send()
        incoming = pltpu.make_async_remote_copy(
            src_ref=near_pieces.at[1, rows],
            dst_ref=far_piece.at[rows],
            send_sem=far_send.at[side],
            recv_sem=far_recv.at[side],
            device_id={gather_axis: source},
            device_id_type=MESH,
        )
        incoming.wait_recv()
    far_to_partner = pltpu.make_async_remote_copy(
        src_ref=far_piece,
        dst_ref=partner_far,
        send_sem=partner_send.at[1],
        recv_sem=partner_recv.at[1],
        device_id={gather_axis: partner},
        device_id_type=MESH,
    )
    far_to_partner.start()
    project(3, far_piece[...])
    to_partner.wait_send()
    to_partner.wait_recv()
    for step in range(3):
        project(4 + step, partner_near[step])
    far_to_partner.wait_send()
    far_to_partner.wait_recv()
    project(7, partner_far[...])

    for offset in range(1, count):
        outgoing[offset - 1].wait_send()
        source = offsets[offset - 1][1](me)
        incoming = pltpu.make_async_remote_copy(
            src_ref=send_ref.at[source],
            dst_ref=got_ref.at[source],
            send_sem=send_sem.at[offset],
            recv_sem=recv_sem.at[offset],
            device_id={axis: source},
            device_id_type=MESH,
        )
        incoming.wait_recv()
    local.wait()

    slots, slot_rows, width = got_ref.shape
    adapter_rows = jnp.dot(
        place_ref[...], got_ref[...].reshape(slots * slot_rows, width),
        preferred_element_type=jnp.float32,
    )
    cosine = cos_ref[...]
    sines = sin_ref[...]
    half_turn = HD // 2

    def rotated(values):
        return values * cosine + pltpu.roll(values, half_turn, 1) * sines

    for head in range(width // HD):
        lanes = slice(head * HD, (head + 1) * HD)
        summed = q_ref[:, lanes] + adapter_rows[:, lanes]
        queries_ref[:, lanes] = rotated(summed).astype(queries_ref.dtype)
    for head in range(key_ref.shape[1] // HD):
        lanes = slice(head * HD, (head + 1) * HD)
        key_ref[:, lanes] = rotated(k_ref[:, lanes]).astype(key_ref.dtype)
    value_ref[...] = v_ref[...].astype(value_ref.dtype)


def exchange_project(values, near_pieces, w_query, w_key, w_value, place_t, cosine, sines,
                     axis, count, gather_axis, collective):
    unused_item, token_count, piece_width = near_pieces.shape
    vmem = pl.BlockSpec(memory_space=pltpu.VMEM)
    return pl.pallas_call(
        lambda *refs: exchange_project_kernel(axis, count, gather_axis, *refs),
        out_shape=(
            jax.ShapeDtypeStruct((token_count, w_query.shape[1]), jnp.bfloat16),
            jax.ShapeDtypeStruct((token_count, w_key.shape[1]), jnp.bfloat16),
            jax.ShapeDtypeStruct((token_count, w_value.shape[1]), jnp.bfloat16),
        ),
        in_specs=[vmem, vmem, pl.BlockSpec(memory_space=pl.ANY), vmem, vmem, vmem, vmem, vmem],
        out_specs=(vmem, vmem, vmem),
        scratch_shapes=[
            pltpu.VMEM(values.shape, values.dtype),
            pltpu.VMEM((token_count, w_query.shape[1]), jnp.float32),
            pltpu.VMEM((token_count, w_key.shape[1]), jnp.float32),
            pltpu.VMEM((token_count, w_value.shape[1]), jnp.float32),
            pltpu.VMEM((token_count, piece_width), near_pieces.dtype),
            pltpu.VMEM(near_pieces.shape, near_pieces.dtype),
            pltpu.VMEM((token_count, piece_width), near_pieces.dtype),
            pltpu.VMEM((2, piece_width, w_query.shape[1]), w_query.dtype),
            pltpu.SemaphoreType.DMA((count,)),
            pltpu.SemaphoreType.DMA((count,)),
            pltpu.SemaphoreType.DMA(()),
            pltpu.SemaphoreType.DMA((2,)),
            pltpu.SemaphoreType.DMA((2,)),
            pltpu.SemaphoreType.DMA((2,)),
            pltpu.SemaphoreType.DMA((2,)),
            pltpu.SemaphoreType.DMA((2,)),
        ],
        compiler_params=pltpu.CompilerParams(
            collective_id=collective, has_side_effects=True, vmem_limit_bytes=60 * 1024 * 1024
        ),
    )(values, near_pieces, w_query, w_key, w_value, place_t, cosine, sines)


def sum_kernel(axis, count, part_ref, total_ref, held, first_send, first_recv, second_send, second_recv):
    me = lax.axis_index(axis)
    barrier = pltpu.get_barrier_semaphore()
    for offset in range(1, count):
        peer = lax.rem(me + offset, count)
        pl.semaphore_signal(barrier, inc=1, device_id={axis: peer}, device_id_type=MESH)
    pl.semaphore_wait(barrier, count - 1)
    outgoing = []
    for offset in range(1, count):
        peer = lax.rem(me + offset, count)
        copy = pltpu.make_async_remote_copy(
            src_ref=part_ref.at[peer],
            dst_ref=held.at[me],
            send_sem=first_send.at[offset],
            recv_sem=first_recv.at[offset],
            device_id={axis: peer},
            device_id_type=MESH,
        )
        copy.start()
        outgoing.append(copy)
    held[me] = part_ref[me]
    for offset in range(1, count):
        outgoing[offset - 1].wait_send()
        source = lax.rem(me + count - offset, count)
        incoming = pltpu.make_async_remote_copy(
            src_ref=part_ref.at[source],
            dst_ref=held.at[source],
            send_sem=first_send.at[offset],
            recv_sem=first_recv.at[offset],
            device_id={axis: source},
            device_id_type=MESH,
        )
        incoming.wait_recv()
    total = held[0]
    for index in range(1, count):
        total = total + held[index]
    total_ref[me] = total.astype(total_ref.dtype)
    outgoing = []
    for offset in range(1, count):
        peer = lax.rem(me + offset, count)
        copy = pltpu.make_async_remote_copy(
            src_ref=total_ref.at[me],
            dst_ref=total_ref.at[me],
            send_sem=second_send.at[offset],
            recv_sem=second_recv.at[offset],
            device_id={axis: peer},
            device_id_type=MESH,
        )
        copy.start()
        outgoing.append(copy)
    for offset in range(1, count):
        outgoing[offset - 1].wait_send()
        source = lax.rem(me + count - offset, count)
        incoming = pltpu.make_async_remote_copy(
            src_ref=total_ref.at[source],
            dst_ref=total_ref.at[source],
            send_sem=second_send.at[offset],
            recv_sem=second_recv.at[offset],
            device_id={axis: source},
            device_id_type=MESH,
        )
        incoming.wait_recv()


def axis_sum(values, axis, count, collective, out_dtype):
    chunks = values.reshape(count, -1, 128)
    summed = pl.pallas_call(
        lambda *refs: sum_kernel(axis, count, *refs),
        out_shape=jax.ShapeDtypeStruct(chunks.shape, out_dtype),
        in_specs=[pl.BlockSpec(memory_space=pltpu.VMEM)],
        out_specs=pl.BlockSpec(memory_space=pltpu.VMEM),
        scratch_shapes=[
            pltpu.VMEM(chunks.shape, values.dtype),
            pltpu.SemaphoreType.DMA((count,)),
            pltpu.SemaphoreType.DMA((count,)),
            pltpu.SemaphoreType.DMA((count,)),
            pltpu.SemaphoreType.DMA((count,)),
        ],
        compiler_params=pltpu.CompilerParams(collective_id=collective, has_side_effects=True),
    )(chunks)
    return summed.reshape(values.shape)


def owner_adapter_term(received, slot_ids, down_local, up_local):
    sources, rows, part_width = received.shape
    local_adapters, unused_item, adapter_rank = down_local.shape
    query_width = up_local.shape[2]
    token_rows = received.reshape(sources * rows, part_width)
    every_down = jnp.einsum(
        "td,adr->tar", token_rows, down_local, preferred_element_type=jnp.float32
    )
    pick = slot_ids.reshape(sources * rows)[:, None] == jnp.arange(local_adapters, dtype=jnp.int32)[None, :]
    partial_value_sum = jnp.sum(jnp.where(pick[:, :, None], every_down, 0.0), axis=1)
    tp_count = lax.axis_size("tp")
    summed = axis_sum(partial_value_sum.reshape(-1, 128), "tp", tp_count, 2, jnp.bfloat16)
    adapter_middle = summed.reshape(sources * rows, adapter_rank)
    spread_rows = jnp.where(pick[:, :, None], adapter_middle[:, None, :], jnp.zeros((), jnp.bfloat16))
    spread_rows = spread_rows.reshape(sources * rows, local_adapters * adapter_rank)
    adapter_output = jnp.dot(
        spread_rows,
        up_local.reshape(local_adapters * adapter_rank, query_width),
        preferred_element_type=jnp.float32,
    ).astype(jnp.bfloat16)
    return adapter_output.reshape(sources, rows, query_width)


def body(
    tokens,
    adapter_id,
    pool_slot,
    lengths,
    w_query,
    w_key,
    w_value,
    pooled_down_weights,
    pool_up,
    cache_key,
    cache_value,
):
    group_count = lax.axis_size("grp")
    tp_count = lax.axis_size("tp")
    row_count, step_count, part_width = tokens.shape
    local_adapter_rows, unused_item, adapter_rank = pooled_down_weights.shape
    query_width = w_query.shape[1]
    kv_width = w_key.shape[1]
    kv_local = kv_width // HD
    q_local = query_width // HD
    group_size = q_local // kv_local
    count_of_tokens = row_count * step_count
    adapter_span = jnp.arange(pool_slot.shape[0], dtype=jnp.int32)
    pool_pos = jnp.sum(
        jnp.where(adapter_id[:, None] == adapter_span[None, :], pool_slot[None, :], 0), axis=1
    )
    owner_grp = pool_pos // local_adapter_rows
    local_slot = pool_pos % local_adapter_rows
    row_span = jnp.arange(row_count, dtype=jnp.int32)
    same_owner = (owner_grp[:, None] == owner_grp[None, :]) & (row_span[None, :] < row_span[:, None])
    owner_rank = jnp.sum(same_owner.astype(jnp.int32), axis=1)
    send_slot = owner_grp * CAP + owner_rank
    slot_span = jnp.arange(group_count * CAP, dtype=jnp.int32)
    place = (slot_span[:, None] == send_slot[None, :]).astype(jnp.bfloat16)
    token_slot = (send_slot[:, None] * step_count + jnp.arange(step_count, dtype=jnp.int32)[None, :]).reshape(-1)
    token_span = jnp.arange(group_count * CAP * step_count, dtype=jnp.int32)
    place_tokens = (token_span[:, None] == token_slot[None, :]).astype(jnp.bfloat16)
    token_rows = tokens.reshape(count_of_tokens, part_width)
    send_tokens = jnp.dot(place_tokens, token_rows, preferred_element_type=jnp.bfloat16)
    send_tokens = send_tokens.reshape(group_count, CAP * step_count, part_width)
    send_ids = jnp.dot(
        place, local_slot.astype(jnp.bfloat16)[:, None], preferred_element_type=jnp.float32
    ).astype(jnp.bfloat16)
    send_ids = jnp.broadcast_to(send_ids.reshape(group_count, CAP, 1), (group_count, CAP, 128))
    send_ids = jnp.concatenate([send_ids, jnp.zeros_like(send_ids)], axis=1)
    (got_tokens, got_ids), chip_pieces = exchange_ring(
        (send_tokens, send_ids), token_rows, "grp", group_count, "tp", 0
    )
    got_ids = jnp.repeat(got_ids[:, :CAP, 0].astype(jnp.int32), step_count, axis=1)
    owner_out = owner_adapter_term(got_tokens, got_ids, pooled_down_weights, pool_up)
    position = lengths[:, None] + jnp.arange(step_count, dtype=jnp.int32)[None, :]
    half_width = HD // 2
    inv_freq = jnp.exp(
        jnp.arange(half_width, dtype=jnp.float32) * (-2.0 * math.log(rope_base) / HD)
    )
    both_halves = jnp.concatenate([inv_freq, inv_freq])
    turn_sign = jnp.where(jnp.arange(HD, dtype=jnp.int32) < half_width, -1.0, 1.0).astype(jnp.float32)
    angles = position.reshape(count_of_tokens).astype(jnp.float32)[:, None] * both_halves[None, :]
    cosine = jnp.cos(angles)
    sines = jnp.sin(angles) * turn_sign[None, :]
    place_back = (token_slot[:, None] == token_span[None, :]).astype(jnp.bfloat16)
    queries, key_new, value_new = exchange_project(
        owner_out, chip_pieces, w_query, w_key, w_value, place_back, cosine, sines,
        "grp", group_count, "tp", 1
    )
    queries = queries.reshape(row_count, step_count, kv_local, group_size, HD)
    key_new = key_new.reshape(row_count, step_count, kv_local, HD)
    value_new = value_new.reshape(row_count, step_count, kv_local, HD)
    cache_keys = cache_key.reshape(row_count, cache_key.shape[1], kv_local, HD)
    cache_values = cache_value.reshape(row_count, cache_value.shape[1], kv_local, HD)
    combined = attend(queries, key_new, value_new, cache_keys, cache_values, lengths)
    return combined.reshape(row_count, step_count, query_width)


def solution(mesh):
    in_specs = (
        P("grp", None, "tp"),
        P("grp"),
        P(),
        P("grp"),
        P(None, "tp"),
        P(None, "tp"),
        P(None, "tp"),
        P("grp", "tp", None),
        P("grp", None, "tp"),
        P("grp", None, "tp"),
        P("grp", None, "tp"),
    )
    out_specs = P("grp", None, "tp")
    return jax.shard_map(body, mesh=mesh, in_specs=in_specs, out_specs=out_specs, check_vma=False)
```
